32 devices in a mesh: rep: 4 (over y, core), shard: 8 (over z, x).
Axes of the slice: x: 2, y: 2, z: 4, core: 2. Of those that a mesh axis runs over, the one named last changes fastest.
Arguments:
- tokens: bfloat16 [2, 32, 128, 768], P(None, ('rep', 'shard')), may hold values from -6 to 6
- segment_ids: int32 [2, 32, 128], P(None, ('rep', 'shard')), may hold values from 0 to 5, never falling along the last dimension, each value on 1 to 64 neighbouring positions
- cotangent: bfloat16 [2, 32, 128, 768], P(None, ('rep', 'shard')), may hold values from -6 to 6
- first_gain: bfloat16 [768], P('shard'), may hold values from 0.5 to 1.5
- first_shift: bfloat16 [768], P('shard'), may hold values from -1.75 to 1.75
- input_weight: bfloat16 [768, 2304], P('shard'), may hold values from -0.21875 to 0.21875
- input_bias: bfloat16 [2304], P('shard'), may hold values from -1.75 to 1.75
- short_weight: bfloat16 [3, 2304], P(None, 'shard'), may hold values from -3.5 to 3.5
- short_bias: bfloat16 [2304], P('shard'), may hold values from -1.75 to 1.75
- inner_weight: bfloat16 [33, 64], P(None, 'shard'), may hold values from -1 to 1
- inner_bias: bfloat16 [64], P('shard'), may hold values from -3 to 3
- sine_scale: bfloat16 [64], P('shard'), may hold values from 0.59765625 to 1.3984375
- middle_weight: bfloat16 [64, 64], P('shard'), may hold values from -0.75 to 0.75
- middle_bias: bfloat16 [64], P('shard'), may hold values from -3 to 3
- filter_weight: bfloat16 [64, 768], P(None, 'shard'), may hold values from -0.1875 to 0.1875
- direct_gain: bfloat16 [768], P('shard'), may hold values from -3 to 3
- output_weight: bfloat16 [768, 768], P('shard'), may hold values from -0.21875 to 0.21875
- output_bias: bfloat16 [768], P('shard'), may hold values from -1.75 to 1.75
- second_gain: bfloat16 [768], P('shard'), may hold values from 0.5 to 1.5
- second_shift: bfloat16 [768], P('shard'), may hold values from -1.75 to 1.75
- expand_weight: bfloat16 [768, 3072], P('shard'), may hold values from -0.21875 to 0.21875
- expand_bias: bfloat16 [3072], P('shard'), may hold values from -1.75 to 1.75
- contract_weight: bfloat16 [3072, 768], P('shard'), may hold values from -0.109375 to 0.109375
- contract_bias: bfloat16 [768], P('shard'), may hold values from -1.75 to 1.75
Outputs:
- output: bfloat16 [2, 32, 128, 768], P(None, ('rep', 'shard'))
- gradient_tokens: float32 [2, 32, 128, 768], P(None, ('rep', 'shard'))
- gradient_first_gain: float32 [768], P('shard')
- gradient_first_shift: float32 [768], P('shard')
- gradient_input_weight: float32 [768, 2304], P('shard')
- gradient_input_bias: float32 [2304], P('shard')
- gradient_short_weight: float32 [3, 2304], P(None, 'shard')
- gradient_short_bias: float32 [2304], P('shard')
- gradient_inner_weight: float32 [33, 64], P(None, 'shard')
- gradient_inner_bias: float32 [64], P('shard')
- gradient_sine_scale: float32 [64], P('shard')
- gradient_middle_weight: float32 [64, 64], P('shard')
- gradient_middle_bias: float32 [64], P('shard')
- gradient_filter_weight: float32 [64, 768], P(None, 'shard')
- gradient_direct_gain: float32 [768], P('shard')
- gradient_output_weight: float32 [768, 768], P('shard')
- gradient_output_bias: float32 [768], P('shard')
- gradient_second_gain: float32 [768], P('shard')
- gradient_second_shift: float32 [768], P('shard')
- gradient_expand_weight: float32 [768, 3072], P('shard')
- gradient_expand_bias: float32 [3072], P('shard')
- gradient_contract_weight: float32 [3072, 768], P('shard')
- gradient_contract_bias: float32 [768], P('shard')
The draws below stay inside these ranges and needn't reach their ends.
Inputs may be any that keep to these rules, and one draw needn't show every extreme that they name: `segment_ids`: within each sequence the document numbers never fall; each of the 6 numbers covers 1 to 64 consecutive tokens, and one covers exactly 64.
All inputs are finite; a program needn't handle non-finite values.
Results may differ from the reference program's by a relative error of at most 0.0078.
Values may be sent and summed in bfloat16 or wider, within the bound.
A program may use at most 192 MiB of HBM per device.

```python
import math
import jax
import jax.numpy as jnp
import numpy as np
from jax import lax

D = 768
F = 3072
FH = 64
EMB = 33
SEQ = 128
MB = 2
DOCS = 6
P_SIZE = 2304
MOST = 64
SEQS = 32


def shard_levels(own_key, dims, shards, low, largest):
    gain = 1.0
    for dim, blocks in shards:
        draws = jax.random.uniform(jax.random.fold_in(jax.random.fold_in(own_key, 6), dim), (blocks,), jnp.float32, low / len(shards), largest / len(shards))
        gain = gain * jnp.repeat(jnp.exp(draws), dims[dim] // blocks).reshape((-1,) + (1,) * (len(dims) - 1 - dim))
    return gain


def profile(number_of, total, limit, slope):
    loads = [(1 << 20) // math.isqrt(rank ** slope) + 1 for rank in range(2, number_of + 1)]
    rest, counts = total - limit - (number_of - 1), [1] * (number_of - 1)
    while rest > 0:
        candidates = [i for i in range(number_of - 1) if counts[i] < limit]
        mass, budget = sum([loads[i] for i in candidates]), rest
        for i in candidates:
            addition = min(limit - counts[i], max(1, budget * loads[i] // mass), rest)
            counts[i] = counts[i] + addition
            rest = rest - addition
    return np.array([limit] + counts)


def uneven_parts(stream_key, count, total, reach, skew):
    if count == 2:
        one = jax.random.randint(stream_key, (), max(1, total - reach), min(reach, total - 1) + 1)
        return jnp.stack([one, total - one])
    lengths = jnp.asarray(profile(count, total, reach, skew), jnp.int32)
    pairs = (count - 1) // 2
    source_of, taker = lengths[1:1 + 2 * pairs:2], lengths[2:2 + 2 * pairs:2]
    slack = jnp.minimum(source_of - 1, reach - taker)
    passed = jax.random.randint(jax.random.fold_in(stream_key, 1), (pairs,), 0, 1 << 20) % (slack + 1)
    lengths = lengths.at[1:1 + 2 * pairs:2].set(source_of - passed).at[2:2 + 2 * pairs:2].set(taker + passed)
    return lengths[jax.random.permutation(jax.random.fold_in(stream_key, 2), count)]


def centred(stream_key, extent, scale, most, cuts=(), held_as=jnp.bfloat16):
    values = jax.random.normal(stream_key, extent, jnp.float32) * scale
    if len(cuts) > 0:
        values = shard_levels(stream_key, extent, cuts, -0.22, 0.18) * values
    return jnp.clip(values, min=-most, max=most).astype(held_as)


def setup_inputs(seed: int = 0) -> dict:
    seeds = jax.random.split(jax.random.key(seed), 25)
    return {
        "tokens": centred(seeds[0], (MB, SEQS, SEQ, D), 1.0, 6.0, ((1, 32),)),
        "segment_ids": jax.vmap(lambda own: jnp.searchsorted(jnp.cumsum(uneven_parts(own, DOCS, SEQ, MOST, 2)), jnp.arange(SEQ), side="right"))(jax.random.split(seeds[1], MB * SEQS)).reshape((MB, SEQS, SEQ)).astype(jnp.int32),
        "cotangent": centred(seeds[2], (MB, SEQS, SEQ, D), 1.0, 6.0, ((1, 32),)),
        "first_gain": jnp.clip(1.0 + 0.1 * jax.random.normal(seeds[3], (D,), jnp.float32), 0.5, 1.5).astype(jnp.bfloat16),
        "first_shift": centred(seeds[4], (D,), 0.3, 1.75, ((0, 8),)),
        "input_weight": centred(seeds[5], (D, P_SIZE), D ** -0.5, 0.21875, ((0, 8),)),
        "input_bias": centred(seeds[6], (P_SIZE,), 0.3, 1.75, ((0, 8),)),
        "short_weight": centred(seeds[7], (3, P_SIZE), 0.6, 3.5, ((1, 8),)),
        "short_bias": centred(seeds[8], (P_SIZE,), 0.3, 1.75, ((0, 8),)),
        "inner_weight": centred(seeds[9], (EMB, FH), EMB ** -0.5, 1.0, ((1, 8),)),
        "inner_bias": centred(seeds[10], (FH,), 0.5, 3.0, ((0, 8),)),
        "sine_scale": jnp.clip(1.0 + 0.08 * jax.random.normal(seeds[11], (FH,), jnp.float32), 0.59765625, 1.3984375).astype(jnp.bfloat16),
        "middle_weight": centred(seeds[12], (FH, FH), FH ** -0.5, 0.75, ((0, 8),)),
        "middle_bias": centred(seeds[13], (FH,), 0.5, 3.0, ((0, 8),)),
        "filter_weight": centred(seeds[14], (FH, D), (8 * SEQ) ** -0.5, 0.1875, ((1, 8),)),
        "direct_gain": centred(seeds[15], (D,), 0.5, 3.0, ((0, 8),)),
        "output_weight": centred(seeds[16], (D, D), D ** -0.5, 0.21875, ((0, 8),)),
        "output_bias": centred(seeds[17], (D,), 0.3, 1.75, ((0, 8),)),
        "second_gain": jnp.clip(1.0 + 0.1 * jax.random.normal(seeds[18], (D,), jnp.float32), 0.5, 1.5).astype(jnp.bfloat16),
        "second_shift": centred(seeds[19], (D,), 0.3, 1.75, ((0, 8),)),
        "expand_weight": centred(seeds[20], (D, F), D ** -0.5, 0.21875, ((0, 8),)),
        "expand_bias": centred(seeds[21], (F,), 0.3, 1.75, ((0, 8),)),
        "contract_weight": centred(seeds[22], (F, D), F ** -0.5, 0.109375, ((0, 8),)),
        "contract_bias": centred(seeds[23], (D,), 0.3, 1.75, ((0, 8),)),
    }


EPSILON = 1e-05
HIGHEST = lax.Precision.HIGHEST

@jax.custom_vjp
def low(v):
    return lax.optimization_barrier(v.astype(jnp.bfloat16)).astype(jnp.float32)

@jax.custom_vjp
def low_back(v):
    return v

def low_keep(v):
    return (low(v), None)

def low_pass(kept, grad):
    return (grad,)

def back_keep(v):
    return (v, None)

def back_low(kept, grad):
    return (low(grad),)
low.defvjp(low_keep, low_pass)
low_back.defvjp(back_keep, back_low)

def positions(length):
    places = jnp.arange(length, dtype=jnp.float32)
    linear_ramp = places / (length - 1)
    angles = 2.0 * math.pi * places / length
    scales = 0.0001 + jnp.arange(16, dtype=jnp.float32) * ((15.0 - 0.0001) / 15.0)
    phases = angles[:, None] * scales[None, :]
    return jnp.concatenate([linear_ramp[:, None], jnp.cos(phases), -jnp.sin(phases)], axis=1)

def decay_table(length, width):
    linear_ramp = jnp.arange(length, dtype=jnp.float32) / (length - 1)
    rates = math.log(100.0) * (1.0 / 1.5 + (1.0 / 0.3 - 1.0 / 1.5) * jnp.arange(width, dtype=jnp.float32) / (width - 1))
    return jnp.exp(-linear_ramp[:, None] * rates[None, :])

def filter_taps(inner_weight, inner_bias, sine_scale, middle_weight, middle_bias, filter_weight, length):
    features = positions(length)
    first_sine = jnp.sin(sine_scale * (jnp.dot(features, inner_weight, precision=HIGHEST) + inner_bias))
    second_sine = jnp.sin(sine_scale * (jnp.dot(first_sine, middle_weight, precision=HIGHEST) + middle_bias))
    return jnp.dot(second_sine, filter_weight, precision=HIGHEST) * decay_table(length, filter_weight.shape[1])

def normalize(values, gain_row, shift_row):
    center = values - lax.optimization_barrier(jnp.mean(values, axis=-1, keepdims=True))
    spread = lax.optimization_barrier(jnp.mean(center * center, axis=-1, keepdims=True))
    return center * lax.rsqrt(spread + EPSILON) * gain_row + shift_row

def smooth_gate(values):
    return jax.nn.gelu(values, approximate=True)

def short_filter(projected, segments, weight, offset):
    running = offset + weight[0] * projected
    for step_back in (1, 2):
        moved_rows = jnp.concatenate([jnp.zeros_like(projected[:, :step_back]), projected[:, :-step_back]], axis=1)
        moved_ids = jnp.concatenate([jnp.full_like(segments[:, :step_back], -1), segments[:, :-step_back]], axis=1)
        same_doc = (moved_ids == segments).astype(projected.dtype)
        running = running + weight[step_back] * moved_rows * same_doc[:, :, None]
    return running

def long_filter(carried, segments, kernel):
    length = carried.shape[1]
    padded_size = 2 * length
    spectrum = jnp.fft.rfft(kernel, n=padded_size, axis=0)
    membership = (segments[:, None, :] == jnp.arange(DOCS, dtype=jnp.int32)[None, :, None]).astype(jnp.float32)
    pieces = jnp.fft.rfft(carried[:, None, :, :] * membership[:, :, :, None], n=padded_size, axis=2)
    result = jnp.fft.irfft(pieces * spectrum[None, None], n=padded_size, axis=2)[:, :, :length]
    return lax.optimization_barrier(jnp.sum(result * membership[:, :, :, None], axis=1))

def forward(weights, token_rows, segments):
    first_gain, first_shift, input_weight, input_bias, short_weight, short_bias, inner_weight, inner_bias, sine_scale, middle_weight, middle_bias, filter_weight, direct_gain, output_weight, output_bias, second_gain, second_shift, expand_weight, expand_bias, contract_weight, contract_bias = weights
    width = token_rows.shape[-1]
    length = token_rows.shape[1]
    normed_first = low(normalize(token_rows, first_gain, first_shift))
    projected = low_back(jnp.einsum('gtd,dp->gtp', normed_first, input_weight, precision=HIGHEST) + input_bias)
    short_out = short_filter(projected, segments, short_weight, short_bias)
    gate_out = short_out[:, :, :width]
    gate_in = short_out[:, :, width:2 * width]
    values = short_out[:, :, 2 * width:]
    carried = values * gate_in
    kernel = filter_taps(inner_weight, inner_bias, sine_scale, middle_weight, middle_bias, filter_weight, length)
    convolved = long_filter(carried, segments, kernel) + direct_gain * carried
    gated_low = low(convolved * gate_out)
    mixed_out = low_back(jnp.einsum('gtd,de->gte', gated_low, output_weight, precision=HIGHEST) + output_bias)
    residual = token_rows + mixed_out
    normed_second = low(normalize(residual, second_gain, second_shift))
    hidden_pre = low_back(jnp.einsum('gtd,df->gtf', normed_second, expand_weight, precision=HIGHEST) + expand_bias)
    hidden_post = low(smooth_gate(hidden_pre))
    return residual + jnp.einsum('gtf,fd->gtd', hidden_post, contract_weight, precision=HIGHEST) + contract_bias

def reference(tokens, segment_ids, cotangent, first_gain, first_shift, input_weight, input_bias, short_weight, short_bias, inner_weight, inner_bias, sine_scale, middle_weight, middle_bias, filter_weight, direct_gain, output_weight, output_bias, second_gain, second_shift, expand_weight, expand_bias, contract_weight, contract_bias):
    weights = tuple((member.astype(jnp.float32) for member in (first_gain, first_shift, input_weight, input_bias, short_weight, short_bias, inner_weight, inner_bias, sine_scale, middle_weight, middle_bias, filter_weight, direct_gain, output_weight, output_bias, second_gain, second_shift, expand_weight, expand_bias, contract_weight, contract_bias)))
    group_size = math.gcd(MB * SEQS, max(1, 4096 // SEQ))
    group_count = MB * SEQS // group_size
    token_groups = tokens.astype(jnp.float32).reshape(group_count, group_size, SEQ, D)
    segment_groups = segment_ids.astype(jnp.int32).reshape(group_count, group_size, SEQ)
    cotangent_groups = cotangent.astype(jnp.float32).reshape(group_count, group_size, SEQ, D)

    def accumulate(totals, batch_parts):
        token_part, segment_part, cotangent_part = batch_parts
        group_out, pull_back = jax.vjp(lambda weight_set, rows_in: forward(weight_set, rows_in, segment_part), weights, token_part)
        weight_deltas, token_deltas = pull_back(cotangent_part)
        totals = jax.tree.map(jnp.add, totals, weight_deltas)
        return (totals, (group_out.astype(jnp.bfloat16), token_deltas))
    starting = tuple((jnp.zeros_like(member) for member in weights))
    totals, (outputs, token_deltas) = lax.scan(accumulate, starting, (token_groups, segment_groups, cotangent_groups))
    output = outputs.reshape(MB, SEQS, SEQ, D)
    gradient_tokens = token_deltas.reshape(MB, SEQS, SEQ, D)
    return (output, gradient_tokens, totals[0], totals[1], totals[2], totals[3], totals[4], totals[5], totals[6], totals[7], totals[8], totals[9], totals[10], totals[11], totals[12], totals[13], totals[14], totals[15], totals[16], totals[17], totals[18], totals[19], totals[20])
```

```python
import math

import jax
import jax.numpy as jnp
from jax import lax
from jax.sharding import PartitionSpec as P
from jax.experimental import pallas as pl
from jax.experimental.pallas import tpu as pltpu

DOCS = 6


EPSILON = 1e-05
HIGHEST = lax.Precision.HIGHEST


def positions(length):
    places = jnp.arange(length, dtype=jnp.float32)
    linear_ramp = places / (length - 1)
    angles = 2.0 * math.pi * places / length
    scales = 0.0001 + jnp.arange(16, dtype=jnp.float32) * ((15.0 - 0.0001) / 15.0)
    phases = angles[:, None] * scales[None, :]
    return jnp.concatenate([linear_ramp[:, None], jnp.cos(phases), -jnp.sin(phases)], axis=1)


def decay_table(length, width):
    linear_ramp = jnp.arange(length, dtype=jnp.float32) / (length - 1)
    rates = math.log(100.0) * (
        1.0 / 1.5 + (1.0 / 0.3 - 1.0 / 1.5) * jnp.arange(width, dtype=jnp.float32) / (width - 1)
    )
    return jnp.exp(-linear_ramp[:, None] * rates[None, :])


def filter_taps(
    inner_weight, inner_bias, sine_scale, middle_weight, middle_bias, filter_weight, length
):
    features = positions(length)
    first_sine = jnp.sin(
        sine_scale * (jnp.dot(features, inner_weight, precision=HIGHEST) + inner_bias)
    )
    second_sine = jnp.sin(
        sine_scale * (jnp.dot(first_sine, middle_weight, precision=HIGHEST) + middle_bias)
    )
    return jnp.dot(second_sine, filter_weight, precision=HIGHEST) * decay_table(
        length, filter_weight.shape[1]
    )


def normalize(values, gain_row, shift_row):
    center = values - jnp.mean(values, axis=-1, keepdims=True)
    spread = jnp.mean(center * center, axis=-1, keepdims=True)
    return center * lax.rsqrt(spread + EPSILON) * gain_row + shift_row


def smooth_gate(values):
    return jax.nn.gelu(values, approximate=True)


def to_float(member):
    return member.astype(jnp.float32)


def short_filter(projected, segments, weight, offset):
    running = offset + weight[0] * projected
    for step_back in (1, 2):
        moved_rows = jnp.concatenate(
            [jnp.zeros_like(projected[:, :step_back]), projected[:, :-step_back]], axis=1
        )
        moved_ids = jnp.concatenate(
            [jnp.full_like(segments[:, :step_back], -1), segments[:, :-step_back]], axis=1
        )
        same_doc = (moved_ids == segments).astype(projected.dtype)
        running = running + weight[step_back] * moved_rows * same_doc[:, :, None]
    return running


def wave_tables(length):
    padded_size = 2 * length
    freq_index = jnp.arange(length + 1, dtype=jnp.int32)
    place_index = jnp.arange(length, dtype=jnp.int32)
    wrapped = freq_index[:, None] * place_index[None, :] % padded_size
    angles = 2.0 * math.pi / padded_size * wrapped.astype(jnp.float32)
    weights_row = (
        jnp.where((freq_index == 0) | (freq_index == length), 1.0, 2.0).astype(jnp.float32)
        / padded_size
    )
    return (jnp.cos(angles), jnp.sin(angles), weights_row)


def spectrum(tables, signal):
    cosine, sine, weights_row = tables
    real_part = jnp.einsum("ft,...td->...fd", cosine, signal, precision=HIGHEST)
    imag_part = -jnp.einsum("ft,...td->...fd", sine, signal, precision=HIGHEST)
    return (real_part, imag_part)


def inverse(tables, real_part, imag_part):
    cosine, sine, weights_row = tables
    scaled_real = real_part * weights_row[:, None]
    scaled_imag = imag_part * weights_row[:, None]
    return jnp.einsum("ft,...fd->...td", cosine, scaled_real, precision=HIGHEST) - jnp.einsum(
        "ft,...fd->...td", sine, scaled_imag, precision=HIGHEST
    )


MESH_ID = pl.DeviceIdType.MESH
HALF = 48
WIDE = 768
GATHER_CHUNKS = (
    (0, 0, 0, True),
    (0, 0, 768, True),
    (0, 0, 1536, True),
    (1, 0, 0, True),
    (2, 0, 0, True),
    (3, 0, 0, False),
    (2, 1, 0, True),
    (3, 0, 768, False),
    (2, 2, 0, True),
    (3, 0, 1536, False),
    (2, 3, 0, True),
    (3, 0, 2304, False),
)
REDUCE_CHUNKS = (
    (2, 0, 0, True),
    (2, 1, 0, False),
    (2, 2, 0, True),
    (2, 3, 0, False),
    (3, 0, 0, True),
    (3, 0, 768, False),
    (3, 0, 1536, True),
    (3, 0, 2304, False),
    (1, 0, 0, True),
    (0, 0, 0, False),
    (0, 0, 768, True),
    (0, 0, 1536, False),
)


def place():
    rep = lax.axis_index("rep")
    shard = lax.axis_index("shard")
    return rep, shard, rep // 2, rep % 2, shard // 2, shard % 2


def enter(targets):
    barrier = pltpu.get_barrier_semaphore()
    for target in targets:
        pl.semaphore_signal(barrier, inc=1, device_id=target, device_id_type=MESH_ID)
    pl.semaphore_wait(barrier, len(targets))


def gather_kernel(
    small_ref, in0, in1, in2, in3, small_full, full0, full1, full2, full3,
    send_sem, recv_sem, small_send, small_recv, own_sem,
):
    rep, shard, y, c, z, x = place()
    shards = (in0, in1, in2, in3)
    fulls = (full0, full1, full2, full3)
    across_x = (rep, z * 2 + (1 - x))
    across_y = ((1 - y) * 2 + c, shard)
    across_c = (y * 2 + (1 - c), shard)

    def along_z(step):
        return (rep, ((z + step) % 4) * 2 + x)

    group = [(rep, (shard + step) % 8) for step in range(1, 8)]
    enter(group + [across_y, across_c])

    def source_of(j):
        if j < 3:
            return ((z + 3 - j) % 4) * 2 + x
        if j == 3:
            return z * 2 + (1 - x)
        return ((z + 7 - j) % 4) * 2 + (1 - x)

    def region(ref, chunk, row, half, quarter):
        matrix, block, column, split = chunk
        start = pl.multiple_of(row + block * 96 + half * HALF, 16)
        if split:
            columns = pl.ds(pl.multiple_of(column + quarter * (WIDE // 2), 128), WIDE // 2)
        else:
            columns = pl.ds(column, WIDE)
        return ref.at[pl.ds(start, HALF), columns]

    def landed(chunk, j, half, quarter):
        matrix = chunk[0]
        depth = shards[matrix].shape[0]
        return region(fulls[matrix], chunk, source_of(j) * depth, half, quarter)

    def copy(index, slot, source, target_ref, device):
        return pltpu.make_async_remote_copy(
            src_ref=source, dst_ref=target_ref,
            send_sem=send_sem.at[index, slot], recv_sem=recv_sem.at[index, slot],
            device_id=device, device_id_type=MESH_ID,
        )

    started = []
    for step in range(1, 8):
        out = pltpu.make_async_remote_copy(
            src_ref=small_ref, dst_ref=small_full.at[shard],
            send_sem=small_send.at[step - 1], recv_sem=small_recv.at[step - 1],
            device_id=group[step - 1], device_id_type=MESH_ID,
        )
        out.start()
        started.append(out)
    locals_ = [pltpu.make_async_copy(small_ref, small_full.at[shard], own_sem.at[4])]
    for matrix in range(4):
        depth = shards[matrix].shape[0]
        locals_.append(
            pltpu.make_async_copy(
                shards[matrix],
                fulls[matrix].at[pl.ds(pl.multiple_of(shard * depth, 16), depth)],
                own_sem.at[matrix],
            )
        )
    for item in locals_:
        item.start()

    def begin(index, slot, source, target_ref, device):
        out = copy(index, slot, source, target_ref, device)
        out.start()
        started.append(out)

    def arrive(index, slot, target_ref):
        copy(index, slot, target_ref, target_ref, across_c).wait_recv()

    chunks = GATHER_CHUNKS
    count = len(chunks)

    def first(index):
        chunk = chunks[index]
        matrix = chunk[0]
        depth = shards[matrix].shape[0]
        own = region(shards[matrix], chunk, 0, c, y)
        target_ref = region(fulls[matrix], chunk, shard * depth, c, y)
        for step in range(1, 4):
            begin(index, step - 1, own, target_ref, along_z(step))
        begin(index, 3, own, target_ref, across_x)

    def pass_on(index, j):
        chunk = chunks[index]
        piece = landed(chunk, j, c, y)
        if j < 3:
            begin(index, 4 + j, piece, piece, across_x)
        if chunk[3]:
            begin(index, 7 + j, piece, piece, across_y)
        begin(index, 14 + j, piece, piece, across_c)

    def second(index):
        for j in range(4):
            arrive(index, j, landed(chunks[index], j, c, y))
            pass_on(index, j)

    def third(index):
        for j in range(4, 7):
            arrive(index, j, landed(chunks[index], j, c, y))
            pass_on(index, j)

    def fourth(index):
        if chunks[index][3]:
            for j in range(7):
                piece = landed(chunks[index], j, c, 1 - y)
                arrive(index, 7 + j, piece)
                begin(index, 21 + j, piece, piece, across_c)

    ahead = 3
    for index in range(min(ahead, count)):
        first(index)
    for step in range(count + 2):
        if step + ahead < count:
            first(step + ahead)
        if step < count:
            second(step)
        if 0 <= step - 1 < count:
            third(step - 1)
        if 0 <= step - 2 < count:
            fourth(step - 2)
    for index in range(count):
        for j in range(7):
            arrive(index, 14 + j, landed(chunks[index], j, 1 - c, y))
            if chunks[index][3]:
                arrive(index, 21 + j, landed(chunks[index], j, 1 - c, 1 - y))
    for step in range(1, 8):
        pltpu.make_async_remote_copy(
            src_ref=small_ref, dst_ref=small_full.at[(shard + 8 - step) % 8],
            send_sem=small_send.at[step - 1], recv_sem=small_recv.at[step - 1],
            device_id=group[step - 1], device_id_type=MESH_ID,
        ).wait_recv()
    for out in started:
        out.wait_send()
    for item in locals_:
        item.wait()


def gather_weights(small, shards):
    count = len(GATHER_CHUNKS)
    fulls = [
        jax.ShapeDtypeStruct((8 * member.shape[0], member.shape[1]), member.dtype)
        for member in shards
    ]
    return pl.pallas_call(
        gather_kernel,
        out_shape=[jax.ShapeDtypeStruct((8,) + small.shape, small.dtype)] + fulls,
        in_specs=[pl.BlockSpec(memory_space=pltpu.VMEM)] * 5,
        out_specs=[pl.BlockSpec(memory_space=pl.ANY)] * 5,
        scratch_shapes=[
            pltpu.SemaphoreType.DMA((count, 28)),
            pltpu.SemaphoreType.DMA((count, 28)),
            pltpu.SemaphoreType.DMA((7,)),
            pltpu.SemaphoreType.DMA((7,)),
            pltpu.SemaphoreType.DMA((5,)),
        ],
        compiler_params=pltpu.CompilerParams(collective_id=0, has_side_effects=True),
    )(small, *shards)


def reduce_kernel(
    small_ref, in0, in1, in2, in3, small_out, out0, out1, out2, out3,
    core_buf, y_buf, x_split, x_whole, z_split, z_whole, end_split, end_whole,
    small_group, small_rep, send_sem, recv_sem, small_send, small_recv,
):
    rep, shard, y, c, z, x = place()
    grads = (in0, in1, in2, in3)
    outs = (out0, out1, out2, out3)
    across_x = (rep, z * 2 + (1 - x))
    across_y = ((1 - y) * 2 + c, shard)
    across_c = (y * 2 + (1 - c), shard)

    def along_z(step):
        return (rep, ((z + step) % 4) * 2 + x)

    group = [(rep, (shard + step) % 8) for step in range(1, 8)]
    reps = [((rep + step) % 4, shard) for step in range(1, 4)]
    enter(group + reps)

    chunks = REDUCE_CHUNKS
    count = len(chunks)
    split_index = []
    seen = [0, 0]
    for chunk in chunks:
        split_index.append(seen[0] if chunk[3] else seen[1])
        seen[0 if chunk[3] else 1] += 1

    started = []

    def copy(index, slot, source, target_ref, device):
        return pltpu.make_async_remote_copy(
            src_ref=source, dst_ref=target_ref,
            send_sem=send_sem.at[index, slot], recv_sem=recv_sem.at[index, slot],
            device_id=device, device_id_type=MESH_ID,
        )

    def begin(index, slot, source, target_ref, device):
        out = copy(index, slot, source, target_ref, device)
        out.start()
        started.append(out)

    def arrive(index, slot, target_ref):
        copy(index, slot, target_ref, target_ref, across_c).wait_recv()

    def columns_of(chunk):
        return pl.ds(chunk[2], WIDE)

    def quarter_columns(quarter):
        return pl.ds(pl.multiple_of(quarter * (WIDE // 2), 128), WIDE // 2)

    def small_copy(kind, step, source, target_ref, device):
        return pltpu.make_async_remote_copy(
            src_ref=source, dst_ref=target_ref,
            send_sem=small_send.at[kind + step - 1], recv_sem=small_recv.at[kind + step - 1],
            device_id=device, device_id_type=MESH_ID,
        )

    for step in range(1, 8):
        out = small_copy(0, step, small_ref.at[(shard + step) % 8], small_group.at[step - 1], group[step - 1])
        out.start()
        started.append(out)

    def stage_core(index):
        chunk = chunks[index]
        source = grads[chunk[0]].at[:, :, chunk[1], 1 - c, :, columns_of(chunk)]
        begin(index, 0, source, core_buf.at[index], across_c)

    def add_core(index):
        chunk = chunks[index]
        arrive(index, 0, core_buf.at[index])

        def body(position, carry):
            own = grads[chunk[0]][position // 2, position % 2, chunk[1], c, :, columns_of(chunk)]
            other = core_buf[index, position // 2, position % 2]
            core_buf[index, position // 2, position % 2] = (
                own.astype(jnp.float32) + other.astype(jnp.float32)
            ).astype(jnp.bfloat16)
            return carry

        lax.fori_loop(0, 8, body, 0)
        if chunk[3]:
            source = core_buf.at[index, :, :, :, quarter_columns(1 - y)]
            begin(index, 1, source, y_buf.at[split_index[index]], across_y)
        else:
            begin(index, 2, core_buf.at[index, :, 1 - x], x_whole.at[split_index[index]], across_x)

    def add_y(index):
        chunk = chunks[index]
        if not chunk[3]:
            return
        slot = split_index[index]
        arrive(index, 1, y_buf.at[slot])

        def body(position, carry):
            own = core_buf[index, position // 2, position % 2, :, quarter_columns(y)]
            other = y_buf[slot, position // 2, position % 2]
            y_buf[slot, position // 2, position % 2] = (
                own.astype(jnp.float32) + other.astype(jnp.float32)
            ).astype(jnp.bfloat16)
            return carry

        lax.fori_loop(0, 8, body, 0)
        begin(index, 2, y_buf.at[slot, :, 1 - x], x_split.at[slot], across_x)

    def add_x(index):
        chunk = chunks[index]
        slot = split_index[index]
        landing = x_split if chunk[3] else x_whole
        arrive(index, 2, landing.at[slot])
        ends = z_split if chunk[3] else z_whole
        for step in (1, 2, 3, 0):
            row = (z + step) % 4
            if chunk[3]:
                own = y_buf[slot, row, x]
            else:
                own = core_buf[index, row, x]
            landing[slot, row] = (
                own.astype(jnp.float32) + landing[slot, row].astype(jnp.float32)
            ).astype(jnp.bfloat16)
            if step > 0:
                begin(index, 2 + step, landing.at[slot, row], ends.at[slot, step - 1], along_z(step))

    def add_z(index):
        chunk = chunks[index]
        slot = split_index[index]
        landing = x_split if chunk[3] else x_whole
        ends = z_split if chunk[3] else z_whole
        last = end_split if chunk[3] else end_whole
        total = landing[slot, z].astype(jnp.float32)
        for step in range(1, 4):
            arrive(index, 2 + step, ends.at[slot, step - 1])
            total = total + ends[slot, step - 1].astype(jnp.float32)
        last[slot, 0] = total.astype(jnp.bfloat16)
        begin(index, 6, last.at[slot, 0], last.at[slot, 1], across_y)

    def finish(index):
        chunk = chunks[index]
        matrix, block, column, split = chunk
        slot = split_index[index]
        last = end_split if split else end_whole
        arrive(index, 6, last.at[slot, 1])
        out = outs[matrix]
        if split:
            own_columns = pl.ds(pl.multiple_of(column + y * (WIDE // 2), 128), WIDE // 2)
            other_columns = pl.ds(pl.multiple_of(column + (1 - y) * (WIDE // 2), 128), WIDE // 2)
            out[block, c, :, own_columns] = last[slot, 0].astype(jnp.float32)
            out[block, c, :, other_columns] = last[slot, 1].astype(jnp.float32)
        else:
            out[block, c, :, columns_of(chunk)] = last[slot, 0].astype(jnp.float32) + last[
                slot, 1
            ].astype(jnp.float32)
        piece = out.at[block, c, :, columns_of(chunk)]
        begin(index, 7, piece, piece, across_c)

    ahead = 3
    for index in range(min(ahead, count)):
        stage_core(index)
    for step in range(count + 4):
        if step + ahead < count:
            stage_core(step + ahead)
        if step < count:
            add_core(step)
        if 0 <= step - 1 < count:
            add_y(step - 1)
        if 0 <= step - 2 < count:
            add_x(step - 2)
        if 0 <= step - 3 < count:
            add_z(step - 3)
        if 0 <= step - 4 < count:
            finish(step - 4)
        if step == 2:
            partial = small_ref[shard]
            for hop in range(1, 8):
                small_copy(0, hop, small_group.at[hop - 1], small_group.at[hop - 1], group[hop - 1]).wait_recv()
                partial = partial + small_group[hop - 1]
            small_rep[rep] = partial
            for hop in range(1, 4):
                out = small_copy(7, hop, small_rep.at[rep], small_rep.at[rep], reps[hop - 1])
                out.start()
                started.append(out)
    for hop in range(1, 4):
        landing = small_rep.at[(rep + 4 - hop) % 4]
        small_copy(7, hop, landing, landing, reps[hop - 1]).wait_recv()
    small_out[...] = small_rep[0] + small_rep[1] + small_rep[2] + small_rep[3]
    for index in range(count):
        chunk = chunks[index]
        arrive(index, 7, outs[chunk[0]].at[chunk[1], 1 - c, :, columns_of(chunk)])
    for out in started:
        out.wait_send()


def reduce_gradients(small, grads):
    count = len(REDUCE_CHUNKS)
    splits = sum(1 for chunk in REDUCE_CHUNKS if chunk[3])
    wholes = count - splits
    half = WIDE // 2
    low = jnp.bfloat16
    views = []
    shapes = []
    for member in grads:
        rows, columns = member.shape
        blocks = rows // (8 * 96)
        views.append(member.reshape(4, 2, blocks, 2, HALF, columns))
        shapes.append(jax.ShapeDtypeStruct((blocks, 2, HALF, columns), jnp.float32))
    results = pl.pallas_call(
        reduce_kernel,
        out_shape=[jax.ShapeDtypeStruct(small.shape[1:], jnp.float32)] + shapes,
        in_specs=[pl.BlockSpec(memory_space=pltpu.VMEM)] * 5,
        out_specs=[pl.BlockSpec(memory_space=pltpu.VMEM)] * 5,
        scratch_shapes=[
            pltpu.VMEM((count, 4, 2, HALF, WIDE), low),
            pltpu.VMEM((splits, 4, 2, HALF, half), low),
            pltpu.VMEM((splits, 4, HALF, half), low),
            pltpu.VMEM((wholes, 4, HALF, WIDE), low),
            pltpu.VMEM((splits, 3, HALF, half), low),
            pltpu.VMEM((wholes, 3, HALF, WIDE), low),
            pltpu.VMEM((splits, 2, HALF, half), low),
            pltpu.VMEM((wholes, 2, HALF, WIDE), low),
            pltpu.VMEM((7,) + small.shape[1:], jnp.float32),
            pltpu.VMEM((4,) + small.shape[1:], jnp.float32),
            pltpu.SemaphoreType.DMA((count, 8)),
            pltpu.SemaphoreType.DMA((count, 8)),
            pltpu.SemaphoreType.DMA((10,)),
            pltpu.SemaphoreType.DMA((10,)),
        ],
        compiler_params=pltpu.CompilerParams(
            collective_id=1, has_side_effects=True, vmem_limit_bytes=60 * 1024 * 1024
        ),
    )(small, *views)
    flat = [
        member.reshape(member.shape[0] * 2 * HALF, member.shape[3]) for member in results[1:]
    ]
    return results[0], flat


def blocked(values, start, size):
    return lax.slice_in_dim(values, start, start + size, axis=0)


def shifted_down(values, lag):
    if lag == 0:
        return values
    return pltpu.roll(values, lag, 0)


def conv_forward_kernel(carried_ref, place_ref, taps_ref, out_ref):
    lags = taps_ref.shape[0]
    carried = carried_ref[0]
    length = carried.shape[0]
    places = jnp.broadcast_to(place_ref[0], carried.shape)
    total = jnp.zeros_like(carried)
    for low_lag in range(8):
        turned = shifted_down(carried, low_lag)
        for high in range(lags // 8):
            lag = high * 8 + low_lag
            skip = high * 8
            tap = jnp.broadcast_to(taps_ref[lag : lag + 1, :], (length - skip, carried.shape[1]))
            term = jnp.where(
                blocked(places, skip, length - skip) >= lag,
                tap * blocked(turned, 0, length - skip),
                0.0,
            )
            if skip:
                total = jnp.concatenate(
                    [blocked(total, 0, skip), blocked(total, skip, length - skip) + term], axis=0
                )
            else:
                total = total + term
    out_ref[0] = total


def conv_backward_kernel(
    grad_ref, carried_ref, place_ref, left_ref, taps_ref, out_ref, taps_out_ref
):
    lags = taps_ref.shape[0]
    grad = grad_ref[0]
    carried = carried_ref[0]
    length = carried.shape[0]
    lanes = carried.shape[1]
    places = jnp.broadcast_to(place_ref[0], carried.shape)
    left = jnp.broadcast_to(left_ref[0], carried.shape)
    total = jnp.zeros_like(carried)
    first = pl.program_id(1) == 0

    @pl.when(first)
    def _():
        taps_out_ref[...] = jnp.zeros_like(taps_out_ref)

    for low_lag in range(8):
        turned = grad if low_lag == 0 else pltpu.roll(grad, length - low_lag, 0)
        for high in range(lags // 8):
            lag = high * 8 + low_lag
            skip = high * 8
            size = length - skip
            tap = jnp.broadcast_to(taps_ref[lag : lag + 1, :], (size, lanes))
            moved = jnp.where(
                blocked(left, 0, size) >= lag, blocked(turned, skip, size), 0.0
            )
            term = tap * moved
            if skip:
                total = jnp.concatenate(
                    [blocked(total, 0, size) + term, blocked(total, size, skip)], axis=0
                )
            else:
                total = total + term
            product = moved * blocked(carried, 0, size)
            taps_out_ref[lag : lag + 1, :] += jnp.sum(product, axis=0, keepdims=True)
    out_ref[0] = total


def conv_forward(carried, places, taps):
    count, length, width = carried.shape
    lags = taps.shape[0]
    return pl.pallas_call(
        conv_forward_kernel,
        grid=(width // 128, count),
        in_specs=[
            pl.BlockSpec((1, length, 128), lambda j, i: (i, 0, j)),
            pl.BlockSpec((1, length, 1), lambda j, i: (i, 0, 0)),
            pl.BlockSpec((lags, 128), lambda j, i: (0, j)),
        ],
        out_specs=pl.BlockSpec((1, length, 128), lambda j, i: (i, 0, j)),
        out_shape=jax.ShapeDtypeStruct(carried.shape, jnp.float32),
    )(carried, places, taps)


def conv_backward(grad, carried, places, left, taps):
    count, length, width = carried.shape
    lags = taps.shape[0]
    return pl.pallas_call(
        conv_backward_kernel,
        grid=(width // 128, count),
        in_specs=[
            pl.BlockSpec((1, length, 128), lambda j, i: (i, 0, j)),
            pl.BlockSpec((1, length, 128), lambda j, i: (i, 0, j)),
            pl.BlockSpec((1, length, 1), lambda j, i: (i, 0, 0)),
            pl.BlockSpec((1, length, 1), lambda j, i: (i, 0, 0)),
            pl.BlockSpec((lags, 128), lambda j, i: (0, j)),
        ],
        out_specs=[
            pl.BlockSpec((1, length, 128), lambda j, i: (i, 0, j)),
            pl.BlockSpec((lags, 128), lambda j, i: (0, j)),
        ],
        out_shape=[
            jax.ShapeDtypeStruct(carried.shape, jnp.float32),
            jax.ShapeDtypeStruct((lags, width), jnp.float32),
        ],
    )(grad, carried, places, left, taps)


def pack_small(members, low):
    flat = jnp.concatenate([member.reshape(-1).astype(low) for member in members])
    rows = -(-flat.shape[0] // 128)
    rows = -(-rows // 16) * 16
    flat = jnp.concatenate([flat, jnp.zeros((rows * 128 - flat.shape[0],), low)])
    return flat.reshape(rows, 128)


SMALL_AXES = (0, 0, 0, 1, 0, 1, 0, 0, 0, 0, 1, 0, 0, 0, 0, 0, 0)


def unpack_small(packed, members):
    flat = packed.reshape(8, -1)
    results = []
    offset = 0
    for member, axis in zip(members, SMALL_AXES):
        size = member.size
        piece = lax.slice_in_dim(flat, offset, offset + size, axis=1)
        offset += size
        if member.ndim == 1 or axis == 0:
            results.append(piece.reshape((8 * member.shape[0],) + member.shape[1:]))
        else:
            piece = piece.reshape((8,) + member.shape)
            results.append(
                jnp.swapaxes(piece, 0, 1).reshape(member.shape[0], 8 * member.shape[1])
            )
    return results


def pack_small_gradients(members):
    rows = []
    for member, axis in zip(members, SMALL_AXES):
        if axis == 0:
            rows.append(member.reshape(8, -1))
        else:
            piece = member.reshape(member.shape[0], 8, member.shape[1] // 8)
            rows.append(jnp.swapaxes(piece, 0, 1).reshape(8, -1))
    flat = jnp.concatenate(rows, axis=1)
    height = -(-flat.shape[1] // 1024) * 8
    flat = jnp.pad(flat, ((0, 0), (0, height * 128 - flat.shape[1])))
    return flat.reshape(8, height, 128)


def unpack_small_gradients(packed, members):
    flat = packed.reshape(-1)
    results = []
    offset = 0
    for member in members:
        results.append(lax.slice_in_dim(flat, offset, offset + member.size).reshape(member.shape))
        offset += member.size
    return results


LAGS = 64


def block_device(
    tokens, segment_ids, cotangent, first_gain, first_shift, input_weight, input_bias,
    short_weight, short_bias, inner_weight, inner_bias, sine_scale, middle_weight, middle_bias,
    filter_weight, direct_gain, output_weight, output_bias, second_gain, second_shift,
    expand_weight, expand_bias, contract_weight, contract_bias,
):
    count, sequences, length, width = tokens.shape
    blocks = count * sequences
    row_count = blocks * length
    small_members = (
        first_gain, first_shift, input_bias, short_weight, short_bias, inner_weight, inner_bias,
        sine_scale, middle_weight, middle_bias, filter_weight, direct_gain, output_bias,
        second_gain, second_shift, expand_bias, contract_bias,
    )
    small_all, w_in, w_out, w_con, w_exp = gather_weights(
        pack_small(small_members, jnp.bfloat16),
        (input_weight, output_weight, contract_weight, expand_weight),
    )
    (
        g_first, s_first, b_in, w_short, b_short, w_inner, b_inner, scale, w_middle, b_middle,
        w_filter, direct, b_out, g_second, s_second, b_exp, b_con,
    ) = [to_float(member) for member in unpack_small(small_all, small_members)]

    def taps_of(*parts):
        return filter_taps(*parts, length)[:LAGS]

    filter_parts = (w_inner, b_inner, scale, w_middle, b_middle, w_filter)
    taps, taps_pull = jax.vjp(taps_of, *filter_parts)
    segments = segment_ids.reshape(blocks, length)
    same = segments[:, :, None] == segments[:, None, :]
    index = jnp.arange(length, dtype=jnp.int32)
    places = jnp.sum(same & (index[None, None, :] < index[None, :, None]), axis=2, dtype=jnp.int32)
    left = jnp.sum(same & (index[None, None, :] > index[None, :, None]), axis=2, dtype=jnp.int32)
    places = places[:, :, None]
    left = left[:, :, None]
    flat_tokens = tokens.reshape(row_count, width).astype(jnp.float32)
    upstream = cotangent.reshape(row_count, width)
    upstream_float = upstream.astype(jnp.float32)

    normed, first_pull = jax.vjp(normalize, flat_tokens, g_first, s_first)
    normed_first = normed.astype(jnp.bfloat16)
    projected = jnp.dot(normed_first, w_in, preferred_element_type=jnp.float32) + b_in
    projected_rows = projected.reshape(blocks, length, 3 * width)
    short_out, short_pull = jax.vjp(
        lambda rows_in, taps_in, offset_in: short_filter(rows_in, segments, taps_in, offset_in),
        projected_rows, w_short, b_short,
    )
    gate_out = short_out[:, :, :width]
    gate_in = short_out[:, :, width : 2 * width]
    values = short_out[:, :, 2 * width :]
    carried = values * gate_in
    convolved = conv_forward(carried, places, taps) + direct * carried
    gated_low = (convolved * gate_out).astype(jnp.bfloat16).reshape(row_count, width)
    residual = flat_tokens + jnp.dot(gated_low, w_out, preferred_element_type=jnp.float32) + b_out
    normed, second_pull = jax.vjp(normalize, residual, g_second, s_second)
    normed_second = normed.astype(jnp.bfloat16)
    hidden_pre = jnp.dot(normed_second, w_exp, preferred_element_type=jnp.float32) + b_exp
    hidden, gelu_pull = jax.vjp(smooth_gate, hidden_pre)
    hidden_post = hidden.astype(jnp.bfloat16)
    result = residual + jnp.dot(hidden_post, w_con, preferred_element_type=jnp.float32) + b_con
    result = result.astype(jnp.bfloat16).reshape(tokens.shape)

    def product(left_side, right_side, dims):
        return lax.dot_general(
            left_side, right_side, ((dims[:1], dims[1:]), ((), ())),
            preferred_element_type=jnp.float32,
        )

    d_con = product(hidden_post, upstream, (0, 0)).astype(jnp.bfloat16)
    back_hidden = product(upstream, w_con, (1, 1))
    back_pre = gelu_pull(back_hidden)[0].astype(jnp.bfloat16)
    d_exp = product(normed_second, back_pre, (0, 0)).astype(jnp.bfloat16)
    back_second = product(back_pre, w_exp, (1, 1))
    back_norm, d_g_second, d_s_second = second_pull(back_second)
    back_residual = upstream_float + back_norm
    back_mixed = back_residual.astype(jnp.bfloat16)
    d_out = product(gated_low, back_mixed, (0, 0)).astype(jnp.bfloat16)
    back_gated = product(back_mixed, w_out, (1, 1)).reshape(blocks, length, width)
    back_conv = back_gated * gate_out
    back_carried, d_taps = conv_backward(back_conv, carried, places, left, taps)
    back_carried = back_carried + direct * back_conv
    back_short = jnp.concatenate(
        [back_gated * convolved, back_carried * values, back_carried * gate_in], axis=2
    )
    back_projected, d_w_short, d_b_short = short_pull(back_short)
    back_projected = back_projected.reshape(row_count, 3 * width).astype(jnp.bfloat16)
    d_in = product(normed_first, back_projected, (0, 0)).astype(jnp.bfloat16)
    back_first = product(back_projected, w_in, (1, 1))
    back_norm, d_g_first, d_s_first = first_pull(back_first)
    token_delta = (back_residual + back_norm).reshape(tokens.shape)
    filter_deltas = taps_pull(d_taps)
    small_deltas = (
        d_g_first, d_s_first, jnp.sum(to_float(back_projected), axis=0), d_w_short, d_b_short,
        filter_deltas[0], filter_deltas[1], filter_deltas[2], filter_deltas[3], filter_deltas[4],
        filter_deltas[5], jnp.sum(back_conv * carried, axis=(0, 1)),
        jnp.sum(to_float(back_mixed), axis=0), d_g_second, d_s_second,
        jnp.sum(to_float(back_pre), axis=0), jnp.sum(upstream_float, axis=0),
    )
    small_sum, (s_in, s_out, s_con, s_exp) = reduce_gradients(
        pack_small_gradients(small_deltas), (d_in, d_out, d_con, d_exp)
    )
    done = unpack_small_gradients(small_sum, small_members)
    return (
        result, token_delta, done[0], done[1], s_in, done[2], done[3], done[4], done[5], done[6],
        done[7], done[8], done[9], done[10], done[11], s_out, done[12], done[13], done[14], s_exp,
        done[15], s_con, done[16],
    )


def per_device(
    tokens,
    segment_ids,
    cotangent,
    first_gain,
    first_shift,
    input_weight,
    input_bias,
    short_weight,
    short_bias,
    inner_weight,
    inner_bias,
    sine_scale,
    middle_weight,
    middle_bias,
    filter_weight,
    direct_gain,
    output_weight,
    output_bias,
    second_gain,
    second_shift,
    expand_weight,
    expand_bias,
    contract_weight,
    contract_bias,
):
    micro_count, local_sequences, length, width = tokens.shape
    row_count = local_sequences * length
    tables = wave_tables(length)

    def fetch_mixer():
        return (
            lax.all_gather(first_gain, "shard", axis=0, tiled=True),
            lax.all_gather(first_shift, "shard", axis=0, tiled=True),
            lax.all_gather(input_weight, "shard", axis=0, tiled=True),
            lax.all_gather(input_bias, "shard", axis=0, tiled=True),
            lax.all_gather(short_weight, "shard", axis=1, tiled=True),
            lax.all_gather(short_bias, "shard", axis=0, tiled=True),
            lax.all_gather(inner_weight, "shard", axis=1, tiled=True),
            lax.all_gather(inner_bias, "shard", axis=0, tiled=True),
            lax.all_gather(sine_scale, "shard", axis=0, tiled=True),
            lax.all_gather(middle_weight, "shard", axis=0, tiled=True),
            lax.all_gather(middle_bias, "shard", axis=0, tiled=True),
            lax.all_gather(filter_weight, "shard", axis=1, tiled=True),
            lax.all_gather(direct_gain, "shard", axis=0, tiled=True),
            lax.all_gather(output_weight, "shard", axis=0, tiled=True),
            lax.all_gather(output_bias, "shard", axis=0, tiled=True),
        )

    def fetch_dense():
        return (
            lax.all_gather(second_gain, "shard", axis=0, tiled=True),
            lax.all_gather(second_shift, "shard", axis=0, tiled=True),
            lax.all_gather(expand_weight, "shard", axis=0, tiled=True),
            lax.all_gather(expand_bias, "shard", axis=0, tiled=True),
            lax.all_gather(contract_weight, "shard", axis=0, tiled=True),
            lax.all_gather(contract_bias, "shard", axis=0, tiled=True),
        )

    results = []
    input_deltas = []
    mixer_total = None
    dense_total = None
    for micro_index in range(micro_count):
        mixer_parts = fetch_mixer()
        dense_parts = fetch_dense()
        kernel = filter_taps(
            to_float(mixer_parts[6]),
            to_float(mixer_parts[7]),
            to_float(mixer_parts[8]),
            to_float(mixer_parts[9]),
            to_float(mixer_parts[10]),
            to_float(mixer_parts[11]),
            length,
        )
        kernel, kernel_wave = (kernel, spectrum(tables, kernel))
        kernel_real, kernel_imag = kernel_wave
        segment_block = segment_ids[micro_index]
        membership = (
            segment_block[:, None, :] == jnp.arange(DOCS, dtype=jnp.int32)[None, :, None]
        ).astype(jnp.float32)
        flat_tokens = tokens[micro_index].reshape(row_count, width).astype(jnp.float32)
        normed_first = normalize(
            flat_tokens, to_float(mixer_parts[0]), to_float(mixer_parts[1])
        ).astype(jnp.bfloat16)
        projected = jnp.dot(
            normed_first, mixer_parts[2], preferred_element_type=jnp.float32
        ) + to_float(mixer_parts[3])
        projected_rows = projected.reshape(local_sequences, length, 3 * width)
        short_out = short_filter(
            projected_rows, segment_block, to_float(mixer_parts[4]), to_float(mixer_parts[5])
        )
        gate_out = short_out[:, :, :width]
        gate_in = short_out[:, :, width : 2 * width]
        values = short_out[:, :, 2 * width :]
        carried = values * gate_in
        direct = to_float(mixer_parts[12])
        carried_real, carried_imag = spectrum(tables, carried[:, None] * membership[:, :, :, None])
        conv_pieces = inverse(
            tables,
            carried_real * kernel_real - carried_imag * kernel_imag,
            carried_real * kernel_imag + carried_imag * kernel_real,
        )
        convolved = jnp.sum(conv_pieces * membership[:, :, :, None], axis=1) + direct * carried
        gated_low = (convolved * gate_out).astype(jnp.bfloat16).reshape(row_count, width)
        mixed_out = jnp.dot(
            gated_low, mixer_parts[13], preferred_element_type=jnp.float32
        ) + to_float(mixer_parts[14])
        residual = flat_tokens + mixed_out
        second_gain_f = to_float(dense_parts[0])
        second_shift_f = to_float(dense_parts[1])
        normed_second = normalize(residual, second_gain_f, second_shift_f).astype(jnp.bfloat16)
        hidden_pre = jnp.dot(
            normed_second, dense_parts[2], preferred_element_type=jnp.float32
        ) + to_float(dense_parts[3])
        hidden_post = smooth_gate(hidden_pre).astype(jnp.bfloat16)
        result = (
            residual
            + jnp.dot(hidden_post, dense_parts[4], preferred_element_type=jnp.float32)
            + to_float(dense_parts[5])
        )
        results.append(result.astype(jnp.bfloat16).reshape(local_sequences, length, width))
        back_mixer = fetch_mixer()
        back_dense = fetch_dense()
        upstream = cotangent[micro_index].reshape(row_count, width)
        upstream_float = upstream.astype(jnp.float32)
        delta_contract_weight = jnp.einsum(
            "tf,td->fd", hidden_post, upstream, preferred_element_type=jnp.float32
        )
        delta_contract_bias = jnp.sum(upstream_float, axis=0)
        back_hidden = jnp.einsum(
            "td,fd->tf", upstream, back_dense[4], preferred_element_type=jnp.float32
        )
        back_pre = jax.vjp(smooth_gate, hidden_pre)[1](back_hidden)[0].astype(jnp.bfloat16)
        delta_expand_weight = jnp.einsum(
            "td,tf->df", normed_second, back_pre, preferred_element_type=jnp.float32
        )
        delta_expand_bias = jnp.sum(back_pre.astype(jnp.float32), axis=0)
        back_second = jnp.einsum(
            "tf,df->td", back_pre, back_dense[2], preferred_element_type=jnp.float32
        )
        second_pull = jax.vjp(
            normalize, residual, to_float(back_dense[0]), to_float(back_dense[1])
        )[1]
        back_norm_second, delta_second_gain, delta_second_shift = second_pull(back_second)
        back_residual = upstream_float + back_norm_second
        back_mixed = back_residual.astype(jnp.bfloat16)
        delta_output_weight = jnp.einsum(
            "td,te->de", gated_low, back_mixed, preferred_element_type=jnp.float32
        )
        delta_output_bias = jnp.sum(back_mixed.astype(jnp.float32), axis=0)
        back_gated = jnp.einsum(
            "te,de->td", back_mixed, back_mixer[13], preferred_element_type=jnp.float32
        ).reshape(local_sequences, length, width)
        back_conv = back_gated * gate_out
        grad_real, grad_imag = spectrum(tables, back_conv[:, None] * membership[:, :, :, None])
        carried_back_pieces = inverse(
            tables,
            grad_real * kernel_real + grad_imag * kernel_imag,
            grad_imag * kernel_real - grad_real * kernel_imag,
        )
        back_carried = (
            jnp.sum(carried_back_pieces * membership[:, :, :, None], axis=1) + direct * back_conv
        )
        cross_real = jnp.sum(grad_real * carried_real + grad_imag * carried_imag, axis=(0, 1))
        cross_imag = jnp.sum(grad_imag * carried_real - grad_real * carried_imag, axis=(0, 1))
        back_kernel = inverse(tables, cross_real, cross_imag)
        delta_direct = jnp.sum(back_conv * carried, axis=(0, 1))
        back_short = jnp.concatenate(
            [back_gated * convolved, back_carried * values, back_carried * gate_in], axis=2
        )
        short_pull = jax.vjp(
            lambda rows_in, taps_in, offset_in: short_filter(
                rows_in, segment_block, taps_in, offset_in
            ),
            projected_rows,
            to_float(back_mixer[4]),
            to_float(back_mixer[5]),
        )[1]
        back_projected, delta_short_weight, delta_short_bias = short_pull(back_short)
        back_projected = back_projected.reshape(row_count, 3 * width).astype(jnp.bfloat16)
        delta_input_weight = jnp.einsum(
            "td,tp->dp", normed_first, back_projected, preferred_element_type=jnp.float32
        )
        delta_input_bias = jnp.sum(back_projected.astype(jnp.float32), axis=0)
        back_first = jnp.einsum(
            "tp,dp->td", back_projected, back_mixer[2], preferred_element_type=jnp.float32
        )
        first_pull = jax.vjp(
            normalize, flat_tokens, to_float(back_mixer[0]), to_float(back_mixer[1])
        )[1]
        back_norm_first, delta_first_gain, delta_first_shift = first_pull(back_first)
        input_deltas.append(
            (back_residual + back_norm_first).reshape(local_sequences, length, width)
        )
        filter_pull = jax.vjp(
            lambda weight_one, bias_one, scale_all, weight_two, bias_two, weight_three: filter_taps(
                weight_one, bias_one, scale_all, weight_two, bias_two, weight_three, length
            ),
            to_float(back_mixer[6]),
            to_float(back_mixer[7]),
            to_float(back_mixer[8]),
            to_float(back_mixer[9]),
            to_float(back_mixer[10]),
            to_float(back_mixer[11]),
        )[1]
        filter_deltas = filter_pull(back_kernel)
        mixer_part = (
            delta_first_gain,
            delta_first_shift,
            delta_input_weight,
            delta_input_bias,
            delta_short_weight,
            delta_short_bias,
            filter_deltas[0],
            filter_deltas[1],
            filter_deltas[2],
            filter_deltas[3],
            filter_deltas[4],
            filter_deltas[5],
            delta_direct,
            delta_output_weight,
            delta_output_bias,
        )
        dense_part = (
            delta_second_gain,
            delta_second_shift,
            delta_expand_weight,
            delta_expand_bias,
            delta_contract_weight,
            delta_contract_bias,
        )
        if micro_index == 0:
            mixer_total = mixer_part
            dense_total = dense_part
        else:
            mixer_total = jax.tree.map(jnp.add, mixer_total, mixer_part)
            dense_total = jax.tree.map(jnp.add, dense_total, dense_part)
    dense_total = (
        lax.psum_scatter(dense_total[0], "shard", scatter_dimension=0, tiled=True),
        lax.psum_scatter(dense_total[1], "shard", scatter_dimension=0, tiled=True),
        lax.psum_scatter(dense_total[2], "shard", scatter_dimension=0, tiled=True),
        lax.psum_scatter(dense_total[3], "shard", scatter_dimension=0, tiled=True),
        lax.psum_scatter(dense_total[4], "shard", scatter_dimension=0, tiled=True),
        lax.psum_scatter(dense_total[5], "shard", scatter_dimension=0, tiled=True),
    )
    mixer_total = (
        lax.psum_scatter(mixer_total[0], "shard", scatter_dimension=0, tiled=True),
        lax.psum_scatter(mixer_total[1], "shard", scatter_dimension=0, tiled=True),
        lax.psum_scatter(mixer_total[2], "shard", scatter_dimension=0, tiled=True),
        lax.psum_scatter(mixer_total[3], "shard", scatter_dimension=0, tiled=True),
        lax.psum_scatter(mixer_total[4], "shard", scatter_dimension=1, tiled=True),
        lax.psum_scatter(mixer_total[5], "shard", scatter_dimension=0, tiled=True),
        lax.psum_scatter(mixer_total[6], "shard", scatter_dimension=1, tiled=True),
        lax.psum_scatter(mixer_total[7], "shard", scatter_dimension=0, tiled=True),
        lax.psum_scatter(mixer_total[8], "shard", scatter_dimension=0, tiled=True),
        lax.psum_scatter(mixer_total[9], "shard", scatter_dimension=0, tiled=True),
        lax.psum_scatter(mixer_total[10], "shard", scatter_dimension=0, tiled=True),
        lax.psum_scatter(mixer_total[11], "shard", scatter_dimension=1, tiled=True),
        lax.psum_scatter(mixer_total[12], "shard", scatter_dimension=0, tiled=True),
        lax.psum_scatter(mixer_total[13], "shard", scatter_dimension=0, tiled=True),
        lax.psum_scatter(mixer_total[14], "shard", scatter_dimension=0, tiled=True),
    )
    summed = lax.psum(
        (
            mixer_total[0],
            mixer_total[1],
            mixer_total[2],
            mixer_total[3],
            mixer_total[4],
            mixer_total[5],
            mixer_total[6],
            mixer_total[7],
            mixer_total[8],
            mixer_total[9],
            mixer_total[10],
            mixer_total[11],
            mixer_total[12],
            mixer_total[13],
            mixer_total[14],
            dense_total[0],
            dense_total[1],
            dense_total[2],
            dense_total[3],
            dense_total[4],
            dense_total[5],
        ),
        "rep",
    )
    return (jnp.stack(results), jnp.stack(input_deltas)) + tuple(summed)


def solution(mesh):
    placed = (
        P(None, ("rep", "shard"), None, None),
        P(None, ("rep", "shard"), None),
        P(None, ("rep", "shard"), None, None),
        P("shard"),
        P("shard"),
        P("shard", None),
        P("shard"),
        P(None, "shard"),
        P("shard"),
        P(None, "shard"),
        P("shard"),
        P("shard"),
        P("shard", None),
        P("shard"),
        P(None, "shard"),
        P("shard"),
        P("shard", None),
        P("shard"),
        P("shard"),
        P("shard"),
        P("shard", None),
        P("shard"),
        P("shard", None),
        P("shard"),
    )
    blocked_mesh = dict(mesh.shape) == {"rep": 4, "shard": 8}
    return jax.shard_map(
        block_device if blocked_mesh else per_device,
        mesh=mesh,
        in_specs=placed,
        out_specs=(
            P(None, ("rep", "shard"), None, None),
            P(None, ("rep", "shard"), None, None),
            P("shard"),
            P("shard"),
            P("shard", None),
            P("shard"),
            P(None, "shard"),
            P("shard"),
            P(None, "shard"),
            P("shard"),
            P("shard"),
            P("shard", None),
            P("shard"),
            P(None, "shard"),
            P("shard"),
            P("shard", None),
            P("shard"),
            P("shard"),
            P("shard"),
            P("shard", None),
            P("shard"),
            P("shard", None),
            P("shard"),
        ),
        check_vma=False,
    )
```

```python
import math

import jax
import jax.numpy as jnp
import numpy as np
from jax import lax
from jax.experimental import pallas as pl
from jax.experimental.pallas import tpu as pltpu
from jax.sharding import PartitionSpec as P

DOCS = 6


EPSILON = 1e-05
HIGHEST = lax.Precision.HIGHEST


def positions(length):
    places = jnp.arange(length, dtype=jnp.float32)
    linear_ramp = places / (length - 1)
    angles = 2.0 * math.pi * places / length
    scales = 0.0001 + jnp.arange(16, dtype=jnp.float32) * ((15.0 - 0.0001) / 15.0)
    phases = angles[:, None] * scales[None, :]
    return jnp.concatenate([linear_ramp[:, None], jnp.cos(phases), -jnp.sin(phases)], axis=1)


def decay_table(length, width):
    linear_ramp = jnp.arange(length, dtype=jnp.float32) / (length - 1)
    rates = math.log(100.0) * (
        1.0 / 1.5 + (1.0 / 0.3 - 1.0 / 1.5) * jnp.arange(width, dtype=jnp.float32) / (width - 1)
    )
    return jnp.exp(-linear_ramp[:, None] * rates[None, :])


def filter_taps(
    inner_weight, inner_bias, sine_scale, middle_weight, middle_bias, filter_weight, length
):
    features = positions(length)
    first_sine = jnp.sin(
        sine_scale * (jnp.dot(features, inner_weight, precision=HIGHEST) + inner_bias)
    )
    second_sine = jnp.sin(
        sine_scale * (jnp.dot(first_sine, middle_weight, precision=HIGHEST) + middle_bias)
    )
    return jnp.dot(second_sine, filter_weight, precision=HIGHEST) * decay_table(
        length, filter_weight.shape[1]
    )


def normalize(values, gain_row, shift_row):
    center = values - jnp.mean(values, axis=-1, keepdims=True)
    spread = jnp.mean(center * center, axis=-1, keepdims=True)
    return center * lax.rsqrt(spread + EPSILON) * gain_row + shift_row


def smooth_gate(values):
    return jax.nn.gelu(values, approximate=True)


def to_float(member):
    return member.astype(jnp.float32)


def short_filter(projected, segments, weight, offset):
    running = offset + weight[0] * projected
    for step_back in (1, 2):
        moved_rows = jnp.concatenate(
            [jnp.zeros_like(projected[:, :step_back]), projected[:, :-step_back]], axis=1
        )
        moved_ids = jnp.concatenate(
            [jnp.full_like(segments[:, :step_back], -1), segments[:, :-step_back]], axis=1
        )
        same_doc = (moved_ids == segments).astype(projected.dtype)
        running = running + weight[step_back] * moved_rows * same_doc[:, :, None]
    return running


def wave_tables(length):
    padded_size = 2 * length
    freq_index = jnp.arange(length + 1, dtype=jnp.int32)
    place_index = jnp.arange(length, dtype=jnp.int32)
    wrapped = freq_index[:, None] * place_index[None, :] % padded_size
    angles = 2.0 * math.pi / padded_size * wrapped.astype(jnp.float32)
    weights_row = (
        jnp.where((freq_index == 0) | (freq_index == length), 1.0, 2.0).astype(jnp.float32)
        / padded_size
    )
    return (jnp.cos(angles), jnp.sin(angles), weights_row)


def spectrum(tables, signal):
    cosine, sine, weights_row = tables
    real_part = jnp.einsum("ft,...td->...fd", cosine, signal, precision=HIGHEST)
    imag_part = -jnp.einsum("ft,...td->...fd", sine, signal, precision=HIGHEST)
    return (real_part, imag_part)


def inverse(tables, real_part, imag_part):
    cosine, sine, weights_row = tables
    scaled_real = real_part * weights_row[:, None]
    scaled_imag = imag_part * weights_row[:, None]
    return jnp.einsum("ft,...fd->...td", cosine, scaled_real, precision=HIGHEST) - jnp.einsum(
        "ft,...fd->...td", sine, scaled_imag, precision=HIGHEST
    )


MESH_ID = pl.DeviceIdType.MESH
LAGS = 64
LOW = jnp.bfloat16
FULL = jnp.float32
GATHER_CHUNKS = (
    (4, 0, 128, False),
    (0, 768, 768, True),
    (0, 1536, 768, True),
    (0, 0, 768, True),
    (3, 0, 768, False),
    (3, 768, 768, False),
    (1, 0, 768, True),
    (2, 0, 256, True),
    (3, 1536, 768, False),
    (2, 256, 256, True),
    (2, 512, 256, True),
    (3, 2304, 768, False),
)
REDUCE_GROUPS = (
    (2, (0, 256, 512), 256, True),
    (3, (0, 768, 1536, 2304), 768, False),
    (1, (0,), 768, True),
    (0, (0, 1536), 768, True),
    (0, (768,), 768, False),
    (4, (0,), 128, False),
)
REDUCE_ORDER = (
    (0, 0), (1, 0), (0, 1), (1, 1), (0, 2), (1, 2), (1, 3), (2, 0), (3, 0), (4, 0), (3, 1), (5, 0),
)
AHEAD = 3
SMALL_ROWS = 80


def dot_nn(left_side, right_side):
    return jnp.dot(left_side, right_side, preferred_element_type=FULL)


def dot_nt(left_side, right_side):
    return lax.dot_general(
        left_side, right_side, (((1,), (1,)), ((), ())), preferred_element_type=FULL
    )


def dot_tn(left_side, right_side):
    return lax.dot_general(
        left_side, right_side, (((0,), (0,)), ((), ())), preferred_element_type=FULL
    )


def exact(left_side, right_side, contract):
    return lax.dot_general(
        left_side, right_side, (((contract[0],), (contract[1],)), ((), ())),
        preferred_element_type=FULL, precision=HIGHEST,
    )


def fold8(values):
    rows, columns = values.shape
    return jnp.sum(values.reshape(rows // 8, 8, columns), axis=0)


def widen(values, width):
    rows, columns = values.shape
    if columns == width:
        return values
    return jnp.concatenate([values, jnp.zeros((rows, width - columns), values.dtype)], axis=1)


def turn(values, amount, axis):
    size = values.shape[axis]
    amount = amount % size
    return values if amount == 0 else pltpu.roll(values, amount, axis)


def block_kernel(*refs):
    refs = list(refs)

    def take(number):
        taken = refs[:number]
        del refs[:number]
        return taken

    tokens, segs, cot = take(3)
    (
        r_first_gain, r_first_shift, r_in_bias, r_short_w, r_short_b, r_inner_w, r_inner_b,
        r_scale, r_middle_w, r_middle_b, r_filter_w, r_direct, r_out_bias, r_second_gain,
        r_second_shift, r_exp_bias, r_con_bias,
    ) = take(17)
    own = take(4)
    features, decay = take(2)
    result, delta = take(2)
    sums = take(5)
    full = take(5)
    g_in, g_out, g_small, own_small, pack = take(5)
    v96, v288, vexp, v8 = take(4)
    mid_w, fil_w, taps, d_taps = take(4)
    s_inner1, s_first, s_cos1, s_inner2, s_second, s_cos2 = take(6)
    places, left = take(2)
    normed1, proj, short, conv, gated, resid, normed2 = take(7)
    hidden, post, pre, back_h, gather_out, back_s, back_r, back_m, back_g, bp = take(10)
    acc96, acc288, accexp = take(3)
    groups = []
    for matrix, columns, width, split in REDUCE_GROUPS:
        members = take(7 if split else 6)
        names = ("core", "x", "z1", "z2", "z3", "last") + (("y",) if split else ())
        groups.append(dict(zip(names, members)))
    ag_recv, ag_cross, ag_core, ag_send, own_sem, rs_recv, rs_y, rs_send, rs_end = take(9)
    assert not refs

    own = list(own) + [own_small]
    grads = (g_in, g_out, full[2], full[3], g_small)

    rep = lax.axis_index("rep")
    shard = lax.axis_index("shard")
    y, c = rep // 2, rep % 2
    z, x = shard // 2, shard % 2
    pair = z // 2
    near_z = z + 1 - 2 * (z % 2)
    inner = ((z + 1) // 2) % 2 == 1
    to_near = (rep, near_z * 2 + x)
    to_mirror = (rep, (3 - z) * 2 + x)
    to_x = (rep, z * 2 + 1 - x)
    to_y = ((1 - y) * 2 + c, shard)
    to_c = (y * 2 + 1 - c, shard)
    own_pair = pl.ds(pair * 2, 2)
    other_pair = pl.ds((1 - pair) * 2, 2)

    barrier = pltpu.get_barrier_semaphore()
    for target in (to_near, to_x, to_y, to_c):
        pl.semaphore_signal(barrier, inc=1, device_id=target, device_id_type=MESH_ID)

    @pl.when(inner)
    def _():
        pl.semaphore_signal(barrier, inc=1, device_id=to_mirror, device_id_type=MESH_ID)

    def remote(source, landing, send, recv, device):
        return pltpu.make_async_remote_copy(
            src_ref=source, dst_ref=landing, send_sem=send, recv_sem=recv,
            device_id=device, device_id_type=MESH_ID,
        )

    pack[...] = jnp.zeros_like(pack)
    for row, member in enumerate(
        (r_first_gain, r_first_shift, r_direct, r_out_bias, r_second_gain, r_second_shift, r_con_bias)
    ):
        pack[row : row + 1, 0:96] = member[...].astype(FULL)
    for block in range(3):
        lanes = 128 if block < 2 else 32
        span = slice(block * 128, block * 128 + lanes)
        top = 8 + block * 8
        pack[top : top + 1, 0:lanes] = r_in_bias[:, span].astype(FULL)
        pack[top + 1 : top + 2, 0:lanes] = r_short_b[:, span].astype(FULL)
        pack[top + 2 : top + 5, 0:lanes] = r_short_w[:, span].astype(FULL)
        pack[top + 5 : top + 6, :] = r_exp_bias[:, block * 128 : block * 128 + 128].astype(FULL)
    for row, member in enumerate((r_inner_b, r_scale, r_middle_b)):
        pack[32 + row : 33 + row, 0:8] = member[...].astype(FULL)
    pack[40:73, 0:8] = r_inner_w[...].astype(FULL)
    pack[80:88, 0:64] = r_middle_w[...].astype(FULL)
    pack[88:152, 0:96] = r_filter_w[...].astype(FULL)
    own_small[0] = pack[0:80, :].astype(LOW)
    own_small[1] = pack[80:160, :].astype(LOW)

    acc96[...] = jnp.zeros_like(acc96)
    acc288[...] = jnp.zeros_like(acc288)
    accexp[...] = jnp.zeros_like(accexp)
    d_taps[...] = jnp.zeros_like(d_taps)

    pl.semaphore_wait(barrier, 4 + ((z + 1) // 2) % 2)

    chunks = GATHER_CHUNKS
    count = len(chunks)
    cross_index = {}
    for index, chunk in enumerate(chunks):
        if chunk[3]:
            cross_index[index] = len(cross_index)
    NEAR, FAR, SIDE0, SIDE1 = range(4)
    S_NEAR, S_MIRROR, S_BACK, S_SIDE, S_CROSS, S_CORE = range(6)

    def part(chunk, quarter):
        matrix, column, width, split = chunk
        if split:
            return pl.ds(pl.multiple_of(column + quarter * (width // 2), 128), width // 2)
        return pl.ds(column, width)

    def whole(chunk):
        return pl.ds(chunk[1], chunk[2])

    for matrix in range(5):
        pltpu.make_async_copy(own[matrix].at[c], full[matrix].at[z, x, c], own_sem.at[matrix]).start()

    def first(index):
        chunk = chunks[index]
        m = chunk[0]
        remote(
            own[m].at[c, :, part(chunk, y)], full[m].at[z, x, c, :, part(chunk, y)],
            ag_send.at[S_NEAR, m], ag_recv.at[NEAR, index], to_near,
        ).start()

    def near(index):
        chunk = chunks[index]
        m = chunk[0]
        arrived = full[m].at[near_z, x, c, :, part(chunk, y)]
        remote(arrived, arrived, ag_send.at[S_NEAR, m], ag_recv.at[NEAR, index], to_near).wait_recv()
        both = full[m].at[own_pair, x, c, :, part(chunk, y)]

        @pl.when(inner)
        def _():
            remote(both, both, ag_send.at[S_MIRROR, m], ag_recv.at[FAR, index], to_mirror).start()

        remote(both, both, ag_send.at[S_SIDE, m], ag_recv.at[SIDE0, index], to_x).start()
        if chunk[3]:
            remote(
                arrived, arrived, ag_send.at[S_CROSS, m], ag_cross.at[0, cross_index[index]], to_y
            ).start()

    def far(index):
        chunk = chunks[index]
        m = chunk[0]
        both = full[m].at[other_pair, x, c, :, part(chunk, y)]
        remote(both, both, ag_send.at[S_MIRROR, m], ag_recv.at[FAR, index], to_near).wait_recv()

        @pl.when(inner)
        def _():
            remote(both, both, ag_send.at[S_BACK, m], ag_recv.at[FAR, index], to_near).start()

        remote(both, both, ag_send.at[S_SIDE, m], ag_recv.at[SIDE1, index], to_x).start()
        if chunk[3]:
            remote(
                both, both, ag_send.at[S_CROSS, m], ag_cross.at[1, cross_index[index]], to_y
            ).start()

    def to_core(index):
        chunk = chunks[index]
        m = chunk[0]
        piece = full[m].at[:, :, c, :, whole(chunk)]
        slot = core_slot(index)
        remote(piece, piece, ag_send.at[S_CORE, m], ag_core.at[slot], to_c).start()

    def core_slot(index):
        m, column = chunks[index][0], chunks[index][1]
        return {0: 0, 1: 1, 2: 2, 4: 3}[m] if m != 3 else 4 + column // 768

    def side(index):
        chunk = chunks[index]
        m = chunk[0]
        for place, slot in ((own_pair, SIDE0), (other_pair, SIDE1)):
            both = full[m].at[place, 1 - x, c, :, part(chunk, y)]
            remote(both, both, ag_send.at[S_SIDE, m], ag_recv.at[slot, index], to_x).wait_recv()
        if chunk[3]:
            column = full[m].at[:, 1 - x, c, :, part(chunk, y)]
            remote(
                column, column, ag_send.at[S_CROSS, m], ag_cross.at[2, cross_index[index]], to_y
            ).start()
        else:
            to_core(index)

    def cross(index):
        chunk = chunks[index]
        if not chunk[3]:
            return
        m = chunk[0]
        for slot, piece in enumerate(
            (
                full[m].at[near_z, x, c, :, part(chunk, 1 - y)],
                full[m].at[other_pair, x, c, :, part(chunk, 1 - y)],
                full[m].at[:, 1 - x, c, :, part(chunk, 1 - y)],
            )
        ):
            remote(
                piece, piece, ag_send.at[S_CROSS, m], ag_cross.at[slot, cross_index[index]], to_y
            ).wait_recv()
        to_core(index)

    def settled(m, column=None):
        if column is None:
            piece, slot = full[m].at[:, :, 1 - c], {0: 0, 1: 1, 2: 2, 4: 3}[m]
        else:
            piece, slot = full[m].at[:, :, 1 - c, :, pl.ds(column, 768)], 4 + column // 768
        remote(piece, piece, ag_send.at[S_CORE, m], ag_core.at[slot], to_c).wait_recv()

    plan = ((0, near), (0, far), (1, side), (1, cross))

    def tick(step):
        if step + AHEAD < count:
            first(step + AHEAD)
        for delay, action in plan:
            if 0 <= step - delay < count:
                action(step - delay)

    for index in range(AHEAD):
        first(index)
    for matrix in range(5):
        pltpu.make_async_copy(own[matrix].at[c], full[matrix].at[z, x, c], own_sem.at[matrix]).wait()

    def row_blocks(size, action):
        def body(step, carry):
            action(pl.ds(pl.multiple_of(step * size, size), size))
            return carry

        lax.fori_loop(0, tokens.shape[0] // size, body, 0)

    def find_places():
        rows = lax.broadcasted_iota(jnp.int32, (128, 128), 0)
        columns = lax.broadcasted_iota(jnp.int32, (128, 128), 1)
        for sequence in range(2):
            ids = jnp.broadcast_to(segs[sequence : sequence + 1, :].astype(FULL), (128, 128))
            same = ids == ids.T
            before = jnp.sum(jnp.where(same & (columns < rows), 1.0, 0.0), axis=1, keepdims=True)
            after = jnp.sum(jnp.where(same & (columns > rows), 1.0, 0.0), axis=1, keepdims=True)
            span = slice(sequence * 128, sequence * 128 + 128)
            places[span, :] = jnp.broadcast_to(before.astype(jnp.int32), (128, 128))
            left[span, :] = jnp.broadcast_to(after.astype(jnp.int32), (128, 128))

    def unpack_small():
        total96 = jnp.zeros((8, 768), FULL)
        total288 = jnp.zeros((8, 2304), FULL)
        total8 = jnp.zeros((8, 128), FULL)
        inner_total = jnp.zeros((40, 128), FULL)
        fil_w[...] = jnp.zeros_like(fil_w)
        mid_w[...] = jnp.zeros_like(mid_w)
        for s in range(8):
            top = full[4][s // 2, s % 2, 0].astype(FULL)
            low = full[4][s // 2, s % 2, 1].astype(FULL)
            total96 = total96 + turn(widen(top[0:8], 768), 96 * s, 1)
            wide = jnp.concatenate([top[8:16], top[16:24], top[24:32]], axis=1)
            vexp[:, s * 384 : s * 384 + 384] = wide[5:6]
            total288 = total288 + turn(widen(wide, 2304), 288 * s, 1)
            total8 = total8 + turn(top[32:40], 8 * s, 1)
            inner_total = inner_total + turn(top[40:80], 8 * s, 1)
            mid_w[8 * s : 8 * s + 8, :] = low[0:8]
            fil_w[0:64, :] += turn(widen(low[8:72], 768), 96 * s, 1)
        v96[...] = total96
        v288[...] = total288
        v8[...] = total8
        scale = total8[1:2]
        inner1 = exact(features[...], inner_total, (1, 0)) + total8[0:1]
        s_inner1[...] = inner1
        s_first[...] = jnp.sin(scale * inner1)
        s_cos1[...] = jnp.cos(scale * inner1)
        inner2 = exact(s_first[...], mid_w[...], (1, 0)) + total8[2:3]
        s_inner2[...] = inner2
        s_second[...] = jnp.sin(scale * inner2)
        s_cos2[...] = jnp.cos(scale * inner2)
        taps[...] = exact(s_second[...], fil_w[...], (1, 0)) * decay[...]

    def center(values):
        middle = values - jnp.mean(values, axis=-1, keepdims=True)
        spread = jnp.mean(middle * middle, axis=-1, keepdims=True)
        scale = lax.rsqrt(spread + EPSILON)
        return middle * scale, scale

    def norm_first(rows):
        unit, _ = center(tokens[rows, :].astype(FULL))
        normed1[rows, :] = (unit * v96[0:1, :] + v96[1:2, :]).astype(LOW)

    def matrix_of(m, columns, width):
        value = full[m][:, :, :, :, columns]
        return value.reshape(value.shape[0] * value.shape[1] * value.shape[2] * value.shape[3], width)

    def project(k):
        span = slice(k * 768, k * 768 + 768)
        proj[k] = dot_nn(normed1[...], matrix_of(0, pl.ds(k * 768, 768), 768)) + v288[0:1, span]

        def body(step, carry):
            rows = pl.ds(pl.multiple_of((step // 6) * 128, 128), 128)
            lane = pl.multiple_of((step % 6) * 128, 128)
            lanes = pl.ds(lane, 128)
            wide = pl.ds(pl.multiple_of(k * 768 + lane, 128), 128)
            values = proj[k, rows, lanes]
            where = places[rows, :]
            total = v288[1:2, wide] + v288[2:3, wide] * values
            for lag in (1, 2):
                moved = jnp.where(where >= lag, pltpu.roll(values, lag, 0), 0.0)
                total = total + v288[2 + lag : 3 + lag, wide] * moved
            short[k, rows, lanes] = total
            return carry

        lax.fori_loop(0, 12, body, 0)

    def convolve(begin, end):
        def body(step, carry):
            rows = pl.ds(pl.multiple_of((step // 6) * 128, 128), 128)
            lanes = pl.ds(pl.multiple_of((step % 6) * 128, 128), 128)
            carried = short[2, rows, lanes] * short[1, rows, lanes]
            where = places[rows, :]
            total = v96[2:3, lanes] * carried
            for low_lag in range(8):
                moved = turn(carried, low_lag, 0)
                for high in range(LAGS // 8):
                    lag, skip = high * 8 + low_lag, high * 8
                    term = jnp.where(
                        where[skip:] >= lag, taps[lag : lag + 1, lanes] * moved[: 128 - skip], 0.0
                    )
                    if skip:
                        total = jnp.concatenate([total[:skip], total[skip:] + term], axis=0)
                    else:
                        total = total + term
            conv[rows, lanes] = total
            return carry

        lax.fori_loop(begin, end, body, 0)

    def mix_out():
        def gate(rows):
            gated[rows, :] = (conv[rows, :] * short[0, rows, :]).astype(LOW)

        row_blocks(16, gate)
        resid[...] = dot_nn(gated[...], matrix_of(1, pl.ds(0, 768), 768))

        def finish_rows(rows):
            values = resid[rows, :] + tokens[rows, :].astype(FULL) + v96[3:4, :]
            resid[rows, :] = values
            unit, _ = center(values)
            normed2[rows, :] = (unit * v96[4:5, :] + v96[5:6, :]).astype(LOW)

        row_blocks(16, finish_rows)

    def expand(k):
        span = slice(k * 768, k * 768 + 768)
        hidden[:, span] = (
            dot_nn(normed2[...], matrix_of(3, pl.ds(k * 768, 768), 768)) + vexp[:, span]
        )

    def feed(k):
        span = slice(k * 768, k * 768 + 768)
        rows_of = full[2][k].reshape(768, 768)
        back_h[...] = dot_nt(cot[...], rows_of)

        def bend(rows):
            values = hidden[rows, span]
            cube = values * values
            grow = math.sqrt(2.0 / math.pi)
            slope = jnp.tanh(grow * (values + 0.044715 * cube * values))
            half_up = 0.5 + 0.5 * slope
            post[rows, span] = (values * half_up).astype(LOW)
            steep = half_up + (0.5 * values) * (1.0 - slope * slope) * (
                grow * (1.0 + 3.0 * 0.044715 * cube)
            )
            grad = (back_h[rows, :] * steep).astype(LOW)
            pre[rows, span] = grad
            accexp[:, span] += fold8(grad.astype(FULL))

        row_blocks(16, bend)
        out_part = dot_nn(post[:, span], full[2][k].reshape(768, 768))
        back_part = dot_nt(pre[:, span], matrix_of(3, pl.ds(k * 768, 768), 768))
        if k == 0:
            gather_out[...] = out_part
            back_s[...] = back_part
        else:
            gather_out[...] += out_part
            back_s[...] += back_part

    find_places()
    tick(0)
    tick(1)
    settled(4)
    unpack_small()
    row_blocks(16, norm_first)
    tick(2)
    tick(3)
    tick(4)
    tick(5)
    settled(0)
    project(1)
    tick(6)
    project(2)
    tick(7)
    convolve(0, 4)
    tick(8)
    convolve(4, 8)
    tick(9)
    convolve(8, 12)
    tick(10)
    project(0)
    settled(1)
    tick(11)
    mix_out()
    tick(12)
    settled(3, 0)
    expand(0)
    settled(3, 768)
    expand(1)
    settled(3, 1536)
    expand(2)
    settled(2)
    for k in range(3):
        feed(k)
    settled(3, 2304)
    expand(3)
    feed(3)

    for m in range(5):
        quarter = {0: 1152, 1: 384, 2: 384, 3: 3072, 4: 128}[m]
        wide = full[m].shape[4]
        one = full[m].at[0, 0, 0, :, pl.ds(0, quarter)]
        two = full[m].at[pl.ds(0, 2), 0, 0, :, pl.ds(0, quarter)]
        four = full[m].at[:, 0, 0, :, pl.ds(0, quarter)]
        remote(one, one, ag_send.at[S_NEAR, m], ag_recv.at[NEAR, 0], to_near).wait_send()

        @pl.when(inner)
        def _(two=two, m=m):
            remote(two, two, ag_send.at[S_MIRROR, m], ag_recv.at[FAR, 0], to_near).wait_send()
            remote(two, two, ag_send.at[S_BACK, m], ag_recv.at[FAR, 0], to_near).wait_send()

        remote(four, four, ag_send.at[S_SIDE, m], ag_recv.at[FAR, 0], to_near).wait_send()
        if m not in (3, 4):
            near_one = full[m].at[pl.ds(0, 3), 0, 0, :, pl.ds(0, quarter)]
            remote(near_one, near_one, ag_send.at[S_CROSS, m], ag_recv.at[FAR, 0], to_near).wait_send()
            remote(four, four, ag_send.at[S_CROSS, m], ag_recv.at[FAR, 0], to_near).wait_send()
        everything = full[m].at[:, :, 0, :, pl.ds(0, wide)]
        remote(everything, everything, ag_send.at[S_CORE, m], ag_recv.at[FAR, 0], to_near).wait_send()

    position = {}
    split_position = {}
    for index, key in enumerate(REDUCE_ORDER):
        position[key] = index
        if REDUCE_GROUPS[key[0]][3]:
            split_position[key] = len(split_position)
    R_CORE, R_X, R_Z1, R_Z2, R_Z3, R_LAST = range(6)
    W_CORE, W_Y, W_X, W_Z1, W_Z2, W_Z3, W_LAST, W_END = range(8)

    def info(key):
        g, i = key
        matrix, columns, width, split = REDUCE_GROUPS[g]
        return g, i, matrix, columns[i], width, split, groups[g], position[key]

    def halves(width, which):
        return pl.ds(pl.multiple_of(which * (width // 2), 128), width // 2)

    def stage(key):
        g, i, m, column, width, split, buf, n = info(key)
        remote(
            grads[m].at[:, :, 1 - c, :, pl.ds(column, width)], buf["core"].at[i],
            rs_send.at[W_CORE, g], rs_recv.at[R_CORE, n], to_c,
        ).start()

    def add_core(key):
        g, i, m, column, width, split, buf, n = info(key)
        landing = buf["core"].at[i]
        remote(landing, landing, rs_send.at[W_CORE, g], rs_recv.at[R_CORE, n], to_c).wait_recv()

        def body(step, carry):
            a, b = step // 2, step % 2
            buf["core"][i, a, b] = buf["core"][i, a, b] + grads[m][a, b, c, :, pl.ds(column, width)]
            return carry

        lax.fori_loop(0, 8, body, 0)
        if split:
            remote(
                buf["core"].at[i, :, :, :, halves(width, 1 - y)], buf["y"].at[i],
                rs_send.at[W_Y, g], rs_y.at[split_position[key]], to_y,
            ).start()
        else:
            remote(
                buf["core"].at[i, :, 1 - x], buf["x"].at[i],
                rs_send.at[W_X, g], rs_recv.at[R_X, n], to_x,
            ).start()

    def add_y(key):
        g, i, m, column, width, split, buf, n = info(key)
        if not split:
            return
        landing = buf["y"].at[i]
        remote(landing, landing, rs_send.at[W_Y, g], rs_y.at[split_position[key]], to_y).wait_recv()

        def body(step, carry):
            a, b = step // 2, step % 2
            buf["y"][i, a, b] = buf["y"][i, a, b] + buf["core"][i, a, b, :, halves(width, y)]
            return carry

        lax.fori_loop(0, 8, body, 0)
        remote(
            buf["y"].at[i, :, 1 - x], buf["x"].at[i], rs_send.at[W_X, g], rs_recv.at[R_X, n], to_x
        ).start()

    def add_x(key):
        g, i, m, column, width, split, buf, n = info(key)
        landing = buf["x"].at[i]
        remote(landing, landing, rs_send.at[W_X, g], rs_recv.at[R_X, n], to_x).wait_recv()
        own_part = buf["y"] if split else buf["core"]

        def body(step, carry):
            buf["x"][i, step] = buf["x"][i, step] + own_part[i, step, x]
            return carry

        lax.fori_loop(0, 4, body, 0)

        @pl.when(jnp.logical_not(inner))
        def _():
            remote(
                buf["x"].at[i, other_pair], buf["z1"].at[i],
                rs_send.at[W_Z1, g], rs_recv.at[R_Z1, n], to_near,
            ).start()
            remote(
                buf["x"].at[i, near_z], buf["z3"].at[i],
                rs_send.at[W_Z3, g], rs_recv.at[R_Z3, n], to_near,
            ).start()

    def add_z1(key):
        g, i, m, column, width, split, buf, n = info(key)

        @pl.when(inner)
        def _():
            landing = buf["z1"].at[i]
            remote(landing, landing, rs_send.at[W_Z1, g], rs_recv.at[R_Z1, n], to_near).wait_recv()
            for step in range(2):
                at = (1 - pair) * 2 + step
                buf["x"][i, at] = buf["x"][i, at] + buf["z1"][i, step]
            remote(
                buf["x"].at[i, other_pair], buf["z2"].at[i],
                rs_send.at[W_Z2, g], rs_recv.at[R_Z2, n], to_mirror,
            ).start()

    def add_z2(key):
        g, i, m, column, width, split, buf, n = info(key)

        @pl.when(inner)
        def _():
            landing = buf["z2"].at[i]
            remote(landing, landing, rs_send.at[W_Z2, g], rs_recv.at[R_Z2, n], to_mirror).wait_recv()
            for step in range(2):
                at = pair * 2 + step
                buf["x"][i, at] = buf["x"][i, at] + buf["z2"][i, step]
            remote(
                buf["x"].at[i, near_z], buf["z3"].at[i],
                rs_send.at[W_Z3, g], rs_recv.at[R_Z3, n], to_near,
            ).start()

    def add_z3(key):
        g, i, m, column, width, split, buf, n = info(key)
        landing = buf["z3"].at[i]
        remote(landing, landing, rs_send.at[W_Z3, g], rs_recv.at[R_Z3, n], to_near).wait_recv()
        buf["last"][i, 0] = buf["x"][i, z] + buf["z3"][i]
        remote(
            buf["last"].at[i, 0], buf["last"].at[i, 1],
            rs_send.at[W_LAST, g], rs_recv.at[R_LAST, n], to_y,
        ).start()

    def finish(key):
        g, i, m, column, width, split, buf, n = info(key)
        landing = buf["last"].at[i, 1]
        remote(landing, landing, rs_send.at[W_LAST, g], rs_recv.at[R_LAST, n], to_y).wait_recv()
        if split:
            for which, slot in ((y, 0), (1 - y, 1)):
                columns = pl.ds(pl.multiple_of(column + which * (width // 2), 128), width // 2)
                sums[m][c, :, columns] = buf["last"][i, slot].astype(FULL)
        else:
            sums[m][c, :, pl.ds(column, width)] = buf["last"][i, 0].astype(FULL) + buf["last"][
                i, 1
            ].astype(FULL)
        piece = sums[m].at[c, :, pl.ds(column, width)]
        remote(piece, piece, rs_send.at[W_END, g], rs_end.at[g], to_c).start()

    reduce_plan = (
        (0, add_core), (1, add_y), (2, add_x), (3, add_z1), (4, add_z2), (5, add_z3), (6, finish),
    )
    steps_left = [0]

    def advance(limit=None):
        step = steps_left[0]
        steps_left[0] += 1
        for delay, action in reduce_plan:
            if 0 <= step - delay < len(REDUCE_ORDER):
                action(REDUCE_ORDER[step - delay])

    def grad_contract(i):
        columns = pl.ds(i * 256, 256)

        def body(s, carry):
            lanes = pl.ds(pl.multiple_of(s * 384, 128), 384)
            value = dot_tn(post[:, lanes], cot[:, columns]).astype(LOW)
            full[2][s // 2, s % 2, :, :, columns] = value.reshape(2, 192, 256)
            return carry

        lax.fori_loop(0, 8, body, 0)

    def grad_rows(source, other, target, columns, width):
        for half in range(2):
            value = dot_tn(source[:, half * 384 : half * 384 + 384], other).astype(LOW)
            target[2 * half : 2 * half + 2, :, :, :, columns] = value.reshape(2, 2, 2, 48, width)

    def grad_expand(i):
        span = slice(i * 768, i * 768 + 768)
        grad_rows(normed2, pre[:, span], full[3], pl.ds(i * 768, 768), 768)

    def norm_second_back(rows):
        unit, scale = center(resid[rows, :])
        grad = back_s[rows, :]
        top = cot[rows, :].astype(FULL)
        e = grad * v96[4:5, :]
        value = (
            e - jnp.mean(e, axis=-1, keepdims=True) - unit * jnp.mean(e * unit, axis=-1, keepdims=True)
        ) * scale + top
        back_r[rows, :] = value
        rounded = value.astype(LOW)
        back_m[rows, :] = rounded
        acc96[4] += fold8(grad * unit)
        acc96[5] += fold8(grad)
        acc96[3] += fold8(rounded.astype(FULL))
        acc96[6] += fold8(top)
        result[rows, :] = (resid[rows, :] + gather_out[rows, :] + v96[6:7, :]).astype(LOW)

    def convolve_back(begin, end):
        def body(step, carry):
            rows = pl.ds(pl.multiple_of((step // 6) * 128, 128), 128)
            lane = pl.multiple_of((step % 6) * 128, 128)
            lanes = pl.ds(lane, 128)
            where = places[rows, :]
            rest = left[rows, :]
            gate_in = short[1, rows, lanes]
            values = short[2, rows, lanes]
            top = back_g[rows, lanes]
            carried = values * gate_in
            back_conv = top * short[0, rows, lanes]
            acc96[2, :, lanes] += fold8(back_conv * carried)
            total = v96[2:3, lanes] * back_conv
            for low_lag in range(8):
                turned = turn(back_conv, -low_lag, 0)
                for high in range(LAGS // 8):
                    lag, skip = high * 8 + low_lag, high * 8
                    size = 128 - skip
                    moved = jnp.where(rest[:size] >= lag, turned[skip:], 0.0)
                    term = taps[lag : lag + 1, lanes] * moved
                    if skip:
                        total = jnp.concatenate([total[:size] + term, total[size:]], axis=0)
                    else:
                        total = total + term
                    d_taps[lag : lag + 1, lanes] += jnp.sum(
                        moved * carried[:size], axis=0, keepdims=True
                    )
            streams = (top * conv[rows, lanes], total * values, total * gate_in)
            for k in range(3):
                wide = pl.ds(pl.multiple_of(k * 768 + lane, 128), 128)
                grad = streams[k]
                before = proj[k, rows, lanes]
                acc288[1, :, wide] += fold8(grad)
                acc288[2, :, wide] += fold8(grad * before)
                value = v288[2:3, wide] * grad
                for lag in (1, 2):
                    moved = jnp.where(where >= lag, pltpu.roll(before, lag, 0), 0.0)
                    acc288[2 + lag, :, wide] += fold8(grad * moved)
                    later = jnp.where(rest >= lag, pltpu.roll(grad, 128 - lag, 0), 0.0)
                    value = value + v288[2 + lag : 3 + lag, wide] * later
                rounded = value.astype(LOW)
                bp[k, rows, lanes] = rounded
                acc288[0, :, wide] += fold8(rounded.astype(FULL))
            return carry

        lax.fori_loop(begin, end, body, 0)

    def norm_first_back(rows):
        unit, scale = center(tokens[rows, :].astype(FULL))
        grad = back_s[rows, :]
        e = grad * v96[0:1, :]
        delta[rows, :] = back_r[rows, :] + (
            e - jnp.mean(e, axis=-1, keepdims=True) - unit * jnp.mean(e * unit, axis=-1, keepdims=True)
        ) * scale
        acc96[0] += fold8(grad * unit)
        acc96[1] += fold8(grad)

    def small_grads():
        scale = v8[1:2, :]
        raw = d_taps[...] * decay[...]
        d_fil = exact(s_second[...], raw, (0, 0))
        b2 = exact(raw, fil_w[...], (1, 1)) * s_cos2[...]
        b2s = b2 * scale
        d_mid = exact(s_first[...], b2s, (0, 0))
        b1 = exact(b2s, mid_w[...], (1, 1)) * s_cos1[...]
        b1s = b1 * scale
        d_inner = exact(features[...], b1s, (0, 0))
        d_scale = jnp.sum(b2 * s_inner2[...] + b1 * s_inner1[...], axis=0, keepdims=True)
        rows8 = jnp.concatenate(
            [
                jnp.sum(b1s, axis=0, keepdims=True), d_scale, jnp.sum(b2s, axis=0, keepdims=True),
                jnp.zeros((5, 128), FULL),
            ],
            axis=0,
        )
        rows96 = jnp.concatenate(
            [jnp.sum(acc96[f], axis=0, keepdims=True) for f in range(7)] + [jnp.zeros((1, 768), FULL)],
            axis=0,
        )
        rows288 = jnp.concatenate(
            [jnp.sum(acc288[f], axis=0, keepdims=True) for f in range(5)]
            + [jnp.zeros((3, 2304), FULL)],
            axis=0,
        )
        rows_exp = jnp.sum(accexp[...], axis=0, keepdims=True)
        lane = lax.broadcasted_iota(jnp.int32, (8, 128), 1)
        row = lax.broadcasted_iota(jnp.int32, (8, 128), 0)
        wide_lane = lax.broadcasted_iota(jnp.int32, (64, 128), 1)
        long_lane = lax.broadcasted_iota(jnp.int32, (40, 128), 1)
        for s in range(8):
            a, b = s // 2, s % 2
            g_small[a, b, 0, 0:8, :] = jnp.where(lane < 96, turn(rows96, -96 * s, 1)[:, :128], 0.0)
            turned = turn(rows288, -288 * s, 1)
            for block in range(3):
                value = turned[:, block * 128 : block * 128 + 128]
                if block == 2:
                    value = jnp.where(lane < 32, value, 0.0)
                bias = rows_exp[:, s * 384 + block * 128 : s * 384 + block * 128 + 128]
                value = jnp.where(row == 5, jnp.broadcast_to(bias, (8, 128)), value)
                g_small[a, b, 0, 8 + block * 8 : 16 + block * 8, :] = value
            g_small[a, b, 0, 32:40, :] = jnp.where(lane < 8, turn(rows8, -8 * s, 1), 0.0)
            g_small[a, b, 0, 40:80, :] = jnp.where(long_lane < 8, turn(d_inner, -8 * s, 1), 0.0)
            g_small[a, b, 1, 0:8, :] = d_mid[8 * s : 8 * s + 8]
            g_small[a, b, 1, 8:72, :] = jnp.where(
                wide_lane < 96, turn(d_fil[0:64], -96 * s, 1)[:, :128], 0.0
            )
            g_small[a, b, 1, 72:80, :] = jnp.zeros((8, 128), FULL)

    grad_contract(0)
    stage((0, 0))
    grad_expand(0)
    stage((1, 0))
    grad_contract(1)
    stage((0, 1))
    advance()
    grad_expand(1)
    stage((1, 1))
    grad_contract(2)
    stage((0, 2))
    advance()
    row_blocks(16, norm_second_back)
    grad_expand(2)
    stage((1, 2))
    advance()
    grad_expand(3)
    stage((1, 3))
    advance()
    back_g[...] = dot_nt(back_m[...], matrix_of(1, pl.ds(0, 768), 768))
    grad_rows(gated, back_m[...], g_out, pl.ds(0, 768), 768)
    stage((2, 0))
    advance()
    convolve_back(0, 3)
    advance()
    convolve_back(3, 6)
    advance()
    convolve_back(6, 9)
    advance()
    convolve_back(9, 12)
    for key, k in (((3, 0), 0), ((4, 0), 1), ((3, 1), 2)):
        grad_rows(normed1, bp[k], g_in, pl.ds(k * 768, 768), 768)
        stage(key)
        advance()
    for k in range(3):
        value = dot_nt(bp[k], matrix_of(0, pl.ds(k * 768, 768), 768))
        if k == 0:
            back_s[...] = value
        else:
            back_s[...] += value
    row_blocks(16, norm_first_back)
    small_grads()
    stage((5, 0))
    while steps_left[0] < len(REDUCE_ORDER) + 6:
        advance()

    for g, (matrix, columns, width, split) in enumerate(REDUCE_GROUPS):
        piece = sums[matrix].at[1 - c, :, pl.ds(0, width * len(columns))]
        remote(piece, piece, rs_send.at[W_END, g], rs_end.at[g], to_c).wait_recv()
    for g, (matrix, columns, width, split) in enumerate(REDUCE_GROUPS):
        buf = groups[g]

        def leave(kind, ref, g=g):
            remote(ref, ref, rs_send.at[kind, g], rs_end.at[g], to_c).wait_send()

        leave(W_CORE, buf["core"])
        if split:
            leave(W_Y, buf["y"])
        leave(W_X, buf["x"])
        leave(W_Z3, buf["z3"])
        leave(W_LAST, buf["last"].at[:, 0])
        leave(W_END, sums[matrix].at[1 - c, :, pl.ds(0, width * len(columns))])

        @pl.when(inner)
        def _(leave=leave, buf=buf):
            leave(W_Z2, buf["z2"])

        @pl.when(jnp.logical_not(inner))
        def _(leave=leave, buf=buf):
            leave(W_Z1, buf["z1"])


def unpack_kernel(result, delta, s_in, s_out, s_con, s_exp, s_small, *outs):
    (
        o_result, o_delta, o_first_gain, o_first_shift, o_in, o_in_bias, o_short_w, o_short_b,
        o_inner_w, o_inner_b, o_scale, o_middle_w, o_middle_b, o_filter_w, o_direct, o_out,
        o_out_bias, o_second_gain, o_second_shift, o_exp, o_exp_bias, o_con, o_con_bias,
    ) = outs
    o_result[...] = result[...]
    o_delta[...] = delta[...]
    for source, target in ((s_in, o_in), (s_out, o_out), (s_con, o_con), (s_exp, o_exp)):
        height = source.shape[1]
        for half in range(2):
            target[half * height : half * height + height, :] = source[half]
    for row, target in enumerate(
        (o_first_gain, o_first_shift, o_direct, o_out_bias, o_second_gain, o_second_shift, o_con_bias)
    ):
        target[...] = s_small[0, row : row + 1, 0:96].reshape(96)
    wide = jnp.concatenate([s_small[0, 8:16, :], s_small[0, 16:24, :], s_small[0, 24:32, :]], axis=1)
    o_in_bias[...] = wide[0:1, 0:288].reshape(288)
    o_short_b[...] = wide[1:2, 0:288].reshape(288)
    o_short_w[...] = wide[2:5, 0:288]
    o_exp_bias[...] = wide[5:6].reshape(384)
    for row, target in enumerate((o_inner_b, o_scale, o_middle_b)):
        target[...] = s_small[0, 32 + row : 33 + row, 0:8].reshape(8)
    o_inner_w[...] = s_small[0, 40:73, 0:8]
    o_middle_w[...] = s_small[1, 0:8, 0:64]
    o_filter_w[...] = s_small[1, 8:72, 0:96]


def filter_constants(length, width):
    places = np.arange(LAGS, dtype=np.float64)
    scales = 0.0001 + np.arange(16, dtype=np.float64) * ((15.0 - 0.0001) / 15.0)
    phases = (2.0 * math.pi * places / length)[:, None] * scales[None, :]
    ramp = places / (length - 1)
    table = np.zeros((LAGS, 40), np.float32)
    table[:, 0] = ramp
    table[:, 1:17] = np.cos(phases)
    table[:, 17:33] = -np.sin(phases)
    rates = math.log(100.0) * (
        1.0 / 1.5 + (1.0 / 0.3 - 1.0 / 1.5) * np.arange(width, dtype=np.float64) / (width - 1)
    )
    return table, np.exp(-ramp[:, None] * rates[None, :]).astype(np.float32)


def block_device(
    tokens, segment_ids, cotangent, first_gain, first_shift, input_weight, input_bias,
    short_weight, short_bias, inner_weight, inner_bias, sine_scale, middle_weight, middle_bias,
    filter_weight, direct_gain, output_weight, output_bias, second_gain, second_shift,
    expand_weight, expand_bias, contract_weight, contract_bias,
):
    blocks, _, length, width = tokens.shape
    rows = blocks * length
    features, decay = filter_constants(length, width)

    def line(member):
        return member.reshape(1, -1) if member.ndim == 1 else member

    small_members = (
        first_gain, first_shift, input_bias, short_weight, short_bias, inner_weight, inner_bias,
        sine_scale, middle_weight, middle_bias, filter_weight, direct_gain, output_bias,
        second_gain, second_shift, expand_bias, contract_bias,
    )

    def halved(member):
        return member.reshape(2, member.shape[0] // 2, member.shape[1])

    shards = [halved(m) for m in (input_weight, output_weight, contract_weight, expand_weight)]
    inputs = (
        tokens.reshape(rows, width), segment_ids.reshape(blocks, length),
        cotangent.reshape(rows, width),
    ) + tuple(line(m) for m in small_members) + tuple(shards) + (
        jnp.asarray(features), jnp.asarray(decay),
    )
    shapes = [m.shape[1:] for m in shards] + [(SMALL_ROWS, 128)]
    outs = [
        jax.ShapeDtypeStruct((rows, width), LOW),
        jax.ShapeDtypeStruct((rows, width), FULL),
    ] + [jax.ShapeDtypeStruct((2,) + s, FULL) for s in shapes]
    count = len(GATHER_CHUNKS)
    crossing = sum(1 for chunk in GATHER_CHUNKS if chunk[3])
    vm = pltpu.VMEM
    scratch = [vm((4, 2, 2) + s, LOW) for s in shapes]
    scratch += [
        vm((4, 2, 2) + shapes[0], LOW), vm((4, 2, 2) + shapes[1], LOW),
        vm((4, 2, 2) + shapes[4], FULL), vm((2, SMALL_ROWS, 128), LOW),
        vm((2 * SMALL_ROWS, 128), FULL),
        vm((8, width), FULL), vm((8, 3 * width), FULL), vm((1, 4 * width), FULL), vm((8, 128), FULL),
        vm((128, 128), FULL), vm((128, width), FULL), vm((LAGS, width), FULL), vm((LAGS, width), FULL),
    ]
    scratch += [vm((LAGS, 128), FULL)] * 6
    scratch += [vm((rows, 128), jnp.int32)] * 2
    scratch += [
        vm((rows, width), LOW), vm((3, rows, width), FULL), vm((3, rows, width), FULL),
        vm((rows, width), FULL), vm((rows, width), LOW), vm((rows, width), FULL),
        vm((rows, width), LOW),
        vm((rows, 4 * width), FULL), vm((rows, 4 * width), LOW), vm((rows, 4 * width), LOW),
        vm((rows, width), FULL), vm((rows, width), FULL), vm((rows, width), FULL),
        vm((rows, width), FULL), vm((rows, width), LOW), vm((rows, width), FULL),
        vm((3, rows, width), LOW),
        vm((7, 8, width), FULL), vm((5, 8, 3 * width), FULL), vm((8, 4 * width), FULL),
    ]
    for matrix, columns, span, split in REDUCE_GROUPS:
        n, high = len(columns), shapes[matrix][0]
        kind = FULL if matrix == 4 else LOW
        v = span // 2 if split else span
        scratch += [
            vm((n, 4, 2, high, span), kind), vm((n, 4, high, v), kind), vm((n, 2, high, v), kind),
            vm((n, 2, high, v), kind), vm((n, high, v), kind), vm((n, 2, high, v), kind),
        ]
        if split:
            scratch.append(vm((n, 4, 2, high, v), kind))
    total = len(REDUCE_ORDER)
    splits = sum(len(g[1]) for g in REDUCE_GROUPS if g[3])
    dma = pltpu.SemaphoreType.DMA
    scratch += [
        dma((4, count)), dma((3, crossing)), dma((8,)), dma((6, 5)), dma((5,)),
        dma((6, total)), dma((splits,)), dma((8, len(REDUCE_GROUPS))), dma((len(REDUCE_GROUPS),)),
    ]
    in_vmem = pl.BlockSpec(memory_space=pltpu.VMEM)
    parts = pl.pallas_call(
        block_kernel,
        out_shape=outs,
        in_specs=[in_vmem] * len(inputs),
        out_specs=[in_vmem] * len(outs),
        scratch_shapes=scratch,
        compiler_params=pltpu.CompilerParams(
            collective_id=0, has_side_effects=True, vmem_limit_bytes=67043328
        ),
    )(*inputs)
    members = (
        first_gain, first_shift, input_weight, input_bias, short_weight, short_bias, inner_weight,
        inner_bias, sine_scale, middle_weight, middle_bias, filter_weight, direct_gain,
        output_weight, output_bias, second_gain, second_shift, expand_weight, expand_bias,
        contract_weight, contract_bias,
    )
    final = [outs[0], outs[1]] + [jax.ShapeDtypeStruct(m.shape, FULL) for m in members]
    done = pl.pallas_call(
        unpack_kernel,
        out_shape=final,
        in_specs=[in_vmem] * 7,
        out_specs=[in_vmem] * len(final),
    )(*parts)
    return (done[0].reshape(tokens.shape), done[1].reshape(tokens.shape)) + tuple(done[2:])


def per_device(
    tokens,
    segment_ids,
    cotangent,
    first_gain,
    first_shift,
    input_weight,
    input_bias,
    short_weight,
    short_bias,
    inner_weight,
    inner_bias,
    sine_scale,
    middle_weight,
    middle_bias,
    filter_weight,
    direct_gain,
    output_weight,
    output_bias,
    second_gain,
    second_shift,
    expand_weight,
    expand_bias,
    contract_weight,
    contract_bias,
):
    micro_count, local_sequences, length, width = tokens.shape
    row_count = local_sequences * length
    tables = wave_tables(length)

    def fetch_mixer():
        return (
            lax.all_gather(first_gain, "shard", axis=0, tiled=True),
            lax.all_gather(first_shift, "shard", axis=0, tiled=True),
            lax.all_gather(input_weight, "shard", axis=0, tiled=True),
            lax.all_gather(input_bias, "shard", axis=0, tiled=True),
            lax.all_gather(short_weight, "shard", axis=1, tiled=True),
            lax.all_gather(short_bias, "shard", axis=0, tiled=True),
            lax.all_gather(inner_weight, "shard", axis=1, tiled=True),
            lax.all_gather(inner_bias, "shard", axis=0, tiled=True),
            lax.all_gather(sine_scale, "shard", axis=0, tiled=True),
            lax.all_gather(middle_weight, "shard", axis=0, tiled=True),
            lax.all_gather(middle_bias, "shard", axis=0, tiled=True),
            lax.all_gather(filter_weight, "shard", axis=1, tiled=True),
            lax.all_gather(direct_gain, "shard", axis=0, tiled=True),
            lax.all_gather(output_weight, "shard", axis=0, tiled=True),
            lax.all_gather(output_bias, "shard", axis=0, tiled=True),
        )

    def fetch_dense():
        return (
            lax.all_gather(second_gain, "shard", axis=0, tiled=True),
            lax.all_gather(second_shift, "shard", axis=0, tiled=True),
            lax.all_gather(expand_weight, "shard", axis=0, tiled=True),
            lax.all_gather(expand_bias, "shard", axis=0, tiled=True),
            lax.all_gather(contract_weight, "shard", axis=0, tiled=True),
            lax.all_gather(contract_bias, "shard", axis=0, tiled=True),
        )

    results = []
    input_deltas = []
    mixer_total = None
    dense_total = None
    for micro_index in range(micro_count):
        mixer_parts = fetch_mixer()
        dense_parts = fetch_dense()
        kernel = filter_taps(
            to_float(mixer_parts[6]),
            to_float(mixer_parts[7]),
            to_float(mixer_parts[8]),
            to_float(mixer_parts[9]),
            to_float(mixer_parts[10]),
            to_float(mixer_parts[11]),
            length,
        )
        kernel, kernel_wave = (kernel, spectrum(tables, kernel))
        kernel_real, kernel_imag = kernel_wave
        segment_block = segment_ids[micro_index]
        membership = (
            segment_block[:, None, :] == jnp.arange(DOCS, dtype=jnp.int32)[None, :, None]
        ).astype(jnp.float32)
        flat_tokens = tokens[micro_index].reshape(row_count, width).astype(jnp.float32)
        normed_first = normalize(
            flat_tokens, to_float(mixer_parts[0]), to_float(mixer_parts[1])
        ).astype(jnp.bfloat16)
        projected = jnp.dot(
            normed_first, mixer_parts[2], preferred_element_type=jnp.float32
        ) + to_float(mixer_parts[3])
        projected_rows = projected.reshape(local_sequences, length, 3 * width)
        short_out = short_filter(
            projected_rows, segment_block, to_float(mixer_parts[4]), to_float(mixer_parts[5])
        )
        gate_out = short_out[:, :, :width]
        gate_in = short_out[:, :, width : 2 * width]
        values = short_out[:, :, 2 * width :]
        carried = values * gate_in
        direct = to_float(mixer_parts[12])
        carried_real, carried_imag = spectrum(tables, carried[:, None] * membership[:, :, :, None])
        conv_pieces = inverse(
            tables,
            carried_real * kernel_real - carried_imag * kernel_imag,
            carried_real * kernel_imag + carried_imag * kernel_real,
        )
        convolved = jnp.sum(conv_pieces * membership[:, :, :, None], axis=1) + direct * carried
        gated_low = (convolved * gate_out).astype(jnp.bfloat16).reshape(row_count, width)
        mixed_out = jnp.dot(
            gated_low, mixer_parts[13], preferred_element_type=jnp.float32
        ) + to_float(mixer_parts[14])
        residual = flat_tokens + mixed_out
        second_gain_f = to_float(dense_parts[0])
        second_shift_f = to_float(dense_parts[1])
        normed_second = normalize(residual, second_gain_f, second_shift_f).astype(jnp.bfloat16)
        hidden_pre = jnp.dot(
            normed_second, dense_parts[2], preferred_element_type=jnp.float32
        ) + to_float(dense_parts[3])
        hidden_post = smooth_gate(hidden_pre).astype(jnp.bfloat16)
        result = (
            residual
            + jnp.dot(hidden_post, dense_parts[4], preferred_element_type=jnp.float32)
            + to_float(dense_parts[5])
        )
        results.append(result.astype(jnp.bfloat16).reshape(local_sequences, length, width))
        back_mixer = fetch_mixer()
        back_dense = fetch_dense()
        upstream = cotangent[micro_index].reshape(row_count, width)
        upstream_float = upstream.astype(jnp.float32)
        delta_contract_weight = jnp.einsum(
            "tf,td->fd", hidden_post, upstream, preferred_element_type=jnp.float32
        )
        delta_contract_bias = jnp.sum(upstream_float, axis=0)
        back_hidden = jnp.einsum(
            "td,fd->tf", upstream, back_dense[4], preferred_element_type=jnp.float32
        )
        back_pre = jax.vjp(smooth_gate, hidden_pre)[1](back_hidden)[0].astype(jnp.bfloat16)
        delta_expand_weight = jnp.einsum(
            "td,tf->df", normed_second, back_pre, preferred_element_type=jnp.float32
        )
        delta_expand_bias = jnp.sum(back_pre.astype(jnp.float32), axis=0)
        back_second = jnp.einsum(
            "tf,df->td", back_pre, back_dense[2], preferred_element_type=jnp.float32
        )
        second_pull = jax.vjp(
            normalize, residual, to_float(back_dense[0]), to_float(back_dense[1])
        )[1]
        back_norm_second, delta_second_gain, delta_second_shift = second_pull(back_second)
        back_residual = upstream_float + back_norm_second
        back_mixed = back_residual.astype(jnp.bfloat16)
        delta_output_weight = jnp.einsum(
            "td,te->de", gated_low, back_mixed, preferred_element_type=jnp.float32
        )
        delta_output_bias = jnp.sum(back_mixed.astype(jnp.float32), axis=0)
        back_gated = jnp.einsum(
            "te,de->td", back_mixed, back_mixer[13], preferred_element_type=jnp.float32
        ).reshape(local_sequences, length, width)
        back_conv = back_gated * gate_out
        grad_real, grad_imag = spectrum(tables, back_conv[:, None] * membership[:, :, :, None])
        carried_back_pieces = inverse(
            tables,
            grad_real * kernel_real + grad_imag * kernel_imag,
            grad_imag * kernel_real - grad_real * kernel_imag,
        )
        back_carried = (
            jnp.sum(carried_back_pieces * membership[:, :, :, None], axis=1) + direct * back_conv
        )
        cross_real = jnp.sum(grad_real * carried_real + grad_imag * carried_imag, axis=(0, 1))
        cross_imag = jnp.sum(grad_imag * carried_real - grad_real * carried_imag, axis=(0, 1))
        back_kernel = inverse(tables, cross_real, cross_imag)
        delta_direct = jnp.sum(back_conv * carried, axis=(0, 1))
        back_short = jnp.concatenate(
            [back_gated * convolved, back_carried * values, back_carried * gate_in], axis=2
        )
        short_pull = jax.vjp(
            lambda rows_in, taps_in, offset_in: short_filter(
                rows_in, segment_block, taps_in, offset_in
            ),
            projected_rows,
            to_float(back_mixer[4]),
            to_float(back_mixer[5]),
        )[1]
        back_projected, delta_short_weight, delta_short_bias = short_pull(back_short)
        back_projected = back_projected.reshape(row_count, 3 * width).astype(jnp.bfloat16)
        delta_input_weight = jnp.einsum(
            "td,tp->dp", normed_first, back_projected, preferred_element_type=jnp.float32
        )
        delta_input_bias = jnp.sum(back_projected.astype(jnp.float32), axis=0)
        back_first = jnp.einsum(
            "tp,dp->td", back_projected, back_mixer[2], preferred_element_type=jnp.float32
        )
        first_pull = jax.vjp(
            normalize, flat_tokens, to_float(back_mixer[0]), to_float(back_mixer[1])
        )[1]
        back_norm_first, delta_first_gain, delta_first_shift = first_pull(back_first)
        input_deltas.append(
            (back_residual + back_norm_first).reshape(local_sequences, length, width)
        )
        filter_pull = jax.vjp(
            lambda weight_one, bias_one, scale_all, weight_two, bias_two, weight_three: filter_taps(
                weight_one, bias_one, scale_all, weight_two, bias_two, weight_three, length
            ),
            to_float(back_mixer[6]),
            to_float(back_mixer[7]),
            to_float(back_mixer[8]),
            to_float(back_mixer[9]),
            to_float(back_mixer[10]),
            to_float(back_mixer[11]),
        )[1]
        filter_deltas = filter_pull(back_kernel)
        mixer_part = (
            delta_first_gain,
            delta_first_shift,
            delta_input_weight,
            delta_input_bias,
            delta_short_weight,
            delta_short_bias,
            filter_deltas[0],
            filter_deltas[1],
            filter_deltas[2],
            filter_deltas[3],
            filter_deltas[4],
            filter_deltas[5],
            delta_direct,
            delta_output_weight,
            delta_output_bias,
        )
        dense_part = (
            delta_second_gain,
            delta_second_shift,
            delta_expand_weight,
            delta_expand_bias,
            delta_contract_weight,
            delta_contract_bias,
        )
        if micro_index == 0:
            mixer_total = mixer_part
            dense_total = dense_part
        else:
            mixer_total = jax.tree.map(jnp.add, mixer_total, mixer_part)
            dense_total = jax.tree.map(jnp.add, dense_total, dense_part)
    dense_total = (
        lax.psum_scatter(dense_total[0], "shard", scatter_dimension=0, tiled=True),
        lax.psum_scatter(dense_total[1], "shard", scatter_dimension=0, tiled=True),
        lax.psum_scatter(dense_total[2], "shard", scatter_dimension=0, tiled=True),
        lax.psum_scatter(dense_total[3], "shard", scatter_dimension=0, tiled=True),
        lax.psum_scatter(dense_total[4], "shard", scatter_dimension=0, tiled=True),
        lax.psum_scatter(dense_total[5], "shard", scatter_dimension=0, tiled=True),
    )
    mixer_total = (
        lax.psum_scatter(mixer_total[0], "shard", scatter_dimension=0, tiled=True),
        lax.psum_scatter(mixer_total[1], "shard", scatter_dimension=0, tiled=True),
        lax.psum_scatter(mixer_total[2], "shard", scatter_dimension=0, tiled=True),
        lax.psum_scatter(mixer_total[3], "shard", scatter_dimension=0, tiled=True),
        lax.psum_scatter(mixer_total[4], "shard", scatter_dimension=1, tiled=True),
        lax.psum_scatter(mixer_total[5], "shard", scatter_dimension=0, tiled=True),
        lax.psum_scatter(mixer_total[6], "shard", scatter_dimension=1, tiled=True),
        lax.psum_scatter(mixer_total[7], "shard", scatter_dimension=0, tiled=True),
        lax.psum_scatter(mixer_total[8], "shard", scatter_dimension=0, tiled=True),
        lax.psum_scatter(mixer_total[9], "shard", scatter_dimension=0, tiled=True),
        lax.psum_scatter(mixer_total[10], "shard", scatter_dimension=0, tiled=True),
        lax.psum_scatter(mixer_total[11], "shard", scatter_dimension=1, tiled=True),
        lax.psum_scatter(mixer_total[12], "shard", scatter_dimension=0, tiled=True),
        lax.psum_scatter(mixer_total[13], "shard", scatter_dimension=0, tiled=True),
        lax.psum_scatter(mixer_total[14], "shard", scatter_dimension=0, tiled=True),
    )
    summed = lax.psum(
        (
            mixer_total[0],
            mixer_total[1],
            mixer_total[2],
            mixer_total[3],
            mixer_total[4],
            mixer_total[5],
            mixer_total[6],
            mixer_total[7],
            mixer_total[8],
            mixer_total[9],
            mixer_total[10],
            mixer_total[11],
            mixer_total[12],
            mixer_total[13],
            mixer_total[14],
            dense_total[0],
            dense_total[1],
            dense_total[2],
            dense_total[3],
            dense_total[4],
            dense_total[5],
        ),
        "rep",
    )
    return (jnp.stack(results), jnp.stack(input_deltas)) + tuple(summed)


def solution(mesh):
    placed = (
        P(None, ("rep", "shard"), None, None),
        P(None, ("rep", "shard"), None),
        P(None, ("rep", "shard"), None, None),
        P("shard"),
        P("shard"),
        P("shard", None),
        P("shard"),
        P(None, "shard"),
        P("shard"),
        P(None, "shard"),
        P("shard"),
        P("shard"),
        P("shard", None),
        P("shard"),
        P(None, "shard"),
        P("shard"),
        P("shard", None),
        P("shard"),
        P("shard"),
        P("shard"),
        P("shard", None),
        P("shard"),
        P("shard", None),
        P("shard"),
    )
    blocked = dict(mesh.shape) == {"rep": 4, "shard": 8}
    return jax.shard_map(
        block_device if blocked else per_device,
        mesh=mesh,
        in_specs=placed,
        out_specs=(
            P(None, ("rep", "shard"), None, None),
            P(None, ("rep", "shard"), None, None),
            P("shard"),
            P("shard"),
            P("shard", None),
            P("shard"),
            P(None, "shard"),
            P("shard"),
            P(None, "shard"),
            P("shard"),
            P("shard"),
            P("shard", None),
            P("shard"),
            P(None, "shard"),
            P("shard"),
            P("shard", None),
            P("shard"),
            P("shard"),
            P("shard"),
            P("shard", None),
            P("shard"),
            P("shard", None),
            P("shard"),
        ),
        check_vma=False,
    )
```

```python
import math

import jax
import jax.numpy as jnp
import numpy as np
from jax import lax
from jax.experimental import pallas as pl
from jax.experimental.pallas import tpu as pltpu
from jax.sharding import PartitionSpec as P

DOCS = 6


EPSILON = 1e-05
HIGHEST = lax.Precision.HIGHEST


def positions(length):
    places = jnp.arange(length, dtype=jnp.float32)
    linear_ramp = places / (length - 1)
    angles = 2.0 * math.pi * places / length
    scales = 0.0001 + jnp.arange(16, dtype=jnp.float32) * ((15.0 - 0.0001) / 15.0)
    phases = angles[:, None] * scales[None, :]
    return jnp.concatenate([linear_ramp[:, None], jnp.cos(phases), -jnp.sin(phases)], axis=1)


def decay_table(length, width):
    linear_ramp = jnp.arange(length, dtype=jnp.float32) / (length - 1)
    rates = math.log(100.0) * (
        1.0 / 1.5 + (1.0 / 0.3 - 1.0 / 1.5) * jnp.arange(width, dtype=jnp.float32) / (width - 1)
    )
    return jnp.exp(-linear_ramp[:, None] * rates[None, :])


def filter_taps(
    inner_weight, inner_bias, sine_scale, middle_weight, middle_bias, filter_weight, length
):
    features = positions(length)
    first_sine = jnp.sin(
        sine_scale * (jnp.dot(features, inner_weight, precision=HIGHEST) + inner_bias)
    )
    second_sine = jnp.sin(
        sine_scale * (jnp.dot(first_sine, middle_weight, precision=HIGHEST) + middle_bias)
    )
    return jnp.dot(second_sine, filter_weight, precision=HIGHEST) * decay_table(
        length, filter_weight.shape[1]
    )


def normalize(values, gain_row, shift_row):
    center = values - jnp.mean(values, axis=-1, keepdims=True)
    spread = jnp.mean(center * center, axis=-1, keepdims=True)
    return center * lax.rsqrt(spread + EPSILON) * gain_row + shift_row


def smooth_gate(values):
    return jax.nn.gelu(values, approximate=True)


def to_float(member):
    return member.astype(jnp.float32)


def short_filter(projected, segments, weight, offset):
    running = offset + weight[0] * projected
    for step_back in (1, 2):
        moved_rows = jnp.concatenate(
            [jnp.zeros_like(projected[:, :step_back]), projected[:, :-step_back]], axis=1
        )
        moved_ids = jnp.concatenate(
            [jnp.full_like(segments[:, :step_back], -1), segments[:, :-step_back]], axis=1
        )
        same_doc = (moved_ids == segments).astype(projected.dtype)
        running = running + weight[step_back] * moved_rows * same_doc[:, :, None]
    return running


def wave_tables(length):
    padded_size = 2 * length
    freq_index = jnp.arange(length + 1, dtype=jnp.int32)
    place_index = jnp.arange(length, dtype=jnp.int32)
    wrapped = freq_index[:, None] * place_index[None, :] % padded_size
    angles = 2.0 * math.pi / padded_size * wrapped.astype(jnp.float32)
    weights_row = (
        jnp.where((freq_index == 0) | (freq_index == length), 1.0, 2.0).astype(jnp.float32)
        / padded_size
    )
    return (jnp.cos(angles), jnp.sin(angles), weights_row)


def spectrum(tables, signal):
    cosine, sine, weights_row = tables
    real_part = jnp.einsum("ft,...td->...fd", cosine, signal, precision=HIGHEST)
    imag_part = -jnp.einsum("ft,...td->...fd", sine, signal, precision=HIGHEST)
    return (real_part, imag_part)


def inverse(tables, real_part, imag_part):
    cosine, sine, weights_row = tables
    scaled_real = real_part * weights_row[:, None]
    scaled_imag = imag_part * weights_row[:, None]
    return jnp.einsum("ft,...fd->...td", cosine, scaled_real, precision=HIGHEST) - jnp.einsum(
        "ft,...fd->...td", sine, scaled_imag, precision=HIGHEST
    )


MESH_ID = pl.DeviceIdType.MESH
LAGS = 64
LOW = jnp.bfloat16
FULL = jnp.float32
WHOLE, SPLIT, LINE = range(3)
GATHER_CHUNKS = (
    (4, 0, 128, WHOLE),
    (0, 768, 768, SPLIT),
    (0, 1536, 768, SPLIT),
    (0, 0, 768, SPLIT),
    (1, 0, 768, SPLIT),
    (3, 0, 768, WHOLE),
    (2, 0, 256, SPLIT),
    (2, 256, 256, SPLIT),
    (3, 768, 768, LINE),
    (2, 512, 256, SPLIT),
    (3, 1536, 768, WHOLE),
    (3, 2304, 768, WHOLE),
)
REDUCE_GROUPS = (
    (2, (0, 256), 256, SPLIT),
    (2, (512,), 256, WHOLE),
    (3, (0, 1536), 768, WHOLE),
    (3, (2304,), 768, LINE),
    (3, (768,), 768, SPLIT),
    (1, (0,), 768, SPLIT),
    (0, (0, 512), 512, SPLIT),
    (0, (1024, 1408), 384, WHOLE),
    (0, (1792,), 512, SPLIT),
    (4, (0,), 128, WHOLE),
)
REDUCE_ORDER = (
    (2, 0), (4, 0), (2, 1), (3, 0), (0, 0), (0, 1), (1, 0), (5, 0), (6, 0), (6, 1), (7, 0), (7, 1), (8, 0), (9, 0),
)
(
    DO_FIRST, DO_NEAR, DO_FAR, DO_SIDE, DO_CROSS, DO_PLACES, DO_UNPACK, DO_NORM1,
    DO_PROJECT, DO_CONV, DO_MIX, DO_EXPAND, DO_FEED, DO_DRAIN, DO_GCON, DO_GEXP,
    DO_NORM2B, DO_BACKG, DO_GOUT, DO_CONVB, DO_GIN, DO_BFIRST, DO_NORM1B, DO_SMALL,
    DO_STAGE, DO_ACORE, DO_AY, DO_AX, DO_AZ1, DO_AZ2, DO_AZ3, DO_FIN,
    DO_END,
) = range(33)
SCHEDULE = (
    (DO_FIRST, 0), (DO_FIRST, 8), (DO_FIRST, 1), (DO_FIRST, 2), (DO_FIRST, 3), (DO_FIRST, 4),
    (DO_NEAR, 1), (DO_NEAR, 2), (DO_FIRST, 5), (DO_NEAR, 3), (DO_NEAR, 4), (DO_FAR, 1), (DO_FAR, 2),
    (DO_NEAR, 0), (DO_PLACES, 0), (DO_FAR, 3), (DO_FAR, 4), (DO_SIDE, 1), (DO_FIRST, 6),
    (DO_FIRST, 7), (DO_SIDE, 2), (DO_FAR, 0), (DO_FIRST, 9), (DO_FIRST, 10), (DO_FIRST, 11),
    (DO_NEAR, 8), (DO_CROSS, 1), (DO_NEAR, 6), (DO_SIDE, 4), (DO_NEAR, 9), (DO_SIDE, 3),
    (DO_SIDE, 0), (DO_CROSS, 2), (DO_NEAR, 7), (DO_FAR, 9), (DO_NEAR, 5), (DO_FAR, 6),
    (DO_UNPACK, 0), (DO_NORM1, 0), (DO_NEAR, 11), (DO_PROJECT, 1), (DO_FAR, 8), (DO_CROSS, 4),
    (DO_SIDE, 9), (DO_FAR, 7), (DO_PROJECT, 2), (DO_CONV, 0), (DO_FAR, 5), (DO_CONV, 1),
    (DO_FAR, 11), (DO_CROSS, 3), (DO_CONV, 2), (DO_CONV, 3), (DO_SIDE, 6), (DO_PROJECT, 0),
    (DO_NEAR, 10), (DO_SIDE, 8), (DO_SIDE, 5), (DO_SIDE, 7), (DO_CROSS, 9), (DO_MIX, 0),
    (DO_EXPAND, 0), (DO_SIDE, 11), (DO_FAR, 10), (DO_EXPAND, 1), (DO_CROSS, 6), (DO_CROSS, 7),
    (DO_EXPAND, 3), (DO_SIDE, 10), (DO_FEED, 0), (DO_GEXP, 0), (DO_STAGE, (2, 0)), (DO_FEED, 1),
    (DO_GEXP, 1), (DO_STAGE, (4, 0)), (DO_ACORE, (2, 0)), (DO_EXPAND, 2), (DO_FEED, 2),
    (DO_GEXP, 2), (DO_STAGE, (2, 1)), (DO_ACORE, (4, 0)), (DO_FEED, 3), (DO_DRAIN, 0),
    (DO_ACORE, (2, 1)), (DO_GCON, 0), (DO_STAGE, (0, 0)), (DO_STAGE, (0, 1)), (DO_STAGE, (1, 0)),
    (DO_AX, (2, 0)), (DO_NORM2B, 0), (DO_GEXP, 3), (DO_ACORE, (0, 0)), (DO_BACKG, 0),
    (DO_STAGE, (3, 0)), (DO_AX, (2, 1)), (DO_GOUT, 0), (DO_STAGE, (5, 0)), (DO_AY, (4, 0)),
    (DO_ACORE, (1, 0)), (DO_ACORE, (3, 0)), (DO_ACORE, (0, 1)), (DO_CONVB, 0), (DO_CONVB, 1),
    (DO_CONVB, 2), (DO_AZ1, (2, 1)), (DO_AY, (0, 0)), (DO_ACORE, (5, 0)), (DO_AX, (1, 0)),
    (DO_CONVB, 3), (DO_AY, (0, 1)), (DO_GIN, 1), (DO_AZ1, (2, 0)), (DO_STAGE, (7, 0)), (DO_GIN, 0),
    (DO_STAGE, (6, 0)), (DO_GIN, 2), (DO_STAGE, (7, 1)), (DO_STAGE, (6, 1)), (DO_AZ1, (3, 0)),
    (DO_AX, (4, 0)), (DO_ACORE, (7, 0)), (DO_ACORE, (6, 0)), (DO_AX, (0, 0)), (DO_ACORE, (7, 1)),
    (DO_AX, (0, 1)), (DO_ACORE, (6, 1)), (DO_AY, (5, 0)), (DO_BFIRST, 0), (DO_STAGE, (8, 0)),
    (DO_AZ1, (4, 0)), (DO_NORM1B, 0), (DO_AX, (7, 0)), (DO_AZ1, (1, 0)), (DO_SMALL, 0),
    (DO_STAGE, (9, 0)), (DO_AY, (6, 0)), (DO_ACORE, (8, 0)), (DO_AZ2, (2, 1)), (DO_AZ3, (2, 1)),
    (DO_AX, (7, 1)), (DO_AZ2, (3, 0)), (DO_AZ1, (0, 0)), (DO_ACORE, (9, 0)), (DO_AX, (5, 0)),
    (DO_AZ2, (1, 0)), (DO_AZ3, (1, 0)), (DO_AZ1, (0, 1)), (DO_AX, (6, 0)), (DO_AY, (6, 1)),
    (DO_AZ2, (2, 0)), (DO_AY, (8, 0)), (DO_AZ3, (2, 0)), (DO_AZ3, (3, 0)), (DO_AZ1, (7, 1)),
    (DO_AZ2, (4, 0)), (DO_AX, (9, 0)), (DO_AZ2, (0, 1)), (DO_AZ1, (7, 0)), (DO_AZ2, (0, 0)),
    (DO_AZ3, (0, 1)), (DO_AX, (6, 1)), (DO_AZ3, (4, 0)), (DO_AZ2, (7, 1)), (DO_AZ3, (7, 1)),
    (DO_AZ1, (5, 0)), (DO_AZ1, (6, 0)), (DO_AZ2, (7, 0)), (DO_AZ3, (7, 0)), (DO_AZ1, (9, 0)),
    (DO_AX, (8, 0)), (DO_FIN, (2, 0)), (DO_AZ3, (0, 0)), (DO_AZ1, (6, 1)), (DO_AZ2, (6, 0)),
    (DO_AX, (3, 0)), (DO_AZ2, (5, 0)), (DO_AZ3, (6, 0)), (DO_AZ3, (5, 0)), (DO_FIN, (7, 0)),
    (DO_AZ2, (9, 0)), (DO_FIN, (0, 0)), (DO_AZ1, (8, 0)), (DO_AZ2, (6, 1)), (DO_AZ3, (6, 1)),
    (DO_AZ2, (8, 0)), (DO_FIN, (6, 0)), (DO_AZ3, (9, 0)), (DO_AZ3, (8, 0)), (DO_FIN, (0, 1)),
    (DO_FIN, (4, 0)), (DO_FIN, (2, 1)), (DO_FIN, (1, 0)), (DO_FIN, (6, 1)), (DO_FIN, (7, 1)),
    (DO_FIN, (5, 0)), (DO_FIN, (3, 0)), (DO_FIN, (9, 0)), (DO_FIN, (8, 0)), (DO_END, 0),
)
SMALL_ROWS = 80
NORM_ROWS = 128
INNER_OUT = 8


def dot_nn(left_side, right_side):
    return jnp.dot(left_side, right_side, preferred_element_type=FULL)


def dot_nt(left_side, right_side):
    return lax.dot_general(
        left_side, right_side, (((1,), (1,)), ((), ())), preferred_element_type=FULL
    )


def dot_tn(left_side, right_side):
    return lax.dot_general(
        left_side, right_side, (((0,), (0,)), ((), ())), preferred_element_type=FULL
    )


def exact(left_side, right_side, contract):
    return lax.dot_general(
        left_side, right_side, (((contract[0],), (contract[1],)), ((), ())),
        preferred_element_type=FULL, precision=HIGHEST,
    )


def fold8(values):
    rows, columns = values.shape
    return jnp.sum(values.reshape(rows // 8, 8, columns), axis=0)


def widen(values, width):
    rows, columns = values.shape
    if columns == width:
        return values
    return jnp.concatenate([values, jnp.zeros((rows, width - columns), values.dtype)], axis=1)


def turn(values, amount, axis):
    size = values.shape[axis]
    amount = amount % size
    return values if amount == 0 else pltpu.roll(values, amount, axis)


def block_kernel(*refs):
    refs = list(refs)

    def take(number):
        taken = refs[:number]
        del refs[:number]
        return taken

    tokens, segs, cot = take(3)
    (
        r_first_gain, r_first_shift, r_in_bias, r_short_w, r_short_b, r_inner_w, r_inner_b,
        r_scale, r_middle_w, r_middle_b, r_filter_w, r_direct, r_out_bias, r_second_gain,
        r_second_shift, r_exp_bias, r_con_bias,
    ) = take(17)
    own = take(4)
    features, decay = take(2)
    result, delta = take(2)
    sums = take(5)
    full = take(5)
    g_in, g_out, g_small, own_small, pack = take(5)
    v96, v288, vexp, v8 = take(4)
    mid_w, fil_w, taps, d_taps = take(4)
    s_inner1, s_first, s_cos1, s_inner2, s_second, s_cos2 = take(6)
    places, left = take(2)
    normed1, proj, short, conv, gated, resid, normed2 = take(7)
    hidden, post, pre, back_h, gather_out, back_s, back_m, bp = take(8)
    back_r, back_g = back_h, gather_out
    acc96, acc288, accexp = take(3)
    groups = []
    for matrix, columns, width, kind in REDUCE_GROUPS:
        members = take(7 if kind == SPLIT else 6)
        names = ("core", "x", "z1", "z2", "z3", "last") + (("y",) if kind == SPLIT else ())
        groups.append(dict(zip(names, members)))
    ag_recv, ag_cross, ag_core, ag_send, own_sem, rs_recv, rs_y, rs_send, rs_end = take(9)
    assert not refs

    own = list(own) + [own_small]
    grads = (g_in, g_out, full[2], full[3], g_small)

    rep = lax.axis_index("rep")
    shard = lax.axis_index("shard")
    y, c = rep // 2, rep % 2
    z, x = shard // 2, shard % 2
    pair = z // 2
    near_z = z + 1 - 2 * (z % 2)
    inner = ((z + 1) // 2) % 2 == 1
    to_near = (rep, near_z * 2 + x)
    to_mirror = (rep, (3 - z) * 2 + x)
    to_x = (rep, z * 2 + 1 - x)
    to_y = ((1 - y) * 2 + c, shard)
    to_c = (y * 2 + 1 - c, shard)
    own_pair = pl.ds(pair * 2, 2)
    other_pair = pl.ds((1 - pair) * 2, 2)

    barrier = pltpu.get_barrier_semaphore()
    for target in (to_near, to_x, to_y, to_c):
        pl.semaphore_signal(barrier, inc=1, device_id=target, device_id_type=MESH_ID)

    @pl.when(inner)
    def _():
        pl.semaphore_signal(barrier, inc=1, device_id=to_mirror, device_id_type=MESH_ID)

    def remote(source, landing, send, recv, device):
        return pltpu.make_async_remote_copy(
            src_ref=source, dst_ref=landing, send_sem=send, recv_sem=recv,
            device_id=device, device_id_type=MESH_ID,
        )

    pack[...] = jnp.zeros_like(pack)
    for row, member in enumerate(
        (r_first_gain, r_first_shift, r_direct, r_out_bias, r_second_gain, r_second_shift, r_con_bias)
    ):
        pack[row : row + 1, 0:96] = member[...].astype(FULL).reshape(1, 96)
    in_bias, short_b = (m[...].astype(FULL).reshape(1, 288) for m in (r_in_bias, r_short_b))
    exp_bias = r_exp_bias[...].astype(FULL).reshape(1, 384)
    for block in range(3):
        lanes = 128 if block < 2 else 32
        span = slice(block * 128, block * 128 + lanes)
        top = 8 + block * 8
        pack[top : top + 1, 0:lanes] = in_bias[:, span]
        pack[top + 1 : top + 2, 0:lanes] = short_b[:, span]
        pack[top + 2 : top + 5, 0:lanes] = r_short_w[:, span].astype(FULL)
        pack[top + 5 : top + 6, :] = exp_bias[:, block * 128 : block * 128 + 128]
    for row, member in enumerate((r_inner_b, r_scale, r_middle_b)):
        pack[32 + row : 33 + row, 0:8] = member[...].astype(FULL).reshape(1, 8)
    pack[40:80, :] = jnp.concatenate(
        [widen(r_inner_w[...].astype(FULL), 128), jnp.zeros((120, 128), FULL)], axis=0
    ).T[0:40]
    pack[80:88, 0:64] = r_middle_w[...].astype(FULL)
    pack[88:152, 0:96] = r_filter_w[...].astype(FULL)
    own_small[0] = pack[0:80, :].astype(LOW)
    own_small[1] = pack[80:160, :].astype(LOW)

    acc96[...] = jnp.zeros_like(acc96)
    acc288[...] = jnp.zeros_like(acc288)
    accexp[...] = jnp.zeros_like(accexp)
    d_taps[...] = jnp.zeros_like(d_taps)

    pl.semaphore_wait(barrier, 4 + ((z + 1) // 2) % 2)

    chunks = GATHER_CHUNKS
    count = len(chunks)
    cross_index = {}
    for index, chunk in enumerate(chunks):
        if chunk[3] == SPLIT:
            cross_index[index] = len(cross_index)
    NEAR, FAR, SIDE0, SIDE1 = range(4)
    S_NEAR, S_MIRROR, S_BACK, S_SIDE, S_CROSS, S_CORE = range(6)

    def part(chunk, quarter):
        matrix, column, width, kind = chunk
        if kind == SPLIT:
            return pl.ds(pl.multiple_of(column + quarter * (width // 2), 128), width // 2)
        return pl.ds(column, width)

    def whole(chunk):
        return pl.ds(chunk[1], chunk[2])

    for matrix in range(5):
        pltpu.make_async_copy(own[matrix].at[c], full[matrix].at[z, x, c], own_sem.at[matrix]).start()

    send_groups = []
    for chunk in chunks:
        key = chunk[:1] if chunk[0] != 3 else chunk[:2]
        if key not in send_groups:
            send_groups.append(key)

    def group_of(chunk):
        return send_groups.index(chunk[:1] if chunk[0] != 3 else chunk[:2])

    def first(index):
        chunk = chunks[index]
        m, s = chunk[0], group_of(chunk)
        piece = own[m].at[c, :, part(chunk, y)]
        landing = full[m].at[z, x, c, :, part(chunk, y)]
        if chunk[3] == LINE:
            remote(piece, landing, ag_send.at[S_SIDE, s], ag_recv.at[SIDE0, index], to_x).start()
        else:
            remote(piece, landing, ag_send.at[S_NEAR, s], ag_recv.at[NEAR, index], to_near).start()

    def line_near(index):
        chunk = chunks[index]
        m, s = chunk[0], group_of(chunk)
        arrived = full[m].at[z, 1 - x, c, :, whole(chunk)]
        remote(arrived, arrived, ag_send.at[S_SIDE, s], ag_recv.at[SIDE0, index], to_x).wait_recv()
        both = full[m].at[z, :, c, :, whole(chunk)]
        remote(both, both, ag_send.at[S_NEAR, s], ag_recv.at[NEAR, index], to_near).start()

    def line_far(index):
        chunk = chunks[index]
        m, s = chunk[0], group_of(chunk)
        arrived = full[m].at[near_z, :, c, :, whole(chunk)]
        remote(arrived, arrived, ag_send.at[S_NEAR, s], ag_recv.at[NEAR, index], to_near).wait_recv()

        @pl.when(inner)
        def _():
            four = full[m].at[own_pair, :, c, :, whole(chunk)]
            remote(four, four, ag_send.at[S_MIRROR, s], ag_recv.at[FAR, index], to_mirror).start()

    def line_side(index):
        chunk = chunks[index]
        m, s = chunk[0], group_of(chunk)
        four = full[m].at[other_pair, :, c, :, whole(chunk)]
        remote(four, four, ag_send.at[S_MIRROR, s], ag_recv.at[FAR, index], to_near).wait_recv()

        @pl.when(inner)
        def _():
            remote(four, four, ag_send.at[S_BACK, s], ag_recv.at[FAR, index], to_near).start()

        to_core(index)

    def near(index):
        chunk = chunks[index]
        if chunk[3] == LINE:
            return line_near(index)
        m, s = chunk[0], group_of(chunk)
        arrived = full[m].at[near_z, x, c, :, part(chunk, y)]
        remote(arrived, arrived, ag_send.at[S_NEAR, s], ag_recv.at[NEAR, index], to_near).wait_recv()
        both = full[m].at[own_pair, x, c, :, part(chunk, y)]

        @pl.when(inner)
        def _():
            remote(both, both, ag_send.at[S_MIRROR, s], ag_recv.at[FAR, index], to_mirror).start()

        remote(both, both, ag_send.at[S_SIDE, s], ag_recv.at[SIDE0, index], to_x).start()
        if chunk[3] == SPLIT:
            remote(
                arrived, arrived, ag_send.at[S_CROSS, s], ag_cross.at[0, cross_index[index]], to_y
            ).start()

    def far(index):
        chunk = chunks[index]
        if chunk[3] == LINE:
            return line_far(index)
        m, s = chunk[0], group_of(chunk)
        both = full[m].at[other_pair, x, c, :, part(chunk, y)]
        remote(both, both, ag_send.at[S_MIRROR, s], ag_recv.at[FAR, index], to_near).wait_recv()

        @pl.when(inner)
        def _():
            remote(both, both, ag_send.at[S_BACK, s], ag_recv.at[FAR, index], to_near).start()

        remote(both, both, ag_send.at[S_SIDE, s], ag_recv.at[SIDE1, index], to_x).start()
        if chunk[3] == SPLIT:
            remote(
                both, both, ag_send.at[S_CROSS, s], ag_cross.at[1, cross_index[index]], to_y
            ).start()

    def to_core(index):
        chunk = chunks[index]
        m, s = chunk[0], group_of(chunk)
        piece = full[m].at[:, :, c, :, whole(chunk)]
        remote(piece, piece, ag_send.at[S_CORE, s], ag_core.at[index], to_c).start()

    def side(index):
        chunk = chunks[index]
        if chunk[3] == LINE:
            return line_side(index)
        m, s = chunk[0], group_of(chunk)
        for place, slot in ((own_pair, SIDE0), (other_pair, SIDE1)):
            both = full[m].at[place, 1 - x, c, :, part(chunk, y)]
            remote(both, both, ag_send.at[S_SIDE, s], ag_recv.at[slot, index], to_x).wait_recv()
        if chunk[3] == SPLIT:
            column = full[m].at[:, 1 - x, c, :, part(chunk, y)]
            remote(
                column, column, ag_send.at[S_CROSS, s], ag_cross.at[2, cross_index[index]], to_y
            ).start()
        else:
            to_core(index)

    def cross(index):
        chunk = chunks[index]
        m, s = chunk[0], group_of(chunk)
        for slot, piece in enumerate(
            (
                full[m].at[near_z, x, c, :, part(chunk, 1 - y)],
                full[m].at[other_pair, x, c, :, part(chunk, 1 - y)],
                full[m].at[:, 1 - x, c, :, part(chunk, 1 - y)],
            )
        ):
            remote(
                piece, piece, ag_send.at[S_CROSS, s], ag_cross.at[slot, cross_index[index]], to_y
            ).wait_recv()
        to_core(index)

    waited = set()

    def settled(m, low, high):
        for index, chunk in enumerate(chunks):
            inside = chunk[0] == m and chunk[1] < high and chunk[1] + chunk[2] > low
            if inside and index not in waited:
                waited.add(index)
                piece = full[m].at[:, :, 1 - c, :, whole(chunk)]
                send = ag_send.at[S_CORE, group_of(chunk)]
                remote(piece, piece, send, ag_core.at[index], to_c).wait_recv()

    for matrix in range(5):
        pltpu.make_async_copy(own[matrix].at[c], full[matrix].at[z, x, c], own_sem.at[matrix]).wait()

    def row_blocks(size, action):
        def body(step, carry):
            action(pl.ds(pl.multiple_of(step * size, size), size))
            return carry

        lax.fori_loop(0, tokens.shape[0] // size, body, 0)

    def find_places():
        rows = lax.broadcasted_iota(jnp.int32, (128, 128), 0)
        columns = lax.broadcasted_iota(jnp.int32, (128, 128), 1)
        for sequence in range(2):
            ids = jnp.broadcast_to(segs[sequence : sequence + 1, :].astype(FULL), (128, 128))
            same = ids == ids.T
            before = jnp.sum(jnp.where(same & (columns < rows), 1.0, 0.0), axis=1, keepdims=True)
            after = jnp.sum(jnp.where(same & (columns > rows), 1.0, 0.0), axis=1, keepdims=True)
            span = slice(sequence * 128, sequence * 128 + 128)
            places[span, :] = jnp.broadcast_to(before.astype(jnp.int32), (128, 128))
            left[span, :] = jnp.broadcast_to(after.astype(jnp.int32), (128, 128))

    def unpack_small():
        total96 = jnp.zeros((8, 768), FULL)
        total288 = jnp.zeros((8, 2304), FULL)
        total8 = jnp.zeros((8, 128), FULL)
        inner_total = jnp.zeros((40, 128), FULL)
        fil_w[...] = jnp.zeros_like(fil_w)
        mid_w[...] = jnp.zeros_like(mid_w)
        for s in range(8):
            top = full[4][s // 2, s % 2, 0].astype(FULL)
            low = full[4][s // 2, s % 2, 1].astype(FULL)
            total96 = total96 + turn(widen(top[0:8], 768), 96 * s, 1)
            wide = jnp.concatenate([top[8:16], top[16:24], top[24:32]], axis=1)
            vexp[:, s * 384 : s * 384 + 384] = wide[5:6]
            total288 = total288 + turn(widen(wide, 2304), 288 * s, 1)
            total8 = total8 + turn(top[32:40], 8 * s, 1)
            inner_total = inner_total + turn(top[40:80], 8 * s, 1)
            mid_w[8 * s : 8 * s + 8, :] = low[0:8]
            fil_w[0:64, :] += turn(widen(low[8:72], 768), 96 * s, 1)
        v96[...] = total96
        v288[...] = total288
        v8[...] = total8
        scale = total8[1:2]
        inner1 = exact(features[...], inner_total, (1, 0)) + total8[0:1]
        s_inner1[...] = inner1
        s_first[...] = jnp.sin(scale * inner1)
        s_cos1[...] = jnp.cos(scale * inner1)
        inner2 = exact(s_first[...], mid_w[...], (1, 0)) + total8[2:3]
        s_inner2[...] = inner2
        s_second[...] = jnp.sin(scale * inner2)
        s_cos2[...] = jnp.cos(scale * inner2)
        taps[...] = exact(s_second[...], fil_w[...], (1, 0)) * decay[...]

    def center(values):
        middle = values - jnp.mean(values, axis=-1, keepdims=True)
        spread = jnp.mean(middle * middle, axis=-1, keepdims=True)
        scale = lax.rsqrt(spread + EPSILON)
        return middle * scale, scale

    def norm_first(rows):
        unit, _ = center(tokens[rows, :].astype(FULL))
        normed1[rows, :] = (unit * v96[0:1, :] + v96[1:2, :]).astype(LOW)

    def matrix_of(m, columns, width):
        value = full[m][:, :, :, :, columns]
        return value.reshape(value.shape[0] * value.shape[1] * value.shape[2] * value.shape[3], width)

    def project(k):
        span = slice(k * 768, k * 768 + 768)
        proj[k] = dot_nn(normed1[...], matrix_of(0, pl.ds(k * 768, 768), 768)) + v288[0:1, span]

        def body(step, carry):
            rows = pl.ds(pl.multiple_of((step // 6) * 128, 128), 128)
            lane = pl.multiple_of((step % 6) * 128, 128)
            lanes = pl.ds(lane, 128)
            wide = pl.ds(pl.multiple_of(k * 768 + lane, 128), 128)
            values = proj[k, rows, lanes]
            where = places[rows, :]
            total = v288[1:2, wide] + v288[2:3, wide] * values
            for lag in (1, 2):
                moved = jnp.where(where >= lag, pltpu.roll(values, lag, 0), 0.0)
                total = total + v288[2 + lag : 3 + lag, wide] * moved
            short[k, rows, lanes] = total
            return carry

        lax.fori_loop(0, 12, body, 0)

    def convolve(begin, end):
        def body(step, carry):
            rows = pl.ds(pl.multiple_of((step // 6) * 128, 128), 128)
            lanes = pl.ds(pl.multiple_of((step % 6) * 128, 128), 128)
            carried = short[2, rows, lanes] * short[1, rows, lanes]
            where = places[rows, :]
            total = v96[2:3, lanes] * carried
            for low_lag in range(8):
                moved = turn(carried, low_lag, 0)
                for high in range(LAGS // 8):
                    lag, skip = high * 8 + low_lag, high * 8
                    term = jnp.where(
                        where[skip:] >= lag, taps[lag : lag + 1, lanes] * moved[: 128 - skip], 0.0
                    )
                    if skip:
                        total = jnp.concatenate([total[:skip], total[skip:] + term], axis=0)
                    else:
                        total = total + term
            conv[rows, lanes] = total
            return carry

        lax.fori_loop(begin, end, body, 0)

    def mix_out():
        def gate(rows):
            gated[rows, :] = (conv[rows, :] * short[0, rows, :]).astype(LOW)

        row_blocks(NORM_ROWS, gate)
        resid[...] = dot_nn(gated[...], matrix_of(1, pl.ds(0, 768), 768))

        def finish_rows(rows):
            values = resid[rows, :] + tokens[rows, :].astype(FULL) + v96[3:4, :]
            resid[rows, :] = values
            unit, _ = center(values)
            normed2[rows, :] = (unit * v96[4:5, :] + v96[5:6, :]).astype(LOW)

        row_blocks(NORM_ROWS, finish_rows)

    def expand(k):
        span = slice(k * 768, k * 768 + 768)
        hidden[:, span] = (
            dot_nn(normed2[...], matrix_of(3, pl.ds(k * 768, 768), 768)) + vexp[:, span]
        )

    fed_before = []

    def feed(k):
        span = slice(k * 768, k * 768 + 768)
        rows_of = full[2][k].reshape(768, 768)
        back_h[...] = dot_nt(cot[...], rows_of)

        def bend(rows):
            values = hidden[rows, span]
            cube = values * values
            grow = math.sqrt(2.0 / math.pi)
            slope = jnp.tanh(grow * (values + 0.044715 * cube * values))
            half_up = 0.5 + 0.5 * slope
            post[rows, span] = (values * half_up).astype(LOW)
            steep = half_up + (0.5 * values) * (1.0 - slope * slope) * (
                grow * (1.0 + 3.0 * 0.044715 * cube)
            )
            grad = (back_h[rows, :] * steep).astype(LOW)
            pre[rows, span] = grad
            accexp[:, span] += fold8(grad.astype(FULL))

        row_blocks(16, bend)
        out_part = dot_nn(post[:, span], full[2][k].reshape(768, 768))
        back_part = dot_nt(pre[:, span], matrix_of(3, pl.ds(k * 768, 768), 768))
        if not fed_before:
            gather_out[...] = out_part
            back_s[...] = back_part
            fed_before.append(k)
        else:
            gather_out[...] += out_part
            back_s[...] += back_part

    drained = set()

    def drain(m, low, high):
        for s, key in enumerate(send_groups):
            members = [
                chunk for chunk in chunks
                if group_of(chunk) == s and m == chunk[0]
                and chunk[1] < high and chunk[1] + chunk[2] > low
            ]
            if not members or s in drained:
                continue
            drained.add(s)
            members = [chunk for chunk in chunks if group_of(chunk) == s]
            kind = members[0][3]
            assert all(chunk[3] == kind for chunk in members)
            wide = sum(chunk[2] for chunk in members)
            thin = wide // 2 if kind == SPLIT else wide

            def gone(slot, planes, rows, width=thin, s=s):
                ref = full[m].at[pl.ds(0, planes), pl.ds(0, rows), 0, :, pl.ds(0, width)]
                remote(ref, ref, ag_send.at[slot, s], ag_recv.at[FAR, 0], to_near).wait_send()

            if kind == LINE:
                gone(S_SIDE, 1, 1)
                gone(S_NEAR, 2, 1)
            else:
                gone(S_NEAR, 1, 1)
                gone(S_SIDE, 4, 1)

            @pl.when(inner)
            def _(gone=gone, kind=kind):
                gone(S_MIRROR, 2, 2 if kind == LINE else 1)
                gone(S_BACK, 2, 2 if kind == LINE else 1)

            if kind == SPLIT:
                gone(S_CROSS, 3, 1)
                gone(S_CROSS, 4, 1)
            gone(S_CORE, 4, 2, wide)

    position = {}
    split_position = {}
    for index, key in enumerate(REDUCE_ORDER):
        position[key] = index
        if REDUCE_GROUPS[key[0]][3] == SPLIT:
            split_position[key] = len(split_position)
    R_CORE, R_X, R_Z1, R_Z2, R_Z3, R_LAST = range(6)
    W_CORE, W_Y, W_X, W_Z1, W_Z2, W_Z3, W_LAST, W_END = range(8)

    def info(key):
        g, i = key
        matrix, columns, width, kind = REDUCE_GROUPS[g]
        return g, i, matrix, columns[i], width, kind, groups[g], position[key]

    def halves(width, which):
        return pl.ds(pl.multiple_of(which * (width // 2), 128), width // 2)

    def stage(key):
        g, i, m, column, width, kind, buf, n = info(key)
        remote(
            grads[m].at[:, :, 1 - c, :, pl.ds(column, width)], buf["core"].at[i],
            rs_send.at[W_CORE, g], rs_recv.at[R_CORE, n], to_c,
        ).start()

    def running(key):
        g, i, m, column, width, kind, buf, n = info(key)
        return buf["core"] if kind == LINE else buf["x"]

    def send_line(key):
        g, i, m, column, width, kind, buf, n = info(key)
        sums_ref = running(key)

        @pl.when(jnp.logical_not(inner))
        def _():
            remote(
                sums_ref.at[i, other_pair], buf["z1"].at[i],
                rs_send.at[W_Z1, g], rs_recv.at[R_Z1, n], to_near,
            ).start()
            remote(
                sums_ref.at[i, near_z], buf["z3"].at[i],
                rs_send.at[W_Z3, g], rs_recv.at[R_Z3, n], to_near,
            ).start()

    def add_core(key):
        g, i, m, column, width, kind, buf, n = info(key)
        landing = buf["core"].at[i]
        remote(landing, landing, rs_send.at[W_CORE, g], rs_recv.at[R_CORE, n], to_c).wait_recv()

        def body(step, carry):
            a, b = step // 2, step % 2
            buf["core"][i, a, b] = buf["core"][i, a, b] + grads[m][a, b, c, :, pl.ds(column, width)]
            return carry

        lax.fori_loop(0, 8, body, 0)
        if kind == SPLIT:
            remote(
                buf["core"].at[i, :, :, :, halves(width, 1 - y)], buf["y"].at[i],
                rs_send.at[W_Y, g], rs_y.at[split_position[key]], to_y,
            ).start()
        elif kind == WHOLE:
            remote(
                buf["core"].at[i, :, 1 - x], buf["x"].at[i],
                rs_send.at[W_X, g], rs_recv.at[R_X, n], to_x,
            ).start()
        else:
            send_line(key)

    def add_y(key):
        g, i, m, column, width, kind, buf, n = info(key)
        landing = buf["y"].at[i]
        remote(landing, landing, rs_send.at[W_Y, g], rs_y.at[split_position[key]], to_y).wait_recv()

        def body(step, carry):
            a, b = step // 2, step % 2
            buf["y"][i, a, b] = buf["y"][i, a, b] + buf["core"][i, a, b, :, halves(width, y)]
            return carry

        lax.fori_loop(0, 8, body, 0)
        remote(
            buf["y"].at[i, :, 1 - x], buf["x"].at[i], rs_send.at[W_X, g], rs_recv.at[R_X, n], to_x
        ).start()

    def send_last(key):
        g, i, m, column, width, kind, buf, n = info(key)
        remote(
            buf["last"].at[i, 0], buf["last"].at[i, 1],
            rs_send.at[W_LAST, g], rs_recv.at[R_LAST, n], to_y,
        ).start()

    def add_x(key):
        g, i, m, column, width, kind, buf, n = info(key)
        landing = buf["x"].at[i]
        remote(landing, landing, rs_send.at[W_X, g], rs_recv.at[R_X, n], to_x).wait_recv()
        if kind == LINE:
            buf["last"][i, 0] = buf["core"][i, z, x] + buf["x"][i]
            send_last(key)
            return
        own_part = buf["y"] if kind == SPLIT else buf["core"]

        def body(step, carry):
            buf["x"][i, step] = buf["x"][i, step] + own_part[i, step, x]
            return carry

        lax.fori_loop(0, 4, body, 0)
        send_line(key)

    def add_z1(key):
        g, i, m, column, width, kind, buf, n = info(key)
        sums_ref = running(key)

        @pl.when(inner)
        def _():
            landing = buf["z1"].at[i]
            remote(landing, landing, rs_send.at[W_Z1, g], rs_recv.at[R_Z1, n], to_near).wait_recv()
            for step in range(2):
                at = (1 - pair) * 2 + step
                sums_ref[i, at] = sums_ref[i, at] + buf["z1"][i, step]
            remote(
                sums_ref.at[i, other_pair], buf["z2"].at[i],
                rs_send.at[W_Z2, g], rs_recv.at[R_Z2, n], to_mirror,
            ).start()

    def add_z2(key):
        g, i, m, column, width, kind, buf, n = info(key)
        sums_ref = running(key)

        @pl.when(inner)
        def _():
            landing = buf["z2"].at[i]
            remote(landing, landing, rs_send.at[W_Z2, g], rs_recv.at[R_Z2, n], to_mirror).wait_recv()
            for step in range(2):
                at = pair * 2 + step
                sums_ref[i, at] = sums_ref[i, at] + buf["z2"][i, step]
            remote(
                sums_ref.at[i, near_z], buf["z3"].at[i],
                rs_send.at[W_Z3, g], rs_recv.at[R_Z3, n], to_near,
            ).start()

    def add_z3(key):
        g, i, m, column, width, kind, buf, n = info(key)
        landing = buf["z3"].at[i]
        remote(landing, landing, rs_send.at[W_Z3, g], rs_recv.at[R_Z3, n], to_near).wait_recv()
        if kind == LINE:
            buf["core"][i, z] = buf["core"][i, z] + buf["z3"][i]
            remote(
                buf["core"].at[i, z, 1 - x], buf["x"].at[i],
                rs_send.at[W_X, g], rs_recv.at[R_X, n], to_x,
            ).start()
            return
        buf["last"][i, 0] = buf["x"][i, z] + buf["z3"][i]
        send_last(key)

    def finish(key):
        g, i, m, column, width, kind, buf, n = info(key)
        landing = buf["last"].at[i, 1]
        remote(landing, landing, rs_send.at[W_LAST, g], rs_recv.at[R_LAST, n], to_y).wait_recv()
        if kind == SPLIT:
            for which, slot in ((y, 0), (1 - y, 1)):
                columns = pl.ds(pl.multiple_of(column + which * (width // 2), 128), width // 2)
                sums[m][c, :, columns] = buf["last"][i, slot].astype(FULL)
        else:
            sums[m][c, :, pl.ds(column, width)] = buf["last"][i, 0].astype(FULL) + buf["last"][
                i, 1
            ].astype(FULL)
        piece = sums[m].at[c, :, pl.ds(column, width)]
        remote(piece, piece, rs_send.at[W_END, g], rs_end.at[g], to_c).start()

    def grad_contract():
        def body(s, carry):
            lanes = pl.ds(pl.multiple_of(s * 384, 128), 384)
            value = dot_tn(post[:, lanes], cot[...]).astype(LOW)
            full[2][s // 2, s % 2] = value.reshape(2, 192, 768)
            return carry

        lax.fori_loop(0, 8, body, 0)

    def grad_rows(source, other, target, columns, width):
        for half in range(2):
            value = dot_tn(source[:, half * 384 : half * 384 + 384], other).astype(LOW)
            target[2 * half : 2 * half + 2, :, :, :, columns] = value.reshape(2, 2, 2, 48, width)

    def grad_expand(i):
        span = slice(i * 768, i * 768 + 768)
        grad_rows(normed2, pre[:, span], full[3], pl.ds(i * 768, 768), 768)

    def norm_second_back(rows):
        unit, scale = center(resid[rows, :])
        grad = back_s[rows, :]
        top = cot[rows, :].astype(FULL)
        e = grad * v96[4:5, :]
        value = (
            e - jnp.mean(e, axis=-1, keepdims=True) - unit * jnp.mean(e * unit, axis=-1, keepdims=True)
        ) * scale + top
        back_r[rows, :] = value
        rounded = value.astype(LOW)
        back_m[rows, :] = rounded
        acc96[4] += fold8(grad * unit)
        acc96[5] += fold8(grad)
        acc96[3] += fold8(rounded.astype(FULL))
        acc96[6] += fold8(top)
        result[rows, :] = (resid[rows, :] + gather_out[rows, :] + v96[6:7, :]).astype(LOW)

    def convolve_back(begin, end):
        def body(step, carry):
            rows = pl.ds(pl.multiple_of((step // 6) * 128, 128), 128)
            lane = pl.multiple_of((step % 6) * 128, 128)
            lanes = pl.ds(lane, 128)
            where = places[rows, :]
            rest = left[rows, :]
            gate_in = short[1, rows, lanes]
            values = short[2, rows, lanes]
            top = back_g[rows, lanes]
            carried = values * gate_in
            back_conv = top * short[0, rows, lanes]
            acc96[2, :, lanes] += fold8(back_conv * carried)
            total = v96[2:3, lanes] * back_conv
            for low_lag in range(8):
                turned = turn(back_conv, -low_lag, 0)
                for high in range(LAGS // 8):
                    lag, skip = high * 8 + low_lag, high * 8
                    size = 128 - skip
                    moved = jnp.where(rest[:size] >= lag, turned[skip:], 0.0)
                    term = taps[lag : lag + 1, lanes] * moved
                    if skip:
                        total = jnp.concatenate([total[:size] + term, total[size:]], axis=0)
                    else:
                        total = total + term
                    d_taps[lag : lag + 1, lanes] += jnp.sum(
                        moved * carried[:size], axis=0, keepdims=True
                    )
            streams = (top * conv[rows, lanes], total * values, total * gate_in)
            for k in range(3):
                wide = pl.ds(pl.multiple_of(k * 768 + lane, 128), 128)
                grad = streams[k]
                before = proj[k, rows, lanes]
                acc288[1, :, wide] += fold8(grad)
                acc288[2, :, wide] += fold8(grad * before)
                value = v288[2:3, wide] * grad
                for lag in (1, 2):
                    moved = jnp.where(where >= lag, pltpu.roll(before, lag, 0), 0.0)
                    acc288[2 + lag, :, wide] += fold8(grad * moved)
                    later = jnp.where(rest >= lag, pltpu.roll(grad, 128 - lag, 0), 0.0)
                    value = value + v288[2 + lag : 3 + lag, wide] * later
                rounded = value.astype(LOW)
                bp[k, rows, lanes] = rounded
                acc288[0, :, wide] += fold8(rounded.astype(FULL))
            return carry

        lax.fori_loop(begin, end, body, 0)

    def norm_first_back(rows):
        unit, scale = center(tokens[rows, :].astype(FULL))
        grad = back_s[rows, :]
        e = grad * v96[0:1, :]
        delta[rows, :] = back_r[rows, :] + (
            e - jnp.mean(e, axis=-1, keepdims=True) - unit * jnp.mean(e * unit, axis=-1, keepdims=True)
        ) * scale
        acc96[0] += fold8(grad * unit)
        acc96[1] += fold8(grad)

    def small_grads():
        scale = v8[1:2, :]
        raw = d_taps[...] * decay[...]
        d_fil = exact(s_second[...], raw, (0, 0))
        b2 = exact(raw, fil_w[...], (1, 1)) * s_cos2[...]
        b2s = b2 * scale
        d_mid = exact(s_first[...], b2s, (0, 0))
        b1 = exact(b2s, mid_w[...], (1, 1)) * s_cos1[...]
        b1s = b1 * scale
        d_inner = exact(features[...], b1s, (0, 0))
        d_scale = jnp.sum(b2 * s_inner2[...] + b1 * s_inner1[...], axis=0, keepdims=True)
        rows8 = jnp.concatenate(
            [
                jnp.sum(b1s, axis=0, keepdims=True), d_scale, jnp.sum(b2s, axis=0, keepdims=True),
                jnp.zeros((5, 128), FULL),
            ],
            axis=0,
        )
        rows96 = jnp.concatenate(
            [jnp.sum(acc96[f], axis=0, keepdims=True) for f in range(7)] + [jnp.zeros((1, 768), FULL)],
            axis=0,
        )
        rows288 = jnp.concatenate(
            [jnp.sum(acc288[f], axis=0, keepdims=True) for f in range(5)]
            + [jnp.zeros((3, 2304), FULL)],
            axis=0,
        )
        rows_exp = jnp.sum(accexp[...], axis=0, keepdims=True)
        lane = lax.broadcasted_iota(jnp.int32, (8, 128), 1)
        row = lax.broadcasted_iota(jnp.int32, (8, 128), 0)
        wide_lane = lax.broadcasted_iota(jnp.int32, (64, 128), 1)
        long_lane = lax.broadcasted_iota(jnp.int32, (40, 128), 1)
        for s in range(8):
            a, b = s // 2, s % 2
            g_small[a, b, 0, 0:8, :] = jnp.where(lane < 96, turn(rows96, -96 * s, 1)[:, :128], 0.0)
            turned = turn(rows288, -288 * s, 1)
            for block in range(3):
                value = turned[:, block * 128 : block * 128 + 128]
                if block == 2:
                    value = jnp.where(lane < 32, value, 0.0)
                bias = rows_exp[:, s * 384 + block * 128 : s * 384 + block * 128 + 128]
                value = jnp.where(row == 5, jnp.broadcast_to(bias, (8, 128)), value)
                g_small[a, b, 0, 8 + block * 8 : 16 + block * 8, :] = value
            g_small[a, b, 0, 32:40, :] = jnp.where(lane < 8, turn(rows8, -8 * s, 1), 0.0)
            g_small[a, b, 0, 40:80, :] = jnp.where(long_lane < 8, turn(d_inner, -8 * s, 1), 0.0)
            g_small[a, b, 1, 0:8, :] = d_mid[8 * s : 8 * s + 8]
            g_small[a, b, 1, 8:72, :] = jnp.where(
                wide_lane < 96, turn(d_fil[0:64], -96 * s, 1)[:, :128], 0.0
            )
            g_small[a, b, 1, 72:80, :] = jnp.zeros((8, 128), FULL)

    def back_gate():
        back_g[...] = dot_nt(back_m[...], matrix_of(1, pl.ds(0, 768), 768))

    def back_first():
        for k in range(3):
            value = dot_nt(bp[k], matrix_of(0, pl.ds(k * 768, 768), 768))
            if k == 0:
                back_s[...] = value
            else:
                back_s[...] += value

    def unpack(k):
        settled(4, 0, 128)
        unpack_small()

    def projected(k):
        settled(0, k * 768, k * 768 + 768)
        project(k)

    def mix(k):
        settled(1, 0, 768)
        mix_out()

    def expanded(k):
        settled(3, k * 768, k * 768 + 768)
        expand(k)

    def fed(k):
        settled(2, 0, 768)
        feed(k)

    def expand_back(k):
        drain(3, k * 768, k * 768 + 768)
        grad_expand(k)

    def end(k):
        for m in range(5):
            drain(m, 0, full[m].shape[4])

    actions = {
        DO_FIRST: first, DO_NEAR: near, DO_FAR: far, DO_SIDE: side, DO_CROSS: cross,
        DO_PLACES: lambda k: find_places(),
        DO_UNPACK: unpack,
        DO_NORM1: lambda k: row_blocks(NORM_ROWS, norm_first),
        DO_PROJECT: projected,
        DO_CONV: lambda k: convolve(3 * k, 3 * k + 3),
        DO_MIX: mix,
        DO_EXPAND: expanded,
        DO_FEED: fed,
        DO_DRAIN: lambda k: drain(2, 0, 768),
        DO_GCON: lambda k: grad_contract(),
        DO_GEXP: expand_back,
        DO_NORM2B: lambda k: row_blocks(NORM_ROWS, norm_second_back),
        DO_BACKG: lambda k: back_gate(),
        DO_GOUT: lambda k: grad_rows(gated, back_m[...], g_out, pl.ds(0, 768), 768),
        DO_CONVB: lambda k: convolve_back(3 * k, 3 * k + 3),
        DO_GIN: lambda k: grad_rows(normed1, bp[k], g_in, pl.ds(k * 768, 768), 768),
        DO_BFIRST: lambda k: back_first(),
        DO_NORM1B: lambda k: row_blocks(NORM_ROWS, norm_first_back),
        DO_SMALL: lambda k: small_grads(),
        DO_STAGE: stage, DO_ACORE: add_core, DO_AY: add_y, DO_AX: add_x, DO_AZ1: add_z1,
        DO_AZ2: add_z2, DO_AZ3: add_z3, DO_FIN: finish, DO_END: end,
    }
    for name, which in SCHEDULE:
        actions[name](which)

    for g, (matrix, columns, width, kind) in enumerate(REDUCE_GROUPS):
        piece = sums[matrix].at[1 - c, :, pl.ds(0, width * len(columns))]
        remote(piece, piece, rs_send.at[W_END, g], rs_end.at[g], to_c).wait_recv()
    for g, (matrix, columns, width, kind) in enumerate(REDUCE_GROUPS):
        buf = groups[g]

        def leave(kind, ref, g=g):
            remote(ref, ref, rs_send.at[kind, g], rs_end.at[g], to_c).wait_send()

        leave(W_CORE, buf["core"])
        if kind == SPLIT:
            leave(W_Y, buf["y"])
        leave(W_X, buf["x"])
        leave(W_Z3, buf["z3"])
        leave(W_LAST, buf["last"].at[:, 0])
        leave(W_END, sums[matrix].at[1 - c, :, pl.ds(0, width * len(columns))])

        @pl.when(inner)
        def _(leave=leave, buf=buf):
            leave(W_Z2, buf["z2"])

        @pl.when(jnp.logical_not(inner))
        def _(leave=leave, buf=buf):
            leave(W_Z1, buf["z1"])


def unpack_kernel(result, delta, s_in, s_out, s_con, s_exp, s_small, *outs):
    (
        o_result, o_delta, o_first_gain, o_first_shift, o_in, o_in_bias, o_short_w, o_short_b,
        o_inner_w, o_inner_b, o_scale, o_middle_w, o_middle_b, o_filter_w, o_direct, o_out,
        o_out_bias, o_second_gain, o_second_shift, o_exp, o_exp_bias, o_con, o_con_bias,
    ) = outs
    o_result[...] = result[...]
    o_delta[...] = delta[...]
    for source, target in ((s_in, o_in), (s_out, o_out), (s_con, o_con), (s_exp, o_exp)):
        height = source.shape[1]
        for half in range(2):
            target[half * height : half * height + height, :] = source[half]
    for row, target in enumerate(
        (o_first_gain, o_first_shift, o_direct, o_out_bias, o_second_gain, o_second_shift, o_con_bias)
    ):
        target[...] = s_small[0, row : row + 1, 0:96].reshape(96)
    wide = jnp.concatenate([s_small[0, 8:16, :], s_small[0, 16:24, :], s_small[0, 24:32, :]], axis=1)
    o_in_bias[...] = wide[0:1, 0:288].reshape(288)
    o_short_b[...] = wide[1:2, 0:288].reshape(288)
    o_short_w[...] = wide[2:5, 0:288]
    o_exp_bias[...] = wide[5:6].reshape(384)
    for row, target in enumerate((o_inner_b, o_scale, o_middle_b)):
        target[...] = s_small[0, 32 + row : 33 + row, 0:8].reshape(8)
    tile = jnp.concatenate([s_small[0, 40:80, :], jnp.zeros((88, 128), FULL)], axis=0).T
    o_inner_w[...] = tile[0:8, 0:33]
    o_middle_w[...] = s_small[1, 0:8, 0:64]
    o_filter_w[...] = s_small[1, 8:72, 0:96]


def filter_constants(length, width):
    places = np.arange(LAGS, dtype=np.float64)
    scales = 0.0001 + np.arange(16, dtype=np.float64) * ((15.0 - 0.0001) / 15.0)
    phases = (2.0 * math.pi * places / length)[:, None] * scales[None, :]
    ramp = places / (length - 1)
    table = np.zeros((LAGS, 40), np.float32)
    table[:, 0] = ramp
    table[:, 1:17] = np.cos(phases)
    table[:, 17:33] = -np.sin(phases)
    rates = math.log(100.0) * (
        1.0 / 1.5 + (1.0 / 0.3 - 1.0 / 1.5) * np.arange(width, dtype=np.float64) / (width - 1)
    )
    return table, np.exp(-ramp[:, None] * rates[None, :]).astype(np.float32)


def block_device(
    tokens, segment_ids, cotangent, first_gain, first_shift, input_weight, input_bias,
    short_weight, short_bias, inner_weight, inner_bias, sine_scale, middle_weight, middle_bias,
    filter_weight, direct_gain, output_weight, output_bias, second_gain, second_shift,
    expand_weight, expand_bias, contract_weight, contract_bias,
):
    blocks, _, length, width = tokens.shape
    rows = blocks * length
    features, decay = filter_constants(length, width)

    small_members = (
        first_gain, first_shift, input_bias, short_weight, short_bias, inner_weight, inner_bias,
        sine_scale, middle_weight, middle_bias, filter_weight, direct_gain, output_bias,
        second_gain, second_shift, expand_bias, contract_bias,
    )

    def halved(member):
        return member.reshape(2, member.shape[0] // 2, member.shape[1])

    shards = [halved(m) for m in (input_weight, output_weight, contract_weight, expand_weight)]
    inputs = (
        tokens.reshape(rows, width), segment_ids.reshape(blocks, length),
        cotangent.reshape(rows, width),
    ) + tuple(m.T if m is inner_weight else m for m in small_members) + tuple(shards) + (
        jnp.asarray(features), jnp.asarray(decay),
    )
    shapes = [m.shape[1:] for m in shards] + [(SMALL_ROWS, 128)]
    outs = [
        jax.ShapeDtypeStruct((rows, width), LOW),
        jax.ShapeDtypeStruct((rows, width), FULL),
    ] + [jax.ShapeDtypeStruct((2,) + s, FULL) for s in shapes]
    count = len(GATHER_CHUNKS)
    crossing = sum(1 for chunk in GATHER_CHUNKS if chunk[3] == SPLIT)
    vm = pltpu.VMEM
    scratch = [vm((4, 2, 2) + s, LOW) for s in shapes]
    scratch += [
        vm((4, 2, 2) + shapes[0], LOW), vm((4, 2, 2) + shapes[1], LOW),
        vm((4, 2, 2) + shapes[4], FULL), vm((2, SMALL_ROWS, 128), LOW),
        vm((2 * SMALL_ROWS, 128), FULL),
        vm((8, width), FULL), vm((8, 3 * width), FULL), vm((1, 4 * width), FULL), vm((8, 128), FULL),
        vm((128, 128), FULL), vm((128, width), FULL), vm((LAGS, width), FULL), vm((LAGS, width), FULL),
    ]
    scratch += [vm((LAGS, 128), FULL)] * 6
    scratch += [vm((rows, 128), jnp.int32)] * 2
    scratch += [
        vm((rows, width), LOW), vm((3, rows, width), FULL), vm((3, rows, width), FULL),
        vm((rows, width), FULL), vm((rows, width), LOW), vm((rows, width), FULL),
        vm((rows, width), LOW),
        vm((rows, 4 * width), FULL), vm((rows, 4 * width), LOW), vm((rows, 4 * width), LOW),
        vm((rows, width), FULL), vm((rows, width), FULL), vm((rows, width), FULL),
        vm((rows, width), LOW), vm((3, rows, width), LOW),
        vm((7, 8, width), FULL), vm((5, 8, 3 * width), FULL), vm((8, 4 * width), FULL),
    ]
    for matrix, columns, span, kind in REDUCE_GROUPS:
        n, high = len(columns), shapes[matrix][0]
        of = FULL if matrix == 4 else LOW
        v = span // 2 if kind == SPLIT else span
        side_planes, line_planes = ((), (2,)) if kind == LINE else ((4,), ())
        scratch += [
            vm((n, 4, 2, high, span), of), vm((n,) + side_planes + (high, v), of),
            vm((n, 2) + line_planes + (high, v), of), vm((n, 2) + line_planes + (high, v), of),
            vm((n,) + line_planes + (high, v), of), vm((n, 2, high, v), of),
        ]
        if kind == SPLIT:
            scratch.append(vm((n, 4, 2, high, v), of))
    total = len(REDUCE_ORDER)
    splits = sum(len(g[1]) for g in REDUCE_GROUPS if g[3] == SPLIT)
    dma = pltpu.SemaphoreType.DMA
    scratch += [
        dma((4, count)), dma((3, crossing)), dma((count,)), dma((6, 8)), dma((5,)),
        dma((6, total)), dma((splits,)), dma((8, len(REDUCE_GROUPS))), dma((len(REDUCE_GROUPS),)),
    ]
    in_vmem = pl.BlockSpec(memory_space=pltpu.VMEM)
    parts = pl.pallas_call(
        block_kernel,
        out_shape=outs,
        in_specs=[in_vmem] * len(inputs),
        out_specs=[in_vmem] * len(outs),
        scratch_shapes=scratch,
        compiler_params=pltpu.CompilerParams(
            collective_id=0, has_side_effects=True, vmem_limit_bytes=67043328
        ),
    )(*inputs)
    members = (
        first_gain, first_shift, input_weight, input_bias, short_weight, short_bias, inner_weight,
        inner_bias, sine_scale, middle_weight, middle_bias, filter_weight, direct_gain,
        output_weight, output_bias, second_gain, second_shift, expand_weight, expand_bias,
        contract_weight, contract_bias,
    )
    final = [outs[0], outs[1]] + [
        jax.ShapeDtypeStruct(m.shape[::-1] if m is inner_weight else m.shape, FULL) for m in members
    ]
    done = pl.pallas_call(
        unpack_kernel,
        out_shape=final,
        in_specs=[in_vmem] * 7,
        out_specs=[in_vmem] * len(final),
    )(*parts)
    done = [m.T if n == INNER_OUT else m for n, m in enumerate(done)]
    return (done[0].reshape(tokens.shape), done[1].reshape(tokens.shape)) + tuple(done[2:])


def per_device(
    tokens,
    segment_ids,
    cotangent,
    first_gain,
    first_shift,
    input_weight,
    input_bias,
    short_weight,
    short_bias,
    inner_weight,
    inner_bias,
    sine_scale,
    middle_weight,
    middle_bias,
    filter_weight,
    direct_gain,
    output_weight,
    output_bias,
    second_gain,
    second_shift,
    expand_weight,
    expand_bias,
    contract_weight,
    contract_bias,
):
    micro_count, local_sequences, length, width = tokens.shape
    row_count = local_sequences * length
    tables = wave_tables(length)

    def fetch_mixer():
        return (
            lax.all_gather(first_gain, "shard", axis=0, tiled=True),
            lax.all_gather(first_shift, "shard", axis=0, tiled=True),
            lax.all_gather(input_weight, "shard", axis=0, tiled=True),
            lax.all_gather(input_bias, "shard", axis=0, tiled=True),
            lax.all_gather(short_weight, "shard", axis=1, tiled=True),
            lax.all_gather(short_bias, "shard", axis=0, tiled=True),
            lax.all_gather(inner_weight, "shard", axis=1, tiled=True),
            lax.all_gather(inner_bias, "shard", axis=0, tiled=True),
            lax.all_gather(sine_scale, "shard", axis=0, tiled=True),
            lax.all_gather(middle_weight, "shard", axis=0, tiled=True),
            lax.all_gather(middle_bias, "shard", axis=0, tiled=True),
            lax.all_gather(filter_weight, "shard", axis=1, tiled=True),
            lax.all_gather(direct_gain, "shard", axis=0, tiled=True),
            lax.all_gather(output_weight, "shard", axis=0, tiled=True),
            lax.all_gather(output_bias, "shard", axis=0, tiled=True),
        )

    def fetch_dense():
        return (
            lax.all_gather(second_gain, "shard", axis=0, tiled=True),
            lax.all_gather(second_shift, "shard", axis=0, tiled=True),
            lax.all_gather(expand_weight, "shard", axis=0, tiled=True),
            lax.all_gather(expand_bias, "shard", axis=0, tiled=True),
            lax.all_gather(contract_weight, "shard", axis=0, tiled=True),
            lax.all_gather(contract_bias, "shard", axis=0, tiled=True),
        )

    results = []
    input_deltas = []
    mixer_total = None
    dense_total = None
    for micro_index in range(micro_count):
        mixer_parts = fetch_mixer()
        dense_parts = fetch_dense()
        kernel = filter_taps(
            to_float(mixer_parts[6]),
            to_float(mixer_parts[7]),
            to_float(mixer_parts[8]),
            to_float(mixer_parts[9]),
            to_float(mixer_parts[10]),
            to_float(mixer_parts[11]),
            length,
        )
        kernel, kernel_wave = (kernel, spectrum(tables, kernel))
        kernel_real, kernel_imag = kernel_wave
        segment_block = segment_ids[micro_index]
        membership = (
            segment_block[:, None, :] == jnp.arange(DOCS, dtype=jnp.int32)[None, :, None]
        ).astype(jnp.float32)
        flat_tokens = tokens[micro_index].reshape(row_count, width).astype(jnp.float32)
        normed_first = normalize(
            flat_tokens, to_float(mixer_parts[0]), to_float(mixer_parts[1])
        ).astype(jnp.bfloat16)
        projected = jnp.dot(
            normed_first, mixer_parts[2], preferred_element_type=jnp.float32
        ) + to_float(mixer_parts[3])
        projected_rows = projected.reshape(local_sequences, length, 3 * width)
        short_out = short_filter(
            projected_rows, segment_block, to_float(mixer_parts[4]), to_float(mixer_parts[5])
        )
        gate_out = short_out[:, :, :width]
        gate_in = short_out[:, :, width : 2 * width]
        values = short_out[:, :, 2 * width :]
        carried = values * gate_in
        direct = to_float(mixer_parts[12])
        carried_real, carried_imag = spectrum(tables, carried[:, None] * membership[:, :, :, None])
        conv_pieces = inverse(
            tables,
            carried_real * kernel_real - carried_imag * kernel_imag,
            carried_real * kernel_imag + carried_imag * kernel_real,
        )
        convolved = jnp.sum(conv_pieces * membership[:, :, :, None], axis=1) + direct * carried
        gated_low = (convolved * gate_out).astype(jnp.bfloat16).reshape(row_count, width)
        mixed_out = jnp.dot(
            gated_low, mixer_parts[13], preferred_element_type=jnp.float32
        ) + to_float(mixer_parts[14])
        residual = flat_tokens + mixed_out
        second_gain_f = to_float(dense_parts[0])
        second_shift_f = to_float(dense_parts[1])
        normed_second = normalize(residual, second_gain_f, second_shift_f).astype(jnp.bfloat16)
        hidden_pre = jnp.dot(
            normed_second, dense_parts[2], preferred_element_type=jnp.float32
        ) + to_float(dense_parts[3])
        hidden_post = smooth_gate(hidden_pre).astype(jnp.bfloat16)
        result = (
            residual
            + jnp.dot(hidden_post, dense_parts[4], preferred_element_type=jnp.float32)
            + to_float(dense_parts[5])
        )
        results.append(result.astype(jnp.bfloat16).reshape(local_sequences, length, width))
        back_mixer = fetch_mixer()
        back_dense = fetch_dense()
        upstream = cotangent[micro_index].reshape(row_count, width)
        upstream_float = upstream.astype(jnp.float32)
        delta_contract_weight = jnp.einsum(
            "tf,td->fd", hidden_post, upstream, preferred_element_type=jnp.float32
        )
        delta_contract_bias = jnp.sum(upstream_float, axis=0)
        back_hidden = jnp.einsum(
            "td,fd->tf", upstream, back_dense[4], preferred_element_type=jnp.float32
        )
        back_pre = jax.vjp(smooth_gate, hidden_pre)[1](back_hidden)[0].astype(jnp.bfloat16)
        delta_expand_weight = jnp.einsum(
            "td,tf->df", normed_second, back_pre, preferred_element_type=jnp.float32
        )
        delta_expand_bias = jnp.sum(back_pre.astype(jnp.float32), axis=0)
        back_second = jnp.einsum(
            "tf,df->td", back_pre, back_dense[2], preferred_element_type=jnp.float32
        )
        second_pull = jax.vjp(
            normalize, residual, to_float(back_dense[0]), to_float(back_dense[1])
        )[1]
        back_norm_second, delta_second_gain, delta_second_shift = second_pull(back_second)
        back_residual = upstream_float + back_norm_second
        back_mixed = back_residual.astype(jnp.bfloat16)
        delta_output_weight = jnp.einsum(
            "td,te->de", gated_low, back_mixed, preferred_element_type=jnp.float32
        )
        delta_output_bias = jnp.sum(back_mixed.astype(jnp.float32), axis=0)
        back_gated = jnp.einsum(
            "te,de->td", back_mixed, back_mixer[13], preferred_element_type=jnp.float32
        ).reshape(local_sequences, length, width)
        back_conv = back_gated * gate_out
        grad_real, grad_imag = spectrum(tables, back_conv[:, None] * membership[:, :, :, None])
        carried_back_pieces = inverse(
            tables,
            grad_real * kernel_real + grad_imag * kernel_imag,
            grad_imag * kernel_real - grad_real * kernel_imag,
        )
        back_carried = (
            jnp.sum(carried_back_pieces * membership[:, :, :, None], axis=1) + direct * back_conv
        )
        cross_real = jnp.sum(grad_real * carried_real + grad_imag * carried_imag, axis=(0, 1))
        cross_imag = jnp.sum(grad_imag * carried_real - grad_real * carried_imag, axis=(0, 1))
        back_kernel = inverse(tables, cross_real, cross_imag)
        delta_direct = jnp.sum(back_conv * carried, axis=(0, 1))
        back_short = jnp.concatenate(
            [back_gated * convolved, back_carried * values, back_carried * gate_in], axis=2
        )
        short_pull = jax.vjp(
            lambda rows_in, taps_in, offset_in: short_filter(
                rows_in, segment_block, taps_in, offset_in
            ),
            projected_rows,
            to_float(back_mixer[4]),
            to_float(back_mixer[5]),
        )[1]
        back_projected, delta_short_weight, delta_short_bias = short_pull(back_short)
        back_projected = back_projected.reshape(row_count, 3 * width).astype(jnp.bfloat16)
        delta_input_weight = jnp.einsum(
            "td,tp->dp", normed_first, back_projected, preferred_element_type=jnp.float32
        )
        delta_input_bias = jnp.sum(back_projected.astype(jnp.float32), axis=0)
        back_first = jnp.einsum(
            "tp,dp->td", back_projected, back_mixer[2], preferred_element_type=jnp.float32
        )
        first_pull = jax.vjp(
            normalize, flat_tokens, to_float(back_mixer[0]), to_float(back_mixer[1])
        )[1]
        back_norm_first, delta_first_gain, delta_first_shift = first_pull(back_first)
        input_deltas.append(
            (back_residual + back_norm_first).reshape(local_sequences, length, width)
        )
        filter_pull = jax.vjp(
            lambda weight_one, bias_one, scale_all, weight_two, bias_two, weight_three: filter_taps(
                weight_one, bias_one, scale_all, weight_two, bias_two, weight_three, length
            ),
            to_float(back_mixer[6]),
            to_float(back_mixer[7]),
            to_float(back_mixer[8]),
            to_float(back_mixer[9]),
            to_float(back_mixer[10]),
            to_float(back_mixer[11]),
        )[1]
        filter_deltas = filter_pull(back_kernel)
        mixer_part = (
            delta_first_gain,
            delta_first_shift,
            delta_input_weight,
            delta_input_bias,
            delta_short_weight,
            delta_short_bias,
            filter_deltas[0],
            filter_deltas[1],
            filter_deltas[2],
            filter_deltas[3],
            filter_deltas[4],
            filter_deltas[5],
            delta_direct,
            delta_output_weight,
            delta_output_bias,
        )
        dense_part = (
            delta_second_gain,
            delta_second_shift,
            delta_expand_weight,
            delta_expand_bias,
            delta_contract_weight,
            delta_contract_bias,
        )
        if micro_index == 0:
            mixer_total = mixer_part
            dense_total = dense_part
        else:
            mixer_total = jax.tree.map(jnp.add, mixer_total, mixer_part)
            dense_total = jax.tree.map(jnp.add, dense_total, dense_part)
    dense_total = (
        lax.psum_scatter(dense_total[0], "shard", scatter_dimension=0, tiled=True),
        lax.psum_scatter(dense_total[1], "shard", scatter_dimension=0, tiled=True),
        lax.psum_scatter(dense_total[2], "shard", scatter_dimension=0, tiled=True),
        lax.psum_scatter(dense_total[3], "shard", scatter_dimension=0, tiled=True),
        lax.psum_scatter(dense_total[4], "shard", scatter_dimension=0, tiled=True),
        lax.psum_scatter(dense_total[5], "shard", scatter_dimension=0, tiled=True),
    )
    mixer_total = (
        lax.psum_scatter(mixer_total[0], "shard", scatter_dimension=0, tiled=True),
        lax.psum_scatter(mixer_total[1], "shard", scatter_dimension=0, tiled=True),
        lax.psum_scatter(mixer_total[2], "shard", scatter_dimension=0, tiled=True),
        lax.psum_scatter(mixer_total[3], "shard", scatter_dimension=0, tiled=True),
        lax.psum_scatter(mixer_total[4], "shard", scatter_dimension=1, tiled=True),
        lax.psum_scatter(mixer_total[5], "shard", scatter_dimension=0, tiled=True),
        lax.psum_scatter(mixer_total[6], "shard", scatter_dimension=1, tiled=True),
        lax.psum_scatter(mixer_total[7], "shard", scatter_dimension=0, tiled=True),
        lax.psum_scatter(mixer_total[8], "shard", scatter_dimension=0, tiled=True),
        lax.psum_scatter(mixer_total[9], "shard", scatter_dimension=0, tiled=True),
        lax.psum_scatter(mixer_total[10], "shard", scatter_dimension=0, tiled=True),
        lax.psum_scatter(mixer_total[11], "shard", scatter_dimension=1, tiled=True),
        lax.psum_scatter(mixer_total[12], "shard", scatter_dimension=0, tiled=True),
        lax.psum_scatter(mixer_total[13], "shard", scatter_dimension=0, tiled=True),
        lax.psum_scatter(mixer_total[14], "shard", scatter_dimension=0, tiled=True),
    )
    summed = lax.psum(
        (
            mixer_total[0],
            mixer_total[1],
            mixer_total[2],
            mixer_total[3],
            mixer_total[4],
            mixer_total[5],
            mixer_total[6],
            mixer_total[7],
            mixer_total[8],
            mixer_total[9],
            mixer_total[10],
            mixer_total[11],
            mixer_total[12],
            mixer_total[13],
            mixer_total[14],
            dense_total[0],
            dense_total[1],
            dense_total[2],
            dense_total[3],
            dense_total[4],
            dense_total[5],
        ),
        "rep",
    )
    return (jnp.stack(results), jnp.stack(input_deltas)) + tuple(summed)


def solution(mesh):
    placed = (
        P(None, ("rep", "shard"), None, None),
        P(None, ("rep", "shard"), None),
        P(None, ("rep", "shard"), None, None),
        P("shard"),
        P("shard"),
        P("shard", None),
        P("shard"),
        P(None, "shard"),
        P("shard"),
        P(None, "shard"),
        P("shard"),
        P("shard"),
        P("shard", None),
        P("shard"),
        P(None, "shard"),
        P("shard"),
        P("shard", None),
        P("shard"),
        P("shard"),
        P("shard"),
        P("shard", None),
        P("shard"),
        P("shard", None),
        P("shard"),
    )
    blocked = dict(mesh.shape) == {"rep": 4, "shard": 8}
    return jax.shard_map(
        block_device if blocked else per_device,
        mesh=mesh,
        in_specs=placed,
        out_specs=(
            P(None, ("rep", "shard"), None, None),
            P(None, ("rep", "shard"), None, None),
            P("shard"),
            P("shard"),
            P("shard", None),
            P("shard"),
            P(None, "shard"),
            P("shard"),
            P(None, "shard"),
            P("shard"),
            P("shard"),
            P("shard", None),
            P("shard"),
            P(None, "shard"),
            P("shard"),
            P("shard", None),
            P("shard"),
            P("shard"),
            P("shard"),
            P("shard", None),
            P("shard"),
            P("shard", None),
            P("shard"),
        ),
        check_vma=False,
    )
```

```python
import math

import jax
import jax.numpy as jnp
import numpy as np
from jax import lax
from jax.experimental import pallas as pl
from jax.experimental.pallas import tpu as pltpu
from jax.sharding import PartitionSpec as P

DOCS = 6


EPSILON = 1e-05
HIGHEST = lax.Precision.HIGHEST


def positions(length):
    places = jnp.arange(length, dtype=jnp.float32)
    linear_ramp = places / (length - 1)
    angles = 2.0 * math.pi * places / length
    scales = 0.0001 + jnp.arange(16, dtype=jnp.float32) * ((15.0 - 0.0001) / 15.0)
    phases = angles[:, None] * scales[None, :]
    return jnp.concatenate([linear_ramp[:, None], jnp.cos(phases), -jnp.sin(phases)], axis=1)


def decay_table(length, width):
    linear_ramp = jnp.arange(length, dtype=jnp.float32) / (length - 1)
    rates = math.log(100.0) * (
        1.0 / 1.5 + (1.0 / 0.3 - 1.0 / 1.5) * jnp.arange(width, dtype=jnp.float32) / (width - 1)
    )
    return jnp.exp(-linear_ramp[:, None] * rates[None, :])


def filter_taps(
    inner_weight, inner_bias, sine_scale, middle_weight, middle_bias, filter_weight, length
):
    features = positions(length)
    first_sine = jnp.sin(
        sine_scale * (jnp.dot(features, inner_weight, precision=HIGHEST) + inner_bias)
    )
    second_sine = jnp.sin(
        sine_scale * (jnp.dot(first_sine, middle_weight, precision=HIGHEST) + middle_bias)
    )
    return jnp.dot(second_sine, filter_weight, precision=HIGHEST) * decay_table(
        length, filter_weight.shape[1]
    )


def normalize(values, gain_row, shift_row):
    center = values - jnp.mean(values, axis=-1, keepdims=True)
    spread = jnp.mean(center * center, axis=-1, keepdims=True)
    return center * lax.rsqrt(spread + EPSILON) * gain_row + shift_row


def smooth_gate(values):
    return jax.nn.gelu(values, approximate=True)


def to_float(member):
    return member.astype(jnp.float32)


def short_filter(projected, segments, weight, offset):
    running = offset + weight[0] * projected
    for step_back in (1, 2):
        moved_rows = jnp.concatenate(
            [jnp.zeros_like(projected[:, :step_back]), projected[:, :-step_back]], axis=1
        )
        moved_ids = jnp.concatenate(
            [jnp.full_like(segments[:, :step_back], -1), segments[:, :-step_back]], axis=1
        )
        same_doc = (moved_ids == segments).astype(projected.dtype)
        running = running + weight[step_back] * moved_rows * same_doc[:, :, None]
    return running


def wave_tables(length):
    padded_size = 2 * length
    freq_index = jnp.arange(length + 1, dtype=jnp.int32)
    place_index = jnp.arange(length, dtype=jnp.int32)
    wrapped = freq_index[:, None] * place_index[None, :] % padded_size
    angles = 2.0 * math.pi / padded_size * wrapped.astype(jnp.float32)
    weights_row = (
        jnp.where((freq_index == 0) | (freq_index == length), 1.0, 2.0).astype(jnp.float32)
        / padded_size
    )
    return (jnp.cos(angles), jnp.sin(angles), weights_row)


def spectrum(tables, signal):
    cosine, sine, weights_row = tables
    real_part = jnp.einsum("ft,...td->...fd", cosine, signal, precision=HIGHEST)
    imag_part = -jnp.einsum("ft,...td->...fd", sine, signal, precision=HIGHEST)
    return (real_part, imag_part)


def inverse(tables, real_part, imag_part):
    cosine, sine, weights_row = tables
    scaled_real = real_part * weights_row[:, None]
    scaled_imag = imag_part * weights_row[:, None]
    return jnp.einsum("ft,...fd->...td", cosine, scaled_real, precision=HIGHEST) - jnp.einsum(
        "ft,...fd->...td", sine, scaled_imag, precision=HIGHEST
    )


MESH_ID = pl.DeviceIdType.MESH
LAGS = 64
LOW = jnp.bfloat16
FULL = jnp.float32
WHOLE, SPLIT, LINE = range(3)
GATHER_CHUNKS = (
    (4, 0, 128, WHOLE),
    (0, 768, 768, SPLIT),
    (0, 1536, 768, SPLIT),
    (0, 0, 768, SPLIT),
    (1, 0, 768, SPLIT),
    (3, 0, 768, LINE),
    (2, 0, 256, SPLIT),
    (2, 256, 256, SPLIT),
    (2, 512, 256, SPLIT),
    (3, 768, 768, WHOLE),
    (3, 1536, 768, WHOLE),
    (3, 2304, 384, WHOLE),
    (3, 2688, 384, WHOLE),
)
REDUCE_GROUPS = (
    (2, (0, 256), 256, SPLIT),
    (2, (512,), 256, WHOLE),
    (3, (0, 1536), 768, WHOLE),
    (3, (2304,), 768, LINE),
    (3, (768,), 768, SPLIT),
    (1, (0,), 768, SPLIT),
    (0, (0, 512), 512, SPLIT),
    (0, (1024, 1408), 384, WHOLE),
    (0, (1792,), 512, SPLIT),
    (4, (0,), 128, WHOLE),
)
REDUCE_ORDER = (
    (2, 0), (4, 0), (2, 1), (3, 0), (0, 0), (0, 1), (1, 0), (5, 0), (6, 0), (6, 1), (7, 0), (7, 1), (8, 0), (9, 0),
)
(
    DO_FIRST, DO_NEAR, DO_FAR, DO_SIDE, DO_CROSS, DO_PLACES, DO_UNPACK, DO_NORM1,
    DO_PROJECT, DO_CONV, DO_MIX, DO_EXPAND, DO_FEED, DO_DRAIN, DO_GCON, DO_GEXP,
    DO_NORM2B, DO_BACKG, DO_GOUT, DO_CONVB, DO_GIN, DO_BFIRST, DO_NORM1B, DO_SMALL,
    DO_STAGE, DO_ACORE, DO_AY, DO_AX, DO_AZ1, DO_AZ2, DO_AZ3, DO_FIN,
    DO_END,
) = range(33)
SCHEDULE = (
    (DO_FIRST, 0), (DO_FIRST, 5), (DO_FIRST, 1), (DO_FIRST, 2), (DO_FIRST, 3), (DO_NEAR, 0),
    (DO_FIRST, 4), (DO_NEAR, 1), (DO_FIRST, 6), (DO_FIRST, 7), (DO_PLACES, 0), (DO_NEAR, 2),
    (DO_NEAR, 3), (DO_FIRST, 8), (DO_NEAR, 4), (DO_NEAR, 6), (DO_FAR, 1), (DO_FAR, 2), (DO_FAR, 3),
    (DO_FAR, 4), (DO_FAR, 0), (DO_FIRST, 9), (DO_FIRST, 10), (DO_NEAR, 8), (DO_SIDE, 1),
    (DO_NEAR, 7), (DO_FIRST, 11), (DO_FIRST, 12), (DO_SIDE, 2), (DO_FAR, 8), (DO_SIDE, 3),
    (DO_SIDE, 0), (DO_NEAR, 11), (DO_FAR, 6), (DO_UNPACK, 0), (DO_CROSS, 1), (DO_NEAR, 12),
    (DO_SIDE, 4), (DO_NEAR, 5), (DO_CROSS, 2), (DO_NEAR, 10), (DO_NORM1, 0), (DO_PROJECT, 2),
    (DO_PROJECT, 1), (DO_SIDE, 8), (DO_FAR, 11), (DO_FAR, 7), (DO_FAR, 12), (DO_NEAR, 9),
    (DO_CONV, 0), (DO_CONV, 1), (DO_SIDE, 6), (DO_FAR, 10), (DO_FAR, 5), (DO_CROSS, 3),
    (DO_CONV, 2), (DO_CONV, 3), (DO_FAR, 9), (DO_SIDE, 11), (DO_PROJECT, 0), (DO_SIDE, 12),
    (DO_CROSS, 4), (DO_SIDE, 7), (DO_CROSS, 8), (DO_SIDE, 5), (DO_SIDE, 10), (DO_CROSS, 6),
    (DO_MIX, 0), (DO_EXPAND, 0), (DO_CROSS, 7), (DO_SIDE, 9), (DO_EXPAND, 3), (DO_EXPAND, 2),
    (DO_FEED, 2), (DO_GEXP, 2), (DO_STAGE, (2, 1)), (DO_EXPAND, 1), (DO_FEED, 1), (DO_GEXP, 1),
    (DO_STAGE, (4, 0)), (DO_ACORE, (2, 1)), (DO_FEED, 0), (DO_GEXP, 0), (DO_STAGE, (2, 0)),
    (DO_ACORE, (4, 0)), (DO_FEED, 3), (DO_DRAIN, 0), (DO_GCON, 0), (DO_STAGE, (0, 0)),
    (DO_ACORE, (2, 0)), (DO_STAGE, (1, 0)), (DO_AX, (2, 1)), (DO_GEXP, 3), (DO_STAGE, (3, 0)),
    (DO_STAGE, (0, 1)), (DO_ACORE, (0, 0)), (DO_NORM2B, 0), (DO_GOUT, 0), (DO_ACORE, (3, 0)),
    (DO_ACORE, (1, 0)), (DO_STAGE, (5, 0)), (DO_AY, (4, 0)), (DO_BACKG, 0), (DO_CONVB, 0),
    (DO_ACORE, (5, 0)), (DO_AX, (2, 0)), (DO_CONVB, 1), (DO_CONVB, 2), (DO_AY, (0, 0)),
    (DO_AX, (1, 0)), (DO_AZ1, (2, 1)), (DO_ACORE, (0, 1)), (DO_AY, (5, 0)), (DO_CONVB, 3),
    (DO_GIN, 1), (DO_STAGE, (7, 0)), (DO_AZ1, (2, 0)), (DO_AX, (4, 0)), (DO_GIN, 2),
    (DO_STAGE, (7, 1)), (DO_STAGE, (8, 0)), (DO_ACORE, (7, 0)), (DO_GIN, 0), (DO_STAGE, (6, 1)),
    (DO_AZ1, (3, 0)), (DO_ACORE, (7, 1)), (DO_ACORE, (8, 0)), (DO_AX, (0, 0)), (DO_BFIRST, 0),
    (DO_AZ2, (2, 1)), (DO_STAGE, (6, 0)), (DO_AZ2, (2, 0)), (DO_AY, (0, 1)), (DO_AX, (5, 0)),
    (DO_ACORE, (6, 1)), (DO_AZ1, (1, 0)), (DO_ACORE, (6, 0)), (DO_AX, (7, 0)), (DO_NORM1B, 0),
    (DO_SMALL, 0), (DO_STAGE, (9, 0)), (DO_ACORE, (9, 0)), (DO_AZ2, (3, 0)), (DO_AX, (7, 1)),
    (DO_AZ1, (0, 0)), (DO_AZ3, (2, 0)), (DO_AX, (0, 1)), (DO_AY, (8, 0)), (DO_AZ1, (5, 0)),
    (DO_AY, (6, 1)), (DO_AZ1, (4, 0)), (DO_AZ2, (1, 0)), (DO_AZ3, (1, 0)), (DO_AX, (9, 0)),
    (DO_AY, (6, 0)), (DO_AZ3, (3, 0)), (DO_AZ1, (7, 1)), (DO_AZ3, (2, 1)), (DO_AZ1, (7, 0)),
    (DO_AX, (8, 0)), (DO_AZ2, (0, 0)), (DO_AZ2, (5, 0)), (DO_AZ3, (0, 0)), (DO_AZ3, (5, 0)),
    (DO_AZ1, (0, 1)), (DO_AX, (6, 1)), (DO_AZ2, (7, 1)), (DO_FIN, (1, 0)), (DO_AX, (6, 0)),
    (DO_AZ3, (7, 1)), (DO_AZ1, (9, 0)), (DO_AZ2, (7, 0)), (DO_AZ3, (7, 0)), (DO_FIN, (2, 1)),
    (DO_AX, (3, 0)), (DO_AZ2, (0, 1)), (DO_AZ1, (8, 0)), (DO_AZ1, (6, 1)), (DO_FIN, (7, 1)),
    (DO_FIN, (0, 0)), (DO_AZ3, (0, 1)), (DO_AZ2, (9, 0)), (DO_AZ3, (9, 0)), (DO_AZ1, (6, 0)),
    (DO_AZ2, (8, 0)), (DO_AZ3, (8, 0)), (DO_FIN, (7, 0)), (DO_AZ2, (4, 0)), (DO_AZ3, (4, 0)),
    (DO_AZ2, (6, 1)), (DO_FIN, (0, 1)), (DO_AZ3, (6, 1)), (DO_AZ2, (6, 0)), (DO_AZ3, (6, 0)),
    (DO_FIN, (2, 0)), (DO_FIN, (4, 0)), (DO_FIN, (9, 0)), (DO_FIN, (6, 1)), (DO_FIN, (3, 0)),
    (DO_FIN, (5, 0)), (DO_FIN, (8, 0)), (DO_FIN, (6, 0)), (DO_END, 0),
)
SMALL_ROWS = 64
NORM_ROWS = 128
INNER_OUT = 8


def dot_nn(left_side, right_side):
    return jnp.dot(left_side, right_side, preferred_element_type=FULL)


def dot_nt(left_side, right_side):
    return lax.dot_general(
        left_side, right_side, (((1,), (1,)), ((), ())), preferred_element_type=FULL
    )


def dot_tn(left_side, right_side):
    return lax.dot_general(
        left_side, right_side, (((0,), (0,)), ((), ())), preferred_element_type=FULL
    )


def exact(left_side, right_side, contract):
    return lax.dot_general(
        left_side, right_side, (((contract[0],), (contract[1],)), ((), ())),
        preferred_element_type=FULL, precision=HIGHEST,
    )


def fold8(values):
    rows, columns = values.shape
    return jnp.sum(values.reshape(rows // 8, 8, columns), axis=0)


def widen(values, width):
    rows, columns = values.shape
    if columns == width:
        return values
    return jnp.concatenate([values, jnp.zeros((rows, width - columns), values.dtype)], axis=1)


def turn(values, amount, axis):
    size = values.shape[axis]
    amount = amount % size
    return values if amount == 0 else pltpu.roll(values, amount, axis)


def block_kernel(*refs):
    refs = list(refs)

    def take(number):
        taken = refs[:number]
        del refs[:number]
        return taken

    tokens_in, segs, cot_in = take(3)
    (
        r_first_gain, r_first_shift, r_in_bias, r_short_w, r_short_b, r_inner_w, r_inner_b,
        r_scale, r_middle_w, r_middle_b, r_filter_w, r_direct, r_out_bias, r_second_gain,
        r_second_shift, r_exp_bias, r_con_bias,
    ) = take(17)
    own = take(4)
    features, decay = take(2)
    result_out, delta_out = take(2)
    sums_out = take(5)
    tokens, cot, result, delta = take(4)
    sums = take(5)
    full = take(5)
    g_in, g_out, g_small, own_small, pack = take(5)
    v96, v288, vexp, v8 = take(4)
    mid_w, fil_w, taps, d_taps = take(4)
    s_inner1, s_first, s_cos1, s_inner2, s_second, s_cos2 = take(6)
    places, left = take(2)
    normed1, proj, short, conv, gated, resid, normed2 = take(7)
    hidden, post, pre, back_h, gather_out, back_s, back_m, bp = take(8)
    back_r, back_g = back_h, gather_out
    acc96, acc288, accexp = take(3)
    groups = []
    for matrix, columns, width, kind in REDUCE_GROUPS:
        members = take(7 if kind == SPLIT else 6)
        names = ("core", "x", "z1", "z2", "z3", "last") + (("y",) if kind == SPLIT else ())
        groups.append(dict(zip(names, members)))
    ag_recv, ag_cross, ag_core, ag_send, own_sem, rs_recv, rs_y, rs_send, rs_end, out_sem = take(10)
    assert not refs

    own = list(own) + [own_small]
    grads = (g_in, g_out, full[2], full[3], g_small)

    rep = lax.axis_index("rep")
    shard = lax.axis_index("shard")
    y, c = rep // 2, rep % 2
    z, x = shard // 2, shard % 2
    pair = z // 2
    near_z = z + 1 - 2 * (z % 2)
    inner = ((z + 1) // 2) % 2 == 1
    to_near = (rep, near_z * 2 + x)
    to_mirror = (rep, (3 - z) * 2 + x)
    to_x = (rep, z * 2 + 1 - x)
    to_y = ((1 - y) * 2 + c, shard)
    to_c = (y * 2 + 1 - c, shard)
    own_pair = pl.ds(pair * 2, 2)
    other_pair = pl.ds((1 - pair) * 2, 2)

    loads = [
        pltpu.make_async_copy(own[m].at[c], full[m].at[z, x, c], own_sem.at[m]) for m in range(4)
    ] + [
        pltpu.make_async_copy(tokens_in, tokens, own_sem.at[5]),
        pltpu.make_async_copy(cot_in, cot, own_sem.at[6]),
    ]
    barrier = pltpu.get_barrier_semaphore()
    for target in (to_near, to_x, to_y, to_c):
        pl.semaphore_signal(barrier, inc=1, device_id=target, device_id_type=MESH_ID)

    @pl.when(inner)
    def _():
        pl.semaphore_signal(barrier, inc=1, device_id=to_mirror, device_id_type=MESH_ID)

    for load in loads:
        load.start()

    def remote(source, landing, send, recv, device):
        return pltpu.make_async_remote_copy(
            src_ref=source, dst_ref=landing, send_sem=send, recv_sem=recv,
            device_id=device, device_id_type=MESH_ID,
        )

    pack[...] = jnp.zeros_like(pack)
    for row, member in enumerate(
        (r_first_gain, r_first_shift, r_direct, r_out_bias, r_second_gain, r_second_shift, r_con_bias)
    ):
        pack[row : row + 1, 0:96] = member[...].astype(FULL).reshape(1, 96)
    in_bias, short_b = (m[...].astype(FULL).reshape(1, 288) for m in (r_in_bias, r_short_b))
    exp_bias = r_exp_bias[...].astype(FULL).reshape(1, 384)
    for block in range(3):
        lanes = 128 if block < 2 else 32
        span = slice(block * 128, block * 128 + lanes)
        top = 8 + block * 8
        pack[top : top + 1, 0:lanes] = in_bias[:, span]
        pack[top + 1 : top + 2, 0:lanes] = short_b[:, span]
        pack[top + 2 : top + 5, 0:lanes] = r_short_w[:, span].astype(FULL)
        pack[top + 5 : top + 6, :] = exp_bias[:, block * 128 : block * 128 + 128]
    for row, member in enumerate((r_inner_b, r_scale, r_middle_b)):
        pack[32 + row : 33 + row, 0:8] = member[...].astype(FULL).reshape(1, 8)
    pack[40:48, 0:64] = r_middle_w[...].astype(FULL)
    pack[48:56, 0:33] = r_inner_w[...].astype(FULL)
    pack[64:128, 0:96] = r_filter_w[...].astype(FULL)
    own_small[0] = pack[0:64, :].astype(LOW)
    own_small[1] = pack[64:128, :].astype(LOW)

    acc96[...] = jnp.zeros_like(acc96)
    acc288[...] = jnp.zeros_like(acc288)
    accexp[...] = jnp.zeros_like(accexp)
    d_taps[...] = jnp.zeros_like(d_taps)

    pl.semaphore_wait(barrier, 4 + ((z + 1) // 2) % 2)

    chunks = GATHER_CHUNKS
    count = len(chunks)
    cross_index = {}
    for index, chunk in enumerate(chunks):
        if chunk[3] == SPLIT:
            cross_index[index] = len(cross_index)
    NEAR, FAR, SIDE0, SIDE1 = range(4)
    S_NEAR, S_MIRROR, S_BACK, S_SIDE, S_CROSS, S_CORE = range(6)

    def part(chunk, quarter):
        matrix, column, width, kind = chunk
        if kind == SPLIT:
            return pl.ds(pl.multiple_of(column + quarter * (width // 2), 128), width // 2)
        return pl.ds(column, width)

    def whole(chunk):
        return pl.ds(chunk[1], chunk[2])

    small_load = pltpu.make_async_copy(own_small.at[c], full[4].at[z, x, c], own_sem.at[4])
    small_load.start()
    loads.append(small_load)

    send_groups = []
    for chunk in chunks:
        key = chunk[:1] if chunk[0] != 3 else chunk[:2]
        if key not in send_groups:
            send_groups.append(key)

    def group_of(chunk):
        return send_groups.index(chunk[:1] if chunk[0] != 3 else chunk[:2])

    def first(index):
        chunk = chunks[index]
        m, s = chunk[0], group_of(chunk)
        piece = own[m].at[c, :, part(chunk, y)]
        landing = full[m].at[z, x, c, :, part(chunk, y)]
        if chunk[3] == LINE:
            remote(piece, landing, ag_send.at[S_SIDE, s], ag_recv.at[SIDE0, index], to_x).start()
        else:
            remote(piece, landing, ag_send.at[S_NEAR, s], ag_recv.at[NEAR, index], to_near).start()

    def line_near(index):
        chunk = chunks[index]
        m, s = chunk[0], group_of(chunk)
        arrived = full[m].at[z, 1 - x, c, :, whole(chunk)]
        remote(arrived, arrived, ag_send.at[S_SIDE, s], ag_recv.at[SIDE0, index], to_x).wait_recv()
        both = full[m].at[z, :, c, :, whole(chunk)]
        remote(both, both, ag_send.at[S_NEAR, s], ag_recv.at[NEAR, index], to_near).start()

    def line_far(index):
        chunk = chunks[index]
        m, s = chunk[0], group_of(chunk)
        arrived = full[m].at[near_z, :, c, :, whole(chunk)]
        remote(arrived, arrived, ag_send.at[S_NEAR, s], ag_recv.at[NEAR, index], to_near).wait_recv()

        @pl.when(inner)
        def _():
            four = full[m].at[own_pair, :, c, :, whole(chunk)]
            remote(four, four, ag_send.at[S_MIRROR, s], ag_recv.at[FAR, index], to_mirror).start()

    def line_side(index):
        chunk = chunks[index]
        m, s = chunk[0], group_of(chunk)
        four = full[m].at[other_pair, :, c, :, whole(chunk)]
        remote(four, four, ag_send.at[S_MIRROR, s], ag_recv.at[FAR, index], to_near).wait_recv()

        @pl.when(inner)
        def _():
            remote(four, four, ag_send.at[S_BACK, s], ag_recv.at[FAR, index], to_near).start()

        to_core(index)

    def near(index):
        chunk = chunks[index]
        if chunk[3] == LINE:
            return line_near(index)
        m, s = chunk[0], group_of(chunk)
        arrived = full[m].at[near_z, x, c, :, part(chunk, y)]
        remote(arrived, arrived, ag_send.at[S_NEAR, s], ag_recv.at[NEAR, index], to_near).wait_recv()
        both = full[m].at[own_pair, x, c, :, part(chunk, y)]

        @pl.when(inner)
        def _():
            remote(both, both, ag_send.at[S_MIRROR, s], ag_recv.at[FAR, index], to_mirror).start()

        remote(both, both, ag_send.at[S_SIDE, s], ag_recv.at[SIDE0, index], to_x).start()
        if chunk[3] == SPLIT:
            remote(
                arrived, arrived, ag_send.at[S_CROSS, s], ag_cross.at[0, cross_index[index]], to_y
            ).start()

    def far(index):
        chunk = chunks[index]
        if chunk[3] == LINE:
            return line_far(index)
        m, s = chunk[0], group_of(chunk)
        both = full[m].at[other_pair, x, c, :, part(chunk, y)]
        remote(both, both, ag_send.at[S_MIRROR, s], ag_recv.at[FAR, index], to_near).wait_recv()

        @pl.when(inner)
        def _():
            remote(both, both, ag_send.at[S_BACK, s], ag_recv.at[FAR, index], to_near).start()

        remote(both, both, ag_send.at[S_SIDE, s], ag_recv.at[SIDE1, index], to_x).start()
        if chunk[3] == SPLIT:
            remote(
                both, both, ag_send.at[S_CROSS, s], ag_cross.at[1, cross_index[index]], to_y
            ).start()

    def to_core(index):
        chunk = chunks[index]
        m, s = chunk[0], group_of(chunk)
        piece = full[m].at[:, :, c, :, whole(chunk)]
        remote(piece, piece, ag_send.at[S_CORE, s], ag_core.at[index], to_c).start()

    def side(index):
        chunk = chunks[index]
        if chunk[3] == LINE:
            return line_side(index)
        m, s = chunk[0], group_of(chunk)
        for place, slot in ((own_pair, SIDE0), (other_pair, SIDE1)):
            both = full[m].at[place, 1 - x, c, :, part(chunk, y)]
            remote(both, both, ag_send.at[S_SIDE, s], ag_recv.at[slot, index], to_x).wait_recv()
        if chunk[3] == SPLIT:
            column = full[m].at[:, 1 - x, c, :, part(chunk, y)]
            remote(
                column, column, ag_send.at[S_CROSS, s], ag_cross.at[2, cross_index[index]], to_y
            ).start()
        else:
            to_core(index)

    def cross(index):
        chunk = chunks[index]
        m, s = chunk[0], group_of(chunk)
        for slot, piece in enumerate(
            (
                full[m].at[near_z, x, c, :, part(chunk, 1 - y)],
                full[m].at[other_pair, x, c, :, part(chunk, 1 - y)],
                full[m].at[:, 1 - x, c, :, part(chunk, 1 - y)],
            )
        ):
            remote(
                piece, piece, ag_send.at[S_CROSS, s], ag_cross.at[slot, cross_index[index]], to_y
            ).wait_recv()
        to_core(index)

    waited = set()

    def settled(m, low, high):
        for index, chunk in enumerate(chunks):
            inside = chunk[0] == m and chunk[1] < high and chunk[1] + chunk[2] > low
            if inside and index not in waited:
                waited.add(index)
                piece = full[m].at[:, :, 1 - c, :, whole(chunk)]
                send = ag_send.at[S_CORE, group_of(chunk)]
                remote(piece, piece, send, ag_core.at[index], to_c).wait_recv()

    loaded = []

    def ready():
        if not loaded:
            loaded.append(True)
            for load in loads:
                load.wait()


    def row_blocks(size, action):
        def body(step, carry):
            action(pl.ds(pl.multiple_of(step * size, size), size))
            return carry

        lax.fori_loop(0, tokens.shape[0] // size, body, 0)

    def find_places():
        rows = lax.broadcasted_iota(jnp.int32, (128, 128), 0)
        columns = lax.broadcasted_iota(jnp.int32, (128, 128), 1)
        for sequence in range(2):
            ids = jnp.broadcast_to(segs[sequence : sequence + 1, :].astype(FULL), (128, 128))
            same = ids == ids.T
            before = jnp.sum(jnp.where(same & (columns < rows), 1.0, 0.0), axis=1, keepdims=True)
            after = jnp.sum(jnp.where(same & (columns > rows), 1.0, 0.0), axis=1, keepdims=True)
            span = slice(sequence * 128, sequence * 128 + 128)
            places[span, :] = jnp.broadcast_to(before.astype(jnp.int32), (128, 128))
            left[span, :] = jnp.broadcast_to(after.astype(jnp.int32), (128, 128))

    def unpack_small():
        total96 = jnp.zeros((8, 768), FULL)
        total288 = jnp.zeros((8, 2304), FULL)
        total8 = jnp.zeros((8, 128), FULL)
        inner_rows = []
        fil_w[...] = jnp.zeros_like(fil_w)
        mid_w[...] = jnp.zeros_like(mid_w)
        for s in range(8):
            top = full[4][s // 2, s % 2, 0].astype(FULL)
            low = full[4][s // 2, s % 2, 1].astype(FULL)
            total96 = total96 + turn(widen(top[0:8], 768), 96 * s, 1)
            wide = jnp.concatenate([top[8:16], top[16:24], top[24:32]], axis=1)
            vexp[:, s * 384 : s * 384 + 384] = wide[5:6]
            total288 = total288 + turn(widen(wide, 2304), 288 * s, 1)
            total8 = total8 + turn(top[32:40], 8 * s, 1)
            inner_rows.append(top[48:56])
            mid_w[8 * s : 8 * s + 8, :] = top[40:48]
            fil_w[0:64, :] += turn(widen(low, 768), 96 * s, 1)
        v96[...] = total96
        v288[...] = total288
        v8[...] = total8
        scale = total8[1:2]
        inner_all = jnp.concatenate(inner_rows + [jnp.zeros((64, 128), FULL)], axis=0)
        inner1 = exact(features[...], inner_all, (1, 1)) + total8[0:1]
        s_inner1[...] = inner1
        s_first[...] = jnp.sin(scale * inner1)
        s_cos1[...] = jnp.cos(scale * inner1)
        inner2 = exact(s_first[...], mid_w[...], (1, 0)) + total8[2:3]
        s_inner2[...] = inner2
        s_second[...] = jnp.sin(scale * inner2)
        s_cos2[...] = jnp.cos(scale * inner2)
        taps[...] = exact(s_second[...], fil_w[...], (1, 0)) * decay[...]

    def center(values):
        middle = values - jnp.mean(values, axis=-1, keepdims=True)
        spread = jnp.mean(middle * middle, axis=-1, keepdims=True)
        scale = lax.rsqrt(spread + EPSILON)
        return middle * scale, scale

    def norm_first(rows):
        unit, _ = center(tokens[rows, :].astype(FULL))
        normed1[rows, :] = (unit * v96[0:1, :] + v96[1:2, :]).astype(LOW)

    def matrix_of(m, columns, width):
        value = full[m][:, :, :, :, columns]
        return value.reshape(value.shape[0] * value.shape[1] * value.shape[2] * value.shape[3], width)

    def project(k):
        span = slice(k * 768, k * 768 + 768)
        proj[k] = dot_nn(normed1[...], matrix_of(0, pl.ds(k * 768, 768), 768)) + v288[0:1, span]

        def body(step, carry):
            rows = pl.ds(pl.multiple_of((step // 6) * 128, 128), 128)
            lane = pl.multiple_of((step % 6) * 128, 128)
            lanes = pl.ds(lane, 128)
            wide = pl.ds(pl.multiple_of(k * 768 + lane, 128), 128)
            values = proj[k, rows, lanes]
            where = places[rows, :]
            total = v288[1:2, wide] + v288[2:3, wide] * values
            for lag in (1, 2):
                moved = jnp.where(where >= lag, pltpu.roll(values, lag, 0), 0.0)
                total = total + v288[2 + lag : 3 + lag, wide] * moved
            short[k, rows, lanes] = total
            return carry

        lax.fori_loop(0, 12, body, 0)

    def convolve(begin, end):
        def body(step, carry):
            rows = pl.ds(pl.multiple_of((step // 6) * 128, 128), 128)
            lanes = pl.ds(pl.multiple_of((step % 6) * 128, 128), 128)
            carried = short[2, rows, lanes] * short[1, rows, lanes]
            where = places[rows, :]
            total = v96[2:3, lanes] * carried
            for low_lag in range(8):
                moved = turn(carried, low_lag, 0)
                for high in range(LAGS // 8):
                    lag, skip = high * 8 + low_lag, high * 8
                    term = jnp.where(
                        where[skip:] >= lag, taps[lag : lag + 1, lanes] * moved[: 128 - skip], 0.0
                    )
                    if skip:
                        total = jnp.concatenate([total[:skip], total[skip:] + term], axis=0)
                    else:
                        total = total + term
            conv[rows, lanes] = total
            return carry

        lax.fori_loop(begin, end, body, 0)

    def mix_out():
        def gate(rows):
            gated[rows, :] = (conv[rows, :] * short[0, rows, :]).astype(LOW)

        row_blocks(NORM_ROWS, gate)
        resid[...] = dot_nn(gated[...], matrix_of(1, pl.ds(0, 768), 768))

        def finish_rows(rows):
            values = resid[rows, :] + tokens[rows, :].astype(FULL) + v96[3:4, :]
            resid[rows, :] = values
            unit, _ = center(values)
            normed2[rows, :] = (unit * v96[4:5, :] + v96[5:6, :]).astype(LOW)

        row_blocks(NORM_ROWS, finish_rows)

    def expand(k):
        span = slice(k * 768, k * 768 + 768)
        hidden[:, span] = (
            dot_nn(normed2[...], matrix_of(3, pl.ds(k * 768, 768), 768)) + vexp[:, span]
        )

    fed_before = []

    def feed(k):
        span = slice(k * 768, k * 768 + 768)
        rows_of = full[2][k].reshape(768, 768)
        back_h[...] = dot_nt(cot[...], rows_of)

        def bend(rows):
            values = hidden[rows, span]
            cube = values * values
            grow = math.sqrt(2.0 / math.pi)
            slope = jnp.tanh(grow * (values + 0.044715 * cube * values))
            half_up = 0.5 + 0.5 * slope
            post[rows, span] = (values * half_up).astype(LOW)
            steep = half_up + (0.5 * values) * (1.0 - slope * slope) * (
                grow * (1.0 + 3.0 * 0.044715 * cube)
            )
            grad = (back_h[rows, :] * steep).astype(LOW)
            pre[rows, span] = grad
            accexp[:, span] += fold8(grad.astype(FULL))

        row_blocks(16, bend)
        out_part = dot_nn(post[:, span], full[2][k].reshape(768, 768))
        back_part = dot_nt(pre[:, span], matrix_of(3, pl.ds(k * 768, 768), 768))
        if not fed_before:
            gather_out[...] = out_part
            back_s[...] = back_part
            fed_before.append(k)
        else:
            gather_out[...] += out_part
            back_s[...] += back_part

    drained = set()

    def drain(m, low, high):
        for s, key in enumerate(send_groups):
            members = [
                chunk for chunk in chunks
                if group_of(chunk) == s and m == chunk[0]
                and chunk[1] < high and chunk[1] + chunk[2] > low
            ]
            if not members or s in drained:
                continue
            drained.add(s)
            members = [chunk for chunk in chunks if group_of(chunk) == s]
            kind = members[0][3]
            assert all(chunk[3] == kind for chunk in members)
            wide = sum(chunk[2] for chunk in members)
            thin = wide // 2 if kind == SPLIT else wide

            def gone(slot, planes, rows, width=thin, s=s):
                ref = full[m].at[pl.ds(0, planes), pl.ds(0, rows), 0, :, pl.ds(0, width)]
                remote(ref, ref, ag_send.at[slot, s], ag_recv.at[FAR, 0], to_near).wait_send()

            if kind == LINE:
                gone(S_SIDE, 1, 1)
                gone(S_NEAR, 2, 1)
            else:
                gone(S_NEAR, 1, 1)
                gone(S_SIDE, 4, 1)

            @pl.when(inner)
            def _(gone=gone, kind=kind):
                gone(S_MIRROR, 2, 2 if kind == LINE else 1)
                gone(S_BACK, 2, 2 if kind == LINE else 1)

            if kind == SPLIT:
                gone(S_CROSS, 3, 1)
                gone(S_CROSS, 4, 1)
            gone(S_CORE, 4, 2, wide)

    position = {}
    split_position = {}
    for index, key in enumerate(REDUCE_ORDER):
        position[key] = index
        if REDUCE_GROUPS[key[0]][3] == SPLIT:
            split_position[key] = len(split_position)
    R_CORE, R_X, R_Z1, R_Z2, R_Z3, R_LAST = range(6)
    W_CORE, W_Y, W_X, W_Z1, W_Z3, W_LAST, W_END = range(7)
    W_Z2 = W_Z1

    def info(key):
        g, i = key
        matrix, columns, width, kind = REDUCE_GROUPS[g]
        return g, i, matrix, columns[i], width, kind, groups[g], position[key]

    def halves(width, which):
        return pl.ds(pl.multiple_of(which * (width // 2), 128), width // 2)

    def stage(key):
        g, i, m, column, width, kind, buf, n = info(key)
        remote(
            grads[m].at[:, :, 1 - c, :, pl.ds(column, width)], buf["core"].at[i],
            rs_send.at[W_CORE, g], rs_recv.at[R_CORE, n], to_c,
        ).start()

    def running(key):
        g, i, m, column, width, kind, buf, n = info(key)
        return buf["core"] if kind == LINE else buf["x"]

    def send_line(key):
        g, i, m, column, width, kind, buf, n = info(key)
        sums_ref = running(key)

        @pl.when(jnp.logical_not(inner))
        def _():
            remote(
                sums_ref.at[i, other_pair], buf["z1"].at[i],
                rs_send.at[W_Z1, g], rs_recv.at[R_Z1, n], to_near,
            ).start()
            remote(
                sums_ref.at[i, near_z], buf["z3"].at[i],
                rs_send.at[W_Z3, g], rs_recv.at[R_Z3, n], to_near,
            ).start()

    def add_core(key):
        g, i, m, column, width, kind, buf, n = info(key)
        landing = buf["core"].at[i]
        remote(landing, landing, rs_send.at[W_CORE, g], rs_recv.at[R_CORE, n], to_c).wait_recv()

        def body(step, carry):
            a, b = step // 2, step % 2
            buf["core"][i, a, b] = buf["core"][i, a, b] + grads[m][a, b, c, :, pl.ds(column, width)]
            return carry

        lax.fori_loop(0, 8, body, 0)
        if kind == SPLIT:
            remote(
                buf["core"].at[i, :, :, :, halves(width, 1 - y)], buf["y"].at[i],
                rs_send.at[W_Y, g], rs_y.at[split_position[key]], to_y,
            ).start()
        elif kind == WHOLE:
            remote(
                buf["core"].at[i, :, 1 - x], buf["x"].at[i],
                rs_send.at[W_X, g], rs_recv.at[R_X, n], to_x,
            ).start()
        else:
            send_line(key)

    def add_y(key):
        g, i, m, column, width, kind, buf, n = info(key)
        landing = buf["y"].at[i]
        remote(landing, landing, rs_send.at[W_Y, g], rs_y.at[split_position[key]], to_y).wait_recv()

        def body(step, carry):
            a, b = step // 2, step % 2
            buf["y"][i, a, b] = buf["y"][i, a, b] + buf["core"][i, a, b, :, halves(width, y)]
            return carry

        lax.fori_loop(0, 8, body, 0)
        remote(
            buf["y"].at[i, :, 1 - x], buf["x"].at[i], rs_send.at[W_X, g], rs_recv.at[R_X, n], to_x
        ).start()

    def send_last(key):
        g, i, m, column, width, kind, buf, n = info(key)
        remote(
            buf["last"].at[i, 0], buf["last"].at[i, 1],
            rs_send.at[W_LAST, g], rs_recv.at[R_LAST, n], to_y,
        ).start()

    def add_x(key):
        g, i, m, column, width, kind, buf, n = info(key)
        landing = buf["x"].at[i]
        remote(landing, landing, rs_send.at[W_X, g], rs_recv.at[R_X, n], to_x).wait_recv()
        if kind == LINE:
            buf["last"][i, 0] = buf["core"][i, z, x] + buf["x"][i]
            send_last(key)
            return
        own_part = buf["y"] if kind == SPLIT else buf["core"]

        def body(step, carry):
            buf["x"][i, step] = buf["x"][i, step] + own_part[i, step, x]
            return carry

        lax.fori_loop(0, 4, body, 0)
        send_line(key)

    def add_z1(key):
        g, i, m, column, width, kind, buf, n = info(key)
        sums_ref = running(key)

        @pl.when(inner)
        def _():
            landing = buf["z1"].at[i]
            remote(landing, landing, rs_send.at[W_Z1, g], rs_recv.at[R_Z1, n], to_near).wait_recv()
            for step in range(2):
                at = (1 - pair) * 2 + step
                sums_ref[i, at] = sums_ref[i, at] + buf["z1"][i, step]
            remote(
                sums_ref.at[i, other_pair], buf["z2"].at[i],
                rs_send.at[W_Z2, g], rs_recv.at[R_Z2, n], to_mirror,
            ).start()

    def add_z2(key):
        g, i, m, column, width, kind, buf, n = info(key)
        sums_ref = running(key)

        @pl.when(inner)
        def _():
            landing = buf["z2"].at[i]
            remote(landing, landing, rs_send.at[W_Z2, g], rs_recv.at[R_Z2, n], to_mirror).wait_recv()
            for step in range(2):
                at = pair * 2 + step
                sums_ref[i, at] = sums_ref[i, at] + buf["z2"][i, step]
            remote(
                sums_ref.at[i, near_z], buf["z3"].at[i],
                rs_send.at[W_Z3, g], rs_recv.at[R_Z3, n], to_near,
            ).start()

    def add_z3(key):
        g, i, m, column, width, kind, buf, n = info(key)
        landing = buf["z3"].at[i]
        remote(landing, landing, rs_send.at[W_Z3, g], rs_recv.at[R_Z3, n], to_near).wait_recv()
        if kind == LINE:
            buf["core"][i, z] = buf["core"][i, z] + buf["z3"][i]
            remote(
                buf["core"].at[i, z, 1 - x], buf["x"].at[i],
                rs_send.at[W_X, g], rs_recv.at[R_X, n], to_x,
            ).start()
            return
        buf["last"][i, 0] = buf["x"][i, z] + buf["z3"][i]
        send_last(key)

    def finish(key):
        g, i, m, column, width, kind, buf, n = info(key)
        landing = buf["last"].at[i, 1]
        remote(landing, landing, rs_send.at[W_LAST, g], rs_recv.at[R_LAST, n], to_y).wait_recv()
        if kind == SPLIT:
            for which, slot in ((y, 0), (1 - y, 1)):
                columns = pl.ds(pl.multiple_of(column + which * (width // 2), 128), width // 2)
                sums[m][:, columns] = buf["last"][i, slot].astype(FULL)
        else:
            sums[m][:, pl.ds(column, width)] = buf["last"][i, 0].astype(FULL) + buf["last"][
                i, 1
            ].astype(FULL)
        piece = sums[m].at[:, pl.ds(column, width)]
        place = sums_out[m].at[c, :, pl.ds(column, width)]
        remote(piece, place, rs_send.at[W_END, g], rs_end.at[g], to_c).start()
        pltpu.make_async_copy(piece, place, out_sem.at[g]).start()

    def grad_contract():
        def body(s, carry):
            lanes = pl.ds(pl.multiple_of(s * 384, 128), 384)
            value = dot_tn(post[:, lanes], cot[...]).astype(LOW)
            full[2][s // 2, s % 2] = value.reshape(2, 192, 768)
            return carry

        lax.fori_loop(0, 8, body, 0)

    def grad_rows(source, other, target, columns, width):
        for half in range(2):
            value = dot_tn(source[:, half * 384 : half * 384 + 384], other).astype(LOW)
            target[2 * half : 2 * half + 2, :, :, :, columns] = value.reshape(2, 2, 2, 48, width)

    def grad_expand(i):
        span = slice(i * 768, i * 768 + 768)
        grad_rows(normed2, pre[:, span], full[3], pl.ds(i * 768, 768), 768)

    def norm_second_back(rows):
        unit, scale = center(resid[rows, :])
        grad = back_s[rows, :]
        top = cot[rows, :].astype(FULL)
        e = grad * v96[4:5, :]
        value = (
            e - jnp.mean(e, axis=-1, keepdims=True) - unit * jnp.mean(e * unit, axis=-1, keepdims=True)
        ) * scale + top
        back_r[rows, :] = value
        rounded = value.astype(LOW)
        back_m[rows, :] = rounded
        acc96[4] += fold8(grad * unit)
        acc96[5] += fold8(grad)
        acc96[3] += fold8(rounded.astype(FULL))
        acc96[6] += fold8(top)
        result[rows, :] = (resid[rows, :] + gather_out[rows, :] + v96[6:7, :]).astype(LOW)

    def convolve_back(begin, end):
        def body(step, carry):
            rows = pl.ds(pl.multiple_of((step // 6) * 128, 128), 128)
            lane = pl.multiple_of((step % 6) * 128, 128)
            lanes = pl.ds(lane, 128)
            where = places[rows, :]
            rest = left[rows, :]
            gate_in = short[1, rows, lanes]
            values = short[2, rows, lanes]
            top = back_g[rows, lanes]
            carried = values * gate_in
            back_conv = top * short[0, rows, lanes]
            acc96[2, :, lanes] += fold8(back_conv * carried)
            total = v96[2:3, lanes] * back_conv
            for low_lag in range(8):
                turned = turn(back_conv, -low_lag, 0)
                for high in range(LAGS // 8):
                    lag, skip = high * 8 + low_lag, high * 8
                    size = 128 - skip
                    moved = jnp.where(rest[:size] >= lag, turned[skip:], 0.0)
                    term = taps[lag : lag + 1, lanes] * moved
                    if skip:
                        total = jnp.concatenate([total[:size] + term, total[size:]], axis=0)
                    else:
                        total = total + term
                    d_taps[lag : lag + 1, lanes] += jnp.sum(
                        moved * carried[:size], axis=0, keepdims=True
                    )
            streams = (top * conv[rows, lanes], total * values, total * gate_in)
            for k in range(3):
                wide = pl.ds(pl.multiple_of(k * 768 + lane, 128), 128)
                grad = streams[k]
                before = proj[k, rows, lanes]
                acc288[1, :, wide] += fold8(grad)
                acc288[2, :, wide] += fold8(grad * before)
                value = v288[2:3, wide] * grad
                for lag in (1, 2):
                    moved = jnp.where(where >= lag, pltpu.roll(before, lag, 0), 0.0)
                    acc288[2 + lag, :, wide] += fold8(grad * moved)
                    later = jnp.where(rest >= lag, pltpu.roll(grad, 128 - lag, 0), 0.0)
                    value = value + v288[2 + lag : 3 + lag, wide] * later
                rounded = value.astype(LOW)
                bp[k, rows, lanes] = rounded
                acc288[0, :, wide] += fold8(rounded.astype(FULL))
            return carry

        lax.fori_loop(begin, end, body, 0)

    def norm_first_back(rows):
        unit, scale = center(tokens[rows, :].astype(FULL))
        grad = back_s[rows, :]
        e = grad * v96[0:1, :]
        delta[rows, :] = back_r[rows, :] + (
            e - jnp.mean(e, axis=-1, keepdims=True) - unit * jnp.mean(e * unit, axis=-1, keepdims=True)
        ) * scale
        acc96[0] += fold8(grad * unit)
        acc96[1] += fold8(grad)

    def small_grads():
        scale = v8[1:2, :]
        raw = d_taps[...] * decay[...]
        d_fil = exact(s_second[...], raw, (0, 0))
        b2 = exact(raw, fil_w[...], (1, 1)) * s_cos2[...]
        b2s = b2 * scale
        d_mid = exact(s_first[...], b2s, (0, 0))
        b1 = exact(b2s, mid_w[...], (1, 1)) * s_cos1[...]
        b1s = b1 * scale
        d_inner = exact(b1s, features[...], (0, 0))
        d_scale = jnp.sum(b2 * s_inner2[...] + b1 * s_inner1[...], axis=0, keepdims=True)
        rows8 = jnp.concatenate(
            [
                jnp.sum(b1s, axis=0, keepdims=True), d_scale, jnp.sum(b2s, axis=0, keepdims=True),
                jnp.zeros((5, 128), FULL),
            ],
            axis=0,
        )
        rows96 = jnp.concatenate(
            [jnp.sum(acc96[f], axis=0, keepdims=True) for f in range(7)] + [jnp.zeros((1, 768), FULL)],
            axis=0,
        )
        rows288 = jnp.concatenate(
            [jnp.sum(acc288[f], axis=0, keepdims=True) for f in range(5)]
            + [jnp.zeros((3, 2304), FULL)],
            axis=0,
        )
        rows_exp = jnp.sum(accexp[...], axis=0, keepdims=True)
        lane = lax.broadcasted_iota(jnp.int32, (8, 128), 1)
        row = lax.broadcasted_iota(jnp.int32, (8, 128), 0)
        wide_lane = lax.broadcasted_iota(jnp.int32, (64, 128), 1)
        for s in range(8):
            a, b = s // 2, s % 2
            g_small[a, b, 0, 0:8, :] = jnp.where(lane < 96, turn(rows96, -96 * s, 1)[:, :128], 0.0)
            turned = turn(rows288, -288 * s, 1)
            for block in range(3):
                value = turned[:, block * 128 : block * 128 + 128]
                if block == 2:
                    value = jnp.where(lane < 32, value, 0.0)
                bias = rows_exp[:, s * 384 + block * 128 : s * 384 + block * 128 + 128]
                value = jnp.where(row == 5, jnp.broadcast_to(bias, (8, 128)), value)
                g_small[a, b, 0, 8 + block * 8 : 16 + block * 8, :] = value
            g_small[a, b, 0, 32:40, :] = jnp.where(lane < 8, turn(rows8, -8 * s, 1), 0.0)
            g_small[a, b, 0, 40:48, :] = d_mid[8 * s : 8 * s + 8]
            g_small[a, b, 0, 48:56, :] = d_inner[8 * s : 8 * s + 8]
            g_small[a, b, 0, 56:64, :] = jnp.zeros((8, 128), FULL)
            g_small[a, b, 1] = jnp.where(
                wide_lane < 96, turn(d_fil[0:64], -96 * s, 1)[:, :128], 0.0
            )

    def back_gate():
        back_g[...] = dot_nt(back_m[...], matrix_of(1, pl.ds(0, 768), 768))

    def back_first():
        for k in range(3):
            value = dot_nt(bp[k], matrix_of(0, pl.ds(k * 768, 768), 768))
            if k == 0:
                back_s[...] = value
            else:
                back_s[...] += value

    def unpack(k):
        settled(4, 0, 128)
        unpack_small()

    def projected(k):
        settled(0, k * 768, k * 768 + 768)
        project(k)

    def mix(k):
        settled(1, 0, 768)
        mix_out()

    def expanded(k):
        settled(3, k * 768, k * 768 + 768)
        expand(k)

    def fed(k):
        settled(2, 0, 768)
        feed(k)

    outgoing = [
        pltpu.make_async_copy(result, result_out, own_sem.at[7]),
        pltpu.make_async_copy(delta, delta_out, own_sem.at[8]),
    ]

    def second_back(k):
        row_blocks(NORM_ROWS, norm_second_back)
        outgoing[0].start()

    def first_back(k):
        row_blocks(NORM_ROWS, norm_first_back)
        outgoing[1].start()

    def expand_back(k):
        drain(3, k * 768, k * 768 + 768)
        grad_expand(k)

    def end(k):
        for copy in outgoing:
            copy.wait()
        for m in range(5):
            drain(m, 0, full[m].shape[4])

    actions = {
        DO_FIRST: first, DO_NEAR: near, DO_FAR: far, DO_SIDE: side, DO_CROSS: cross,
        DO_PLACES: lambda k: find_places(),
        DO_UNPACK: unpack,
        DO_NORM1: lambda k: row_blocks(NORM_ROWS, norm_first),
        DO_PROJECT: projected,
        DO_CONV: lambda k: convolve(3 * k, 3 * k + 3),
        DO_MIX: mix,
        DO_EXPAND: expanded,
        DO_FEED: fed,
        DO_DRAIN: lambda k: drain(2, 0, 768),
        DO_GCON: lambda k: grad_contract(),
        DO_GEXP: expand_back,
        DO_NORM2B: second_back,
        DO_BACKG: lambda k: back_gate(),
        DO_GOUT: lambda k: grad_rows(gated, back_m[...], g_out, pl.ds(0, 768), 768),
        DO_CONVB: lambda k: convolve_back(3 * k, 3 * k + 3),
        DO_GIN: lambda k: grad_rows(normed1, bp[k], g_in, pl.ds(k * 768, 768), 768),
        DO_BFIRST: lambda k: back_first(),
        DO_NORM1B: first_back,
        DO_SMALL: lambda k: small_grads(),
        DO_STAGE: stage, DO_ACORE: add_core, DO_AY: add_y, DO_AX: add_x, DO_AZ1: add_z1,
        DO_AZ2: add_z2, DO_AZ3: add_z3, DO_FIN: finish, DO_END: end,
    }
    for name, which in SCHEDULE:
        if name != DO_FIRST:
            ready()
        actions[name](which)

    for g, (matrix, columns, width, kind) in enumerate(REDUCE_GROUPS):
        held = sums[matrix].at[:, pl.ds(0, width * len(columns))]
        place = sums_out[matrix].at[1 - c, :, pl.ds(0, width * len(columns))]
        remote(held, place, rs_send.at[W_END, g], rs_end.at[g], to_c).wait_recv()
        pltpu.make_async_copy(held, place, out_sem.at[g]).wait()
    for g, (matrix, columns, width, kind) in enumerate(REDUCE_GROUPS):
        buf = groups[g]

        def leave(kind, ref, g=g):
            remote(ref, ref, rs_send.at[kind, g], rs_end.at[g], to_c).wait_send()

        leave(W_CORE, buf["core"])
        if kind == SPLIT:
            leave(W_Y, buf["y"])
        leave(W_X, buf["x"])
        leave(W_Z3, buf["z3"])
        leave(W_LAST, buf["last"].at[:, 0])
        leave(W_END, sums[matrix].at[:, pl.ds(0, width * len(columns))])

        leave(W_Z1, buf["z1"])


def unpack_kernel(result, delta, s_in, s_out, s_con, s_exp, s_small, *outs):
    (
        o_result, o_delta, o_first_gain, o_first_shift, o_in, o_in_bias, o_short_w, o_short_b,
        o_inner_w, o_inner_b, o_scale, o_middle_w, o_middle_b, o_filter_w, o_direct, o_out,
        o_out_bias, o_second_gain, o_second_shift, o_exp, o_exp_bias, o_con, o_con_bias,
    ) = outs
    o_result[...] = result[...]
    o_delta[...] = delta[...]
    for source, target in ((s_in, o_in), (s_out, o_out), (s_con, o_con), (s_exp, o_exp)):
        height = source.shape[1]
        for half in range(2):
            target[half * height : half * height + height, :] = source[half]
    for row, target in enumerate(
        (o_first_gain, o_first_shift, o_direct, o_out_bias, o_second_gain, o_second_shift, o_con_bias)
    ):
        target[...] = s_small[0, row : row + 1, 0:96].reshape(96)
    wide = jnp.concatenate([s_small[0, 8:16, :], s_small[0, 16:24, :], s_small[0, 24:32, :]], axis=1)
    o_in_bias[...] = wide[0:1, 0:288].reshape(288)
    o_short_b[...] = wide[1:2, 0:288].reshape(288)
    o_short_w[...] = wide[2:5, 0:288]
    o_exp_bias[...] = wide[5:6].reshape(384)
    for row, target in enumerate((o_inner_b, o_scale, o_middle_b)):
        target[...] = s_small[0, 32 + row : 33 + row, 0:8].reshape(8)
    o_inner_w[...] = s_small[0, 48:56, 0:33]
    o_middle_w[...] = s_small[0, 40:48, 0:64]
    o_filter_w[...] = s_small[1, :, 0:96]


def filter_constants(length, width):
    places = np.arange(LAGS, dtype=np.float64)
    scales = 0.0001 + np.arange(16, dtype=np.float64) * ((15.0 - 0.0001) / 15.0)
    phases = (2.0 * math.pi * places / length)[:, None] * scales[None, :]
    ramp = places / (length - 1)
    table = np.zeros((LAGS, 128), np.float32)
    table[:, 0] = ramp
    table[:, 1:17] = np.cos(phases)
    table[:, 17:33] = -np.sin(phases)
    rates = math.log(100.0) * (
        1.0 / 1.5 + (1.0 / 0.3 - 1.0 / 1.5) * np.arange(width, dtype=np.float64) / (width - 1)
    )
    return table, np.exp(-ramp[:, None] * rates[None, :]).astype(np.float32)


def block_device(
    tokens, segment_ids, cotangent, first_gain, first_shift, input_weight, input_bias,
    short_weight, short_bias, inner_weight, inner_bias, sine_scale, middle_weight, middle_bias,
    filter_weight, direct_gain, output_weight, output_bias, second_gain, second_shift,
    expand_weight, expand_bias, contract_weight, contract_bias,
):
    blocks, _, length, width = tokens.shape
    rows = blocks * length
    features, decay = filter_constants(length, width)

    small_members = (
        first_gain, first_shift, input_bias, short_weight, short_bias, inner_weight, inner_bias,
        sine_scale, middle_weight, middle_bias, filter_weight, direct_gain, output_bias,
        second_gain, second_shift, expand_bias, contract_bias,
    )

    def halved(member):
        return member.reshape(2, member.shape[0] // 2, member.shape[1])

    shards = [halved(m) for m in (input_weight, output_weight, contract_weight, expand_weight)]
    inputs = (
        tokens.reshape(rows, width), segment_ids.reshape(blocks, length),
        cotangent.reshape(rows, width),
    ) + tuple(m.T if m is inner_weight else m for m in small_members) + tuple(shards) + (
        jnp.asarray(features), jnp.asarray(decay),
    )
    shapes = [m.shape[1:] for m in shards] + [(SMALL_ROWS, 128)]
    outs = [
        jax.ShapeDtypeStruct((rows, width), LOW),
        jax.ShapeDtypeStruct((rows, width), FULL),
    ] + [jax.ShapeDtypeStruct((2,) + s, FULL) for s in shapes]
    count = len(GATHER_CHUNKS)
    crossing = sum(1 for chunk in GATHER_CHUNKS if chunk[3] == SPLIT)
    leaving = len({chunk[:1] if chunk[0] != 3 else chunk[:2] for chunk in GATHER_CHUNKS})
    vm = pltpu.VMEM
    scratch = [vm((rows, width), kind) for kind in (LOW, LOW, LOW, FULL)]
    scratch += [vm(s, FULL) for s in shapes]
    scratch += [vm((4, 2, 2) + s, LOW) for s in shapes]
    scratch += [
        vm((4, 2, 2) + shapes[0], LOW), vm((4, 2, 2) + shapes[1], LOW),
        vm((4, 2, 2) + shapes[4], FULL), vm((2, SMALL_ROWS, 128), LOW),
        vm((2 * SMALL_ROWS, 128), FULL),
        vm((8, width), FULL), vm((8, 3 * width), FULL), vm((1, 4 * width), FULL), vm((8, 128), FULL),
        vm((128, 128), FULL), vm((128, width), FULL), vm((LAGS, width), FULL), vm((LAGS, width), FULL),
    ]
    scratch += [vm((LAGS, 128), FULL)] * 6
    scratch += [vm((rows, 128), jnp.int32)] * 2
    scratch += [
        vm((rows, width), LOW), vm((3, rows, width), FULL), vm((3, rows, width), FULL),
        vm((rows, width), FULL), vm((rows, width), LOW), vm((rows, width), FULL),
        vm((rows, width), LOW),
        vm((rows, 4 * width), FULL), vm((rows, 4 * width), LOW), vm((rows, 4 * width), LOW),
        vm((rows, width), FULL), vm((rows, width), FULL), vm((rows, width), FULL),
        vm((rows, width), LOW), vm((3, rows, width), LOW),
        vm((7, 8, width), FULL), vm((5, 8, 3 * width), FULL), vm((8, 4 * width), FULL),
    ]
    for matrix, columns, span, kind in REDUCE_GROUPS:
        n, high = len(columns), shapes[matrix][0]
        of = FULL if matrix == 4 else LOW
        v = span // 2 if kind == SPLIT else span
        side_planes, line_planes = ((), (2,)) if kind == LINE else ((4,), ())
        scratch += [
            vm((n, 4, 2, high, span), of), vm((n,) + side_planes + (high, v), of),
            vm((n, 2) + line_planes + (high, v), of), vm((n, 2) + line_planes + (high, v), of),
            vm((n,) + line_planes + (high, v), of), vm((n, 2, high, v), of),
        ]
        if kind == SPLIT:
            scratch.append(vm((n, 4, 2, high, v), of))
    total = len(REDUCE_ORDER)
    splits = sum(len(g[1]) for g in REDUCE_GROUPS if g[3] == SPLIT)
    dma = pltpu.SemaphoreType.DMA
    scratch += [
        dma((4, count)), dma((3, crossing)), dma((count,)), dma((6, leaving)), dma((9,)),
        dma((6, total)), dma((splits,)), dma((7, len(REDUCE_GROUPS))), dma((len(REDUCE_GROUPS),)),
        dma((len(REDUCE_GROUPS),)),
    ]
    in_vmem = pl.BlockSpec(memory_space=pltpu.VMEM)
    anywhere = pl.BlockSpec(memory_space=pl.ANY)
    parts = pl.pallas_call(
        block_kernel,
        out_shape=outs,
        in_specs=[anywhere, in_vmem, anywhere] + [in_vmem] * 17 + [anywhere] * 4 + [in_vmem] * 2,
        out_specs=[anywhere] * len(outs),
        scratch_shapes=scratch,
        compiler_params=pltpu.CompilerParams(
            collective_id=0, has_side_effects=True, vmem_limit_bytes=67043328
        ),
    )(*inputs)
    members = (
        first_gain, first_shift, input_weight, input_bias, short_weight, short_bias, inner_weight,
        inner_bias, sine_scale, middle_weight, middle_bias, filter_weight, direct_gain,
        output_weight, output_bias, second_gain, second_shift, expand_weight, expand_bias,
        contract_weight, contract_bias,
    )
    final = [outs[0], outs[1]] + [
        jax.ShapeDtypeStruct(m.shape[::-1] if m is inner_weight else m.shape, FULL) for m in members
    ]
    done = pl.pallas_call(
        unpack_kernel,
        out_shape=final,
        in_specs=[in_vmem] * 7,
        out_specs=[in_vmem] * len(final),
    )(*parts)
    done = [m.T if n == INNER_OUT else m for n, m in enumerate(done)]
    return (done[0].reshape(tokens.shape), done[1].reshape(tokens.shape)) + tuple(done[2:])


def per_device(
    tokens,
    segment_ids,
    cotangent,
    first_gain,
    first_shift,
    input_weight,
    input_bias,
    short_weight,
    short_bias,
    inner_weight,
    inner_bias,
    sine_scale,
    middle_weight,
    middle_bias,
    filter_weight,
    direct_gain,
    output_weight,
    output_bias,
    second_gain,
    second_shift,
    expand_weight,
    expand_bias,
    contract_weight,
    contract_bias,
):
    micro_count, local_sequences, length, width = tokens.shape
    row_count = local_sequences * length
    tables = wave_tables(length)

    def fetch_mixer():
        return (
            lax.all_gather(first_gain, "shard", axis=0, tiled=True),
            lax.all_gather(first_shift, "shard", axis=0, tiled=True),
            lax.all_gather(input_weight, "shard", axis=0, tiled=True),
            lax.all_gather(input_bias, "shard", axis=0, tiled=True),
            lax.all_gather(short_weight, "shard", axis=1, tiled=True),
            lax.all_gather(short_bias, "shard", axis=0, tiled=True),
            lax.all_gather(inner_weight, "shard", axis=1, tiled=True),
            lax.all_gather(inner_bias, "shard", axis=0, tiled=True),
            lax.all_gather(sine_scale, "shard", axis=0, tiled=True),
            lax.all_gather(middle_weight, "shard", axis=0, tiled=True),
            lax.all_gather(middle_bias, "shard", axis=0, tiled=True),
            lax.all_gather(filter_weight, "shard", axis=1, tiled=True),
            lax.all_gather(direct_gain, "shard", axis=0, tiled=True),
            lax.all_gather(output_weight, "shard", axis=0, tiled=True),
            lax.all_gather(output_bias, "shard", axis=0, tiled=True),
        )

    def fetch_dense():
        return (
            lax.all_gather(second_gain, "shard", axis=0, tiled=True),
            lax.all_gather(second_shift, "shard", axis=0, tiled=True),
            lax.all_gather(expand_weight, "shard", axis=0, tiled=True),
            lax.all_gather(expand_bias, "shard", axis=0, tiled=True),
            lax.all_gather(contract_weight, "shard", axis=0, tiled=True),
            lax.all_gather(contract_bias, "shard", axis=0, tiled=True),
        )

    results = []
    input_deltas = []
    mixer_total = None
    dense_total = None
    for micro_index in range(micro_count):
        mixer_parts = fetch_mixer()
        dense_parts = fetch_dense()
        kernel = filter_taps(
            to_float(mixer_parts[6]),
            to_float(mixer_parts[7]),
            to_float(mixer_parts[8]),
            to_float(mixer_parts[9]),
            to_float(mixer_parts[10]),
            to_float(mixer_parts[11]),
            length,
        )
        kernel, kernel_wave = (kernel, spectrum(tables, kernel))
        kernel_real, kernel_imag = kernel_wave
        segment_block = segment_ids[micro_index]
        membership = (
            segment_block[:, None, :] == jnp.arange(DOCS, dtype=jnp.int32)[None, :, None]
        ).astype(jnp.float32)
        flat_tokens = tokens[micro_index].reshape(row_count, width).astype(jnp.float32)
        normed_first = normalize(
            flat_tokens, to_float(mixer_parts[0]), to_float(mixer_parts[1])
        ).astype(jnp.bfloat16)
        projected = jnp.dot(
            normed_first, mixer_parts[2], preferred_element_type=jnp.float32
        ) + to_float(mixer_parts[3])
        projected_rows = projected.reshape(local_sequences, length, 3 * width)
        short_out = short_filter(
            projected_rows, segment_block, to_float(mixer_parts[4]), to_float(mixer_parts[5])
        )
        gate_out = short_out[:, :, :width]
        gate_in = short_out[:, :, width : 2 * width]
        values = short_out[:, :, 2 * width :]
        carried = values * gate_in
        direct = to_float(mixer_parts[12])
        carried_real, carried_imag = spectrum(tables, carried[:, None] * membership[:, :, :, None])
        conv_pieces = inverse(
            tables,
            carried_real * kernel_real - carried_imag * kernel_imag,
            carried_real * kernel_imag + carried_imag * kernel_real,
        )
        convolved = jnp.sum(conv_pieces * membership[:, :, :, None], axis=1) + direct * carried
        gated_low = (convolved * gate_out).astype(jnp.bfloat16).reshape(row_count, width)
        mixed_out = jnp.dot(
            gated_low, mixer_parts[13], preferred_element_type=jnp.float32
        ) + to_float(mixer_parts[14])
        residual = flat_tokens + mixed_out
        second_gain_f = to_float(dense_parts[0])
        second_shift_f = to_float(dense_parts[1])
        normed_second = normalize(residual, second_gain_f, second_shift_f).astype(jnp.bfloat16)
        hidden_pre = jnp.dot(
            normed_second, dense_parts[2], preferred_element_type=jnp.float32
        ) + to_float(dense_parts[3])
        hidden_post = smooth_gate(hidden_pre).astype(jnp.bfloat16)
        result = (
            residual
            + jnp.dot(hidden_post, dense_parts[4], preferred_element_type=jnp.float32)
            + to_float(dense_parts[5])
        )
        results.append(result.astype(jnp.bfloat16).reshape(local_sequences, length, width))
        back_mixer = fetch_mixer()
        back_dense = fetch_dense()
        upstream = cotangent[micro_index].reshape(row_count, width)
        upstream_float = upstream.astype(jnp.float32)
        delta_contract_weight = jnp.einsum(
            "tf,td->fd", hidden_post, upstream, preferred_element_type=jnp.float32
        )
        delta_contract_bias = jnp.sum(upstream_float, axis=0)
        back_hidden = jnp.einsum(
            "td,fd->tf", upstream, back_dense[4], preferred_element_type=jnp.float32
        )
        back_pre = jax.vjp(smooth_gate, hidden_pre)[1](back_hidden)[0].astype(jnp.bfloat16)
        delta_expand_weight = jnp.einsum(
            "td,tf->df", normed_second, back_pre, preferred_element_type=jnp.float32
        )
        delta_expand_bias = jnp.sum(back_pre.astype(jnp.float32), axis=0)
        back_second = jnp.einsum(
            "tf,df->td", back_pre, back_dense[2], preferred_element_type=jnp.float32
        )
        second_pull = jax.vjp(
            normalize, residual, to_float(back_dense[0]), to_float(back_dense[1])
        )[1]
        back_norm_second, delta_second_gain, delta_second_shift = second_pull(back_second)
        back_residual = upstream_float + back_norm_second
        back_mixed = back_residual.astype(jnp.bfloat16)
        delta_output_weight = jnp.einsum(
            "td,te->de", gated_low, back_mixed, preferred_element_type=jnp.float32
        )
        delta_output_bias = jnp.sum(back_mixed.astype(jnp.float32), axis=0)
        back_gated = jnp.einsum(
            "te,de->td", back_mixed, back_mixer[13], preferred_element_type=jnp.float32
        ).reshape(local_sequences, length, width)
        back_conv = back_gated * gate_out
        grad_real, grad_imag = spectrum(tables, back_conv[:, None] * membership[:, :, :, None])
        carried_back_pieces = inverse(
            tables,
            grad_real * kernel_real + grad_imag * kernel_imag,
            grad_imag * kernel_real - grad_real * kernel_imag,
        )
        back_carried = (
            jnp.sum(carried_back_pieces * membership[:, :, :, None], axis=1) + direct * back_conv
        )
        cross_real = jnp.sum(grad_real * carried_real + grad_imag * carried_imag, axis=(0, 1))
        cross_imag = jnp.sum(grad_imag * carried_real - grad_real * carried_imag, axis=(0, 1))
        back_kernel = inverse(tables, cross_real, cross_imag)
        delta_direct = jnp.sum(back_conv * carried, axis=(0, 1))
        back_short = jnp.concatenate(
            [back_gated * convolved, back_carried * values, back_carried * gate_in], axis=2
        )
        short_pull = jax.vjp(
            lambda rows_in, taps_in, offset_in: short_filter(
                rows_in, segment_block, taps_in, offset_in
            ),
            projected_rows,
            to_float(back_mixer[4]),
            to_float(back_mixer[5]),
        )[1]
        back_projected, delta_short_weight, delta_short_bias = short_pull(back_short)
        back_projected = back_projected.reshape(row_count, 3 * width).astype(jnp.bfloat16)
        delta_input_weight = jnp.einsum(
            "td,tp->dp", normed_first, back_projected, preferred_element_type=jnp.float32
        )
        delta_input_bias = jnp.sum(back_projected.astype(jnp.float32), axis=0)
        back_first = jnp.einsum(
            "tp,dp->td", back_projected, back_mixer[2], preferred_element_type=jnp.float32
        )
        first_pull = jax.vjp(
            normalize, flat_tokens, to_float(back_mixer[0]), to_float(back_mixer[1])
        )[1]
        back_norm_first, delta_first_gain, delta_first_shift = first_pull(back_first)
        input_deltas.append(
            (back_residual + back_norm_first).reshape(local_sequences, length, width)
        )
        filter_pull = jax.vjp(
            lambda weight_one, bias_one, scale_all, weight_two, bias_two, weight_three: filter_taps(
                weight_one, bias_one, scale_all, weight_two, bias_two, weight_three, length
            ),
            to_float(back_mixer[6]),
            to_float(back_mixer[7]),
            to_float(back_mixer[8]),
            to_float(back_mixer[9]),
            to_float(back_mixer[10]),
            to_float(back_mixer[11]),
        )[1]
        filter_deltas = filter_pull(back_kernel)
        mixer_part = (
            delta_first_gain,
            delta_first_shift,
            delta_input_weight,
            delta_input_bias,
            delta_short_weight,
            delta_short_bias,
            filter_deltas[0],
            filter_deltas[1],
            filter_deltas[2],
            filter_deltas[3],
            filter_deltas[4],
            filter_deltas[5],
            delta_direct,
            delta_output_weight,
            delta_output_bias,
        )
        dense_part = (
            delta_second_gain,
            delta_second_shift,
            delta_expand_weight,
            delta_expand_bias,
            delta_contract_weight,
            delta_contract_bias,
        )
        if micro_index == 0:
            mixer_total = mixer_part
            dense_total = dense_part
        else:
            mixer_total = jax.tree.map(jnp.add, mixer_total, mixer_part)
            dense_total = jax.tree.map(jnp.add, dense_total, dense_part)
    dense_total = (
        lax.psum_scatter(dense_total[0], "shard", scatter_dimension=0, tiled=True),
        lax.psum_scatter(dense_total[1], "shard", scatter_dimension=0, tiled=True),
        lax.psum_scatter(dense_total[2], "shard", scatter_dimension=0, tiled=True),
        lax.psum_scatter(dense_total[3], "shard", scatter_dimension=0, tiled=True),
        lax.psum_scatter(dense_total[4], "shard", scatter_dimension=0, tiled=True),
        lax.psum_scatter(dense_total[5], "shard", scatter_dimension=0, tiled=True),
    )
    mixer_total = (
        lax.psum_scatter(mixer_total[0], "shard", scatter_dimension=0, tiled=True),
        lax.psum_scatter(mixer_total[1], "shard", scatter_dimension=0, tiled=True),
        lax.psum_scatter(mixer_total[2], "shard", scatter_dimension=0, tiled=True),
        lax.psum_scatter(mixer_total[3], "shard", scatter_dimension=0, tiled=True),
        lax.psum_scatter(mixer_total[4], "shard", scatter_dimension=1, tiled=True),
        lax.psum_scatter(mixer_total[5], "shard", scatter_dimension=0, tiled=True),
        lax.psum_scatter(mixer_total[6], "shard", scatter_dimension=1, tiled=True),
        lax.psum_scatter(mixer_total[7], "shard", scatter_dimension=0, tiled=True),
        lax.psum_scatter(mixer_total[8], "shard", scatter_dimension=0, tiled=True),
        lax.psum_scatter(mixer_total[9], "shard", scatter_dimension=0, tiled=True),
        lax.psum_scatter(mixer_total[10], "shard", scatter_dimension=0, tiled=True),
        lax.psum_scatter(mixer_total[11], "shard", scatter_dimension=1, tiled=True),
        lax.psum_scatter(mixer_total[12], "shard", scatter_dimension=0, tiled=True),
        lax.psum_scatter(mixer_total[13], "shard", scatter_dimension=0, tiled=True),
        lax.psum_scatter(mixer_total[14], "shard", scatter_dimension=0, tiled=True),
    )
    summed = lax.psum(
        (
            mixer_total[0],
            mixer_total[1],
            mixer_total[2],
            mixer_total[3],
            mixer_total[4],
            mixer_total[5],
            mixer_total[6],
            mixer_total[7],
            mixer_total[8],
            mixer_total[9],
            mixer_total[10],
            mixer_total[11],
            mixer_total[12],
            mixer_total[13],
            mixer_total[14],
            dense_total[0],
            dense_total[1],
            dense_total[2],
            dense_total[3],
            dense_total[4],
            dense_total[5],
        ),
        "rep",
    )
    return (jnp.stack(results), jnp.stack(input_deltas)) + tuple(summed)


def solution(mesh):
    placed = (
        P(None, ("rep", "shard"), None, None),
        P(None, ("rep", "shard"), None),
        P(None, ("rep", "shard"), None, None),
        P("shard"),
        P("shard"),
        P("shard", None),
        P("shard"),
        P(None, "shard"),
        P("shard"),
        P(None, "shard"),
        P("shard"),
        P("shard"),
        P("shard", None),
        P("shard"),
        P(None, "shard"),
        P("shard"),
        P("shard", None),
        P("shard"),
        P("shard"),
        P("shard"),
        P("shard", None),
        P("shard"),
        P("shard", None),
        P("shard"),
    )
    blocked = dict(mesh.shape) == {"rep": 4, "shard": 8}
    return jax.shard_map(
        block_device if blocked else per_device,
        mesh=mesh,
        in_specs=placed,
        out_specs=(
            P(None, ("rep", "shard"), None, None),
            P(None, ("rep", "shard"), None, None),
            P("shard"),
            P("shard"),
            P("shard", None),
            P("shard"),
            P(None, "shard"),
            P("shard"),
            P(None, "shard"),
            P("shard"),
            P("shard"),
            P("shard", None),
            P("shard"),
            P(None, "shard"),
            P("shard"),
            P("shard", None),
            P("shard"),
            P("shard"),
            P("shard"),
            P("shard", None),
            P("shard"),
            P("shard", None),
            P("shard"),
        ),
        check_vma=False,
    )
```

```python
import math

import jax
import jax.numpy as jnp
import numpy as np
from jax import lax
from jax.experimental import pallas as pl
from jax.experimental.pallas import tpu as pltpu
from jax.sharding import PartitionSpec as P

DOCS = 6


EPSILON = 1e-05
HIGHEST = lax.Precision.HIGHEST


def positions(length):
    places = jnp.arange(length, dtype=jnp.float32)
    linear_ramp = places / (length - 1)
    angles = 2.0 * math.pi * places / length
    scales = 0.0001 + jnp.arange(16, dtype=jnp.float32) * ((15.0 - 0.0001) / 15.0)
    phases = angles[:, None] * scales[None, :]
    return jnp.concatenate([linear_ramp[:, None], jnp.cos(phases), -jnp.sin(phases)], axis=1)


def decay_table(length, width):
    linear_ramp = jnp.arange(length, dtype=jnp.float32) / (length - 1)
    rates = math.log(100.0) * (
        1.0 / 1.5 + (1.0 / 0.3 - 1.0 / 1.5) * jnp.arange(width, dtype=jnp.float32) / (width - 1)
    )
    return jnp.exp(-linear_ramp[:, None] * rates[None, :])


def filter_taps(
    inner_weight, inner_bias, sine_scale, middle_weight, middle_bias, filter_weight, length
):
    features = positions(length)
    first_sine = jnp.sin(
        sine_scale * (jnp.dot(features, inner_weight, precision=HIGHEST) + inner_bias)
    )
    second_sine = jnp.sin(
        sine_scale * (jnp.dot(first_sine, middle_weight, precision=HIGHEST) + middle_bias)
    )
    return jnp.dot(second_sine, filter_weight, precision=HIGHEST) * decay_table(
        length, filter_weight.shape[1]
    )


def normalize(values, gain_row, shift_row):
    center = values - jnp.mean(values, axis=-1, keepdims=True)
    spread = jnp.mean(center * center, axis=-1, keepdims=True)
    return center * lax.rsqrt(spread + EPSILON) * gain_row + shift_row


def smooth_gate(values):
    return jax.nn.gelu(values, approximate=True)


def to_float(member):
    return member.astype(jnp.float32)


def short_filter(projected, segments, weight, offset):
    running = offset + weight[0] * projected
    for step_back in (1, 2):
        moved_rows = jnp.concatenate(
            [jnp.zeros_like(projected[:, :step_back]), projected[:, :-step_back]], axis=1
        )
        moved_ids = jnp.concatenate(
            [jnp.full_like(segments[:, :step_back], -1), segments[:, :-step_back]], axis=1
        )
        same_doc = (moved_ids == segments).astype(projected.dtype)
        running = running + weight[step_back] * moved_rows * same_doc[:, :, None]
    return running


def wave_tables(length):
    padded_size = 2 * length
    freq_index = jnp.arange(length + 1, dtype=jnp.int32)
    place_index = jnp.arange(length, dtype=jnp.int32)
    wrapped = freq_index[:, None] * place_index[None, :] % padded_size
    angles = 2.0 * math.pi / padded_size * wrapped.astype(jnp.float32)
    weights_row = (
        jnp.where((freq_index == 0) | (freq_index == length), 1.0, 2.0).astype(jnp.float32)
        / padded_size
    )
    return (jnp.cos(angles), jnp.sin(angles), weights_row)


def spectrum(tables, signal):
    cosine, sine, weights_row = tables
    real_part = jnp.einsum("ft,...td->...fd", cosine, signal, precision=HIGHEST)
    imag_part = -jnp.einsum("ft,...td->...fd", sine, signal, precision=HIGHEST)
    return (real_part, imag_part)


def inverse(tables, real_part, imag_part):
    cosine, sine, weights_row = tables
    scaled_real = real_part * weights_row[:, None]
    scaled_imag = imag_part * weights_row[:, None]
    return jnp.einsum("ft,...fd->...td", cosine, scaled_real, precision=HIGHEST) - jnp.einsum(
        "ft,...fd->...td", sine, scaled_imag, precision=HIGHEST
    )


MESH_ID = pl.DeviceIdType.MESH
LAGS = 64
LOW = jnp.bfloat16
FULL = jnp.float32
WHOLE, SPLIT, LINE, WHOLE_FAR, SPLIT_FAR = range(5)
SPLITS = (SPLIT, SPLIT_FAR)
FARS = (WHOLE_FAR, SPLIT_FAR)
GATHER_CHUNKS = (
    (4, 0, 128, WHOLE),
    (0, 768, 768, SPLIT),
    (0, 1536, 768, SPLIT),
    (0, 0, 768, SPLIT),
    (1, 0, 768, SPLIT),
    (3, 0, 768, SPLIT),
    (3, 768, 768, WHOLE),
    (3, 1536, 768, SPLIT),
    (3, 2304, 768, WHOLE),
    (2, 0, 256, SPLIT),
    (2, 256, 256, LINE),
    (2, 512, 256, WHOLE),
)
REDUCE_GROUPS = (
    (2, (0,), 256, LINE),
    (2, (256,), 256, SPLIT),
    (2, (512,), 256, WHOLE),
    (3, (0, 1536), 768, SPLIT),
    (3, (768, 2304), 768, WHOLE),
    (1, (0,), 768, SPLIT),
    (0, (0, 768, 1536), 512, SPLIT_FAR),
    (0, (512, 1280, 2048), 256, WHOLE),
    (4, (0,), 128, WHOLE_FAR),
)
REDUCE_ORDER = (
    (0, 0), (1, 0), (2, 0), (3, 0), (4, 0), (3, 1), (4, 1), (5, 0), (6, 0), (7, 0), (6, 1), (7, 1), (6, 2), (7, 2), (8, 0),
)
(
    DO_FIRST, DO_NEAR, DO_FAR, DO_SIDE, DO_CROSS, DO_PLACES, DO_UNPACK, DO_NORM1,
    DO_PROJECT, DO_CONV, DO_MIX, DO_EXPAND, DO_BEND, DO_FEED, DO_DRAIN, DO_GCON,
    DO_GEXP, DO_NORM2B, DO_BACKG, DO_GOUT, DO_CONVB, DO_GIN, DO_BFIRST, DO_NORM1B,
    DO_SMALL, DO_STAGE, DO_ACORE, DO_AY, DO_AX, DO_AZ1, DO_AZ2, DO_AZ3,
    DO_FIN, DO_END,
) = range(34)
SCHEDULE = (
    (DO_FIRST, 0), (DO_FIRST, 1), (DO_FIRST, 2), (DO_FIRST, 10), (DO_FIRST, 3), (DO_NEAR, 0),
    (DO_FIRST, 4), (DO_FIRST, 5), (DO_FIRST, 6), (DO_FIRST, 7), (DO_FIRST, 8), (DO_NEAR, 1),
    (DO_PLACES, 0), (DO_NEAR, 2), (DO_NEAR, 3), (DO_FAR, 0), (DO_NEAR, 4), (DO_FAR, 1), (DO_FAR, 2),
    (DO_FAR, 3), (DO_FAR, 4), (DO_NEAR, 10), (DO_NEAR, 5), (DO_SIDE, 1), (DO_NEAR, 8), (DO_SIDE, 0),
    (DO_UNPACK, 0), (DO_SIDE, 2), (DO_NORM1, 0), (DO_SIDE, 4), (DO_FIRST, 9), (DO_NEAR, 7),
    (DO_FIRST, 11), (DO_CROSS, 1), (DO_PROJECT, 1), (DO_SIDE, 3), (DO_FAR, 5), (DO_FAR, 7),
    (DO_CROSS, 2), (DO_FAR, 8), (DO_NEAR, 6), (DO_PROJECT, 2), (DO_CONV, 0), (DO_CONV, 1),
    (DO_FAR, 6), (DO_CROSS, 4), (DO_SIDE, 7), (DO_NEAR, 11), (DO_CROSS, 3), (DO_SIDE, 5),
    (DO_CONV, 2), (DO_CONV, 3), (DO_SIDE, 8), (DO_NEAR, 9), (DO_PROJECT, 0), (DO_FAR, 10),
    (DO_MIX, 0), (DO_CROSS, 7), (DO_EXPAND, 3), (DO_BEND, 3), (DO_SIDE, 6), (DO_FAR, 9),
    (DO_EXPAND, 2), (DO_BEND, 2), (DO_CROSS, 5), (DO_EXPAND, 1), (DO_BEND, 1), (DO_FAR, 11),
    (DO_EXPAND, 0), (DO_BEND, 0), (DO_GCON, 0), (DO_STAGE, (2, 0)), (DO_STAGE, (0, 0)),
    (DO_SIDE, 9), (DO_STAGE, (1, 0)), (DO_SIDE, 10), (DO_SIDE, 11), (DO_ACORE, (0, 0)),
    (DO_ACORE, (1, 0)), (DO_CROSS, 9), (DO_ACORE, (2, 0)), (DO_FEED, 0), (DO_FEED, 1), (DO_GEXP, 0),
    (DO_STAGE, (3, 0)), (DO_GEXP, 1), (DO_STAGE, (4, 0)), (DO_FEED, 2), (DO_GEXP, 2),
    (DO_STAGE, (3, 1)), (DO_ACORE, (4, 0)), (DO_ACORE, (3, 0)), (DO_FEED, 3), (DO_GEXP, 3),
    (DO_DRAIN, 0), (DO_STAGE, (4, 1)), (DO_AX, (2, 0)), (DO_NORM2B, 0), (DO_BACKG, 0), (DO_GOUT, 0),
    (DO_STAGE, (5, 0)), (DO_ACORE, (3, 1)), (DO_ACORE, (4, 1)), (DO_AZ1, (0, 0)), (DO_CONVB, 0),
    (DO_AX, (4, 0)), (DO_ACORE, (5, 0)), (DO_AY, (1, 0)), (DO_CONVB, 1), (DO_AY, (3, 1)),
    (DO_AY, (3, 0)), (DO_AX, (4, 1)), (DO_AZ1, (2, 0)), (DO_CONVB, 2), (DO_CONVB, 3),
    (DO_AX, (1, 0)), (DO_AY, (5, 0)), (DO_AZ2, (2, 0)), (DO_AZ3, (2, 0)), (DO_GIN, 1),
    (DO_STAGE, (6, 1)), (DO_AZ2, (0, 0)), (DO_AZ3, (0, 0)), (DO_AX, (3, 1)), (DO_ACORE, (6, 1)),
    (DO_STAGE, (7, 1)), (DO_GIN, 2), (DO_STAGE, (6, 2)), (DO_STAGE, (7, 2)), (DO_AZ1, (4, 0)),
    (DO_ACORE, (7, 1)), (DO_GIN, 0), (DO_AZ1, (4, 1)), (DO_STAGE, (7, 0)), (DO_STAGE, (6, 0)),
    (DO_AX, (3, 0)), (DO_AX, (5, 0)), (DO_ACORE, (6, 2)), (DO_ACORE, (7, 2)), (DO_ACORE, (7, 0)),
    (DO_ACORE, (6, 0)), (DO_BFIRST, 0), (DO_AX, (7, 1)), (DO_AZ1, (1, 0)), (DO_AY, (6, 1)),
    (DO_NORM1B, 0), (DO_SMALL, 0), (DO_STAGE, (8, 0)), (DO_AZ1, (3, 1)), (DO_AX, (7, 2)),
    (DO_AZ2, (4, 0)), (DO_ACORE, (8, 0)), (DO_AY, (6, 2)), (DO_AX, (0, 0)), (DO_AX, (7, 0)),
    (DO_AZ1, (3, 0)), (DO_AZ2, (3, 1)), (DO_AZ2, (4, 1)), (DO_AZ3, (3, 1)), (DO_AZ3, (4, 1)),
    (DO_AX, (6, 1)), (DO_AZ1, (5, 0)), (DO_AZ1, (7, 1)), (DO_AY, (6, 0)), (DO_AZ2, (3, 0)),
    (DO_AZ3, (3, 0)), (DO_AZ2, (1, 0)), (DO_AZ3, (1, 0)), (DO_AX, (8, 0)), (DO_AZ1, (7, 2)),
    (DO_AZ2, (7, 1)), (DO_AZ1, (7, 0)), (DO_AX, (6, 2)), (DO_AZ3, (4, 0)), (DO_AZ2, (5, 0)),
    (DO_AZ3, (5, 0)), (DO_FIN, (0, 0)), (DO_AX, (6, 0)), (DO_AZ3, (6, 1)), (DO_AZ3, (7, 1)),
    (DO_AZ3, (8, 0)), (DO_AZ2, (7, 2)), (DO_FIN, (4, 0)), (DO_AZ2, (7, 0)), (DO_FIN, (3, 0)),
    (DO_AZ3, (6, 2)), (DO_FIN, (4, 1)), (DO_FIN, (3, 1)), (DO_AZ3, (7, 2)), (DO_AZ3, (7, 0)),
    (DO_FIN, (6, 1)), (DO_AZ3, (6, 0)), (DO_FIN, (7, 1)), (DO_FIN, (1, 0)), (DO_FIN, (2, 0)),
    (DO_FIN, (6, 2)), (DO_FIN, (5, 0)), (DO_FIN, (8, 0)), (DO_FIN, (7, 0)), (DO_FIN, (7, 2)),
    (DO_FIN, (6, 0)), (DO_END, 0),
)
SMALL_ROWS = 64
HALF = 48
NORM_ROWS = 128
INNER_OUT = 8


def dot_nn(left_side, right_side):
    return jnp.dot(left_side, right_side, preferred_element_type=FULL)


def dot_nt(left_side, right_side):
    return lax.dot_general(
        left_side, right_side, (((1,), (1,)), ((), ())), preferred_element_type=FULL
    )


def dot_tn(left_side, right_side):
    return lax.dot_general(
        left_side, right_side, (((0,), (0,)), ((), ())), preferred_element_type=FULL
    )


def exact(left_side, right_side, contract):
    return lax.dot_general(
        left_side, right_side, (((contract[0],), (contract[1],)), ((), ())),
        preferred_element_type=FULL, precision=HIGHEST,
    )


def fold8(values):
    rows, columns = values.shape
    return jnp.sum(values.reshape(rows // 8, 8, columns), axis=0)


def widen(values, width):
    rows, columns = values.shape
    if columns == width:
        return values
    return jnp.concatenate([values, jnp.zeros((rows, width - columns), values.dtype)], axis=1)


def turn(values, amount, axis):
    size = values.shape[axis]
    amount = amount % size
    return values if amount == 0 else pltpu.roll(values, amount, axis)


def block_kernel(*refs):
    refs = list(refs)

    def take(number):
        taken = refs[:number]
        del refs[:number]
        return taken

    tokens_in, segs, cot_in = take(3)
    (
        r_first_gain, r_first_shift, r_in_bias, r_short_w, r_short_b, r_inner_w, r_inner_b,
        r_scale, r_middle_w, r_middle_b, r_filter_w, r_direct, r_out_bias, r_second_gain,
        r_second_shift, r_exp_bias, r_con_bias,
    ) = take(17)
    own = take(4)
    features, decay = take(2)
    result_out, delta_out = take(2)
    sums_out = take(5)
    tokens, cot, result, delta = take(4)
    sums = take(5)
    full = take(5)
    g_con, g_small, own_small, pack = take(4)
    v96, v288, vexp, v8 = take(4)
    mid_w, fil_w, taps, d_taps = take(4)
    s_inner1, s_first, s_cos1, s_inner2, s_second, s_cos2 = take(6)
    places, left = take(2)
    normed1, proj, short, conv, gated, resid, normed2 = take(7)
    hidden, post, pre, back_h, gather_out, back_s, back_m, bp = take(8)
    back_r, back_g = back_h, gather_out
    acc96, acc288, accexp = take(3)
    groups = []
    for matrix, columns, width, kind in REDUCE_GROUPS:
        names = ("core", "x", "z3", "last") if kind in FARS else ("core", "x", "z1", "z2", "z3", "last")
        names += ("y",) if kind in SPLITS else ()
        groups.append(dict(zip(names, take(len(names)))))
    ag_recv, ag_cross, ag_core, ag_send, own_sem, rs_recv, rs_y, rs_send, rs_end, out_sem = take(10)
    assert not refs

    own = list(own) + [own_small]
    grads = (full[2], full[2], g_con, full[3], g_small)

    def spot(m, column, width):
        if m in (0, 1):
            block = column // 768 if m == 0 else 3
            assert column % 768 + width <= 768
            return pl.ds(block * HALF, HALF), pl.ds(column % 768, width)
        return slice(None), pl.ds(column, width)

    rep = lax.axis_index("rep")
    shard = lax.axis_index("shard")
    y, c = rep // 2, rep % 2
    z, x = shard // 2, shard % 2
    pair = z // 2
    near_z = z + 1 - 2 * (z % 2)
    inner = ((z + 1) // 2) % 2 == 1
    to_near = (rep, near_z * 2 + x)
    to_mirror = (rep, (3 - z) * 2 + x)
    to_x = (rep, z * 2 + 1 - x)
    to_y = ((1 - y) * 2 + c, shard)
    to_c = (y * 2 + 1 - c, shard)
    own_pair = pl.ds(pair * 2, 2)
    other_pair = pl.ds((1 - pair) * 2, 2)

    loads = [
        pltpu.make_async_copy(own[m].at[c], full[m].at[z, x, c], own_sem.at[m]) for m in range(4)
    ] + [
        pltpu.make_async_copy(tokens_in, tokens, own_sem.at[5]),
        pltpu.make_async_copy(cot_in, cot, own_sem.at[6]),
    ]
    barrier = pltpu.get_barrier_semaphore()
    for target in (to_near, to_x, to_y, to_c):
        pl.semaphore_signal(barrier, inc=1, device_id=target, device_id_type=MESH_ID)

    @pl.when(inner)
    def _():
        pl.semaphore_signal(barrier, inc=1, device_id=to_mirror, device_id_type=MESH_ID)

    for load in loads:
        load.start()

    def remote(source, landing, send, recv, device):
        return pltpu.make_async_remote_copy(
            src_ref=source, dst_ref=landing, send_sem=send, recv_sem=recv,
            device_id=device, device_id_type=MESH_ID,
        )

    pack[...] = jnp.zeros_like(pack)
    for row, member in enumerate(
        (r_first_gain, r_first_shift, r_direct, r_out_bias, r_second_gain, r_second_shift, r_con_bias)
    ):
        pack[row : row + 1, 0:96] = member[...].astype(FULL).reshape(1, 96)
    in_bias, short_b = (m[...].astype(FULL).reshape(1, 288) for m in (r_in_bias, r_short_b))
    exp_bias = r_exp_bias[...].astype(FULL).reshape(1, 384)
    for block in range(3):
        lanes = 128 if block < 2 else 32
        span = slice(block * 128, block * 128 + lanes)
        top = 8 + block * 8
        pack[top : top + 1, 0:lanes] = in_bias[:, span]
        pack[top + 1 : top + 2, 0:lanes] = short_b[:, span]
        pack[top + 2 : top + 5, 0:lanes] = r_short_w[:, span].astype(FULL)
        pack[top + 5 : top + 6, :] = exp_bias[:, block * 128 : block * 128 + 128]
    for row, member in enumerate((r_inner_b, r_scale, r_middle_b)):
        pack[32 + row : 33 + row, 0:8] = member[...].astype(FULL).reshape(1, 8)
    pack[40:48, 0:64] = r_middle_w[...].astype(FULL)
    pack[48:56, 0:33] = r_inner_w[...].astype(FULL)
    pack[64:128, 0:96] = r_filter_w[...].astype(FULL)
    own_small[0] = pack[0:64, :].astype(LOW)
    own_small[1] = pack[64:128, :].astype(LOW)

    acc96[...] = jnp.zeros_like(acc96)
    acc288[...] = jnp.zeros_like(acc288)
    accexp[...] = jnp.zeros_like(accexp)
    d_taps[...] = jnp.zeros_like(d_taps)

    pl.semaphore_wait(barrier, 4 + ((z + 1) // 2) % 2)

    chunks = GATHER_CHUNKS
    count = len(chunks)
    cross_index = {}
    for index, chunk in enumerate(chunks):
        if chunk[3] == SPLIT:
            cross_index[index] = len(cross_index)
    NEAR, FAR, SIDE0, SIDE1 = range(4)
    S_NEAR, S_MIRROR, S_BACK, S_SIDE, S_CROSS, S_CORE = range(6)

    def part(chunk, quarter):
        matrix, column, width, kind = chunk
        if kind == SPLIT:
            return pl.ds(pl.multiple_of(column + quarter * (width // 2), 128), width // 2)
        return pl.ds(column, width)

    def whole(chunk):
        return pl.ds(chunk[1], chunk[2])

    small_load = pltpu.make_async_copy(own_small.at[c], full[4].at[z, x, c], own_sem.at[4])
    small_load.start()
    loads.append(small_load)

    send_groups = []
    for chunk in chunks:
        key = (chunk[0], chunk[3]) if chunk[0] != 3 else chunk[:2]
        if key not in send_groups:
            send_groups.append(key)

    def group_of(chunk):
        return send_groups.index((chunk[0], chunk[3]) if chunk[0] != 3 else chunk[:2])

    def first(index):
        chunk = chunks[index]
        m, s = chunk[0], group_of(chunk)
        piece = own[m].at[c, :, part(chunk, y)]
        landing = full[m].at[z, x, c, :, part(chunk, y)]
        if chunk[3] == LINE:
            remote(piece, landing, ag_send.at[S_SIDE, s], ag_recv.at[SIDE0, index], to_x).start()
        else:
            remote(piece, landing, ag_send.at[S_NEAR, s], ag_recv.at[NEAR, index], to_near).start()

    def line_near(index):
        chunk = chunks[index]
        m, s = chunk[0], group_of(chunk)
        arrived = full[m].at[z, 1 - x, c, :, whole(chunk)]
        remote(arrived, arrived, ag_send.at[S_SIDE, s], ag_recv.at[SIDE0, index], to_x).wait_recv()
        both = full[m].at[z, :, c, :, whole(chunk)]
        remote(both, both, ag_send.at[S_NEAR, s], ag_recv.at[NEAR, index], to_near).start()

    def line_far(index):
        chunk = chunks[index]
        m, s = chunk[0], group_of(chunk)
        arrived = full[m].at[near_z, :, c, :, whole(chunk)]
        remote(arrived, arrived, ag_send.at[S_NEAR, s], ag_recv.at[NEAR, index], to_near).wait_recv()

        @pl.when(inner)
        def _():
            four = full[m].at[own_pair, :, c, :, whole(chunk)]
            remote(four, four, ag_send.at[S_MIRROR, s], ag_recv.at[FAR, index], to_mirror).start()

    def line_side(index):
        chunk = chunks[index]
        m, s = chunk[0], group_of(chunk)
        four = full[m].at[other_pair, :, c, :, whole(chunk)]
        remote(four, four, ag_send.at[S_MIRROR, s], ag_recv.at[FAR, index], to_near).wait_recv()

        @pl.when(inner)
        def _():
            remote(four, four, ag_send.at[S_BACK, s], ag_recv.at[FAR, index], to_near).start()

        to_core(index)

    def near(index):
        chunk = chunks[index]
        if chunk[3] == LINE:
            return line_near(index)
        m, s = chunk[0], group_of(chunk)
        arrived = full[m].at[near_z, x, c, :, part(chunk, y)]
        remote(arrived, arrived, ag_send.at[S_NEAR, s], ag_recv.at[NEAR, index], to_near).wait_recv()
        both = full[m].at[own_pair, x, c, :, part(chunk, y)]

        @pl.when(inner)
        def _():
            remote(both, both, ag_send.at[S_MIRROR, s], ag_recv.at[FAR, index], to_mirror).start()

        remote(both, both, ag_send.at[S_SIDE, s], ag_recv.at[SIDE0, index], to_x).start()
        if chunk[3] == SPLIT:
            remote(
                arrived, arrived, ag_send.at[S_CROSS, s], ag_cross.at[0, cross_index[index]], to_y
            ).start()

    def far(index):
        chunk = chunks[index]
        if chunk[3] == LINE:
            return line_far(index)
        m, s = chunk[0], group_of(chunk)
        both = full[m].at[other_pair, x, c, :, part(chunk, y)]
        remote(both, both, ag_send.at[S_MIRROR, s], ag_recv.at[FAR, index], to_near).wait_recv()

        @pl.when(inner)
        def _():
            remote(both, both, ag_send.at[S_BACK, s], ag_recv.at[FAR, index], to_near).start()

        remote(both, both, ag_send.at[S_SIDE, s], ag_recv.at[SIDE1, index], to_x).start()
        if chunk[3] == SPLIT:
            remote(
                both, both, ag_send.at[S_CROSS, s], ag_cross.at[1, cross_index[index]], to_y
            ).start()

    def to_core(index):
        chunk = chunks[index]
        m, s = chunk[0], group_of(chunk)
        piece = full[m].at[:, :, c, :, whole(chunk)]
        remote(piece, piece, ag_send.at[S_CORE, s], ag_core.at[index], to_c).start()

    def side(index):
        chunk = chunks[index]
        if chunk[3] == LINE:
            return line_side(index)
        m, s = chunk[0], group_of(chunk)
        for place, slot in ((own_pair, SIDE0), (other_pair, SIDE1)):
            both = full[m].at[place, 1 - x, c, :, part(chunk, y)]
            remote(both, both, ag_send.at[S_SIDE, s], ag_recv.at[slot, index], to_x).wait_recv()
        if chunk[3] == SPLIT:
            column = full[m].at[:, 1 - x, c, :, part(chunk, y)]
            remote(
                column, column, ag_send.at[S_CROSS, s], ag_cross.at[2, cross_index[index]], to_y
            ).start()
        else:
            to_core(index)

    def cross(index):
        chunk = chunks[index]
        m, s = chunk[0], group_of(chunk)
        for slot, piece in enumerate(
            (
                full[m].at[near_z, x, c, :, part(chunk, 1 - y)],
                full[m].at[other_pair, x, c, :, part(chunk, 1 - y)],
                full[m].at[:, 1 - x, c, :, part(chunk, 1 - y)],
            )
        ):
            remote(
                piece, piece, ag_send.at[S_CROSS, s], ag_cross.at[slot, cross_index[index]], to_y
            ).wait_recv()
        to_core(index)

    waited = set()

    def settled(m, low, high):
        for index, chunk in enumerate(chunks):
            inside = chunk[0] == m and chunk[1] < high and chunk[1] + chunk[2] > low
            if inside and index not in waited:
                waited.add(index)
                piece = full[m].at[:, :, 1 - c, :, whole(chunk)]
                send = ag_send.at[S_CORE, group_of(chunk)]
                remote(piece, piece, send, ag_core.at[index], to_c).wait_recv()

    loaded = []

    def ready():
        if not loaded:
            loaded.append(True)
            for load in loads:
                load.wait()


    def row_blocks(size, action):
        def body(step, carry):
            action(pl.ds(pl.multiple_of(step * size, size), size))
            return carry

        lax.fori_loop(0, tokens.shape[0] // size, body, 0)

    def find_places():
        rows = lax.broadcasted_iota(jnp.int32, (128, 128), 0)
        columns = lax.broadcasted_iota(jnp.int32, (128, 128), 1)
        for sequence in range(2):
            ids = jnp.broadcast_to(segs[sequence : sequence + 1, :].astype(FULL), (128, 128))
            same = ids == ids.T
            before = jnp.sum(jnp.where(same & (columns < rows), 1.0, 0.0), axis=1, keepdims=True)
            after = jnp.sum(jnp.where(same & (columns > rows), 1.0, 0.0), axis=1, keepdims=True)
            span = slice(sequence * 128, sequence * 128 + 128)
            places[span, :] = jnp.broadcast_to(before.astype(jnp.int32), (128, 128))
            left[span, :] = jnp.broadcast_to(after.astype(jnp.int32), (128, 128))

    def unpack_small():
        total96 = jnp.zeros((8, 768), FULL)
        total288 = jnp.zeros((8, 2304), FULL)
        total8 = jnp.zeros((8, 128), FULL)
        inner_rows = []
        fil_w[...] = jnp.zeros_like(fil_w)
        mid_w[...] = jnp.zeros_like(mid_w)
        for s in range(8):
            top = full[4][s // 2, s % 2, 0].astype(FULL)
            low = full[4][s // 2, s % 2, 1].astype(FULL)
            total96 = total96 + turn(widen(top[0:8], 768), 96 * s, 1)
            wide = jnp.concatenate([top[8:16], top[16:24], top[24:32]], axis=1)
            vexp[:, s * 384 : s * 384 + 384] = wide[5:6]
            total288 = total288 + turn(widen(wide, 2304), 288 * s, 1)
            total8 = total8 + turn(top[32:40], 8 * s, 1)
            inner_rows.append(top[48:56])
            mid_w[8 * s : 8 * s + 8, :] = top[40:48]
            fil_w[0:64, :] += turn(widen(low, 768), 96 * s, 1)
        v96[...] = total96
        v288[...] = total288
        v8[...] = total8
        scale = total8[1:2]
        inner_all = jnp.concatenate(inner_rows + [jnp.zeros((64, 128), FULL)], axis=0)
        inner1 = exact(features[...], inner_all, (1, 1)) + total8[0:1]
        s_inner1[...] = inner1
        s_first[...] = jnp.sin(scale * inner1)
        s_cos1[...] = jnp.cos(scale * inner1)
        inner2 = exact(s_first[...], mid_w[...], (1, 0)) + total8[2:3]
        s_inner2[...] = inner2
        s_second[...] = jnp.sin(scale * inner2)
        s_cos2[...] = jnp.cos(scale * inner2)
        taps[...] = exact(s_second[...], fil_w[...], (1, 0)) * decay[...]

    def center(values):
        middle = values - jnp.mean(values, axis=-1, keepdims=True)
        spread = jnp.mean(middle * middle, axis=-1, keepdims=True)
        scale = lax.rsqrt(spread + EPSILON)
        return middle * scale, scale

    def norm_first(rows):
        unit, _ = center(tokens[rows, :].astype(FULL))
        normed1[rows, :] = (unit * v96[0:1, :] + v96[1:2, :]).astype(LOW)

    def matrix_of(m, columns, width):
        value = full[m][:, :, :, :, columns]
        return value.reshape(value.shape[0] * value.shape[1] * value.shape[2] * value.shape[3], width)

    def project(k):
        span = slice(k * 768, k * 768 + 768)
        proj[k] = dot_nn(normed1[...], matrix_of(0, pl.ds(k * 768, 768), 768)) + v288[0:1, span]

        def body(step, carry):
            rows = pl.ds(pl.multiple_of((step // 6) * 128, 128), 128)
            lane = pl.multiple_of((step % 6) * 128, 128)
            lanes = pl.ds(lane, 128)
            wide = pl.ds(pl.multiple_of(k * 768 + lane, 128), 128)
            values = proj[k, rows, lanes]
            where = places[rows, :]
            total = v288[1:2, wide] + v288[2:3, wide] * values
            for lag in (1, 2):
                moved = jnp.where(where >= lag, pltpu.roll(values, lag, 0), 0.0)
                total = total + v288[2 + lag : 3 + lag, wide] * moved
            short[k, rows, lanes] = total
            return carry

        lax.fori_loop(0, 12, body, 0)

    def convolve(begin, end):
        def body(step, carry):
            rows = pl.ds(pl.multiple_of((step // 6) * 128, 128), 128)
            lanes = pl.ds(pl.multiple_of((step % 6) * 128, 128), 128)
            carried = short[2, rows, lanes] * short[1, rows, lanes]
            where = places[rows, :]
            total = v96[2:3, lanes] * carried
            for low_lag in range(8):
                moved = turn(carried, low_lag, 0)
                for high in range(LAGS // 8):
                    lag, skip = high * 8 + low_lag, high * 8
                    term = jnp.where(
                        where[skip:] >= lag, taps[lag : lag + 1, lanes] * moved[: 128 - skip], 0.0
                    )
                    if skip:
                        total = jnp.concatenate([total[:skip], total[skip:] + term], axis=0)
                    else:
                        total = total + term
            conv[rows, lanes] = total
            return carry

        lax.fori_loop(begin, end, body, 0)

    def mix_out():
        def gate(rows):
            gated[rows, :] = (conv[rows, :] * short[0, rows, :]).astype(LOW)

        row_blocks(NORM_ROWS, gate)
        resid[...] = dot_nn(gated[...], matrix_of(1, pl.ds(0, 768), 768))

        def finish_rows(rows):
            values = resid[rows, :] + tokens[rows, :].astype(FULL) + v96[3:4, :]
            resid[rows, :] = values
            unit, _ = center(values)
            normed2[rows, :] = (unit * v96[4:5, :] + v96[5:6, :]).astype(LOW)

        row_blocks(NORM_ROWS, finish_rows)

    def expand(k):
        span = slice(k * 768, k * 768 + 768)
        hidden[:, span] = (
            dot_nn(normed2[...], matrix_of(3, pl.ds(k * 768, 768), 768)) + vexp[:, span]
        )

    fed_before = []

    def bend(k):
        span = slice(k * 768, k * 768 + 768)

        def curve(rows):
            values = hidden[rows, span]
            cube = values * values
            grow = math.sqrt(2.0 / math.pi)
            slope = jnp.tanh(grow * (values + 0.044715 * cube * values))
            half_up = 0.5 + 0.5 * slope
            post[rows, span] = (values * half_up).astype(LOW)
            hidden[rows, span] = half_up + (0.5 * values) * (1.0 - slope * slope) * (
                grow * (1.0 + 3.0 * 0.044715 * cube)
            )

        row_blocks(16, curve)

    def feed(k):
        span = slice(k * 768, k * 768 + 768)
        back_h[...] = dot_nt(cot[...], full[2][k].reshape(768, 768))

        def scale_back(rows):
            grad = (back_h[rows, :] * hidden[rows, span]).astype(LOW)
            pre[rows, span] = grad
            accexp[:, span] += fold8(grad.astype(FULL))

        row_blocks(32, scale_back)
        out_part = dot_nn(post[:, span], full[2][k].reshape(768, 768))
        back_part = dot_nt(pre[:, span], matrix_of(3, pl.ds(k * 768, 768), 768))
        if not fed_before:
            gather_out[...] = out_part
            back_s[...] = back_part
            fed_before.append(k)
        else:
            gather_out[...] += out_part
            back_s[...] += back_part

    drained = set()

    def drain(m, low, high):
        for s, key in enumerate(send_groups):
            members = [
                chunk for chunk in chunks
                if group_of(chunk) == s and m == chunk[0]
                and chunk[1] < high and chunk[1] + chunk[2] > low
            ]
            if not members or s in drained:
                continue
            drained.add(s)
            members = [chunk for chunk in chunks if group_of(chunk) == s]
            kind = members[0][3]
            assert all(chunk[3] == kind for chunk in members)
            wide = sum(chunk[2] for chunk in members)
            thin = wide // 2 if kind == SPLIT else wide

            def gone(slot, planes, rows, width=thin, s=s):
                ref = full[m].at[pl.ds(0, planes), pl.ds(0, rows), 0, :, pl.ds(0, width)]
                remote(ref, ref, ag_send.at[slot, s], ag_recv.at[FAR, 0], to_near).wait_send()

            if kind == LINE:
                gone(S_SIDE, 1, 1)
                gone(S_NEAR, 2, 1)
            else:
                gone(S_NEAR, 1, 1)
                gone(S_SIDE, 4, 1)

            @pl.when(inner)
            def _(gone=gone, kind=kind):
                gone(S_MIRROR, 2, 2 if kind == LINE else 1)
                gone(S_BACK, 2, 2 if kind == LINE else 1)

            if kind == SPLIT:
                gone(S_CROSS, 3, 1)
                gone(S_CROSS, 4, 1)
            gone(S_CORE, 4, 2, wide)

    position = {}
    split_position = {}
    for index, key in enumerate(REDUCE_ORDER):
        position[key] = index
        if REDUCE_GROUPS[key[0]][3] in SPLITS:
            split_position[key] = len(split_position)
    R_CORE, R_X, R_Z1, R_Z2, R_Z3, R_LAST = range(6)
    W_CORE, W_Y, W_X, W_Z1, W_Z3, W_LAST, W_END, W_Z4 = range(8)
    W_Z2 = W_Z1

    def info(key):
        g, i = key
        matrix, columns, width, kind = REDUCE_GROUPS[g]
        return g, i, matrix, columns[i], width, kind, groups[g], position[key]

    def halves(width, which):
        return pl.ds(pl.multiple_of(which * (width // 2), 128), width // 2)

    def stage(key):
        g, i, m, column, width, kind, buf, n = info(key)
        high, wide = spot(m, column, width)
        remote(
            grads[m].at[:, :, 1 - c, high, wide], buf["core"].at[i],
            rs_send.at[W_CORE, g], rs_recv.at[R_CORE, n], to_c,
        ).start()

    def running(key):
        g, i, m, column, width, kind, buf, n = info(key)
        return buf["core"] if kind == LINE else buf["x"]

    def send_line(key):
        g, i, m, column, width, kind, buf, n = info(key)
        sums_ref = running(key)
        if kind in FARS:
            for step, sent, slot in ((1, W_Z1, R_Z1), (2, W_Z3, R_Z2), (3, W_Z4, R_Z3)):
                at = (z + step) % 4
                remote(
                    sums_ref.at[i, at], buf["z3"].at[i, step - 1],
                    rs_send.at[sent, g], rs_recv.at[slot, n], (rep, at * 2 + x),
                ).start()
            return

        @pl.when(jnp.logical_not(inner))
        def _():
            remote(
                sums_ref.at[i, other_pair], buf["z1"].at[i],
                rs_send.at[W_Z1, g], rs_recv.at[R_Z1, n], to_near,
            ).start()
            remote(
                sums_ref.at[i, near_z], buf["z3"].at[i],
                rs_send.at[W_Z3, g], rs_recv.at[R_Z3, n], to_near,
            ).start()

    def add_core(key):
        g, i, m, column, width, kind, buf, n = info(key)
        landing = buf["core"].at[i]
        remote(landing, landing, rs_send.at[W_CORE, g], rs_recv.at[R_CORE, n], to_c).wait_recv()
        high, wide = spot(m, column, width)

        def body(step, carry):
            a, b = step // 2, step % 2
            buf["core"][i, a, b] = buf["core"][i, a, b] + grads[m][a, b, c, high, wide]
            return carry

        lax.fori_loop(0, 8, body, 0)
        if kind in SPLITS:
            remote(
                buf["core"].at[i, :, :, :, halves(width, 1 - y)], buf["y"].at[i],
                rs_send.at[W_Y, g], rs_y.at[split_position[key]], to_y,
            ).start()
        elif kind != LINE:
            remote(
                buf["core"].at[i, :, 1 - x], buf["x"].at[i],
                rs_send.at[W_X, g], rs_recv.at[R_X, n], to_x,
            ).start()
        else:
            send_line(key)

    def add_y(key):
        g, i, m, column, width, kind, buf, n = info(key)
        landing = buf["y"].at[i]
        remote(landing, landing, rs_send.at[W_Y, g], rs_y.at[split_position[key]], to_y).wait_recv()

        def body(step, carry):
            a, b = step // 2, step % 2
            buf["y"][i, a, b] = buf["y"][i, a, b] + buf["core"][i, a, b, :, halves(width, y)]
            return carry

        lax.fori_loop(0, 8, body, 0)
        remote(
            buf["y"].at[i, :, 1 - x], buf["x"].at[i], rs_send.at[W_X, g], rs_recv.at[R_X, n], to_x
        ).start()

    def send_last(key):
        g, i, m, column, width, kind, buf, n = info(key)
        remote(
            buf["last"].at[i, 0], buf["last"].at[i, 1],
            rs_send.at[W_LAST, g], rs_recv.at[R_LAST, n], to_y,
        ).start()

    def add_x(key):
        g, i, m, column, width, kind, buf, n = info(key)
        landing = buf["x"].at[i]
        remote(landing, landing, rs_send.at[W_X, g], rs_recv.at[R_X, n], to_x).wait_recv()
        if kind == LINE:
            buf["last"][i, 0] = buf["core"][i, z, x] + buf["x"][i]
            send_last(key)
            return
        own_part = buf["y"] if kind in SPLITS else buf["core"]

        def body(step, carry):
            buf["x"][i, step] = buf["x"][i, step] + own_part[i, step, x]
            return carry

        lax.fori_loop(0, 4, body, 0)
        send_line(key)

    def add_z1(key):
        g, i, m, column, width, kind, buf, n = info(key)
        sums_ref = running(key)

        @pl.when(inner)
        def _():
            landing = buf["z1"].at[i]
            remote(landing, landing, rs_send.at[W_Z1, g], rs_recv.at[R_Z1, n], to_near).wait_recv()
            for step in range(2):
                at = (1 - pair) * 2 + step
                sums_ref[i, at] = sums_ref[i, at] + buf["z1"][i, step]
            remote(
                sums_ref.at[i, other_pair], buf["z2"].at[i],
                rs_send.at[W_Z2, g], rs_recv.at[R_Z2, n], to_mirror,
            ).start()

    def add_z2(key):
        g, i, m, column, width, kind, buf, n = info(key)
        sums_ref = running(key)

        @pl.when(inner)
        def _():
            landing = buf["z2"].at[i]
            remote(landing, landing, rs_send.at[W_Z2, g], rs_recv.at[R_Z2, n], to_mirror).wait_recv()
            for step in range(2):
                at = pair * 2 + step
                sums_ref[i, at] = sums_ref[i, at] + buf["z2"][i, step]
            remote(
                sums_ref.at[i, near_z], buf["z3"].at[i],
                rs_send.at[W_Z3, g], rs_recv.at[R_Z3, n], to_near,
            ).start()

    def add_z3(key):
        g, i, m, column, width, kind, buf, n = info(key)
        if kind in FARS:
            total = buf["x"][i, z].astype(FULL)
            for step, sent, slot in ((1, W_Z1, R_Z1), (2, W_Z3, R_Z2), (3, W_Z4, R_Z3)):
                landing = buf["z3"].at[i, step - 1]
                remote(landing, landing, rs_send.at[sent, g], rs_recv.at[slot, n], to_near).wait_recv()
                total = total + buf["z3"][i, step - 1].astype(FULL)
            buf["last"][i, 0] = total.astype(buf["last"].dtype)
            send_last(key)
            return
        landing = buf["z3"].at[i]
        remote(landing, landing, rs_send.at[W_Z3, g], rs_recv.at[R_Z3, n], to_near).wait_recv()
        if kind == LINE:
            buf["core"][i, z] = buf["core"][i, z] + buf["z3"][i]
            remote(
                buf["core"].at[i, z, 1 - x], buf["x"].at[i],
                rs_send.at[W_X, g], rs_recv.at[R_X, n], to_x,
            ).start()
            return
        buf["last"][i, 0] = buf["x"][i, z] + buf["z3"][i]
        send_last(key)

    def finish(key):
        g, i, m, column, width, kind, buf, n = info(key)
        landing = buf["last"].at[i, 1]
        remote(landing, landing, rs_send.at[W_LAST, g], rs_recv.at[R_LAST, n], to_y).wait_recv()
        if kind in SPLITS:
            for which, slot in ((y, 0), (1 - y, 1)):
                columns = pl.ds(pl.multiple_of(column + which * (width // 2), 128), width // 2)
                sums[m][:, columns] = buf["last"][i, slot].astype(FULL)
        else:
            sums[m][:, pl.ds(column, width)] = buf["last"][i, 0].astype(FULL) + buf["last"][
                i, 1
            ].astype(FULL)
        piece = sums[m].at[:, pl.ds(column, width)]
        place = sums_out[m].at[c, :, pl.ds(column, width)]
        remote(piece, place, rs_send.at[W_END, g], rs_end.at[g], to_c).start()
        pltpu.make_async_copy(piece, place, out_sem.at[g]).start()

    def grad_contract():
        def body(s, carry):
            lanes = pl.ds(pl.multiple_of(s * 384, 128), 384)
            value = dot_tn(post[:, lanes], cot[...]).astype(LOW)
            g_con[s // 2, s % 2] = value.reshape(2, 192, 768)
            return carry

        lax.fori_loop(0, 8, body, 0)

    def grad_rows(source, other, target, high, columns, width):
        for half in range(2):
            value = dot_tn(source[:, half * 384 : half * 384 + 384], other).astype(LOW)
            target[2 * half : 2 * half + 2, :, :, high, columns] = value.reshape(2, 2, 2, 48, width)

    def grad_expand(i):
        span = slice(i * 768, i * 768 + 768)
        grad_rows(normed2, pre[:, span], full[3], slice(None), pl.ds(i * 768, 768), 768)

    def norm_second_back(rows):
        unit, scale = center(resid[rows, :])
        grad = back_s[rows, :]
        top = cot[rows, :].astype(FULL)
        e = grad * v96[4:5, :]
        value = (
            e - jnp.mean(e, axis=-1, keepdims=True) - unit * jnp.mean(e * unit, axis=-1, keepdims=True)
        ) * scale + top
        back_r[rows, :] = value
        rounded = value.astype(LOW)
        back_m[rows, :] = rounded
        acc96[4] += fold8(grad * unit)
        acc96[5] += fold8(grad)
        acc96[3] += fold8(rounded.astype(FULL))
        acc96[6] += fold8(top)
        result[rows, :] = (resid[rows, :] + gather_out[rows, :] + v96[6:7, :]).astype(LOW)

    def convolve_back(begin, end):
        def body(step, carry):
            rows = pl.ds(pl.multiple_of((step // 6) * 128, 128), 128)
            lane = pl.multiple_of((step % 6) * 128, 128)
            lanes = pl.ds(lane, 128)
            where = places[rows, :]
            rest = left[rows, :]
            gate_in = short[1, rows, lanes]
            values = short[2, rows, lanes]
            top = back_g[rows, lanes]
            carried = values * gate_in
            back_conv = top * short[0, rows, lanes]
            acc96[2, :, lanes] += fold8(back_conv * carried)
            total = v96[2:3, lanes] * back_conv
            for low_lag in range(8):
                turned = turn(back_conv, -low_lag, 0)
                for high in range(LAGS // 8):
                    lag, skip = high * 8 + low_lag, high * 8
                    size = 128 - skip
                    moved = jnp.where(rest[:size] >= lag, turned[skip:], 0.0)
                    term = taps[lag : lag + 1, lanes] * moved
                    if skip:
                        total = jnp.concatenate([total[:size] + term, total[size:]], axis=0)
                    else:
                        total = total + term
                    d_taps[lag : lag + 1, lanes] += jnp.sum(
                        moved * carried[:size], axis=0, keepdims=True
                    )
            streams = (top * conv[rows, lanes], total * values, total * gate_in)
            for k in range(3):
                wide = pl.ds(pl.multiple_of(k * 768 + lane, 128), 128)
                grad = streams[k]
                before = proj[k, rows, lanes]
                acc288[1, :, wide] += fold8(grad)
                acc288[2, :, wide] += fold8(grad * before)
                value = v288[2:3, wide] * grad
                for lag in (1, 2):
                    moved = jnp.where(where >= lag, pltpu.roll(before, lag, 0), 0.0)
                    acc288[2 + lag, :, wide] += fold8(grad * moved)
                    later = jnp.where(rest >= lag, pltpu.roll(grad, 128 - lag, 0), 0.0)
                    value = value + v288[2 + lag : 3 + lag, wide] * later
                rounded = value.astype(LOW)
                bp[k, rows, lanes] = rounded
                acc288[0, :, wide] += fold8(rounded.astype(FULL))
            return carry

        lax.fori_loop(begin, end, body, 0)

    def norm_first_back(rows):
        unit, scale = center(tokens[rows, :].astype(FULL))
        grad = back_s[rows, :]
        e = grad * v96[0:1, :]
        delta[rows, :] = back_r[rows, :] + (
            e - jnp.mean(e, axis=-1, keepdims=True) - unit * jnp.mean(e * unit, axis=-1, keepdims=True)
        ) * scale
        acc96[0] += fold8(grad * unit)
        acc96[1] += fold8(grad)

    def small_grads():
        scale = v8[1:2, :]
        raw = d_taps[...] * decay[...]
        d_fil = exact(s_second[...], raw, (0, 0))
        b2 = exact(raw, fil_w[...], (1, 1)) * s_cos2[...]
        b2s = b2 * scale
        d_mid = exact(s_first[...], b2s, (0, 0))
        b1 = exact(b2s, mid_w[...], (1, 1)) * s_cos1[...]
        b1s = b1 * scale
        d_inner = exact(b1s, features[...], (0, 0))
        d_scale = jnp.sum(b2 * s_inner2[...] + b1 * s_inner1[...], axis=0, keepdims=True)
        rows8 = jnp.concatenate(
            [
                jnp.sum(b1s, axis=0, keepdims=True), d_scale, jnp.sum(b2s, axis=0, keepdims=True),
                jnp.zeros((5, 128), FULL),
            ],
            axis=0,
        )
        rows96 = jnp.concatenate(
            [jnp.sum(acc96[f], axis=0, keepdims=True) for f in range(7)] + [jnp.zeros((1, 768), FULL)],
            axis=0,
        )
        rows288 = jnp.concatenate(
            [jnp.sum(acc288[f], axis=0, keepdims=True) for f in range(5)]
            + [jnp.zeros((3, 2304), FULL)],
            axis=0,
        )
        rows_exp = jnp.sum(accexp[...], axis=0, keepdims=True)
        lane = lax.broadcasted_iota(jnp.int32, (8, 128), 1)
        row = lax.broadcasted_iota(jnp.int32, (8, 128), 0)
        wide_lane = lax.broadcasted_iota(jnp.int32, (64, 128), 1)
        for s in range(8):
            a, b = s // 2, s % 2
            g_small[a, b, 0, 0:8, :] = jnp.where(lane < 96, turn(rows96, -96 * s, 1)[:, :128], 0.0)
            turned = turn(rows288, -288 * s, 1)
            for block in range(3):
                value = turned[:, block * 128 : block * 128 + 128]
                if block == 2:
                    value = jnp.where(lane < 32, value, 0.0)
                bias = rows_exp[:, s * 384 + block * 128 : s * 384 + block * 128 + 128]
                value = jnp.where(row == 5, jnp.broadcast_to(bias, (8, 128)), value)
                g_small[a, b, 0, 8 + block * 8 : 16 + block * 8, :] = value
            g_small[a, b, 0, 32:40, :] = jnp.where(lane < 8, turn(rows8, -8 * s, 1), 0.0)
            g_small[a, b, 0, 40:48, :] = d_mid[8 * s : 8 * s + 8]
            g_small[a, b, 0, 48:56, :] = d_inner[8 * s : 8 * s + 8]
            g_small[a, b, 0, 56:64, :] = jnp.zeros((8, 128), FULL)
            g_small[a, b, 1] = jnp.where(
                wide_lane < 96, turn(d_fil[0:64], -96 * s, 1)[:, :128], 0.0
            )

    def back_gate():
        back_g[...] = dot_nt(back_m[...], matrix_of(1, pl.ds(0, 768), 768))

    def back_first():
        for k in range(3):
            value = dot_nt(bp[k], matrix_of(0, pl.ds(k * 768, 768), 768))
            if k == 0:
                back_s[...] = value
            else:
                back_s[...] += value

    def unpack(k):
        settled(4, 0, 128)
        unpack_small()

    def projected(k):
        settled(0, k * 768, k * 768 + 768)
        project(k)

    def mix(k):
        settled(1, 0, 768)
        mix_out()

    def expanded(k):
        settled(3, k * 768, k * 768 + 768)
        expand(k)

    def fed(k):
        settled(2, 0, 768)
        feed(k)

    outgoing = [
        pltpu.make_async_copy(result, result_out, own_sem.at[7]),
        pltpu.make_async_copy(delta, delta_out, own_sem.at[8]),
    ]

    def second_back(k):
        row_blocks(NORM_ROWS, norm_second_back)
        outgoing[0].start()

    def first_back(k):
        row_blocks(NORM_ROWS, norm_first_back)
        outgoing[1].start()

    def expand_back(k):
        drain(3, k * 768, k * 768 + 768)
        grad_expand(k)

    def end(k):
        for copy in outgoing:
            copy.wait()
        for m in range(5):
            drain(m, 0, full[m].shape[4])

    actions = {
        DO_FIRST: first, DO_NEAR: near, DO_FAR: far, DO_SIDE: side, DO_CROSS: cross,
        DO_PLACES: lambda k: find_places(),
        DO_UNPACK: unpack,
        DO_NORM1: lambda k: row_blocks(NORM_ROWS, norm_first),
        DO_PROJECT: projected,
        DO_CONV: lambda k: convolve(3 * k, 3 * k + 3),
        DO_MIX: mix,
        DO_EXPAND: expanded,
        DO_BEND: bend,
        DO_FEED: fed,
        DO_DRAIN: lambda k: drain(2, 0, 768),
        DO_GCON: lambda k: grad_contract(),
        DO_GEXP: expand_back,
        DO_NORM2B: second_back,
        DO_BACKG: lambda k: back_gate(),
        DO_GOUT: lambda k: grad_rows(gated, back_m[...], full[2], pl.ds(3 * HALF, HALF), pl.ds(0, 768), 768),
        DO_CONVB: lambda k: convolve_back(3 * k, 3 * k + 3),
        DO_GIN: lambda k: grad_rows(normed1, bp[k], full[2], pl.ds(k * HALF, HALF), pl.ds(0, 768), 768),
        DO_BFIRST: lambda k: back_first(),
        DO_NORM1B: first_back,
        DO_SMALL: lambda k: small_grads(),
        DO_STAGE: stage, DO_ACORE: add_core, DO_AY: add_y, DO_AX: add_x, DO_AZ1: add_z1,
        DO_AZ2: add_z2, DO_AZ3: add_z3, DO_FIN: finish, DO_END: end,
    }
    for name, which in SCHEDULE:
        if name != DO_FIRST:
            ready()
        actions[name](which)

    for g, (matrix, columns, width, kind) in enumerate(REDUCE_GROUPS):
        held = sums[matrix].at[:, pl.ds(0, width * len(columns))]
        place = sums_out[matrix].at[1 - c, :, pl.ds(0, width * len(columns))]
        remote(held, place, rs_send.at[W_END, g], rs_end.at[g], to_c).wait_recv()
        pltpu.make_async_copy(held, place, out_sem.at[g]).wait()
    for g, (matrix, columns, width, kind) in enumerate(REDUCE_GROUPS):
        buf = groups[g]

        def leave(kind, ref, g=g):
            remote(ref, ref, rs_send.at[kind, g], rs_end.at[g], to_c).wait_send()

        leave(W_CORE, buf["core"])
        if kind in SPLITS:
            leave(W_Y, buf["y"])
        leave(W_X, buf["x"])
        if kind in FARS:
            for step, sent in enumerate((W_Z1, W_Z3, W_Z4)):
                leave(sent, buf["z3"].at[:, step])
        else:
            leave(W_Z3, buf["z3"])
            leave(W_Z1, buf["z1"])
        leave(W_LAST, buf["last"].at[:, 0])
        leave(W_END, sums[matrix].at[:, pl.ds(0, width * len(columns))])


def unpack_kernel(result, delta, s_in, s_out, s_con, s_exp, s_small, *outs):
    (
        o_result, o_delta, o_first_gain, o_first_shift, o_in, o_in_bias, o_short_w, o_short_b,
        o_inner_w, o_inner_b, o_scale, o_middle_w, o_middle_b, o_filter_w, o_direct, o_out,
        o_out_bias, o_second_gain, o_second_shift, o_exp, o_exp_bias, o_con, o_con_bias,
    ) = outs
    o_result[...] = result[...]
    o_delta[...] = delta[...]
    for source, target in ((s_in, o_in), (s_out, o_out), (s_con, o_con), (s_exp, o_exp)):
        height = source.shape[1]
        for half in range(2):
            target[half * height : half * height + height, :] = source[half]
    for row, target in enumerate(
        (o_first_gain, o_first_shift, o_direct, o_out_bias, o_second_gain, o_second_shift, o_con_bias)
    ):
        target[...] = s_small[0, row : row + 1, 0:96].reshape(96)
    wide = jnp.concatenate([s_small[0, 8:16, :], s_small[0, 16:24, :], s_small[0, 24:32, :]], axis=1)
    o_in_bias[...] = wide[0:1, 0:288].reshape(288)
    o_short_b[...] = wide[1:2, 0:288].reshape(288)
    o_short_w[...] = wide[2:5, 0:288]
    o_exp_bias[...] = wide[5:6].reshape(384)
    for row, target in enumerate((o_inner_b, o_scale, o_middle_b)):
        target[...] = s_small[0, 32 + row : 33 + row, 0:8].reshape(8)
    o_inner_w[...] = s_small[0, 48:56, 0:33]
    o_middle_w[...] = s_small[0, 40:48, 0:64]
    o_filter_w[...] = s_small[1, :, 0:96]


def filter_constants(length, width):
    places = np.arange(LAGS, dtype=np.float64)
    scales = 0.0001 + np.arange(16, dtype=np.float64) * ((15.0 - 0.0001) / 15.0)
    phases = (2.0 * math.pi * places / length)[:, None] * scales[None, :]
    ramp = places / (length - 1)
    table = np.zeros((LAGS, 128), np.float32)
    table[:, 0] = ramp
    table[:, 1:17] = np.cos(phases)
    table[:, 17:33] = -np.sin(phases)
    rates = math.log(100.0) * (
        1.0 / 1.5 + (1.0 / 0.3 - 1.0 / 1.5) * np.arange(width, dtype=np.float64) / (width - 1)
    )
    return table, np.exp(-ramp[:, None] * rates[None, :]).astype(np.float32)


def block_device(
    tokens, segment_ids, cotangent, first_gain, first_shift, input_weight, input_bias,
    short_weight, short_bias, inner_weight, inner_bias, sine_scale, middle_weight, middle_bias,
    filter_weight, direct_gain, output_weight, output_bias, second_gain, second_shift,
    expand_weight, expand_bias, contract_weight, contract_bias,
):
    blocks, _, length, width = tokens.shape
    rows = blocks * length
    features, decay = filter_constants(length, width)

    small_members = (
        first_gain, first_shift, input_bias, short_weight, short_bias, inner_weight, inner_bias,
        sine_scale, middle_weight, middle_bias, filter_weight, direct_gain, output_bias,
        second_gain, second_shift, expand_bias, contract_bias,
    )

    def halved(member):
        return member.reshape(2, member.shape[0] // 2, member.shape[1])

    shards = [halved(m) for m in (input_weight, output_weight, contract_weight, expand_weight)]
    inputs = (
        tokens.reshape(rows, width), segment_ids.reshape(blocks, length),
        cotangent.reshape(rows, width),
    ) + tuple(m.T if m is inner_weight else m for m in small_members) + tuple(shards) + (
        jnp.asarray(features), jnp.asarray(decay),
    )
    shapes = [m.shape[1:] for m in shards] + [(SMALL_ROWS, 128)]
    outs = [
        jax.ShapeDtypeStruct((rows, width), LOW),
        jax.ShapeDtypeStruct((rows, width), FULL),
    ] + [jax.ShapeDtypeStruct((2,) + s, FULL) for s in shapes]
    count = len(GATHER_CHUNKS)
    crossing = sum(1 for chunk in GATHER_CHUNKS if chunk[3] == SPLIT)
    leaving = len({(chunk[0], chunk[3]) if chunk[0] != 3 else chunk[:2] for chunk in GATHER_CHUNKS})
    vm = pltpu.VMEM
    scratch = [vm((rows, width), kind) for kind in (LOW, LOW, LOW, FULL)]
    scratch += [vm(s, FULL) for s in shapes]
    scratch += [vm((4, 2, 2) + s, LOW) for s in shapes]
    scratch += [
        vm((4, 2, 2) + shapes[2], LOW), vm((4, 2, 2) + shapes[4], FULL), vm((2, SMALL_ROWS, 128), LOW),
        vm((2 * SMALL_ROWS, 128), FULL),
        vm((8, width), FULL), vm((8, 3 * width), FULL), vm((1, 4 * width), FULL), vm((8, 128), FULL),
        vm((128, 128), FULL), vm((128, width), FULL), vm((LAGS, width), FULL), vm((LAGS, width), FULL),
    ]
    scratch += [vm((LAGS, 128), FULL)] * 6
    scratch += [vm((rows, 128), jnp.int32)] * 2
    scratch += [
        vm((rows, width), LOW), vm((3, rows, width), FULL), vm((3, rows, width), FULL),
        vm((rows, width), FULL), vm((rows, width), LOW), vm((rows, width), FULL),
        vm((rows, width), LOW),
        vm((rows, 4 * width), FULL), vm((rows, 4 * width), LOW), vm((rows, 4 * width), LOW),
        vm((rows, width), FULL), vm((rows, width), FULL), vm((rows, width), FULL),
        vm((rows, width), LOW), vm((3, rows, width), LOW),
        vm((7, 8, width), FULL), vm((5, 8, 3 * width), FULL), vm((8, 4 * width), FULL),
    ]
    for matrix, columns, span, kind in REDUCE_GROUPS:
        n, high = len(columns), shapes[matrix][0]
        of = FULL if matrix == 4 else LOW
        v = span // 2 if kind in SPLITS else span
        core = vm((n, 4, 2, high, span), of)
        last = vm((n, 2, high, v), of)
        if kind in FARS:
            scratch += [core, vm((n, 4, high, v), of), vm((n, 3, high, v), of), last]
        else:
            side_planes, line_planes = ((), (2,)) if kind == LINE else ((4,), ())
            scratch += [
                core, vm((n,) + side_planes + (high, v), of),
                vm((n, 2) + line_planes + (high, v), of), vm((n, 2) + line_planes + (high, v), of),
                vm((n,) + line_planes + (high, v), of), last,
            ]
        if kind in SPLITS:
            scratch.append(vm((n, 4, 2, high, v), of))
    total = len(REDUCE_ORDER)
    splits = sum(len(g[1]) for g in REDUCE_GROUPS if g[3] in SPLITS)
    dma = pltpu.SemaphoreType.DMA
    scratch += [
        dma((4, count)), dma((3, crossing)), dma((count,)), dma((6, leaving)), dma((9,)),
        dma((6, total)), dma((splits,)), dma((8, len(REDUCE_GROUPS))), dma((len(REDUCE_GROUPS),)),
        dma((len(REDUCE_GROUPS),)),
    ]
    in_vmem = pl.BlockSpec(memory_space=pltpu.VMEM)
    anywhere = pl.BlockSpec(memory_space=pl.ANY)
    parts = pl.pallas_call(
        block_kernel,
        out_shape=outs,
        in_specs=[anywhere, in_vmem, anywhere] + [in_vmem] * 17 + [anywhere] * 4 + [in_vmem] * 2,
        out_specs=[anywhere] * len(outs),
        scratch_shapes=scratch,
        compiler_params=pltpu.CompilerParams(
            collective_id=0, has_side_effects=True, vmem_limit_bytes=67043328
        ),
    )(*inputs)
    members = (
        first_gain, first_shift, input_weight, input_bias, short_weight, short_bias, inner_weight,
        inner_bias, sine_scale, middle_weight, middle_bias, filter_weight, direct_gain,
        output_weight, output_bias, second_gain, second_shift, expand_weight, expand_bias,
        contract_weight, contract_bias,
    )
    final = [outs[0], outs[1]] + [
        jax.ShapeDtypeStruct(m.shape[::-1] if m is inner_weight else m.shape, FULL) for m in members
    ]
    done = pl.pallas_call(
        unpack_kernel,
        out_shape=final,
        in_specs=[in_vmem] * 7,
        out_specs=[in_vmem] * len(final),
    )(*parts)
    done = [m.T if n == INNER_OUT else m for n, m in enumerate(done)]
    return (done[0].reshape(tokens.shape), done[1].reshape(tokens.shape)) + tuple(done[2:])


def per_device(
    tokens,
    segment_ids,
    cotangent,
    first_gain,
    first_shift,
    input_weight,
    input_bias,
    short_weight,
    short_bias,
    inner_weight,
    inner_bias,
    sine_scale,
    middle_weight,
    middle_bias,
    filter_weight,
    direct_gain,
    output_weight,
    output_bias,
    second_gain,
    second_shift,
    expand_weight,
    expand_bias,
    contract_weight,
    contract_bias,
):
    micro_count, local_sequences, length, width = tokens.shape
    row_count = local_sequences * length
    tables = wave_tables(length)

    def fetch_mixer():
        return (
            lax.all_gather(first_gain, "shard", axis=0, tiled=True),
            lax.all_gather(first_shift, "shard", axis=0, tiled=True),
            lax.all_gather(input_weight, "shard", axis=0, tiled=True),
            lax.all_gather(input_bias, "shard", axis=0, tiled=True),
            lax.all_gather(short_weight, "shard", axis=1, tiled=True),
            lax.all_gather(short_bias, "shard", axis=0, tiled=True),
            lax.all_gather(inner_weight, "shard", axis=1, tiled=True),
            lax.all_gather(inner_bias, "shard", axis=0, tiled=True),
            lax.all_gather(sine_scale, "shard", axis=0, tiled=True),
            lax.all_gather(middle_weight, "shard", axis=0, tiled=True),
            lax.all_gather(middle_bias, "shard", axis=0, tiled=True),
            lax.all_gather(filter_weight, "shard", axis=1, tiled=True),
            lax.all_gather(direct_gain, "shard", axis=0, tiled=True),
            lax.all_gather(output_weight, "shard", axis=0, tiled=True),
            lax.all_gather(output_bias, "shard", axis=0, tiled=True),
        )

    def fetch_dense():
        return (
            lax.all_gather(second_gain, "shard", axis=0, tiled=True),
            lax.all_gather(second_shift, "shard", axis=0, tiled=True),
            lax.all_gather(expand_weight, "shard", axis=0, tiled=True),
            lax.all_gather(expand_bias, "shard", axis=0, tiled=True),
            lax.all_gather(contract_weight, "shard", axis=0, tiled=True),
            lax.all_gather(contract_bias, "shard", axis=0, tiled=True),
        )

    results = []
    input_deltas = []
    mixer_total = None
    dense_total = None
    for micro_index in range(micro_count):
        mixer_parts = fetch_mixer()
        dense_parts = fetch_dense()
        kernel = filter_taps(
            to_float(mixer_parts[6]),
            to_float(mixer_parts[7]),
            to_float(mixer_parts[8]),
            to_float(mixer_parts[9]),
            to_float(mixer_parts[10]),
            to_float(mixer_parts[11]),
            length,
        )
        kernel, kernel_wave = (kernel, spectrum(tables, kernel))
        kernel_real, kernel_imag = kernel_wave
        segment_block = segment_ids[micro_index]
        membership = (
            segment_block[:, None, :] == jnp.arange(DOCS, dtype=jnp.int32)[None, :, None]
        ).astype(jnp.float32)
        flat_tokens = tokens[micro_index].reshape(row_count, width).astype(jnp.float32)
        normed_first = normalize(
            flat_tokens, to_float(mixer_parts[0]), to_float(mixer_parts[1])
        ).astype(jnp.bfloat16)
        projected = jnp.dot(
            normed_first, mixer_parts[2], preferred_element_type=jnp.float32
        ) + to_float(mixer_parts[3])
        projected_rows = projected.reshape(local_sequences, length, 3 * width)
        short_out = short_filter(
            projected_rows, segment_block, to_float(mixer_parts[4]), to_float(mixer_parts[5])
        )
        gate_out = short_out[:, :, :width]
        gate_in = short_out[:, :, width : 2 * width]
        values = short_out[:, :, 2 * width :]
        carried = values * gate_in
        direct = to_float(mixer_parts[12])
        carried_real, carried_imag = spectrum(tables, carried[:, None] * membership[:, :, :, None])
        conv_pieces = inverse(
            tables,
            carried_real * kernel_real - carried_imag * kernel_imag,
            carried_real * kernel_imag + carried_imag * kernel_real,
        )
        convolved = jnp.sum(conv_pieces * membership[:, :, :, None], axis=1) + direct * carried
        gated_low = (convolved * gate_out).astype(jnp.bfloat16).reshape(row_count, width)
        mixed_out = jnp.dot(
            gated_low, mixer_parts[13], preferred_element_type=jnp.float32
        ) + to_float(mixer_parts[14])
        residual = flat_tokens + mixed_out
        second_gain_f = to_float(dense_parts[0])
        second_shift_f = to_float(dense_parts[1])
        normed_second = normalize(residual, second_gain_f, second_shift_f).astype(jnp.bfloat16)
        hidden_pre = jnp.dot(
            normed_second, dense_parts[2], preferred_element_type=jnp.float32
        ) + to_float(dense_parts[3])
        hidden_post = smooth_gate(hidden_pre).astype(jnp.bfloat16)
        result = (
            residual
            + jnp.dot(hidden_post, dense_parts[4], preferred_element_type=jnp.float32)
            + to_float(dense_parts[5])
        )
        results.append(result.astype(jnp.bfloat16).reshape(local_sequences, length, width))
        back_mixer = fetch_mixer()
        back_dense = fetch_dense()
        upstream = cotangent[micro_index].reshape(row_count, width)
        upstream_float = upstream.astype(jnp.float32)
        delta_contract_weight = jnp.einsum(
            "tf,td->fd", hidden_post, upstream, preferred_element_type=jnp.float32
        )
        delta_contract_bias = jnp.sum(upstream_float, axis=0)
        back_hidden = jnp.einsum(
            "td,fd->tf", upstream, back_dense[4], preferred_element_type=jnp.float32
        )
        back_pre = jax.vjp(smooth_gate, hidden_pre)[1](back_hidden)[0].astype(jnp.bfloat16)
        delta_expand_weight = jnp.einsum(
            "td,tf->df", normed_second, back_pre, preferred_element_type=jnp.float32
        )
        delta_expand_bias = jnp.sum(back_pre.astype(jnp.float32), axis=0)
        back_second = jnp.einsum(
            "tf,df->td", back_pre, back_dense[2], preferred_element_type=jnp.float32
        )
        second_pull = jax.vjp(
            normalize, residual, to_float(back_dense[0]), to_float(back_dense[1])
        )[1]
        back_norm_second, delta_second_gain, delta_second_shift = second_pull(back_second)
        back_residual = upstream_float + back_norm_second
        back_mixed = back_residual.astype(jnp.bfloat16)
        delta_output_weight = jnp.einsum(
            "td,te->de", gated_low, back_mixed, preferred_element_type=jnp.float32
        )
        delta_output_bias = jnp.sum(back_mixed.astype(jnp.float32), axis=0)
        back_gated = jnp.einsum(
            "te,de->td", back_mixed, back_mixer[13], preferred_element_type=jnp.float32
        ).reshape(local_sequences, length, width)
        back_conv = back_gated * gate_out
        grad_real, grad_imag = spectrum(tables, back_conv[:, None] * membership[:, :, :, None])
        carried_back_pieces = inverse(
            tables,
            grad_real * kernel_real + grad_imag * kernel_imag,
            grad_imag * kernel_real - grad_real * kernel_imag,
        )
        back_carried = (
            jnp.sum(carried_back_pieces * membership[:, :, :, None], axis=1) + direct * back_conv
        )
        cross_real = jnp.sum(grad_real * carried_real + grad_imag * carried_imag, axis=(0, 1))
        cross_imag = jnp.sum(grad_imag * carried_real - grad_real * carried_imag, axis=(0, 1))
        back_kernel = inverse(tables, cross_real, cross_imag)
        delta_direct = jnp.sum(back_conv * carried, axis=(0, 1))
        back_short = jnp.concatenate(
            [back_gated * convolved, back_carried * values, back_carried * gate_in], axis=2
        )
        short_pull = jax.vjp(
            lambda rows_in, taps_in, offset_in: short_filter(
                rows_in, segment_block, taps_in, offset_in
            ),
            projected_rows,
            to_float(back_mixer[4]),
            to_float(back_mixer[5]),
        )[1]
        back_projected, delta_short_weight, delta_short_bias = short_pull(back_short)
        back_projected = back_projected.reshape(row_count, 3 * width).astype(jnp.bfloat16)
        delta_input_weight = jnp.einsum(
            "td,tp->dp", normed_first, back_projected, preferred_element_type=jnp.float32
        )
        delta_input_bias = jnp.sum(back_projected.astype(jnp.float32), axis=0)
        back_first = jnp.einsum(
            "tp,dp->td", back_projected, back_mixer[2], preferred_element_type=jnp.float32
        )
        first_pull = jax.vjp(
            normalize, flat_tokens, to_float(back_mixer[0]), to_float(back_mixer[1])
        )[1]
        back_norm_first, delta_first_gain, delta_first_shift = first_pull(back_first)
        input_deltas.append(
            (back_residual + back_norm_first).reshape(local_sequences, length, width)
        )
        filter_pull = jax.vjp(
            lambda weight_one, bias_one, scale_all, weight_two, bias_two, weight_three: filter_taps(
                weight_one, bias_one, scale_all, weight_two, bias_two, weight_three, length
            ),
            to_float(back_mixer[6]),
            to_float(back_mixer[7]),
            to_float(back_mixer[8]),
            to_float(back_mixer[9]),
            to_float(back_mixer[10]),
            to_float(back_mixer[11]),
        )[1]
        filter_deltas = filter_pull(back_kernel)
        mixer_part = (
            delta_first_gain,
            delta_first_shift,
            delta_input_weight,
            delta_input_bias,
            delta_short_weight,
            delta_short_bias,
            filter_deltas[0],
            filter_deltas[1],
            filter_deltas[2],
            filter_deltas[3],
            filter_deltas[4],
            filter_deltas[5],
            delta_direct,
            delta_output_weight,
            delta_output_bias,
        )
        dense_part = (
            delta_second_gain,
            delta_second_shift,
            delta_expand_weight,
            delta_expand_bias,
            delta_contract_weight,
            delta_contract_bias,
        )
        if micro_index == 0:
            mixer_total = mixer_part
            dense_total = dense_part
        else:
            mixer_total = jax.tree.map(jnp.add, mixer_total, mixer_part)
            dense_total = jax.tree.map(jnp.add, dense_total, dense_part)
    dense_total = (
        lax.psum_scatter(dense_total[0], "shard", scatter_dimension=0, tiled=True),
        lax.psum_scatter(dense_total[1], "shard", scatter_dimension=0, tiled=True),
        lax.psum_scatter(dense_total[2], "shard", scatter_dimension=0, tiled=True),
        lax.psum_scatter(dense_total[3], "shard", scatter_dimension=0, tiled=True),
        lax.psum_scatter(dense_total[4], "shard", scatter_dimension=0, tiled=True),
        lax.psum_scatter(dense_total[5], "shard", scatter_dimension=0, tiled=True),
    )
    mixer_total = (
        lax.psum_scatter(mixer_total[0], "shard", scatter_dimension=0, tiled=True),
        lax.psum_scatter(mixer_total[1], "shard", scatter_dimension=0, tiled=True),
        lax.psum_scatter(mixer_total[2], "shard", scatter_dimension=0, tiled=True),
        lax.psum_scatter(mixer_total[3], "shard", scatter_dimension=0, tiled=True),
        lax.psum_scatter(mixer_total[4], "shard", scatter_dimension=1, tiled=True),
        lax.psum_scatter(mixer_total[5], "shard", scatter_dimension=0, tiled=True),
        lax.psum_scatter(mixer_total[6], "shard", scatter_dimension=1, tiled=True),
        lax.psum_scatter(mixer_total[7], "shard", scatter_dimension=0, tiled=True),
        lax.psum_scatter(mixer_total[8], "shard", scatter_dimension=0, tiled=True),
        lax.psum_scatter(mixer_total[9], "shard", scatter_dimension=0, tiled=True),
        lax.psum_scatter(mixer_total[10], "shard", scatter_dimension=0, tiled=True),
        lax.psum_scatter(mixer_total[11], "shard", scatter_dimension=1, tiled=True),
        lax.psum_scatter(mixer_total[12], "shard", scatter_dimension=0, tiled=True),
        lax.psum_scatter(mixer_total[13], "shard", scatter_dimension=0, tiled=True),
        lax.psum_scatter(mixer_total[14], "shard", scatter_dimension=0, tiled=True),
    )
    summed = lax.psum(
        (
            mixer_total[0],
            mixer_total[1],
            mixer_total[2],
            mixer_total[3],
            mixer_total[4],
            mixer_total[5],
            mixer_total[6],
            mixer_total[7],
            mixer_total[8],
            mixer_total[9],
            mixer_total[10],
            mixer_total[11],
            mixer_total[12],
            mixer_total[13],
            mixer_total[14],
            dense_total[0],
            dense_total[1],
            dense_total[2],
            dense_total[3],
            dense_total[4],
            dense_total[5],
        ),
        "rep",
    )
    return (jnp.stack(results), jnp.stack(input_deltas)) + tuple(summed)


def solution(mesh):
    placed = (
        P(None, ("rep", "shard"), None, None),
        P(None, ("rep", "shard"), None),
        P(None, ("rep", "shard"), None, None),
        P("shard"),
        P("shard"),
        P("shard", None),
        P("shard"),
        P(None, "shard"),
        P("shard"),
        P(None, "shard"),
        P("shard"),
        P("shard"),
        P("shard", None),
        P("shard"),
        P(None, "shard"),
        P("shard"),
        P("shard", None),
        P("shard"),
        P("shard"),
        P("shard"),
        P("shard", None),
        P("shard"),
        P("shard", None),
        P("shard"),
    )
    blocked = dict(mesh.shape) == {"rep": 4, "shard": 8}
    return jax.shard_map(
        block_device if blocked else per_device,
        mesh=mesh,
        in_specs=placed,
        out_specs=(
            P(None, ("rep", "shard"), None, None),
            P(None, ("rep", "shard"), None, None),
            P("shard"),
            P("shard"),
            P("shard", None),
            P("shard"),
            P(None, "shard"),
            P("shard"),
            P(None, "shard"),
            P("shard"),
            P("shard"),
            P("shard", None),
            P("shard"),
            P(None, "shard"),
            P("shard"),
            P("shard", None),
            P("shard"),
            P("shard"),
            P("shard"),
            P("shard", None),
            P("shard"),
            P("shard", None),
            P("shard"),
        ),
        check_vma=False,
    )
```

```python
import math

import jax
import jax.numpy as jnp
import numpy as np
from jax import lax
from jax.experimental import pallas as pl
from jax.experimental.pallas import tpu as pltpu
from jax.sharding import PartitionSpec as P

DOCS = 6


EPSILON = 1e-05
HIGHEST = lax.Precision.HIGHEST


def positions(length):
    places = jnp.arange(length, dtype=jnp.float32)
    linear_ramp = places / (length - 1)
    angles = 2.0 * math.pi * places / length
    scales = 0.0001 + jnp.arange(16, dtype=jnp.float32) * ((15.0 - 0.0001) / 15.0)
    phases = angles[:, None] * scales[None, :]
    return jnp.concatenate([linear_ramp[:, None], jnp.cos(phases), -jnp.sin(phases)], axis=1)


def decay_table(length, width):
    linear_ramp = jnp.arange(length, dtype=jnp.float32) / (length - 1)
    rates = math.log(100.0) * (
        1.0 / 1.5 + (1.0 / 0.3 - 1.0 / 1.5) * jnp.arange(width, dtype=jnp.float32) / (width - 1)
    )
    return jnp.exp(-linear_ramp[:, None] * rates[None, :])


def filter_taps(
    inner_weight, inner_bias, sine_scale, middle_weight, middle_bias, filter_weight, length
):
    features = positions(length)
    first_sine = jnp.sin(
        sine_scale * (jnp.dot(features, inner_weight, precision=HIGHEST) + inner_bias)
    )
    second_sine = jnp.sin(
        sine_scale * (jnp.dot(first_sine, middle_weight, precision=HIGHEST) + middle_bias)
    )
    return jnp.dot(second_sine, filter_weight, precision=HIGHEST) * decay_table(
        length, filter_weight.shape[1]
    )


def normalize(values, gain_row, shift_row):
    center = values - jnp.mean(values, axis=-1, keepdims=True)
    spread = jnp.mean(center * center, axis=-1, keepdims=True)
    return center * lax.rsqrt(spread + EPSILON) * gain_row + shift_row


def smooth_gate(values):
    return jax.nn.gelu(values, approximate=True)


def to_float(member):
    return member.astype(jnp.float32)


def short_filter(projected, segments, weight, offset):
    running = offset + weight[0] * projected
    for step_back in (1, 2):
        moved_rows = jnp.concatenate(
            [jnp.zeros_like(projected[:, :step_back]), projected[:, :-step_back]], axis=1
        )
        moved_ids = jnp.concatenate(
            [jnp.full_like(segments[:, :step_back], -1), segments[:, :-step_back]], axis=1
        )
        same_doc = (moved_ids == segments).astype(projected.dtype)
        running = running + weight[step_back] * moved_rows * same_doc[:, :, None]
    return running


def wave_tables(length):
    padded_size = 2 * length
    freq_index = jnp.arange(length + 1, dtype=jnp.int32)
    place_index = jnp.arange(length, dtype=jnp.int32)
    wrapped = freq_index[:, None] * place_index[None, :] % padded_size
    angles = 2.0 * math.pi / padded_size * wrapped.astype(jnp.float32)
    weights_row = (
        jnp.where((freq_index == 0) | (freq_index == length), 1.0, 2.0).astype(jnp.float32)
        / padded_size
    )
    return (jnp.cos(angles), jnp.sin(angles), weights_row)


def spectrum(tables, signal):
    cosine, sine, weights_row = tables
    real_part = jnp.einsum("ft,...td->...fd", cosine, signal, precision=HIGHEST)
    imag_part = -jnp.einsum("ft,...td->...fd", sine, signal, precision=HIGHEST)
    return (real_part, imag_part)


def inverse(tables, real_part, imag_part):
    cosine, sine, weights_row = tables
    scaled_real = real_part * weights_row[:, None]
    scaled_imag = imag_part * weights_row[:, None]
    return jnp.einsum("ft,...fd->...td", cosine, scaled_real, precision=HIGHEST) - jnp.einsum(
        "ft,...fd->...td", sine, scaled_imag, precision=HIGHEST
    )


MESH_ID = pl.DeviceIdType.MESH
LAGS = 64
LOW = jnp.bfloat16
FULL = jnp.float32
WHOLE, SPLIT, LINE, WHOLE_FAR, SPLIT_FAR = range(5)
SPLITS = (SPLIT, SPLIT_FAR)
FARS = (WHOLE_FAR, SPLIT_FAR)
GATHER_CHUNKS = (
    (4, 0, 128, WHOLE),
    (0, 768, 768, SPLIT),
    (0, 1536, 768, SPLIT),
    (0, 0, 768, SPLIT),
    (1, 0, 768, SPLIT),
    (3, 0, 768, SPLIT),
    (3, 768, 768, WHOLE),
    (3, 1536, 768, SPLIT),
    (3, 2304, 768, WHOLE),
    (2, 0, 256, SPLIT),
    (2, 256, 256, LINE),
    (2, 512, 256, WHOLE),
)
REDUCE_GROUPS = (
    (2, (0,), 256, LINE),
    (2, (256,), 256, SPLIT),
    (2, (512,), 256, WHOLE),
    (3, (0, 1536), 768, SPLIT),
    (3, (768, 2304), 768, WHOLE),
    (1, (0,), 768, SPLIT),
    (0, (0, 768, 1536), 512, SPLIT_FAR),
    (0, (512, 1280, 2048), 256, WHOLE),
    (4, (0,), 128, WHOLE_FAR),
)
REDUCE_ORDER = (
    (0, 0), (1, 0), (2, 0), (3, 0), (4, 0), (3, 1), (4, 1), (5, 0), (6, 0), (7, 0), (6, 1), (7, 1), (6, 2), (7, 2), (8, 0),
)
(
    DO_FIRST, DO_NEAR, DO_FAR, DO_SIDE, DO_CROSS, DO_PLACES, DO_UNPACK, DO_NORM1,
    DO_PROJECT, DO_CONV, DO_MIX, DO_EXPAND, DO_BEND, DO_FEED, DO_DRAIN, DO_GCON,
    DO_GEXP, DO_NORM2B, DO_BACKG, DO_GOUT, DO_CONVB, DO_GIN, DO_BFIRST, DO_NORM1B,
    DO_SMALL, DO_STAGE, DO_ACORE, DO_AY, DO_AX, DO_AZ1, DO_AZ2, DO_AZ3,
    DO_FIN, DO_END,
) = range(34)
SCHEDULE = (
    (DO_FIRST, 0), (DO_FIRST, 1), (DO_FIRST, 2), (DO_FIRST, 10), (DO_FIRST, 3), (DO_NEAR, 0),
    (DO_FIRST, 4), (DO_FIRST, 5), (DO_FIRST, 6), (DO_FIRST, 7), (DO_FIRST, 8), (DO_NEAR, 1),
    (DO_PLACES, 0), (DO_NEAR, 2), (DO_NEAR, 3), (DO_FAR, 0), (DO_NEAR, 4), (DO_FAR, 1), (DO_FAR, 2),
    (DO_FAR, 3), (DO_FAR, 4), (DO_NEAR, 10), (DO_NEAR, 5), (DO_SIDE, 1), (DO_NEAR, 8), (DO_SIDE, 0),
    (DO_UNPACK, 0), (DO_SIDE, 2), (DO_NORM1, 0), (DO_SIDE, 4), (DO_FIRST, 9), (DO_NEAR, 7),
    (DO_FIRST, 11), (DO_CROSS, 1), (DO_PROJECT, 1), (DO_SIDE, 3), (DO_FAR, 5), (DO_FAR, 7),
    (DO_CROSS, 2), (DO_FAR, 8), (DO_NEAR, 6), (DO_PROJECT, 2), (DO_CONV, 0), (DO_CONV, 1),
    (DO_FAR, 6), (DO_CROSS, 4), (DO_SIDE, 7), (DO_NEAR, 11), (DO_CROSS, 3), (DO_SIDE, 5),
    (DO_CONV, 2), (DO_CONV, 3), (DO_SIDE, 8), (DO_NEAR, 9), (DO_PROJECT, 0), (DO_FAR, 10),
    (DO_MIX, 0), (DO_CROSS, 7), (DO_EXPAND, 3), (DO_BEND, 3), (DO_SIDE, 6), (DO_FAR, 9),
    (DO_EXPAND, 2), (DO_BEND, 2), (DO_CROSS, 5), (DO_EXPAND, 1), (DO_BEND, 1), (DO_FAR, 11),
    (DO_EXPAND, 0), (DO_BEND, 0), (DO_GCON, 0), (DO_STAGE, (2, 0)), (DO_STAGE, (0, 0)),
    (DO_SIDE, 9), (DO_STAGE, (1, 0)), (DO_SIDE, 10), (DO_SIDE, 11), (DO_ACORE, (0, 0)),
    (DO_ACORE, (1, 0)), (DO_CROSS, 9), (DO_ACORE, (2, 0)), (DO_FEED, 0), (DO_FEED, 1), (DO_GEXP, 0),
    (DO_STAGE, (3, 0)), (DO_GEXP, 1), (DO_STAGE, (4, 0)), (DO_FEED, 2), (DO_GEXP, 2),
    (DO_STAGE, (3, 1)), (DO_ACORE, (4, 0)), (DO_ACORE, (3, 0)), (DO_FEED, 3), (DO_GEXP, 3),
    (DO_DRAIN, 0), (DO_STAGE, (4, 1)), (DO_AX, (2, 0)), (DO_NORM2B, 0), (DO_BACKG, 0), (DO_GOUT, 0),
    (DO_STAGE, (5, 0)), (DO_ACORE, (3, 1)), (DO_ACORE, (4, 1)), (DO_AZ1, (0, 0)), (DO_CONVB, 0),
    (DO_AX, (4, 0)), (DO_ACORE, (5, 0)), (DO_AY, (1, 0)), (DO_CONVB, 1), (DO_AY, (3, 1)),
    (DO_AY, (3, 0)), (DO_AX, (4, 1)), (DO_AZ1, (2, 0)), (DO_CONVB, 2), (DO_CONVB, 3),
    (DO_AX, (1, 0)), (DO_AY, (5, 0)), (DO_AZ2, (2, 0)), (DO_AZ3, (2, 0)), (DO_GIN, 1),
    (DO_STAGE, (6, 1)), (DO_AZ2, (0, 0)), (DO_AZ3, (0, 0)), (DO_AX, (3, 1)), (DO_ACORE, (6, 1)),
    (DO_STAGE, (7, 1)), (DO_GIN, 2), (DO_STAGE, (6, 2)), (DO_STAGE, (7, 2)), (DO_AZ1, (4, 0)),
    (DO_ACORE, (7, 1)), (DO_GIN, 0), (DO_AZ1, (4, 1)), (DO_STAGE, (7, 0)), (DO_STAGE, (6, 0)),
    (DO_AX, (3, 0)), (DO_AX, (5, 0)), (DO_ACORE, (6, 2)), (DO_ACORE, (7, 2)), (DO_ACORE, (7, 0)),
    (DO_ACORE, (6, 0)), (DO_BFIRST, 0), (DO_AX, (7, 1)), (DO_AZ1, (1, 0)), (DO_AY, (6, 1)),
    (DO_NORM1B, 0), (DO_SMALL, 0), (DO_STAGE, (8, 0)), (DO_AZ1, (3, 1)), (DO_AX, (7, 2)),
    (DO_AZ2, (4, 0)), (DO_ACORE, (8, 0)), (DO_AY, (6, 2)), (DO_AX, (0, 0)), (DO_AX, (7, 0)),
    (DO_AZ1, (3, 0)), (DO_AZ2, (3, 1)), (DO_AZ2, (4, 1)), (DO_AZ3, (3, 1)), (DO_AZ3, (4, 1)),
    (DO_AX, (6, 1)), (DO_AZ1, (5, 0)), (DO_AZ1, (7, 1)), (DO_AY, (6, 0)), (DO_AZ2, (3, 0)),
    (DO_AZ3, (3, 0)), (DO_AZ2, (1, 0)), (DO_AZ3, (1, 0)), (DO_AX, (8, 0)), (DO_AZ1, (7, 2)),
    (DO_AZ2, (7, 1)), (DO_AZ1, (7, 0)), (DO_AX, (6, 2)), (DO_AZ3, (4, 0)), (DO_AZ2, (5, 0)),
    (DO_AZ3, (5, 0)), (DO_FIN, (0, 0)), (DO_AX, (6, 0)), (DO_AZ3, (6, 1)), (DO_AZ3, (7, 1)),
    (DO_AZ3, (8, 0)), (DO_AZ2, (7, 2)), (DO_FIN, (4, 0)), (DO_AZ2, (7, 0)), (DO_FIN, (3, 0)),
    (DO_AZ3, (6, 2)), (DO_FIN, (4, 1)), (DO_FIN, (3, 1)), (DO_AZ3, (7, 2)), (DO_AZ3, (7, 0)),
    (DO_FIN, (6, 1)), (DO_AZ3, (6, 0)), (DO_FIN, (7, 1)), (DO_FIN, (1, 0)), (DO_FIN, (2, 0)),
    (DO_FIN, (6, 2)), (DO_FIN, (5, 0)), (DO_FIN, (8, 0)), (DO_FIN, (7, 0)), (DO_FIN, (7, 2)),
    (DO_FIN, (6, 0)), (DO_END, 0),
)
SMALL_ROWS = 64
HALF = 48
NORM_ROWS = 128
INNER_OUT = 8


def dot_nn(left_side, right_side):
    return jnp.dot(left_side, right_side, preferred_element_type=FULL)


def dot_nt(left_side, right_side):
    return lax.dot_general(
        left_side, right_side, (((1,), (1,)), ((), ())), preferred_element_type=FULL
    )


def dot_tn(left_side, right_side):
    return lax.dot_general(
        left_side, right_side, (((0,), (0,)), ((), ())), preferred_element_type=FULL
    )


def exact(left_side, right_side, contract):
    return lax.dot_general(
        left_side, right_side, (((contract[0],), (contract[1],)), ((), ())),
        preferred_element_type=FULL, precision=HIGHEST,
    )


def fold8(values):
    rows, columns = values.shape
    return jnp.sum(values.reshape(rows // 8, 8, columns), axis=0)


def widen(values, width):
    rows, columns = values.shape
    if columns == width:
        return values
    return jnp.concatenate([values, jnp.zeros((rows, width - columns), values.dtype)], axis=1)


def turn(values, amount, axis):
    size = values.shape[axis]
    amount = amount % size
    return values if amount == 0 else pltpu.roll(values, amount, axis)


def block_kernel(*refs):
    refs = list(refs)

    def take(number):
        taken = refs[:number]
        del refs[:number]
        return taken

    tokens_in, segs, cot_in = take(3)
    (
        r_first_gain, r_first_shift, r_in_bias, r_short_w, r_short_b, r_inner_w, r_inner_b,
        r_scale, r_middle_w, r_middle_b, r_filter_w, r_direct, r_out_bias, r_second_gain,
        r_second_shift, r_exp_bias, r_con_bias,
    ) = take(17)
    own = take(4)
    features, decay = take(2)
    result_out, delta_out = take(2)
    sums_out = take(5)
    tokens, cot, result, delta = take(4)
    sums = take(5)
    full = take(5)
    g_con, g_small, own_small, pack = take(4)
    v96, v288, vexp, v8 = take(4)
    mid_w, fil_w, taps, d_taps = take(4)
    s_inner1, s_first, s_cos1, s_inner2, s_second, s_cos2 = take(6)
    places, left = take(2)
    normed1, proj, short, conv, gated, resid, normed2 = take(7)
    hidden, post, pre, back_h, gather_out, back_s, back_m, bp = take(8)
    back_r, back_g = back_h, gather_out
    acc96, acc288, accexp = take(3)
    groups = []
    for matrix, columns, width, kind in REDUCE_GROUPS:
        names = ("core", "x", "z3", "last") if kind in FARS else ("core", "x", "z1", "z2", "z3", "last")
        names += ("y",) if kind in SPLITS else ()
        groups.append(dict(zip(names, take(len(names)))))
    ag_recv, ag_cross, ag_core, ag_send, own_sem, rs_recv, rs_y, rs_send, rs_end, out_sem = take(10)
    assert not refs

    own = list(own) + [own_small]
    grads = (full[2], full[2], g_con, full[3], g_small)

    def spot(m, column, width):
        if m in (0, 1):
            block = column // 768 if m == 0 else 3
            assert column % 768 + width <= 768
            return pl.ds(block * HALF, HALF), pl.ds(column % 768, width)
        return slice(None), pl.ds(column, width)

    rep = lax.axis_index("rep")
    shard = lax.axis_index("shard")
    y, c = rep // 2, rep % 2
    z, x = shard // 2, shard % 2
    pair = z // 2
    near_z = z + 1 - 2 * (z % 2)
    inner = ((z + 1) // 2) % 2 == 1
    to_near = (rep, near_z * 2 + x)
    to_mirror = (rep, (3 - z) * 2 + x)
    to_x = (rep, z * 2 + 1 - x)
    to_y = ((1 - y) * 2 + c, shard)
    to_c = (y * 2 + 1 - c, shard)
    own_pair = pl.ds(pair * 2, 2)
    other_pair = pl.ds((1 - pair) * 2, 2)

    loads = [
        pltpu.make_async_copy(own[m].at[c], full[m].at[z, x, c], own_sem.at[m]) for m in range(4)
    ] + [
        pltpu.make_async_copy(tokens_in, tokens, own_sem.at[5]),
        pltpu.make_async_copy(cot_in, cot, own_sem.at[6]),
    ]
    barrier = pltpu.get_barrier_semaphore()
    for target in (to_near, to_x, to_y, to_c):
        pl.semaphore_signal(barrier, inc=1, device_id=target, device_id_type=MESH_ID)

    @pl.when(inner)
    def _():
        pl.semaphore_signal(barrier, inc=1, device_id=to_mirror, device_id_type=MESH_ID)

    for load in loads:
        load.start()

    def remote(source, landing, send, recv, device):
        return pltpu.make_async_remote_copy(
            src_ref=source, dst_ref=landing, send_sem=send, recv_sem=recv,
            device_id=device, device_id_type=MESH_ID,
        )

    pack[...] = jnp.zeros_like(pack)
    for row, member in enumerate(
        (r_first_gain, r_first_shift, r_direct, r_out_bias, r_second_gain, r_second_shift, r_con_bias)
    ):
        pack[row : row + 1, 0:96] = member[...].astype(FULL).reshape(1, 96)
    in_bias, short_b = (m[...].astype(FULL).reshape(1, 288) for m in (r_in_bias, r_short_b))
    exp_bias = r_exp_bias[...].astype(FULL).reshape(1, 384)
    for block in range(3):
        lanes = 128 if block < 2 else 32
        span = slice(block * 128, block * 128 + lanes)
        top = 8 + block * 8
        pack[top : top + 1, 0:lanes] = in_bias[:, span]
        pack[top + 1 : top + 2, 0:lanes] = short_b[:, span]
        pack[top + 2 : top + 5, 0:lanes] = r_short_w[:, span].astype(FULL)
        pack[top + 5 : top + 6, :] = exp_bias[:, block * 128 : block * 128 + 128]
    for row, member in enumerate((r_inner_b, r_scale, r_middle_b)):
        pack[32 + row : 33 + row, 0:8] = member[...].astype(FULL).reshape(1, 8)
    pack[40:48, 0:64] = r_middle_w[...].astype(FULL)
    pack[48:56, 0:33] = r_inner_w[...].astype(FULL)
    pack[64:128, 0:96] = r_filter_w[...].astype(FULL)
    own_small[0] = pack[0:64, :].astype(LOW)
    own_small[1] = pack[64:128, :].astype(LOW)

    acc96[...] = jnp.zeros_like(acc96)
    acc288[...] = jnp.zeros_like(acc288)
    accexp[...] = jnp.zeros_like(accexp)
    d_taps[...] = jnp.zeros_like(d_taps)

    pl.semaphore_wait(barrier, 4 + ((z + 1) // 2) % 2)

    chunks = GATHER_CHUNKS
    count = len(chunks)
    cross_index = {}
    for index, chunk in enumerate(chunks):
        if chunk[3] == SPLIT:
            cross_index[index] = len(cross_index)
    NEAR, FAR, SIDE0, SIDE1 = range(4)
    S_NEAR, S_MIRROR, S_BACK, S_SIDE, S_CROSS, S_CORE = range(6)

    def part(chunk, quarter):
        matrix, column, width, kind = chunk
        if kind == SPLIT:
            return pl.ds(pl.multiple_of(column + quarter * (width // 2), 128), width // 2)
        return pl.ds(column, width)

    def whole(chunk):
        return pl.ds(chunk[1], chunk[2])

    small_load = pltpu.make_async_copy(own_small.at[c], full[4].at[z, x, c], own_sem.at[4])
    small_load.start()
    loads.append(small_load)

    send_groups = []
    for chunk in chunks:
        key = (chunk[0], chunk[3]) if chunk[0] != 3 else chunk[:2]
        if key not in send_groups:
            send_groups.append(key)

    def group_of(chunk):
        return send_groups.index((chunk[0], chunk[3]) if chunk[0] != 3 else chunk[:2])

    def first(index):
        chunk = chunks[index]
        m, s = chunk[0], group_of(chunk)
        piece = own[m].at[c, :, part(chunk, y)]
        landing = full[m].at[z, x, c, :, part(chunk, y)]
        if chunk[3] == LINE:
            remote(piece, landing, ag_send.at[S_SIDE, s], ag_recv.at[SIDE0, index], to_x).start()
        elif chunk[3] == WHOLE_FAR:
            for step, sent, slot in straight:
                remote(
                    piece, landing, ag_send.at[sent, s], ag_recv.at[slot, index],
                    (rep, ((z + step) % 4) * 2 + x),
                ).start()
        else:
            remote(piece, landing, ag_send.at[S_NEAR, s], ag_recv.at[NEAR, index], to_near).start()

    straight = ((1, S_NEAR, NEAR), (2, S_MIRROR, FAR), (3, S_BACK, SIDE1))

    def straight_far(index):
        chunk = chunks[index]
        m, s = chunk[0], group_of(chunk)
        for step, sent, slot in straight:
            arrived = full[m].at[(z + 4 - step) % 4, x, c, :, whole(chunk)]
            remote(arrived, arrived, ag_send.at[sent, s], ag_recv.at[slot, index], to_near).wait_recv()
        column = full[m].at[:, x, c, :, whole(chunk)]
        remote(column, column, ag_send.at[S_SIDE, s], ag_recv.at[SIDE0, index], to_x).start()

    def straight_side(index):
        chunk = chunks[index]
        m, s = chunk[0], group_of(chunk)
        column = full[m].at[:, 1 - x, c, :, whole(chunk)]
        remote(column, column, ag_send.at[S_SIDE, s], ag_recv.at[SIDE0, index], to_x).wait_recv()
        to_core(index)

    def line_near(index):
        chunk = chunks[index]
        m, s = chunk[0], group_of(chunk)
        arrived = full[m].at[z, 1 - x, c, :, whole(chunk)]
        remote(arrived, arrived, ag_send.at[S_SIDE, s], ag_recv.at[SIDE0, index], to_x).wait_recv()
        both = full[m].at[z, :, c, :, whole(chunk)]
        remote(both, both, ag_send.at[S_NEAR, s], ag_recv.at[NEAR, index], to_near).start()

    def line_far(index):
        chunk = chunks[index]
        m, s = chunk[0], group_of(chunk)
        arrived = full[m].at[near_z, :, c, :, whole(chunk)]
        remote(arrived, arrived, ag_send.at[S_NEAR, s], ag_recv.at[NEAR, index], to_near).wait_recv()

        @pl.when(inner)
        def _():
            four = full[m].at[own_pair, :, c, :, whole(chunk)]
            remote(four, four, ag_send.at[S_MIRROR, s], ag_recv.at[FAR, index], to_mirror).start()

    def line_side(index):
        chunk = chunks[index]
        m, s = chunk[0], group_of(chunk)
        four = full[m].at[other_pair, :, c, :, whole(chunk)]
        remote(four, four, ag_send.at[S_MIRROR, s], ag_recv.at[FAR, index], to_near).wait_recv()

        @pl.when(inner)
        def _():
            remote(four, four, ag_send.at[S_BACK, s], ag_recv.at[FAR, index], to_near).start()

        to_core(index)

    def near(index):
        chunk = chunks[index]
        if chunk[3] == LINE:
            return line_near(index)
        m, s = chunk[0], group_of(chunk)
        arrived = full[m].at[near_z, x, c, :, part(chunk, y)]
        remote(arrived, arrived, ag_send.at[S_NEAR, s], ag_recv.at[NEAR, index], to_near).wait_recv()
        both = full[m].at[own_pair, x, c, :, part(chunk, y)]

        @pl.when(inner)
        def _():
            remote(both, both, ag_send.at[S_MIRROR, s], ag_recv.at[FAR, index], to_mirror).start()

        remote(both, both, ag_send.at[S_SIDE, s], ag_recv.at[SIDE0, index], to_x).start()
        if chunk[3] == SPLIT:
            remote(
                arrived, arrived, ag_send.at[S_CROSS, s], ag_cross.at[0, cross_index[index]], to_y
            ).start()

    def far(index):
        chunk = chunks[index]
        if chunk[3] == LINE:
            return line_far(index)
        if chunk[3] == WHOLE_FAR:
            return straight_far(index)
        m, s = chunk[0], group_of(chunk)
        both = full[m].at[other_pair, x, c, :, part(chunk, y)]
        remote(both, both, ag_send.at[S_MIRROR, s], ag_recv.at[FAR, index], to_near).wait_recv()

        @pl.when(inner)
        def _():
            remote(both, both, ag_send.at[S_BACK, s], ag_recv.at[FAR, index], to_near).start()

        remote(both, both, ag_send.at[S_SIDE, s], ag_recv.at[SIDE1, index], to_x).start()
        if chunk[3] == SPLIT:
            remote(
                both, both, ag_send.at[S_CROSS, s], ag_cross.at[1, cross_index[index]], to_y
            ).start()

    def to_core(index):
        chunk = chunks[index]
        m, s = chunk[0], group_of(chunk)
        piece = full[m].at[:, :, c, :, whole(chunk)]
        remote(piece, piece, ag_send.at[S_CORE, s], ag_core.at[index], to_c).start()

    def side(index):
        chunk = chunks[index]
        if chunk[3] == LINE:
            return line_side(index)
        if chunk[3] == WHOLE_FAR:
            return straight_side(index)
        m, s = chunk[0], group_of(chunk)
        for place, slot in ((own_pair, SIDE0), (other_pair, SIDE1)):
            both = full[m].at[place, 1 - x, c, :, part(chunk, y)]
            remote(both, both, ag_send.at[S_SIDE, s], ag_recv.at[slot, index], to_x).wait_recv()
        if chunk[3] == SPLIT:
            column = full[m].at[:, 1 - x, c, :, part(chunk, y)]
            remote(
                column, column, ag_send.at[S_CROSS, s], ag_cross.at[2, cross_index[index]], to_y
            ).start()
        else:
            to_core(index)

    def cross(index):
        chunk = chunks[index]
        m, s = chunk[0], group_of(chunk)
        for slot, piece in enumerate(
            (
                full[m].at[near_z, x, c, :, part(chunk, 1 - y)],
                full[m].at[other_pair, x, c, :, part(chunk, 1 - y)],
                full[m].at[:, 1 - x, c, :, part(chunk, 1 - y)],
            )
        ):
            remote(
                piece, piece, ag_send.at[S_CROSS, s], ag_cross.at[slot, cross_index[index]], to_y
            ).wait_recv()
        to_core(index)

    waited = set()

    def settled(m, low, high):
        for index, chunk in enumerate(chunks):
            inside = chunk[0] == m and chunk[1] < high and chunk[1] + chunk[2] > low
            if inside and index not in waited:
                waited.add(index)
                piece = full[m].at[:, :, 1 - c, :, whole(chunk)]
                send = ag_send.at[S_CORE, group_of(chunk)]
                remote(piece, piece, send, ag_core.at[index], to_c).wait_recv()

    loaded = []

    def ready():
        if not loaded:
            loaded.append(True)
            for load in loads:
                load.wait()


    def row_blocks(size, action):
        def body(step, carry):
            action(pl.ds(pl.multiple_of(step * size, size), size))
            return carry

        lax.fori_loop(0, tokens.shape[0] // size, body, 0)

    def find_places():
        rows = lax.broadcasted_iota(jnp.int32, (128, 128), 0)
        columns = lax.broadcasted_iota(jnp.int32, (128, 128), 1)
        for sequence in range(2):
            ids = jnp.broadcast_to(segs[sequence : sequence + 1, :].astype(FULL), (128, 128))
            same = ids == ids.T
            before = jnp.sum(jnp.where(same & (columns < rows), 1.0, 0.0), axis=1, keepdims=True)
            after = jnp.sum(jnp.where(same & (columns > rows), 1.0, 0.0), axis=1, keepdims=True)
            span = slice(sequence * 128, sequence * 128 + 128)
            places[span, :] = jnp.broadcast_to(before.astype(jnp.int32), (128, 128))
            left[span, :] = jnp.broadcast_to(after.astype(jnp.int32), (128, 128))

    def unpack_small():
        total96 = jnp.zeros((8, 768), FULL)
        total288 = jnp.zeros((8, 2304), FULL)
        total8 = jnp.zeros((8, 128), FULL)
        inner_rows = []
        fil_w[...] = jnp.zeros_like(fil_w)
        mid_w[...] = jnp.zeros_like(mid_w)
        for s in range(8):
            top = full[4][s // 2, s % 2, 0].astype(FULL)
            low = full[4][s // 2, s % 2, 1].astype(FULL)
            total96 = total96 + turn(widen(top[0:8], 768), 96 * s, 1)
            wide = jnp.concatenate([top[8:16], top[16:24], top[24:32]], axis=1)
            vexp[:, s * 384 : s * 384 + 384] = wide[5:6]
            total288 = total288 + turn(widen(wide, 2304), 288 * s, 1)
            total8 = total8 + turn(top[32:40], 8 * s, 1)
            inner_rows.append(top[48:56])
            mid_w[8 * s : 8 * s + 8, :] = top[40:48]
            fil_w[0:64, :] += turn(widen(low, 768), 96 * s, 1)
        v96[...] = total96
        v288[...] = total288
        v8[...] = total8
        scale = total8[1:2]
        inner_all = jnp.concatenate(inner_rows + [jnp.zeros((64, 128), FULL)], axis=0)
        inner1 = exact(features[...], inner_all, (1, 1)) + total8[0:1]
        s_inner1[...] = inner1
        s_first[...] = jnp.sin(scale * inner1)
        s_cos1[...] = jnp.cos(scale * inner1)
        inner2 = exact(s_first[...], mid_w[...], (1, 0)) + total8[2:3]
        s_inner2[...] = inner2
        s_second[...] = jnp.sin(scale * inner2)
        s_cos2[...] = jnp.cos(scale * inner2)
        taps[...] = exact(s_second[...], fil_w[...], (1, 0)) * decay[...]

    def center(values):
        middle = values - jnp.mean(values, axis=-1, keepdims=True)
        spread = jnp.mean(middle * middle, axis=-1, keepdims=True)
        scale = lax.rsqrt(spread + EPSILON)
        return middle * scale, scale

    def norm_first(rows):
        unit, _ = center(tokens[rows, :].astype(FULL))
        normed1[rows, :] = (unit * v96[0:1, :] + v96[1:2, :]).astype(LOW)

    def matrix_of(m, columns, width):
        value = full[m][:, :, :, :, columns]
        return value.reshape(value.shape[0] * value.shape[1] * value.shape[2] * value.shape[3], width)

    def project(k):
        span = slice(k * 768, k * 768 + 768)
        proj[k] = dot_nn(normed1[...], matrix_of(0, pl.ds(k * 768, 768), 768)) + v288[0:1, span]

        def body(step, carry):
            rows = pl.ds(pl.multiple_of((step // 6) * 128, 128), 128)
            lane = pl.multiple_of((step % 6) * 128, 128)
            lanes = pl.ds(lane, 128)
            wide = pl.ds(pl.multiple_of(k * 768 + lane, 128), 128)
            values = proj[k, rows, lanes]
            where = places[rows, :]
            total = v288[1:2, wide] + v288[2:3, wide] * values
            for lag in (1, 2):
                moved = jnp.where(where >= lag, pltpu.roll(values, lag, 0), 0.0)
                total = total + v288[2 + lag : 3 + lag, wide] * moved
            short[k, rows, lanes] = total
            return carry

        lax.fori_loop(0, 12, body, 0)

    def convolve(begin, end):
        def body(step, carry):
            rows = pl.ds(pl.multiple_of((step // 6) * 128, 128), 128)
            lanes = pl.ds(pl.multiple_of((step % 6) * 128, 128), 128)
            carried = short[2, rows, lanes] * short[1, rows, lanes]
            where = places[rows, :]
            total = v96[2:3, lanes] * carried
            for low_lag in range(8):
                moved = turn(carried, low_lag, 0)
                for high in range(LAGS // 8):
                    lag, skip = high * 8 + low_lag, high * 8
                    term = jnp.where(
                        where[skip:] >= lag, taps[lag : lag + 1, lanes] * moved[: 128 - skip], 0.0
                    )
                    if skip:
                        total = jnp.concatenate([total[:skip], total[skip:] + term], axis=0)
                    else:
                        total = total + term
            conv[rows, lanes] = total
            return carry

        lax.fori_loop(begin, end, body, 0)

    def mix_out():
        def gate(rows):
            gated[rows, :] = (conv[rows, :] * short[0, rows, :]).astype(LOW)

        row_blocks(NORM_ROWS, gate)
        resid[...] = dot_nn(gated[...], matrix_of(1, pl.ds(0, 768), 768))

        def finish_rows(rows):
            values = resid[rows, :] + tokens[rows, :].astype(FULL) + v96[3:4, :]
            resid[rows, :] = values
            unit, _ = center(values)
            normed2[rows, :] = (unit * v96[4:5, :] + v96[5:6, :]).astype(LOW)

        row_blocks(NORM_ROWS, finish_rows)

    def expand(k):
        span = slice(k * 768, k * 768 + 768)
        hidden[:, span] = (
            dot_nn(normed2[...], matrix_of(3, pl.ds(k * 768, 768), 768)) + vexp[:, span]
        )

    fed_before = []

    def bend(k):
        span = slice(k * 768, k * 768 + 768)

        def curve(rows):
            values = hidden[rows, span]
            cube = values * values
            grow = math.sqrt(2.0 / math.pi)
            slope = jnp.tanh(grow * (values + 0.044715 * cube * values))
            half_up = 0.5 + 0.5 * slope
            post[rows, span] = (values * half_up).astype(LOW)
            hidden[rows, span] = half_up + (0.5 * values) * (1.0 - slope * slope) * (
                grow * (1.0 + 3.0 * 0.044715 * cube)
            )

        row_blocks(16, curve)

    def feed(k):
        span = slice(k * 768, k * 768 + 768)
        back_h[...] = dot_nt(cot[...], full[2][k].reshape(768, 768))

        def scale_back(rows):
            grad = (back_h[rows, :] * hidden[rows, span]).astype(LOW)
            pre[rows, span] = grad
            accexp[:, span] += fold8(grad.astype(FULL))

        row_blocks(32, scale_back)
        out_part = dot_nn(post[:, span], full[2][k].reshape(768, 768))
        back_part = dot_nt(pre[:, span], matrix_of(3, pl.ds(k * 768, 768), 768))
        if not fed_before:
            gather_out[...] = out_part
            back_s[...] = back_part
            fed_before.append(k)
        else:
            gather_out[...] += out_part
            back_s[...] += back_part

    drained = set()

    def drain(m, low, high):
        for s, key in enumerate(send_groups):
            members = [
                chunk for chunk in chunks
                if group_of(chunk) == s and m == chunk[0]
                and chunk[1] < high and chunk[1] + chunk[2] > low
            ]
            if not members or s in drained:
                continue
            drained.add(s)
            members = [chunk for chunk in chunks if group_of(chunk) == s]
            kind = members[0][3]
            assert all(chunk[3] == kind for chunk in members)
            wide = sum(chunk[2] for chunk in members)
            thin = wide // 2 if kind == SPLIT else wide

            def gone(slot, planes, rows, width=thin, s=s):
                ref = full[m].at[pl.ds(0, planes), pl.ds(0, rows), 0, :, pl.ds(0, width)]
                remote(ref, ref, ag_send.at[slot, s], ag_recv.at[FAR, 0], to_near).wait_send()

            if kind == LINE:
                gone(S_SIDE, 1, 1)
                gone(S_NEAR, 2, 1)
            else:
                gone(S_NEAR, 1, 1)
                gone(S_SIDE, 4, 1)

            if kind == WHOLE_FAR:
                gone(S_MIRROR, 1, 1)
                gone(S_BACK, 1, 1)
                gone(S_CORE, 4, 2, wide)
                continue

            @pl.when(inner)
            def _(gone=gone, kind=kind):
                gone(S_MIRROR, 2, 2 if kind == LINE else 1)
                gone(S_BACK, 2, 2 if kind == LINE else 1)

            if kind == SPLIT:
                gone(S_CROSS, 3, 1)
                gone(S_CROSS, 4, 1)
            gone(S_CORE, 4, 2, wide)

    position = {}
    split_position = {}
    for index, key in enumerate(REDUCE_ORDER):
        position[key] = index
        if REDUCE_GROUPS[key[0]][3] in SPLITS:
            split_position[key] = len(split_position)
    R_CORE, R_X, R_Z1, R_Z2, R_Z3, R_LAST = range(6)
    W_CORE, W_Y, W_X, W_Z1, W_Z3, W_LAST, W_END, W_Z4 = range(8)
    W_Z2 = W_Z1

    def info(key):
        g, i = key
        matrix, columns, width, kind = REDUCE_GROUPS[g]
        return g, i, matrix, columns[i], width, kind, groups[g], position[key]

    def halves(width, which):
        return pl.ds(pl.multiple_of(which * (width // 2), 128), width // 2)

    def stage(key):
        g, i, m, column, width, kind, buf, n = info(key)
        high, wide = spot(m, column, width)
        remote(
            grads[m].at[:, :, 1 - c, high, wide], buf["core"].at[i],
            rs_send.at[W_CORE, g], rs_recv.at[R_CORE, n], to_c,
        ).start()

    def running(key):
        g, i, m, column, width, kind, buf, n = info(key)
        return buf["core"] if kind == LINE else buf["x"]

    def send_line(key):
        g, i, m, column, width, kind, buf, n = info(key)
        sums_ref = running(key)
        if kind in FARS:
            for step, sent, slot in ((1, W_Z1, R_Z1), (2, W_Z3, R_Z2), (3, W_Z4, R_Z3)):
                at = (z + step) % 4
                remote(
                    sums_ref.at[i, at], buf["z3"].at[i, step - 1],
                    rs_send.at[sent, g], rs_recv.at[slot, n], (rep, at * 2 + x),
                ).start()
            return

        @pl.when(jnp.logical_not(inner))
        def _():
            remote(
                sums_ref.at[i, other_pair], buf["z1"].at[i],
                rs_send.at[W_Z1, g], rs_recv.at[R_Z1, n], to_near,
            ).start()
            remote(
                sums_ref.at[i, near_z], buf["z3"].at[i],
                rs_send.at[W_Z3, g], rs_recv.at[R_Z3, n], to_near,
            ).start()

    def add_core(key):
        g, i, m, column, width, kind, buf, n = info(key)
        landing = buf["core"].at[i]
        remote(landing, landing, rs_send.at[W_CORE, g], rs_recv.at[R_CORE, n], to_c).wait_recv()
        high, wide = spot(m, column, width)

        def body(step, carry):
            a, b = step // 2, step % 2
            buf["core"][i, a, b] = buf["core"][i, a, b] + grads[m][a, b, c, high, wide]
            return carry

        lax.fori_loop(0, 8, body, 0)
        if kind in SPLITS:
            remote(
                buf["core"].at[i, :, :, :, halves(width, 1 - y)], buf["y"].at[i],
                rs_send.at[W_Y, g], rs_y.at[split_position[key]], to_y,
            ).start()
        elif kind != LINE:
            remote(
                buf["core"].at[i, :, 1 - x], buf["x"].at[i],
                rs_send.at[W_X, g], rs_recv.at[R_X, n], to_x,
            ).start()
        else:
            send_line(key)

    def add_y(key):
        g, i, m, column, width, kind, buf, n = info(key)
        landing = buf["y"].at[i]
        remote(landing, landing, rs_send.at[W_Y, g], rs_y.at[split_position[key]], to_y).wait_recv()

        def body(step, carry):
            a, b = step // 2, step % 2
            buf["y"][i, a, b] = buf["y"][i, a, b] + buf["core"][i, a, b, :, halves(width, y)]
            return carry

        lax.fori_loop(0, 8, body, 0)
        remote(
            buf["y"].at[i, :, 1 - x], buf["x"].at[i], rs_send.at[W_X, g], rs_recv.at[R_X, n], to_x
        ).start()

    def send_last(key):
        g, i, m, column, width, kind, buf, n = info(key)
        remote(
            buf["last"].at[i, 0], buf["last"].at[i, 1],
            rs_send.at[W_LAST, g], rs_recv.at[R_LAST, n], to_y,
        ).start()

    def add_x(key):
        g, i, m, column, width, kind, buf, n = info(key)
        landing = buf["x"].at[i]
        remote(landing, landing, rs_send.at[W_X, g], rs_recv.at[R_X, n], to_x).wait_recv()
        if kind == LINE:
            buf["last"][i, 0] = buf["core"][i, z, x] + buf["x"][i]
            send_last(key)
            return
        own_part = buf["y"] if kind in SPLITS else buf["core"]

        def body(step, carry):
            buf["x"][i, step] = buf["x"][i, step] + own_part[i, step, x]
            return carry

        lax.fori_loop(0, 4, body, 0)
        send_line(key)

    def add_z1(key):
        g, i, m, column, width, kind, buf, n = info(key)
        sums_ref = running(key)

        @pl.when(inner)
        def _():
            landing = buf["z1"].at[i]
            remote(landing, landing, rs_send.at[W_Z1, g], rs_recv.at[R_Z1, n], to_near).wait_recv()
            for step in range(2):
                at = (1 - pair) * 2 + step
                sums_ref[i, at] = sums_ref[i, at] + buf["z1"][i, step]
            remote(
                sums_ref.at[i, other_pair], buf["z2"].at[i],
                rs_send.at[W_Z2, g], rs_recv.at[R_Z2, n], to_mirror,
            ).start()

    def add_z2(key):
        g, i, m, column, width, kind, buf, n = info(key)
        sums_ref = running(key)

        @pl.when(inner)
        def _():
            landing = buf["z2"].at[i]
            remote(landing, landing, rs_send.at[W_Z2, g], rs_recv.at[R_Z2, n], to_mirror).wait_recv()
            for step in range(2):
                at = pair * 2 + step
                sums_ref[i, at] = sums_ref[i, at] + buf["z2"][i, step]
            remote(
                sums_ref.at[i, near_z], buf["z3"].at[i],
                rs_send.at[W_Z3, g], rs_recv.at[R_Z3, n], to_near,
            ).start()

    def add_z3(key):
        g, i, m, column, width, kind, buf, n = info(key)
        if kind in FARS:
            total = buf["x"][i, z].astype(FULL)
            for step, sent, slot in ((1, W_Z1, R_Z1), (2, W_Z3, R_Z2), (3, W_Z4, R_Z3)):
                landing = buf["z3"].at[i, step - 1]
                remote(landing, landing, rs_send.at[sent, g], rs_recv.at[slot, n], to_near).wait_recv()
                total = total + buf["z3"][i, step - 1].astype(FULL)
            buf["last"][i, 0] = total.astype(buf["last"].dtype)
            send_last(key)
            return
        landing = buf["z3"].at[i]
        remote(landing, landing, rs_send.at[W_Z3, g], rs_recv.at[R_Z3, n], to_near).wait_recv()
        if kind == LINE:
            buf["core"][i, z] = buf["core"][i, z] + buf["z3"][i]
            remote(
                buf["core"].at[i, z, 1 - x], buf["x"].at[i],
                rs_send.at[W_X, g], rs_recv.at[R_X, n], to_x,
            ).start()
            return
        buf["last"][i, 0] = buf["x"][i, z] + buf["z3"][i]
        send_last(key)

    def finish(key):
        g, i, m, column, width, kind, buf, n = info(key)
        landing = buf["last"].at[i, 1]
        remote(landing, landing, rs_send.at[W_LAST, g], rs_recv.at[R_LAST, n], to_y).wait_recv()
        if kind in SPLITS:
            for which, slot in ((y, 0), (1 - y, 1)):
                columns = pl.ds(pl.multiple_of(column + which * (width // 2), 128), width // 2)
                sums[m][:, columns] = buf["last"][i, slot].astype(sums[m].dtype)
        else:
            total = buf["last"][i, 0].astype(FULL) + buf["last"][i, 1].astype(FULL)
            sums[m][:, pl.ds(column, width)] = total.astype(sums[m].dtype)
        piece = sums[m].at[:, pl.ds(column, width)]
        place = sums_out[m].at[c, :, pl.ds(column, width)]
        remote(piece, place, rs_send.at[W_END, g], rs_end.at[g], to_c).start()
        pltpu.make_async_copy(piece, place, out_sem.at[g]).start()

    def grad_contract():
        def body(s, carry):
            lanes = pl.ds(pl.multiple_of(s * 384, 128), 384)
            value = dot_tn(post[:, lanes], cot[...]).astype(LOW)
            g_con[s // 2, s % 2] = value.reshape(2, 192, 768)
            return carry

        lax.fori_loop(0, 8, body, 0)

    def grad_rows(source, other, target, high, columns, width):
        for half in range(2):
            value = dot_tn(source[:, half * 384 : half * 384 + 384], other).astype(LOW)
            target[2 * half : 2 * half + 2, :, :, high, columns] = value.reshape(2, 2, 2, 48, width)

    def grad_expand(i):
        span = slice(i * 768, i * 768 + 768)
        grad_rows(normed2, pre[:, span], full[3], slice(None), pl.ds(i * 768, 768), 768)

    def norm_second_back(rows):
        unit, scale = center(resid[rows, :])
        grad = back_s[rows, :]
        top = cot[rows, :].astype(FULL)
        e = grad * v96[4:5, :]
        value = (
            e - jnp.mean(e, axis=-1, keepdims=True) - unit * jnp.mean(e * unit, axis=-1, keepdims=True)
        ) * scale + top
        back_r[rows, :] = value
        rounded = value.astype(LOW)
        back_m[rows, :] = rounded
        acc96[4] += fold8(grad * unit)
        acc96[5] += fold8(grad)
        acc96[3] += fold8(rounded.astype(FULL))
        acc96[6] += fold8(top)
        result[rows, :] = (resid[rows, :] + gather_out[rows, :] + v96[6:7, :]).astype(LOW)

    def convolve_back(begin, end):
        def body(step, carry):
            rows = pl.ds(pl.multiple_of((step // 6) * 128, 128), 128)
            lane = pl.multiple_of((step % 6) * 128, 128)
            lanes = pl.ds(lane, 128)
            where = places[rows, :]
            rest = left[rows, :]
            gate_in = short[1, rows, lanes]
            values = short[2, rows, lanes]
            top = back_g[rows, lanes]
            carried = values * gate_in
            back_conv = top * short[0, rows, lanes]
            acc96[2, :, lanes] += fold8(back_conv * carried)
            total = v96[2:3, lanes] * back_conv
            for low_lag in range(8):
                turned = turn(back_conv, -low_lag, 0)
                for high in range(LAGS // 8):
                    lag, skip = high * 8 + low_lag, high * 8
                    size = 128 - skip
                    moved = jnp.where(rest[:size] >= lag, turned[skip:], 0.0)
                    term = taps[lag : lag + 1, lanes] * moved
                    if skip:
                        total = jnp.concatenate([total[:size] + term, total[size:]], axis=0)
                    else:
                        total = total + term
                    d_taps[lag : lag + 1, lanes] += jnp.sum(
                        moved * carried[:size], axis=0, keepdims=True
                    )
            streams = (top * conv[rows, lanes], total * values, total * gate_in)
            for k in range(3):
                wide = pl.ds(pl.multiple_of(k * 768 + lane, 128), 128)
                grad = streams[k]
                before = proj[k, rows, lanes]
                acc288[1, :, wide] += fold8(grad)
                acc288[2, :, wide] += fold8(grad * before)
                value = v288[2:3, wide] * grad
                for lag in (1, 2):
                    moved = jnp.where(where >= lag, pltpu.roll(before, lag, 0), 0.0)
                    acc288[2 + lag, :, wide] += fold8(grad * moved)
                    later = jnp.where(rest >= lag, pltpu.roll(grad, 128 - lag, 0), 0.0)
                    value = value + v288[2 + lag : 3 + lag, wide] * later
                rounded = value.astype(LOW)
                bp[k, rows, lanes] = rounded
                acc288[0, :, wide] += fold8(rounded.astype(FULL))
            return carry

        lax.fori_loop(begin, end, body, 0)

    def norm_first_back(rows):
        unit, scale = center(tokens[rows, :].astype(FULL))
        grad = back_s[rows, :]
        e = grad * v96[0:1, :]
        delta[rows, :] = back_r[rows, :] + (
            e - jnp.mean(e, axis=-1, keepdims=True) - unit * jnp.mean(e * unit, axis=-1, keepdims=True)
        ) * scale
        acc96[0] += fold8(grad * unit)
        acc96[1] += fold8(grad)

    def small_grads():
        scale = v8[1:2, :]
        raw = d_taps[...] * decay[...]
        d_fil = exact(s_second[...], raw, (0, 0))
        b2 = exact(raw, fil_w[...], (1, 1)) * s_cos2[...]
        b2s = b2 * scale
        d_mid = exact(s_first[...], b2s, (0, 0))
        b1 = exact(b2s, mid_w[...], (1, 1)) * s_cos1[...]
        b1s = b1 * scale
        d_inner = exact(b1s, features[...], (0, 0))
        d_scale = jnp.sum(b2 * s_inner2[...] + b1 * s_inner1[...], axis=0, keepdims=True)
        rows8 = jnp.concatenate(
            [
                jnp.sum(b1s, axis=0, keepdims=True), d_scale, jnp.sum(b2s, axis=0, keepdims=True),
                jnp.zeros((5, 128), FULL),
            ],
            axis=0,
        )
        rows96 = jnp.concatenate(
            [jnp.sum(acc96[f], axis=0, keepdims=True) for f in range(7)] + [jnp.zeros((1, 768), FULL)],
            axis=0,
        )
        rows288 = jnp.concatenate(
            [jnp.sum(acc288[f], axis=0, keepdims=True) for f in range(5)]
            + [jnp.zeros((3, 2304), FULL)],
            axis=0,
        )
        rows_exp = jnp.sum(accexp[...], axis=0, keepdims=True)
        lane = lax.broadcasted_iota(jnp.int32, (8, 128), 1)
        row = lax.broadcasted_iota(jnp.int32, (8, 128), 0)
        wide_lane = lax.broadcasted_iota(jnp.int32, (64, 128), 1)
        for s in range(8):
            a, b = s // 2, s % 2
            g_small[a, b, 0, 0:8, :] = jnp.where(lane < 96, turn(rows96, -96 * s, 1)[:, :128], 0.0)
            turned = turn(rows288, -288 * s, 1)
            for block in range(3):
                value = turned[:, block * 128 : block * 128 + 128]
                if block == 2:
                    value = jnp.where(lane < 32, value, 0.0)
                bias = rows_exp[:, s * 384 + block * 128 : s * 384 + block * 128 + 128]
                value = jnp.where(row == 5, jnp.broadcast_to(bias, (8, 128)), value)
                g_small[a, b, 0, 8 + block * 8 : 16 + block * 8, :] = value
            g_small[a, b, 0, 32:40, :] = jnp.where(lane < 8, turn(rows8, -8 * s, 1), 0.0)
            g_small[a, b, 0, 40:48, :] = d_mid[8 * s : 8 * s + 8]
            g_small[a, b, 0, 48:56, :] = d_inner[8 * s : 8 * s + 8]
            g_small[a, b, 0, 56:64, :] = jnp.zeros((8, 128), FULL)
            g_small[a, b, 1] = jnp.where(
                wide_lane < 96, turn(d_fil[0:64], -96 * s, 1)[:, :128], 0.0
            )

    def back_gate():
        back_g[...] = dot_nt(back_m[...], matrix_of(1, pl.ds(0, 768), 768))

    def back_first():
        for k in range(3):
            value = dot_nt(bp[k], matrix_of(0, pl.ds(k * 768, 768), 768))
            if k == 0:
                back_s[...] = value
            else:
                back_s[...] += value

    def unpack(k):
        settled(4, 0, 128)
        unpack_small()

    def projected(k):
        settled(0, k * 768, k * 768 + 768)
        project(k)

    def mix(k):
        settled(1, 0, 768)
        mix_out()

    def expanded(k):
        settled(3, k * 768, k * 768 + 768)
        expand(k)

    def fed(k):
        settled(2, 0, 768)
        feed(k)

    outgoing = [
        pltpu.make_async_copy(result, result_out, own_sem.at[7]),
        pltpu.make_async_copy(delta, delta_out, own_sem.at[8]),
    ]

    def second_back(k):
        row_blocks(NORM_ROWS, norm_second_back)
        outgoing[0].start()

    def first_back(k):
        row_blocks(NORM_ROWS, norm_first_back)
        outgoing[1].start()

    def expand_back(k):
        drain(3, k * 768, k * 768 + 768)
        grad_expand(k)

    def end(k):
        for copy in outgoing:
            copy.wait()
        for m in range(5):
            drain(m, 0, full[m].shape[4])

    actions = {
        DO_FIRST: first, DO_NEAR: near, DO_FAR: far, DO_SIDE: side, DO_CROSS: cross,
        DO_PLACES: lambda k: find_places(),
        DO_UNPACK: unpack,
        DO_NORM1: lambda k: row_blocks(NORM_ROWS, norm_first),
        DO_PROJECT: projected,
        DO_CONV: lambda k: convolve(3 * k, 3 * k + 3),
        DO_MIX: mix,
        DO_EXPAND: expanded,
        DO_BEND: bend,
        DO_FEED: fed,
        DO_DRAIN: lambda k: drain(2, 0, 768),
        DO_GCON: lambda k: grad_contract(),
        DO_GEXP: expand_back,
        DO_NORM2B: second_back,
        DO_BACKG: lambda k: back_gate(),
        DO_GOUT: lambda k: grad_rows(gated, back_m[...], full[2], pl.ds(3 * HALF, HALF), pl.ds(0, 768), 768),
        DO_CONVB: lambda k: convolve_back(3 * k, 3 * k + 3),
        DO_GIN: lambda k: grad_rows(normed1, bp[k], full[2], pl.ds(k * HALF, HALF), pl.ds(0, 768), 768),
        DO_BFIRST: lambda k: back_first(),
        DO_NORM1B: first_back,
        DO_SMALL: lambda k: small_grads(),
        DO_STAGE: stage, DO_ACORE: add_core, DO_AY: add_y, DO_AX: add_x, DO_AZ1: add_z1,
        DO_AZ2: add_z2, DO_AZ3: add_z3, DO_FIN: finish, DO_END: end,
    }
    for name, which in SCHEDULE:
        if name != DO_FIRST:
            ready()
        actions[name](which)

    for g, (matrix, columns, width, kind) in enumerate(REDUCE_GROUPS):
        held = sums[matrix].at[:, pl.ds(0, width * len(columns))]
        place = sums_out[matrix].at[1 - c, :, pl.ds(0, width * len(columns))]
        remote(held, place, rs_send.at[W_END, g], rs_end.at[g], to_c).wait_recv()
        pltpu.make_async_copy(held, place, out_sem.at[g]).wait()
    for g, (matrix, columns, width, kind) in enumerate(REDUCE_GROUPS):
        buf = groups[g]

        def leave(kind, ref, g=g):
            remote(ref, ref, rs_send.at[kind, g], rs_end.at[g], to_c).wait_send()

        leave(W_CORE, buf["core"])
        if kind in SPLITS:
            leave(W_Y, buf["y"])
        leave(W_X, buf["x"])
        if kind in FARS:
            for step, sent in enumerate((W_Z1, W_Z3, W_Z4)):
                leave(sent, buf["z3"].at[:, step])
        else:
            leave(W_Z3, buf["z3"])
            leave(W_Z1, buf["z1"])
        leave(W_LAST, buf["last"].at[:, 0])
        leave(W_END, sums[matrix].at[:, pl.ds(0, width * len(columns))])


def unpack_kernel(result, delta, s_in, s_out, s_con, s_exp, s_small, *outs):
    (
        o_result, o_delta, o_first_gain, o_first_shift, o_in, o_in_bias, o_short_w, o_short_b,
        o_inner_w, o_inner_b, o_scale, o_middle_w, o_middle_b, o_filter_w, o_direct, o_out,
        o_out_bias, o_second_gain, o_second_shift, o_exp, o_exp_bias, o_con, o_con_bias,
    ) = outs
    o_result[...] = result[...]
    o_delta[...] = delta[...]
    for source, target in ((s_in, o_in), (s_out, o_out), (s_con, o_con), (s_exp, o_exp)):
        height = source.shape[1]
        for half in range(2):
            target[half * height : half * height + height, :] = source[half].astype(FULL)
    for row, target in enumerate(
        (o_first_gain, o_first_shift, o_direct, o_out_bias, o_second_gain, o_second_shift, o_con_bias)
    ):
        target[...] = s_small[0, row : row + 1, 0:96].reshape(96)
    wide = jnp.concatenate([s_small[0, 8:16, :], s_small[0, 16:24, :], s_small[0, 24:32, :]], axis=1)
    o_in_bias[...] = wide[0:1, 0:288].reshape(288)
    o_short_b[...] = wide[1:2, 0:288].reshape(288)
    o_short_w[...] = wide[2:5, 0:288]
    o_exp_bias[...] = wide[5:6].reshape(384)
    for row, target in enumerate((o_inner_b, o_scale, o_middle_b)):
        target[...] = s_small[0, 32 + row : 33 + row, 0:8].reshape(8)
    o_inner_w[...] = s_small[0, 48:56, 0:33]
    o_middle_w[...] = s_small[0, 40:48, 0:64]
    o_filter_w[...] = s_small[1, :, 0:96]


def filter_constants(length, width):
    places = np.arange(LAGS, dtype=np.float64)
    scales = 0.0001 + np.arange(16, dtype=np.float64) * ((15.0 - 0.0001) / 15.0)
    phases = (2.0 * math.pi * places / length)[:, None] * scales[None, :]
    ramp = places / (length - 1)
    table = np.zeros((LAGS, 128), np.float32)
    table[:, 0] = ramp
    table[:, 1:17] = np.cos(phases)
    table[:, 17:33] = -np.sin(phases)
    rates = math.log(100.0) * (
        1.0 / 1.5 + (1.0 / 0.3 - 1.0 / 1.5) * np.arange(width, dtype=np.float64) / (width - 1)
    )
    return table, np.exp(-ramp[:, None] * rates[None, :]).astype(np.float32)


def block_device(
    tokens, segment_ids, cotangent, first_gain, first_shift, input_weight, input_bias,
    short_weight, short_bias, inner_weight, inner_bias, sine_scale, middle_weight, middle_bias,
    filter_weight, direct_gain, output_weight, output_bias, second_gain, second_shift,
    expand_weight, expand_bias, contract_weight, contract_bias,
):
    blocks, _, length, width = tokens.shape
    rows = blocks * length
    features, decay = filter_constants(length, width)

    small_members = (
        first_gain, first_shift, input_bias, short_weight, short_bias, inner_weight, inner_bias,
        sine_scale, middle_weight, middle_bias, filter_weight, direct_gain, output_bias,
        second_gain, second_shift, expand_bias, contract_bias,
    )

    def halved(member):
        return member.reshape(2, member.shape[0] // 2, member.shape[1])

    shards = [halved(m) for m in (input_weight, output_weight, contract_weight, expand_weight)]
    inputs = (
        tokens.reshape(rows, width), segment_ids.reshape(blocks, length),
        cotangent.reshape(rows, width),
    ) + tuple(m.T if m is inner_weight else m for m in small_members) + tuple(shards) + (
        jnp.asarray(features), jnp.asarray(decay),
    )
    shapes = [m.shape[1:] for m in shards] + [(SMALL_ROWS, 128)]
    outs = [
        jax.ShapeDtypeStruct((rows, width), LOW),
        jax.ShapeDtypeStruct((rows, width), FULL),
    ] + [jax.ShapeDtypeStruct((2,) + s, kind) for s, kind in zip(shapes, (LOW,) * 4 + (FULL,))]
    count = len(GATHER_CHUNKS)
    crossing = sum(1 for chunk in GATHER_CHUNKS if chunk[3] == SPLIT)
    leaving = len({(chunk[0], chunk[3]) if chunk[0] != 3 else chunk[:2] for chunk in GATHER_CHUNKS})
    vm = pltpu.VMEM
    scratch = [vm((rows, width), kind) for kind in (LOW, LOW, LOW, FULL)]
    scratch += [vm(s, kind) for s, kind in zip(shapes, (LOW,) * 4 + (FULL,))]
    scratch += [vm((4, 2, 2) + s, LOW) for s in shapes]
    scratch += [
        vm((4, 2, 2) + shapes[2], LOW), vm((4, 2, 2) + shapes[4], FULL), vm((2, SMALL_ROWS, 128), LOW),
        vm((2 * SMALL_ROWS, 128), FULL),
        vm((8, width), FULL), vm((8, 3 * width), FULL), vm((1, 4 * width), FULL), vm((8, 128), FULL),
        vm((128, 128), FULL), vm((128, width), FULL), vm((LAGS, width), FULL), vm((LAGS, width), FULL),
    ]
    scratch += [vm((LAGS, 128), FULL)] * 6
    scratch += [vm((rows, 128), jnp.int32)] * 2
    scratch += [
        vm((rows, width), LOW), vm((3, rows, width), FULL), vm((3, rows, width), FULL),
        vm((rows, width), FULL), vm((rows, width), LOW), vm((rows, width), FULL),
        vm((rows, width), LOW),
        vm((rows, 4 * width), FULL), vm((rows, 4 * width), LOW), vm((rows, 4 * width), LOW),
        vm((rows, width), FULL), vm((rows, width), FULL), vm((rows, width), FULL),
        vm((rows, width), LOW), vm((3, rows, width), LOW),
        vm((7, 8, width), FULL), vm((5, 8, 3 * width), FULL), vm((8, 4 * width), FULL),
    ]
    for matrix, columns, span, kind in REDUCE_GROUPS:
        n, high = len(columns), shapes[matrix][0]
        of = FULL if matrix == 4 else LOW
        v = span // 2 if kind in SPLITS else span
        core = vm((n, 4, 2, high, span), of)
        last = vm((n, 2, high, v), of)
        if kind in FARS:
            scratch += [core, vm((n, 4, high, v), of), vm((n, 3, high, v), of), last]
        else:
            side_planes, line_planes = ((), (2,)) if kind == LINE else ((4,), ())
            scratch += [
                core, vm((n,) + side_planes + (high, v), of),
                vm((n, 2) + line_planes + (high, v), of), vm((n, 2) + line_planes + (high, v), of),
                vm((n,) + line_planes + (high, v), of), last,
            ]
        if kind in SPLITS:
            scratch.append(vm((n, 4, 2, high, v), of))
    total = len(REDUCE_ORDER)
    splits = sum(len(g[1]) for g in REDUCE_GROUPS if g[3] in SPLITS)
    dma = pltpu.SemaphoreType.DMA
    scratch += [
        dma((4, count)), dma((3, crossing)), dma((count,)), dma((6, leaving)), dma((9,)),
        dma((6, total)), dma((splits,)), dma((8, len(REDUCE_GROUPS))), dma((len(REDUCE_GROUPS),)),
        dma((len(REDUCE_GROUPS),)),
    ]
    in_vmem = pl.BlockSpec(memory_space=pltpu.VMEM)
    anywhere = pl.BlockSpec(memory_space=pl.ANY)
    parts = pl.pallas_call(
        block_kernel,
        out_shape=outs,
        in_specs=[anywhere, in_vmem, anywhere] + [in_vmem] * 17 + [anywhere] * 4 + [in_vmem] * 2,
        out_specs=[anywhere] * len(outs),
        scratch_shapes=scratch,
        compiler_params=pltpu.CompilerParams(
            collective_id=0, has_side_effects=True, vmem_limit_bytes=67043328
        ),
    )(*inputs)
    members = (
        first_gain, first_shift, input_weight, input_bias, short_weight, short_bias, inner_weight,
        inner_bias, sine_scale, middle_weight, middle_bias, filter_weight, direct_gain,
        output_weight, output_bias, second_gain, second_shift, expand_weight, expand_bias,
        contract_weight, contract_bias,
    )
    final = [outs[0], outs[1]] + [
        jax.ShapeDtypeStruct(m.shape[::-1] if m is inner_weight else m.shape, FULL) for m in members
    ]
    done = pl.pallas_call(
        unpack_kernel,
        out_shape=final,
        in_specs=[in_vmem] * 7,
        out_specs=[in_vmem] * len(final),
    )(*parts)
    done = [m.T if n == INNER_OUT else m for n, m in enumerate(done)]
    return (done[0].reshape(tokens.shape), done[1].reshape(tokens.shape)) + tuple(done[2:])


def per_device(
    tokens,
    segment_ids,
    cotangent,
    first_gain,
    first_shift,
    input_weight,
    input_bias,
    short_weight,
    short_bias,
    inner_weight,
    inner_bias,
    sine_scale,
    middle_weight,
    middle_bias,
    filter_weight,
    direct_gain,
    output_weight,
    output_bias,
    second_gain,
    second_shift,
    expand_weight,
    expand_bias,
    contract_weight,
    contract_bias,
):
    micro_count, local_sequences, length, width = tokens.shape
    row_count = local_sequences * length
    tables = wave_tables(length)

    def fetch_mixer():
        return (
            lax.all_gather(first_gain, "shard", axis=0, tiled=True),
            lax.all_gather(first_shift, "shard", axis=0, tiled=True),
            lax.all_gather(input_weight, "shard", axis=0, tiled=True),
            lax.all_gather(input_bias, "shard", axis=0, tiled=True),
            lax.all_gather(short_weight, "shard", axis=1, tiled=True),
            lax.all_gather(short_bias, "shard", axis=0, tiled=True),
            lax.all_gather(inner_weight, "shard", axis=1, tiled=True),
            lax.all_gather(inner_bias, "shard", axis=0, tiled=True),
            lax.all_gather(sine_scale, "shard", axis=0, tiled=True),
            lax.all_gather(middle_weight, "shard", axis=0, tiled=True),
            lax.all_gather(middle_bias, "shard", axis=0, tiled=True),
            lax.all_gather(filter_weight, "shard", axis=1, tiled=True),
            lax.all_gather(direct_gain, "shard", axis=0, tiled=True),
            lax.all_gather(output_weight, "shard", axis=0, tiled=True),
            lax.all_gather(output_bias, "shard", axis=0, tiled=True),
        )

    def fetch_dense():
        return (
            lax.all_gather(second_gain, "shard", axis=0, tiled=True),
            lax.all_gather(second_shift, "shard", axis=0, tiled=True),
            lax.all_gather(expand_weight, "shard", axis=0, tiled=True),
            lax.all_gather(expand_bias, "shard", axis=0, tiled=True),
            lax.all_gather(contract_weight, "shard", axis=0, tiled=True),
            lax.all_gather(contract_bias, "shard", axis=0, tiled=True),
        )

    results = []
    input_deltas = []
    mixer_total = None
    dense_total = None
    for micro_index in range(micro_count):
        mixer_parts = fetch_mixer()
        dense_parts = fetch_dense()
        kernel = filter_taps(
            to_float(mixer_parts[6]),
            to_float(mixer_parts[7]),
            to_float(mixer_parts[8]),
            to_float(mixer_parts[9]),
            to_float(mixer_parts[10]),
            to_float(mixer_parts[11]),
            length,
        )
        kernel, kernel_wave = (kernel, spectrum(tables, kernel))
        kernel_real, kernel_imag = kernel_wave
        segment_block = segment_ids[micro_index]
        membership = (
            segment_block[:, None, :] == jnp.arange(DOCS, dtype=jnp.int32)[None, :, None]
        ).astype(jnp.float32)
        flat_tokens = tokens[micro_index].reshape(row_count, width).astype(jnp.float32)
        normed_first = normalize(
            flat_tokens, to_float(mixer_parts[0]), to_float(mixer_parts[1])
        ).astype(jnp.bfloat16)
        projected = jnp.dot(
            normed_first, mixer_parts[2], preferred_element_type=jnp.float32
        ) + to_float(mixer_parts[3])
        projected_rows = projected.reshape(local_sequences, length, 3 * width)
        short_out = short_filter(
            projected_rows, segment_block, to_float(mixer_parts[4]), to_float(mixer_parts[5])
        )
        gate_out = short_out[:, :, :width]
        gate_in = short_out[:, :, width : 2 * width]
        values = short_out[:, :, 2 * width :]
        carried = values * gate_in
        direct = to_float(mixer_parts[12])
        carried_real, carried_imag = spectrum(tables, carried[:, None] * membership[:, :, :, None])
        conv_pieces = inverse(
            tables,
            carried_real * kernel_real - carried_imag * kernel_imag,
            carried_real * kernel_imag + carried_imag * kernel_real,
        )
        convolved = jnp.sum(conv_pieces * membership[:, :, :, None], axis=1) + direct * carried
        gated_low = (convolved * gate_out).astype(jnp.bfloat16).reshape(row_count, width)
        mixed_out = jnp.dot(
            gated_low, mixer_parts[13], preferred_element_type=jnp.float32
        ) + to_float(mixer_parts[14])
        residual = flat_tokens + mixed_out
        second_gain_f = to_float(dense_parts[0])
        second_shift_f = to_float(dense_parts[1])
        normed_second = normalize(residual, second_gain_f, second_shift_f).astype(jnp.bfloat16)
        hidden_pre = jnp.dot(
            normed_second, dense_parts[2], preferred_element_type=jnp.float32
        ) + to_float(dense_parts[3])
        hidden_post = smooth_gate(hidden_pre).astype(jnp.bfloat16)
        result = (
            residual
            + jnp.dot(hidden_post, dense_parts[4], preferred_element_type=jnp.float32)
            + to_float(dense_parts[5])
        )
        results.append(result.astype(jnp.bfloat16).reshape(local_sequences, length, width))
        back_mixer = fetch_mixer()
        back_dense = fetch_dense()
        upstream = cotangent[micro_index].reshape(row_count, width)
        upstream_float = upstream.astype(jnp.float32)
        delta_contract_weight = jnp.einsum(
            "tf,td->fd", hidden_post, upstream, preferred_element_type=jnp.float32
        )
        delta_contract_bias = jnp.sum(upstream_float, axis=0)
        back_hidden = jnp.einsum(
            "td,fd->tf", upstream, back_dense[4], preferred_element_type=jnp.float32
        )
        back_pre = jax.vjp(smooth_gate, hidden_pre)[1](back_hidden)[0].astype(jnp.bfloat16)
        delta_expand_weight = jnp.einsum(
            "td,tf->df", normed_second, back_pre, preferred_element_type=jnp.float32
        )
        delta_expand_bias = jnp.sum(back_pre.astype(jnp.float32), axis=0)
        back_second = jnp.einsum(
            "tf,df->td", back_pre, back_dense[2], preferred_element_type=jnp.float32
        )
        second_pull = jax.vjp(
            normalize, residual, to_float(back_dense[0]), to_float(back_dense[1])
        )[1]
        back_norm_second, delta_second_gain, delta_second_shift = second_pull(back_second)
        back_residual = upstream_float + back_norm_second
        back_mixed = back_residual.astype(jnp.bfloat16)
        delta_output_weight = jnp.einsum(
            "td,te->de", gated_low, back_mixed, preferred_element_type=jnp.float32
        )
        delta_output_bias = jnp.sum(back_mixed.astype(jnp.float32), axis=0)
        back_gated = jnp.einsum(
            "te,de->td", back_mixed, back_mixer[13], preferred_element_type=jnp.float32
        ).reshape(local_sequences, length, width)
        back_conv = back_gated * gate_out
        grad_real, grad_imag = spectrum(tables, back_conv[:, None] * membership[:, :, :, None])
        carried_back_pieces = inverse(
            tables,
            grad_real * kernel_real + grad_imag * kernel_imag,
            grad_imag * kernel_real - grad_real * kernel_imag,
        )
        back_carried = (
            jnp.sum(carried_back_pieces * membership[:, :, :, None], axis=1) + direct * back_conv
        )
        cross_real = jnp.sum(grad_real * carried_real + grad_imag * carried_imag, axis=(0, 1))
        cross_imag = jnp.sum(grad_imag * carried_real - grad_real * carried_imag, axis=(0, 1))
        back_kernel = inverse(tables, cross_real, cross_imag)
        delta_direct = jnp.sum(back_conv * carried, axis=(0, 1))
        back_short = jnp.concatenate(
            [back_gated * convolved, back_carried * values, back_carried * gate_in], axis=2
        )
        short_pull = jax.vjp(
            lambda rows_in, taps_in, offset_in: short_filter(
                rows_in, segment_block, taps_in, offset_in
            ),
            projected_rows,
            to_float(back_mixer[4]),
            to_float(back_mixer[5]),
        )[1]
        back_projected, delta_short_weight, delta_short_bias = short_pull(back_short)
        back_projected = back_projected.reshape(row_count, 3 * width).astype(jnp.bfloat16)
        delta_input_weight = jnp.einsum(
            "td,tp->dp", normed_first, back_projected, preferred_element_type=jnp.float32
        )
        delta_input_bias = jnp.sum(back_projected.astype(jnp.float32), axis=0)
        back_first = jnp.einsum(
            "tp,dp->td", back_projected, back_mixer[2], preferred_element_type=jnp.float32
        )
        first_pull = jax.vjp(
            normalize, flat_tokens, to_float(back_mixer[0]), to_float(back_mixer[1])
        )[1]
        back_norm_first, delta_first_gain, delta_first_shift = first_pull(back_first)
        input_deltas.append(
            (back_residual + back_norm_first).reshape(local_sequences, length, width)
        )
        filter_pull = jax.vjp(
            lambda weight_one, bias_one, scale_all, weight_two, bias_two, weight_three: filter_taps(
                weight_one, bias_one, scale_all, weight_two, bias_two, weight_three, length
            ),
            to_float(back_mixer[6]),
            to_float(back_mixer[7]),
            to_float(back_mixer[8]),
            to_float(back_mixer[9]),
            to_float(back_mixer[10]),
            to_float(back_mixer[11]),
        )[1]
        filter_deltas = filter_pull(back_kernel)
        mixer_part = (
            delta_first_gain,
            delta_first_shift,
            delta_input_weight,
            delta_input_bias,
            delta_short_weight,
            delta_short_bias,
            filter_deltas[0],
            filter_deltas[1],
            filter_deltas[2],
            filter_deltas[3],
            filter_deltas[4],
            filter_deltas[5],
            delta_direct,
            delta_output_weight,
            delta_output_bias,
        )
        dense_part = (
            delta_second_gain,
            delta_second_shift,
            delta_expand_weight,
            delta_expand_bias,
            delta_contract_weight,
            delta_contract_bias,
        )
        if micro_index == 0:
            mixer_total = mixer_part
            dense_total = dense_part
        else:
            mixer_total = jax.tree.map(jnp.add, mixer_total, mixer_part)
            dense_total = jax.tree.map(jnp.add, dense_total, dense_part)
    dense_total = (
        lax.psum_scatter(dense_total[0], "shard", scatter_dimension=0, tiled=True),
        lax.psum_scatter(dense_total[1], "shard", scatter_dimension=0, tiled=True),
        lax.psum_scatter(dense_total[2], "shard", scatter_dimension=0, tiled=True),
        lax.psum_scatter(dense_total[3], "shard", scatter_dimension=0, tiled=True),
        lax.psum_scatter(dense_total[4], "shard", scatter_dimension=0, tiled=True),
        lax.psum_scatter(dense_total[5], "shard", scatter_dimension=0, tiled=True),
    )
    mixer_total = (
        lax.psum_scatter(mixer_total[0], "shard", scatter_dimension=0, tiled=True),
        lax.psum_scatter(mixer_total[1], "shard", scatter_dimension=0, tiled=True),
        lax.psum_scatter(mixer_total[2], "shard", scatter_dimension=0, tiled=True),
        lax.psum_scatter(mixer_total[3], "shard", scatter_dimension=0, tiled=True),
        lax.psum_scatter(mixer_total[4], "shard", scatter_dimension=1, tiled=True),
        lax.psum_scatter(mixer_total[5], "shard", scatter_dimension=0, tiled=True),
        lax.psum_scatter(mixer_total[6], "shard", scatter_dimension=1, tiled=True),
        lax.psum_scatter(mixer_total[7], "shard", scatter_dimension=0, tiled=True),
        lax.psum_scatter(mixer_total[8], "shard", scatter_dimension=0, tiled=True),
        lax.psum_scatter(mixer_total[9], "shard", scatter_dimension=0, tiled=True),
        lax.psum_scatter(mixer_total[10], "shard", scatter_dimension=0, tiled=True),
        lax.psum_scatter(mixer_total[11], "shard", scatter_dimension=1, tiled=True),
        lax.psum_scatter(mixer_total[12], "shard", scatter_dimension=0, tiled=True),
        lax.psum_scatter(mixer_total[13], "shard", scatter_dimension=0, tiled=True),
        lax.psum_scatter(mixer_total[14], "shard", scatter_dimension=0, tiled=True),
    )
    summed = lax.psum(
        (
            mixer_total[0],
            mixer_total[1],
            mixer_total[2],
            mixer_total[3],
            mixer_total[4],
            mixer_total[5],
            mixer_total[6],
            mixer_total[7],
            mixer_total[8],
            mixer_total[9],
            mixer_total[10],
            mixer_total[11],
            mixer_total[12],
            mixer_total[13],
            mixer_total[14],
            dense_total[0],
            dense_total[1],
            dense_total[2],
            dense_total[3],
            dense_total[4],
            dense_total[5],
        ),
        "rep",
    )
    return (jnp.stack(results), jnp.stack(input_deltas)) + tuple(summed)


def solution(mesh):
    placed = (
        P(None, ("rep", "shard"), None, None),
        P(None, ("rep", "shard"), None),
        P(None, ("rep", "shard"), None, None),
        P("shard"),
        P("shard"),
        P("shard", None),
        P("shard"),
        P(None, "shard"),
        P("shard"),
        P(None, "shard"),
        P("shard"),
        P("shard"),
        P("shard", None),
        P("shard"),
        P(None, "shard"),
        P("shard"),
        P("shard", None),
        P("shard"),
        P("shard"),
        P("shard"),
        P("shard", None),
        P("shard"),
        P("shard", None),
        P("shard"),
    )
    blocked = dict(mesh.shape) == {"rep": 4, "shard": 8}
    return jax.shard_map(
        block_device if blocked else per_device,
        mesh=mesh,
        in_specs=placed,
        out_specs=(
            P(None, ("rep", "shard"), None, None),
            P(None, ("rep", "shard"), None, None),
            P("shard"),
            P("shard"),
            P("shard", None),
            P("shard"),
            P(None, "shard"),
            P("shard"),
            P(None, "shard"),
            P("shard"),
            P("shard"),
            P("shard", None),
            P("shard"),
            P(None, "shard"),
            P("shard"),
            P("shard", None),
            P("shard"),
            P("shard"),
            P("shard"),
            P("shard", None),
            P("shard"),
            P("shard", None),
            P("shard"),
        ),
        check_vma=False,
    )
```
